32 devices in a mesh: dp: 8 (over z, x), tensor: 4 (over y, core).
Axes of the slice: x: 2, y: 2, z: 4, core: 2. Of those that a mesh axis runs over, the one named last changes fastest.
Arguments:
- inputs: bfloat16 [3, 2048, 2048], P(None, ('dp', 'tensor')), may hold values from -6 to 6
- cotangent: bfloat16 [3, 2048, 2048], P(None, ('dp', 'tensor')), may hold values from -6 to 6
- doc_ids: int32 [3, 2048], replicated, may hold values from 0 to 7, never falling along the last dimension, each value on 1 to 1280 neighbouring positions
- attn_gain: bfloat16 [2048], P('dp'), may hold values from 0.5 to 1.5
- attn_shift: bfloat16 [2048], P('dp'), may hold values from -3 to 3
- w_query: bfloat16 [2048, 2048], P('dp', 'tensor'), may hold values from -0.125 to 0.125
- w_keyval: bfloat16 [2048, 256], P('dp'), may hold values from -0.125 to 0.125
- w_attn_out: bfloat16 [2048, 2048], P('tensor', 'dp'), may hold values from -2 to 2
- mlp_gain: bfloat16 [2048], P('dp'), may hold values from 0.5 to 1.5
- mlp_shift: bfloat16 [2048], P('dp'), may hold values from -3 to 3
- w_expand: bfloat16 [2048, 8192], P('dp', 'tensor'), may hold values from -0.125 to 0.125
- w_reduce: bfloat16 [8192, 2048], P('tensor', 'dp'), may hold values from -0.0625 to 0.0625
Outputs:
- outputs: bfloat16 [3, 2048, 2048], P(None, ('dp', 'tensor'))
- grad_inputs: float32 [3, 2048, 2048], P(None, ('dp', 'tensor'))
- grad_attn_gain: float32 [2048], P(('dp', 'tensor'))
- grad_attn_shift: float32 [2048], P(('dp', 'tensor'))
- grad_query: float32 [2048, 2048], P('dp', 'tensor')
- grad_keyval: float32 [2048, 256], P(('dp', 'tensor'))
- grad_attn_out: float32 [2048, 2048], P('tensor', 'dp')
- grad_mlp_gain: float32 [2048], P(('dp', 'tensor'))
- grad_mlp_shift: float32 [2048], P(('dp', 'tensor'))
- grad_expand: float32 [2048, 8192], P('dp', 'tensor')
- grad_reduce: float32 [8192, 2048], P('tensor', 'dp')
The draws below stay inside these ranges and needn't reach their ends.
Inputs may be any that keep to these rules, and one draw needn't show every extreme that they name: `doc_ids`: within each row the ids never fall; each document spans 1 to 1280 tokens, and one spans exactly 1280.
All inputs are finite; a program needn't handle non-finite values.
Results may differ from the reference program's by a relative error of at most 0.02.
Values may be sent and summed in bfloat16 or wider, within the bound.
A program may use at most 120 MiB of HBM per device.

```python
import math
import jax
import jax.numpy as jnp
import numpy as np
from jax import lax

D = 2048
H = 16
HD = 128
FF = 8192
MB = 3
BLOCK = 256
SEQ = 2048
LONGEST = 1280
N_DP = 8


def shard_levels(rng, dims, cuts, low, top_value):
    level = 1.0
    for position, shards_of in cuts:
        heights = jax.random.uniform(jax.random.fold_in(jax.random.fold_in(rng, 6), position), (shards_of,), jnp.float32, low / len(cuts), top_value / len(cuts))
        level = level * jnp.repeat(jnp.exp(heights), dims[position] // shards_of).reshape((-1,) + (1,) * (len(dims) - 1 - position))
    return level


def split_up(number_of, total, most, lean):
    portions = [(1 << 20) // math.isqrt(grade ** lean) + 1 for grade in range(2, number_of + 1)]
    spare, given = total - most - (number_of - 1), [1] * (number_of - 1)
    while spare > 0:
        movable = [i for i in range(number_of - 1) if given[i] < most]
        whole, budget = sum([portions[i] for i in movable]), spare
        for i in movable:
            extra = min(most - given[i], max(1, budget * portions[i] // whole), spare)
            given[i] = given[i] + extra
            spare = spare - extra
    return np.array([most] + given)


def ragged(key, amount, total, most, skew):
    if amount == 2:
        one = jax.random.randint(key, (), max(1, total - most), min(most, total - 1) + 1)
        return jnp.stack([one, total - one])
    tallies = jnp.asarray(split_up(amount, total, most, skew), jnp.int32)
    pairs = (amount - 1) // 2
    source_of, receiver = tallies[1:1 + 2 * pairs:2], tallies[2:2 + 2 * pairs:2]
    room = jnp.minimum(source_of - 1, most - receiver)
    moved = jax.random.randint(jax.random.fold_in(key, 1), (pairs,), 0, 1 << 20) % (room + 1)
    tallies = tallies.at[1:1 + 2 * pairs:2].set(source_of - moved).at[2:2 + 2 * pairs:2].set(receiver + moved)
    return tallies[jax.random.permutation(jax.random.fold_in(key, 2), amount)]


def normal_values(stream_key, shape, scale, bound, shards=(), held_as=jnp.bfloat16):
    entries = scale * jax.random.normal(stream_key, shape, jnp.float32)
    if shards:
        entries = entries * shard_levels(stream_key, shape, shards, -0.22, 0.18)
    return jnp.clip(entries, -bound, bound).astype(held_as)


def setup_inputs(seed: int = 0) -> dict:
    arg_keys = jax.random.split(jax.random.key(seed), 13)
    return {
        "inputs": normal_values(arg_keys[0], (MB, SEQ, D), 1.0, 6.0, ((1, 32),)),
        "cotangent": normal_values(arg_keys[1], (MB, SEQ, D), 1.0, 6.0, ((1, 32),)),
        "doc_ids": jax.vmap(lambda own: jnp.searchsorted(jnp.cumsum(ragged(own, N_DP, SEQ, LONGEST, 0)), jnp.arange(SEQ), side="right"))(jax.random.split(arg_keys[2], MB)).reshape((MB, SEQ)).astype(jnp.int32),
        "attn_gain": jnp.clip(1.0 + 0.1 * jax.random.normal(arg_keys[3], (D,), jnp.float32), 0.5, 1.5).astype(jnp.bfloat16),
        "attn_shift": normal_values(arg_keys[4], (D,), 0.3, 3.0, ((0, 8),)),
        "w_query": normal_values(arg_keys[5], (D, H * HD), D ** -0.5, 0.125, ((0, 8), (1, 4))),
        "w_keyval": normal_values(arg_keys[6], (D, 2 * HD), D ** -0.5, 0.125, ((0, 8),)),
        "w_attn_out": normal_values(arg_keys[7], (H * HD, D), (max(H * HD // 256, 8)) ** -0.5, 2.0, ((0, 4), (1, 8))),
        "mlp_gain": jnp.clip(1.0 + 0.1 * jax.random.normal(arg_keys[8], (D,), jnp.float32), 0.5, 1.5).astype(jnp.bfloat16),
        "mlp_shift": normal_values(arg_keys[9], (D,), 0.3, 3.0, ((0, 8),)),
        "w_expand": normal_values(arg_keys[10], (D, FF), D ** -0.5, 0.125, ((0, 8), (1, 4))),
        "w_reduce": normal_values(arg_keys[11], (FF, D), FF ** -0.5, 0.0625, ((0, 4), (1, 8))),
    }


EPSILON = 1e-05
NEG_FILL = -1e+30
PRECISE = lax.Precision.HIGHEST

@jax.custom_vjp
def low(v):
    return lax.optimization_barrier(v.astype(jnp.bfloat16)).astype(jnp.float32)

@jax.custom_vjp
def low_back(v):
    return v

def low_keep(v):
    return (low(v), None)

def low_pass(kept, grad):
    return (grad,)

def back_keep(v):
    return (v, None)

def back_low(kept, grad):
    return (low(grad),)
low.defvjp(low_keep, low_pass)
low_back.defvjp(back_keep, back_low)

def layer_norm(values, gain, shift):
    center = lax.optimization_barrier(jnp.mean(values, axis=-1, keepdims=True))
    centered = values - center
    variance = lax.optimization_barrier(jnp.mean(centered * centered, axis=-1, keepdims=True))
    return centered * lax.rsqrt(variance + EPSILON) * gain + shift

def attend(query_block, query_pos, query_doc, keys, values, key_doc, key_pos):
    raw = jnp.einsum('qhd,kd->qhk', query_block, keys, precision=PRECISE)
    scores = low_back(raw * (1.0 / math.sqrt(HD)))
    allowed = (query_doc[:, None] == key_doc[None, :]) & (key_pos[None, :] // BLOCK <= query_pos[:, None] // BLOCK)
    scores = jnp.where(allowed[:, None, :], scores, NEG_FILL)
    biggest = lax.optimization_barrier(jnp.max(scores, axis=-1, keepdims=True))
    weights = jnp.exp(scores - biggest)
    probs = weights / lax.optimization_barrier(jnp.sum(weights, axis=-1, keepdims=True))
    mixed = jnp.einsum('qhk,kd->qhd', low(probs), values, precision=PRECISE)
    return low_back(low(mixed))

def one_row(tokens, doc_row, params):
    attn_gain, attn_shift, w_query, w_keyval, w_attn_out, mlp_gain, mlp_shift, w_expand, w_reduce = params
    normed = low(layer_norm(tokens, attn_gain, attn_shift))
    queries = low_back(low(jnp.dot(normed, w_query, precision=PRECISE)))
    keys_vals = low_back(low(jnp.dot(normed, w_keyval, precision=PRECISE)))
    query_len = min(512, SEQ)
    block_count = SEQ // query_len
    positions = jnp.arange(SEQ, dtype=jnp.int32)

    def per_block(pieces):
        query_block, query_pos, query_doc = pieces
        return attend(query_block, query_pos, query_doc, keys_vals[:, :HD], keys_vals[:, HD:], doc_row, positions)
    mixed = lax.map(jax.checkpoint(per_block), (queries.reshape(block_count, query_len, H, HD), positions.reshape(block_count, query_len), doc_row.reshape(block_count, query_len)))
    mixed = mixed.reshape(SEQ, H * HD)
    branch = low_back(jnp.dot(mixed, w_attn_out, precision=PRECISE))
    middle = tokens + branch
    normed_two = low(layer_norm(middle, mlp_gain, mlp_shift))
    hidden = low_back(jnp.dot(normed_two, w_expand, precision=PRECISE))
    active = low(jax.nn.gelu(hidden, approximate=True))
    return middle + low_back(jnp.dot(active, w_reduce, precision=PRECISE))

def reference(inputs, cotangent, doc_ids, attn_gain, attn_shift, w_query, w_keyval, w_attn_out, mlp_gain, mlp_shift, w_expand, w_reduce):
    weight_list = tuple((entry.astype(jnp.float32) for entry in (attn_gain, attn_shift, w_query, w_keyval, w_attn_out, mlp_gain, mlp_shift, w_expand, w_reduce)))

    def forward(tokens, *params):

        def per_row(pieces):
            return one_row(pieces[0], pieces[1], params)
        return lax.map(per_row, (tokens, doc_ids))
    results, pullback = jax.vjp(forward, inputs.astype(jnp.float32), *weight_list)
    gradients = pullback(cotangent.astype(jnp.float32))
    return (results.astype(jnp.bfloat16), gradients[0], gradients[1], gradients[2], gradients[3], gradients[4], gradients[5], gradients[6], gradients[7], gradients[8], gradients[9])
```

```python
import functools
import math

import jax
import jax.numpy as jnp
from jax import lax
from jax.experimental import pallas as pl
from jax.experimental.pallas import tpu as pltpu
from jax.sharding import PartitionSpec as P

BLOCK = 256
EPSILON = 1e-05
NEG_FILL = -1e30
MESH = pl.DeviceIdType.MESH
ANY = pl.BlockSpec(memory_space=pl.ANY)
BF16 = jnp.bfloat16
F32 = jnp.float32


def layer_norm(values, gain, shift):
    center = jnp.mean(values, axis=-1, keepdims=True)
    centered = values - center
    variance = jnp.mean(centered * centered, axis=-1, keepdims=True)
    return centered * lax.rsqrt(variance + EPSILON) * gain + shift


def gelu_tanh(values):
    return jax.nn.gelu(values, approximate=True)


class Net:
    def __init__(self, nz, ny, send, recv, local):
        dp, tensor = lax.axis_index("dp"), lax.axis_index("tensor")
        self.nz, self.ny = nz, ny
        self.z, self.x = lax.div(dp, 2), lax.rem(dp, 2)
        self.y, self.c = lax.div(tensor, 2), lax.rem(tensor, 2)
        self.tensor = tensor
        self.send, self.recv, self.local = send, recv, local
        self.used = [0, 0]
        self.keys = {}

    def flip(self, value, by):
        return value + by - 2 * by * value if by else value

    def xy(self, dx, dy):
        return self.flip(self.x, dx), lax.rem(self.y + dy, self.ny) if dy else self.y

    def rank(self, dx=0, dy=0, dc=0):
        x, y = self.xy(dx, dy)
        return x * (2 * self.ny) + y * 2 + self.flip(self.c, dc)

    def device(self, dx=0, dy=0, dc=0, z=None):
        x, y = self.xy(dx, dy)
        return ((self.z if z is None else z) * 2 + x, y * 2 + self.flip(self.c, dc))

    def slot(self, key):
        if key not in self.keys:
            self.keys[key] = self.used[0]
            self.used[0] += 1
        return self.keys[key]

    def remote(self, key, src, dst, device):
        at = self.slot(key)
        return pltpu.make_async_remote_copy(
            src_ref=src,
            dst_ref=dst,
            send_sem=self.send.at[at],
            recv_sem=self.recv.at[at],
            device_id=device,
            device_id_type=MESH,
        )

    def copy(self, src, dst):
        at = self.used[1]
        self.used[1] += 1
        return pltpu.make_async_copy(src, dst, self.local.at[at])


def add_rows(dst, terms, rows=16):
    lead, height, _ = dst.shape
    rows = min(rows, height)
    steps = height // rows

    def body(step, carry):
        at, off = lax.div(step, steps), pl.multiple_of(lax.rem(step, steps) * rows, rows)
        total = terms[0][at, pl.ds(off, rows), :].astype(F32)
        for term in terms[1:]:
            total = total + term[at, pl.ds(off, rows), :].astype(F32)
        dst[at, pl.ds(off, rows), :] = total.astype(dst.dtype)
        return carry

    lax.fori_loop(0, lead * steps, body, 0)


class FaceGather:
    moves = ("x", "y", "c")

    def __init__(self, own, nz, ny):
        self.ins = [own]
        m, t, d = own.shape
        self.outs = [(jax.ShapeDtypeStruct((m, 4 * ny * t, d), own.dtype), ANY)]
        self.scratch = []
        self.half = t // 2
        self.remotes, self.locals = 8 * ny, 1

    def run(self, net, ins, outs, scratch):
        (own,), (out,), half = ins, outs, self.half
        dys = range(1, net.ny)

        def piece(dx, dy, h):
            return out.at[:, pl.ds(pl.multiple_of(net.rank(dx, dy) * 2 * half + h * half, half), half), :]

        mine = [own.at[:, pl.ds(h * half, half), :] for h in (0, 1)]
        keep = net.copy(own, out.at[:, pl.ds(pl.multiple_of(net.rank() * 2 * half, half), 2 * half), :])
        keep.start()
        sent = {}

        def send(key, src, dst, device):
            sent[key] = net.remote((id(self), key), src, dst, device)
            sent[key].start()

        send(("x", 0), mine[0], piece(0, 0, 0), net.device(1, 0))
        for dy in dys:
            send(("y", dy, 1), mine[1], piece(0, 0, 1), net.device(0, dy))
        send(("x", 1), mine[1], piece(0, 0, 1), net.device(1, 0))
        for dy in dys:
            send(("y", dy, 0), mine[0], piece(0, 0, 0), net.device(0, dy))
        for h in (0, 1):
            send(("c", h), mine[h], piece(0, 0, h), net.device(0, 0, 1))

        def share(key, dx, dy, h):
            send(("c",) + key, piece(dx, dy, h), piece(dx, dy, h), net.device(0, 0, 1))

        yield
        sent["x", 0].wait_recv()
        for dy in dys:
            send(("xy", dy), piece(1, 0, 0), piece(1, 0, 0), net.device(0, dy))
        share(("x", 0), 1, 0, 0)
        for dy in dys:
            yield
            sent["y", dy, 1].wait_recv()
            send(("yx", dy), piece(0, -dy % net.ny, 1), piece(0, -dy % net.ny, 1), net.device(1, 0))
            share(("y", dy, 1), 0, -dy % net.ny, 1)
        yield
        sent["x", 1].wait_recv()
        share(("x", 1), 1, 0, 1)
        for dy in dys:
            yield
            sent["y", dy, 0].wait_recv()
            share(("y", dy, 0), 0, -dy % net.ny, 0)
        for dy in dys:
            yield
            sent["xy", dy].wait_recv()
            share(("xy", dy), 1, -dy % net.ny, 0)
            yield
            sent["yx", dy].wait_recv()
            share(("yx", dy), 1, -dy % net.ny, 1)
        yield
        for key, copy in sent.items():
            if key[0] == "c":
                copy.wait_recv()
        for copy in sent.values():
            copy.wait_send()
        keep.wait()


class FaceScatter:
    moves = ("x", "y", "c")

    def __init__(self, part, nz, ny, dtype=F32):
        self.ins = [part]
        m, rows, d = part.shape
        t = rows // (4 * ny)
        self.outs = [(jax.ShapeDtypeStruct((m, t, d), dtype), pl.BlockSpec(memory_space=pltpu.VMEM))]
        half = t // 2
        self.half = half
        self.scratch = [
            pltpu.VMEM((2 * ny, m, t, d), BF16),
            pltpu.VMEM((2 * ny, m, t, d), BF16),
            pltpu.VMEM((ny, m, half, d), BF16),
            pltpu.VMEM((ny, m, half, d), BF16),
            pltpu.VMEM((2, m, half, d), BF16),
            pltpu.VMEM((2, ny, m, half, d), BF16),
        ]
        self.remotes, self.locals = 6 * ny + 4, 2 * ny

    def run(self, net, ins, outs, scratch):
        (part,), (out,), half = ins, outs, self.half
        work, from_core, x_diag, y_diag, x_in, y_in = scratch
        ny = net.ny
        dys = range(1, ny)
        order = [(1, dy) for dy in dys] + [(1, 0)] + [(0, dy) for dy in dys] + [(0, 0)]
        sent, loads = {}, {}

        def send(key, src, dst, device):
            sent[key] = net.remote((id(self), key), src, dst, device)
            sent[key].start()

        def rows(dx, dy, dc):
            return part.at[:, pl.ds(pl.multiple_of(net.rank(dx, dy, dc) * 2 * half, half), 2 * half), :]

        for dx, dy in order:
            at = dx * ny + dy
            loads[at] = net.copy(rows(dx, dy, 0), work.at[at])
            loads[at].start()
            send(("c", at), rows(dx, dy, 1), from_core.at[at], net.device(0, 0, 1))
        for dx, dy in order:
            at = dx * ny + dy
            yield
            loads[at].wait()
            sent["c", at].wait_recv()
            add_rows(work.at[at], [work.at[at], from_core.at[at]])
            top, low = work.at[at, :, pl.ds(0, half), :], work.at[at, :, pl.ds(half, half), :]
            if dx and dy:
                send(("xd", dy), top, x_diag.at[dy], net.device(1, 0))
                send(("yd", dy), low, y_diag.at[dy], net.device(0, dy))
            elif dx:
                send(("x", 0), top, x_in.at[0], net.device(1, 0))
            elif dy:
                send(("y", dy, 1), low, y_in.at[1, dy], net.device(0, dy))
        for dy in dys:
            yield
            sent["xd", dy].wait_recv()
            top = work.at[dy, :, pl.ds(0, half), :]
            add_rows(top, [top, x_diag.at[dy]])
            send(("y", dy, 0), top, y_in.at[0, dy], net.device(0, dy))
        low = work.at[ny, :, pl.ds(half, half), :]
        for dy in dys:
            yield
            sent["yd", dy].wait_recv()
            add_rows(low, [low, y_diag.at[dy]])
        send(("x", 1), low, x_in.at[1], net.device(1, 0))
        for h in (0, 1):
            yield
            sent["x", h].wait_recv()
            for dy in dys:
                sent["y", dy, h].wait_recv()
            side = pl.ds(h * half, half)
            add_rows(
                out.at[:, side, :],
                [work.at[0, :, side, :], x_in.at[h]] + [y_in.at[h, dy] for dy in dys],
            )
        for copy in sent.values():
            copy.wait_send()


class LineGather:
    moves = ("x", "line", "c")

    def __init__(self, shards, kinds, nz, ny):
        self.ins, self.kinds = list(shards), list(kinds)
        self.outs, self.scratch = [], []
        for shard, kind in zip(shards, kinds):
            rows, columns = shard.shape
            if kind == "row":
                shape = (rows * 2 * nz, columns // 2)
            elif kind == "col":
                shape = (rows // 2, columns * 2 * nz)
            else:
                shape = (rows * 2 * nz, columns)
            self.outs.append((jax.ShapeDtypeStruct(shape, shard.dtype), ANY))
        count = len(self.ins)
        self.remotes = count * (1 + 4 * (nz - 1)) + kinds.count("both") * (1 + 4 * (nz - 1))
        self.locals = count

    def run(self, net, ins, outs, scratch):
        nz, z = net.nz, net.z
        sent, locals_, shared = [], [], []
        weights = []
        for at, (shard, out, kind) in enumerate(zip(ins, outs, self.kinds)):
            rows, columns = shard.shape

            if kind == "row":
                half = columns // 2

                def mine(dx, shard=shard, half=half):
                    return shard.at[:, pl.ds(pl.multiple_of(net.flip(net.x, dx) * half, half), half)]

                def block(line, dx, out=out, rows=rows):
                    first = (line * 2 + net.flip(net.x, dx)) * rows
                    return out.at[pl.ds(pl.multiple_of(first, rows), rows), :]

            elif kind == "col":
                half = rows // 2

                def mine(dx, shard=shard, half=half):
                    return shard.at[pl.ds(pl.multiple_of(net.flip(net.x, dx) * half, half), half), :]

                def block(line, dx, out=out, columns=columns):
                    first = (line * 2 + net.flip(net.x, dx)) * columns
                    return out.at[:, pl.ds(pl.multiple_of(first, columns), columns)]

            else:
                half = rows // 2

                def mine(dx, shard=shard, half=half):
                    return shard.at[pl.ds(pl.multiple_of(net.c * half, half), half), :]

                def block(line, dx, out=out, rows=rows, half=half):
                    first = (line * 2 + net.flip(net.x, dx)) * rows + net.c * half
                    return out.at[pl.ds(pl.multiple_of(first, half), half), :]

            weights.append((at, kind, mine, block))

        def hop(at, dx, step, up, block, src=None):
            origin = z - (step - 1) if up else z + (step - 1)
            there = z + 1 if up else z - 1
            copy = net.remote(
                (id(self), at, dx, step, up),
                block(origin, dx) if src is None else src,
                block(origin, dx),
                net.device(z=there),
            )
            fits = (origin >= 0) & (there < nz) if up else (origin < nz) & (there >= 0)
            return copy, fits

        def start(at, dx, step, up, block, src=None):
            copy, fits = hop(at, dx, step, up, block, src)
            pl.when(fits)(copy.start)
            sent.append((copy, fits))

        def arrived(at, dx, step, up, block, kind):
            copy, _ = hop(at, dx, step, up, block)
            origin = z - step if up else z + step
            fits = origin >= 0 if up else origin < nz
            pl.when(fits)(copy.wait_recv)
            if kind == "both":
                share = net.remote(
                    (id(self), "c", at, dx, step, up), block(origin, dx), block(origin, dx), net.device(0, 0, 1)
                )
                pl.when(fits)(share.start)
                shared.append((share, fits))

        swaps = {}
        for at, kind, mine, block in weights:
            swaps[at] = net.remote((id(self), at, "x"), mine(1), block(z, 0), net.device(1, 0))
            swaps[at].start()
            for up in (True, False):
                start(at, 0, 1, up, block, mine(0))
        for at, kind, mine, block in weights:
            if kind == "both":
                whole = ins[at].shape[0]
                into = outs[at].at[pl.ds(pl.multiple_of((z * 2 + net.x) * whole, whole), whole), :]
                locals_.append(net.copy(ins[at], into))
            else:
                locals_.append(net.copy(mine(0), block(z, 0)))
            locals_[-1].start()
        for at, kind, mine, block in weights:
            yield
            swaps[at].wait_recv()
            for up in (True, False):
                start(at, 1, 1, up, block)
            if kind == "both":
                share = net.remote((id(self), "c", at), block(z, 1), block(z, 1), net.device(0, 0, 1))
                share.start()
                shared.append((share, None))
        for step in range(1, nz):
            for at, kind, mine, block in weights:
                for dx in (0, 1):
                    yield
                    for up in (True, False):
                        arrived(at, dx, step, up, block, kind)
                        if step < nz - 1:
                            start(at, dx, step + 1, up, block)
        yield
        for copy, fits in shared:
            if fits is None:
                copy.wait()
            else:
                pl.when(fits)(copy.wait)
        for copy, fits in sent:
            pl.when(fits)(copy.wait_send)
        for copy in swaps.values():
            copy.wait_send()
        for copy in locals_:
            copy.wait()


class LineScatter:
    moves = ("x", "line")

    def __init__(self, parts, kinds, nz, ny):
        self.ins, self.kinds = list(parts), list(kinds)
        self.outs, self.scratch = [], []
        for part, kind in zip(parts, kinds):
            rows, columns = part.shape
            shape = (rows // (2 * nz), columns) if kind == "row" else (rows, columns // (2 * nz))
            self.outs.append((jax.ShapeDtypeStruct((2,) + shape, BF16), ANY))
            for lead in (nz, nz, nz, 1):
                self.scratch.append(pltpu.VMEM((lead, 2) + shape, BF16))
        count = len(self.ins)
        self.remotes = count * (1 + 4 * (nz - 1))
        self.locals = count * (2 * nz + 1)

    def run(self, net, ins, outs, scratch):
        nz, z = net.nz, net.z
        sent, loads, stores = [], {}, []
        grads = []
        for at, (part, out, kind) in enumerate(zip(ins, outs, self.kinds)):
            work, down, up, mine = scratch[4 * at : 4 * at + 4]
            _, _, rows, columns = work.shape

            def block(line, dx, part=part, kind=kind, rows=rows, columns=columns):
                size = rows if kind == "row" else columns
                first = pl.ds(pl.multiple_of((line * 2 + net.flip(net.x, dx)) * size, size), size)
                return part.at[first, :] if kind == "row" else part.at[:, first]

            grads.append((at, out, work, down, up, mine))
            order = []
            for k in range(nz):
                order += [k, nz - 1 - k]
            for line in dict.fromkeys(order):
                for dx in (1, 0):
                    loads[at, line, dx] = net.copy(block(line, dx), work.at[line, dx])
                    loads[at, line, dx].start()

        for k in range(nz - 1):
            for dx in (1, 0):
                for at, out, work, down, up, mine in grads:
                    yield
                    for line, slots, toward in ((k, down, -1), (nz - 1 - k, up, 1)):
                        here, inbox = work.at[line, dx], slots.at[line, dx]
                        copy = net.remote(
                            (id(self), at, line, dx, toward), here, inbox, net.device(z=z + toward)
                        )
                        first = z == (nz - 1 if toward < 0 else 0)
                        sends = z > line if toward < 0 else z < line

                        def step(copy=copy, here=here, inbox=inbox, first=first, load=loads[at, line, dx]):
                            load.wait()

                            @pl.when(jnp.logical_not(first))
                            def _():
                                copy.wait_recv()
                                add_rows(_lead(here), [_lead(here), _lead(inbox)])

                            copy.start()

                        pl.when(sends)(step)
                        sent.append((copy, sends))
        swaps = []
        for dx in (1, 0):
            for at, out, work, down, up, mine in grads:
                yield
                total = mine.at[0, dx]
                for line in range(nz):

                    @pl.when(z == line)
                    def _(line=line, at=at, total=total, work=work, down=down, up=up):
                        loads[at, line, dx].wait()
                        terms = [_lead(work.at[line, dx])]
                        if line < nz - 1:
                            net.remote(
                                (id(self), at, line, dx, -1), total, down.at[line, dx], net.device(z=z - 1)
                            ).wait_recv()
                            terms.append(_lead(down.at[line, dx]))
                        if line > 0:
                            net.remote(
                                (id(self), at, line, dx, 1), total, up.at[line, dx], net.device(z=z + 1)
                            ).wait_recv()
                            terms.append(_lead(up.at[line, dx]))
                        add_rows(_lead(total), terms)

                if dx:
                    swaps.append(net.remote((id(self), at, "x"), total, out.at[net.x], net.device(1, 0)))
                    swaps[-1].start()
                else:
                    stores.append(net.copy(total, out.at[net.x]))
                    stores[-1].start()
        yield
        for copy, sends in sent:
            pl.when(sends)(copy.wait_send)
        for copy in swaps:
            copy.wait()
        for copy in stores:
            copy.wait()


def _lead(ref):
    return Lead(ref)


class Lead:
    def __init__(self, ref):
        self.ref, self.shape, self.dtype = ref, (1,) + tuple(ref.shape), ref.dtype

    def __getitem__(self, index):
        return self.ref[index[1], index[2]]

    def __setitem__(self, index, value):
        self.ref[index[1], index[2]] = value


class KeysGather:
    moves = ("x", "line", "c")

    def __init__(self, face, nz, ny):
        m, rows, width = face.shape
        self.ins = [face]
        self.outs = [(jax.ShapeDtypeStruct((m, nz * rows, width), face.dtype), ANY)]
        self.scratch = []
        self.remotes, self.locals = 4 * (nz - 1), 1

    def run(self, net, ins, outs, scratch):
        (face,), (out,) = ins, outs
        nz, z = net.nz, net.z
        _, rows, width = face.shape
        part, side = rows // 2, width // 2

        def block(line, dx, dc):
            first = pl.multiple_of(line * rows + net.flip(net.x, dx) * part, part)
            column = pl.multiple_of(net.flip(net.c, dc) * side, side)
            return out.at[:, pl.ds(first, part), pl.ds(column, side)]

        own = face.at[
            :,
            pl.ds(pl.multiple_of(net.x * part, part), part),
            pl.ds(pl.multiple_of(net.c * side, side), side),
        ]
        sent, shared = [], []

        def line_copy(step):
            origin = z - (step - 1)
            src = own if step == 1 else block(origin, 0, 0)
            return net.remote((id(self), step), src, block(origin, 0, 0), net.device(z=z + 1))

        def start(step):
            copy, fits = line_copy(step), (z - (step - 1) >= 0) & (z + 1 < nz)
            pl.when(fits)(copy.start)
            sent.append((copy, fits))

        start(1)
        keep = net.copy(face, out.at[:, pl.ds(pl.multiple_of(z * rows, rows), rows), :])
        keep.start()
        later = []
        for step in range(1, nz):
            yield
            fits = z - step >= 0
            pl.when(fits)(line_copy(step).wait_recv)
            if step < nz - 1:
                start(step + 1)
            here = block(z - step, 0, 0)
            across = net.remote((id(self), "x", step), here, here, net.device(1, 0))
            beside = net.remote((id(self), "c", step), here, here, net.device(0, 0, 1))
            for copy in (across, beside):
                pl.when(fits)(copy.start)
                sent.append((copy, fits))
            later.append((step, fits, across))
            shared.append((beside, fits))
        for step, fits, across in later:
            yield
            pl.when(fits)(across.wait_recv)
            there = block(z - step, 1, 0)
            beside = net.remote((id(self), "xc", step), there, there, net.device(0, 0, 1))
            pl.when(fits)(beside.start)
            sent.append((beside, fits))
            shared.append((beside, fits))
        yield
        for copy, fits in shared:
            pl.when(fits)(copy.wait_recv)
        for copy, fits in sent:
            pl.when(fits)(copy.wait_send)
        keep.wait()


class WholeScatter(FaceScatter):
    moves = ("x", "y", "c", "z")

    def __init__(self, part, nz, ny):
        m, _, rows, d = part.shape
        super().__init__(part.reshape(m * nz, rows, d), nz, ny)
        t = rows // (4 * ny)
        self.m, self.nz = m, nz
        self.outs = [(jax.ShapeDtypeStruct((m, t, d), F32), pl.BlockSpec(memory_space=pltpu.VMEM))]
        self.scratch = self.scratch + [pltpu.VMEM((m * nz, t, d), BF16), pltpu.VMEM((nz, m, t, d), BF16)]
        self.remotes = self.remotes + nz * m
        self.locals = self.locals + m

    def run(self, net, ins, outs, scratch):
        face, inbox = scratch[-2:]
        yield from super().run(net, ins, [face], scratch[:-2])
        nz, m = self.nz, self.m
        copies = []
        for far in range(1, nz):
            line = lax.rem(net.z + far, nz)
            for at in range(m):
                copies.append(
                    pltpu.make_async_remote_copy(
                        src_ref=face.at[at * nz + line],
                        dst_ref=inbox.at[far, at],
                        send_sem=net.send.at[net.slot((id(self), "z", far, at))],
                        recv_sem=net.recv.at[net.slot((id(self), "z", far, at))],
                        device_id=net.device(z=line),
                        device_id_type=MESH,
                    )
                )
                copies[-1].start()
        own = []
        for at in range(m):
            own.append(net.copy(face.at[at * nz + net.z], inbox.at[0, at]))
            own[-1].start()
        yield
        for copy in own:
            copy.wait()
        for copy in copies:
            copy.wait()
        add_rows(outs[0], [inbox.at[far] for far in range(nz)])


class PlaneGather:
    moves = ("plane",)

    def __init__(self, own, nz, ny):
        self.ins = [own]
        self.outs = [(jax.ShapeDtypeStruct((2 * nz,) + own.shape, own.dtype), ANY)]
        self.scratch = []
        self.remotes, self.locals = 2 * nz, 1

    def run(self, net, ins, outs, scratch):
        (own,), (out,) = ins, outs
        here = out.at[net.z * 2 + net.x]
        copies = []
        for far in range(net.nz):
            for dx in (0, 1):
                if far or dx:
                    line = lax.rem(net.z + far, net.nz)
                    copies.append(net.remote((id(self), far, dx), own, here, net.device(dx, z=line)))
                    copies[-1].start()
        keep = net.copy(own, here)
        keep.start()
        yield
        for copy in copies:
            copy.wait()
        keep.wait()


class SmallScatter:
    moves = ("face", "z")

    def __init__(self, part, nz, ny):
        ranks, _, rows, width = part.shape
        self.ins = [part]
        vmem = pl.BlockSpec(memory_space=pltpu.VMEM)
        self.outs = [(jax.ShapeDtypeStruct((rows, width), F32), vmem)]
        self.scratch = [
            pltpu.VMEM((ranks, nz, rows, width), F32),
            pltpu.VMEM((nz, rows, width), F32),
            pltpu.VMEM((nz, rows, width), F32),
        ]
        self.remotes, self.locals = ranks + nz, 2

    def run(self, net, ins, outs, scratch):
        (part,), (out,) = ins, outs
        inbox, total, line_in = scratch
        ny, nz = net.ny, net.nz
        copies = []
        for dx in (0, 1):
            for dy in range(ny):
                for dc in (0, 1):
                    if dx or dy or dc:
                        at = (dx * ny + dy) * 2 + dc
                        copies.append(
                            net.remote(
                                (id(self), at), part.at[net.rank(dx, dy, dc)], inbox.at[at], net.device(dx, dy, dc)
                            )
                        )
                        copies[-1].start()
        keep = net.copy(part.at[net.rank()], inbox.at[0])
        keep.start()
        yield
        keep.wait()
        for copy in copies:
            copy.wait()
        total[...] = jnp.sum(inbox[...], axis=0)
        lines = []
        for far in range(1, nz):
            line = lax.rem(net.z + far, nz)
            lines.append(net.remote((id(self), "z", far), total.at[line], line_in.at[far], net.device(z=line)))
            lines[-1].start()
        own = net.copy(total.at[net.z], line_in.at[0])
        own.start()
        yield
        own.wait()
        for copy in lines:
            copy.wait()
        out[...] = jnp.sum(line_in[...], axis=0)


def exchange(plans, nz, ny, collective_id, name):
    moves = set()
    for plan in plans:
        moves |= set(plan.moves)
    remotes = sum(plan.remotes for plan in plans)
    locals_ = max(1, sum(plan.locals for plan in plans))
    ins = [array for plan in plans for array in plan.ins]
    outs = [out for plan in plans for out in plan.outs]
    scratch = [entry for plan in plans for entry in plan.scratch]

    def kernel(*refs):
        in_refs, refs = refs[: len(ins)], refs[len(ins) :]
        out_refs, refs = refs[: len(outs)], refs[len(outs) :]
        scratch_refs, (send, recv, local) = refs[: len(scratch)], refs[len(scratch) :]
        net = Net(nz, ny, send, recv, local)
        peers = {}
        for far in range(nz):
            for dx in (0, 1):
                for dy in range(ny):
                    for dc in (0, 1):
                        kinds = set()
                        if not far:
                            kinds.add("face")
                            if dx and not dy and not dc:
                                kinds.add("x")
                            if dy and not dx and not dc:
                                kinds.add("y")
                            if dc and not dx and not dy:
                                kinds.add("c")
                        if far and not dx and not dy and not dc:
                            kinds.add("z")
                            if far in (1, nz - 1):
                                kinds.add("line")
                        if not dy and not dc:
                            kinds.add("plane")
                        if (far or dx or dy or dc) and kinds & moves:
                            line = lax.rem(net.z + far, nz) if far else None
                            peers[far, dx, dy, dc] = net.device(dx, dy, dc, line)
        barrier = pltpu.get_barrier_semaphore()
        for device in peers.values():
            pl.semaphore_signal(barrier, inc=1, device_id=device, device_id_type=MESH)
        pl.semaphore_wait(barrier, len(peers))
        running = []
        for plan in plans:
            mine = []
            for refs_of, count in ((in_refs, plan.ins), (out_refs, plan.outs), (scratch_refs, plan.scratch)):
                mine.append(list(refs_of[: len(count)]))
            in_refs = in_refs[len(plan.ins) :]
            out_refs = out_refs[len(plan.outs) :]
            scratch_refs = scratch_refs[len(plan.scratch) :]
            running.append(plan.run(net, *mine))
        while running:
            for steps in list(running):
                try:
                    next(steps)
                except StopIteration:
                    running.remove(steps)

    results = pl.pallas_call(
        kernel,
        out_shape=[shape for shape, _ in outs],
        in_specs=[ANY] * len(ins),
        out_specs=[spec for _, spec in outs],
        scratch_shapes=scratch
        + [
            pltpu.SemaphoreType.DMA((remotes,)),
            pltpu.SemaphoreType.DMA((remotes,)),
            pltpu.SemaphoreType.DMA((locals_,)),
        ],
        compiler_params=pltpu.CompilerParams(
            collective_id=collective_id, has_side_effects=True, vmem_limit_bytes=56 << 20
        ),
        name=name,
    )(*ins)
    results = list(results)
    grouped = []
    for plan in plans:
        grouped.append(results[: len(plan.outs)])
        results = results[len(plan.outs) :]
    return grouped


def masked_scores(queries, keys, query_doc, key_doc, scale):
    raw = lax.dot_general(queries, keys, (((1,), (1,)), ((), ())), preferred_element_type=F32) * scale
    return jnp.where(query_doc == key_doc, raw, NEG_FILL)


def attend_forward(queries, keys_vals, query_doc, key_doc, bounds, heads, head_dim):
    micro_count, rows, _ = queries.shape
    blocks = rows // BLOCK
    scale = 1.0 / math.sqrt(head_dim)
    tall = heads * BLOCK

    def kernel(bounds_ref, q_ref, kv_ref, qd_ref, kd_ref, out_ref, log_ref):
        at = pl.program_id(0) * blocks + pl.program_id(1)
        low, high = bounds_ref[2 * at], bounds_ref[2 * at + 1]
        queries = jnp.concatenate([q_ref[0, :, h * head_dim : (h + 1) * head_dim] for h in range(heads)], axis=0)
        doc = jnp.concatenate([qd_ref[0]] * heads, axis=0)

        def body(block, carry):
            top, total, mixed = carry
            first = pl.multiple_of(block * BLOCK, BLOCK)
            keys = kv_ref[0, pl.ds(first, BLOCK), :head_dim]
            values = kv_ref[0, pl.ds(first, BLOCK), head_dim:]
            scores = masked_scores(queries, keys, doc, kd_ref[0, :, pl.ds(first, BLOCK)], scale)
            new_top = jnp.maximum(top, jnp.max(scores, axis=-1, keepdims=True))
            weights = jnp.where(scores == NEG_FILL, 0.0, jnp.exp(scores - new_top))
            fade = jnp.exp(top - new_top)
            total = total * fade + jnp.sum(weights, axis=-1, keepdims=True)
            mixed = mixed * fade + jnp.dot(weights.astype(BF16), values, preferred_element_type=F32)
            return new_top, total, mixed

        top, total, mixed = lax.fori_loop(
            low,
            high,
            body,
            (
                jnp.full((tall, 1), NEG_FILL, F32),
                jnp.zeros((tall, 1), F32),
                jnp.zeros((tall, head_dim), F32),
            ),
        )
        mixed = (mixed / total).astype(BF16)
        for h in range(heads):
            out_ref[0, :, h * head_dim : (h + 1) * head_dim] = mixed[h * BLOCK : (h + 1) * BLOCK]
        log_ref[0, 0] = top + jnp.log(total)

    return pl.pallas_call(
        kernel,
        out_shape=[
            jax.ShapeDtypeStruct(queries.shape, BF16),
            jax.ShapeDtypeStruct((micro_count, blocks, tall, 1), F32),
        ],
        grid_spec=pltpu.PrefetchScalarGridSpec(
            num_scalar_prefetch=1,
            grid=(micro_count, blocks),
            in_specs=[
                pl.BlockSpec((1, BLOCK, heads * head_dim), lambda m, b, _: (m, b, 0)),
                pl.BlockSpec((1,) + keys_vals.shape[1:], lambda m, b, _: (m, 0, 0)),
                pl.BlockSpec((1, BLOCK, 1), lambda m, b, _: (m, b, 0)),
                pl.BlockSpec((1, 1, keys_vals.shape[1]), lambda m, b, _: (m, 0, 0)),
            ],
            out_specs=[
                pl.BlockSpec((1, BLOCK, heads * head_dim), lambda m, b, _: (m, b, 0)),
                pl.BlockSpec((1, 1, tall, 1), lambda m, b, _: (m, b, 0, 0)),
            ],
        ),
        compiler_params=pltpu.CompilerParams(vmem_limit_bytes=40 << 20),
        name="attend_forward",
    )(bounds, queries, keys_vals, query_doc, key_doc)


def attend_backward(queries, keys_vals, mixed, grad_mixed, log_total, query_doc, key_doc, bounds, heads, head_dim):
    micro_count, rows, _ = queries.shape
    blocks = rows // BLOCK
    seq_len = keys_vals.shape[1]
    scale = 1.0 / math.sqrt(head_dim)
    tall = heads * BLOCK

    def kernel(bounds_ref, q_ref, kv_ref, o_ref, do_ref, log_ref, qd_ref, kd_ref, gq_ref, gkv_ref, acc_ref):
        at = pl.program_id(0) * blocks + pl.program_id(1)
        low, high = bounds_ref[2 * at], bounds_ref[2 * at + 1]

        def stack(ref):
            return jnp.concatenate([ref[0, :, h * head_dim : (h + 1) * head_dim] for h in range(heads)], axis=0)

        @pl.when(pl.program_id(1) == 0)
        def _():
            acc_ref[...] = jnp.zeros_like(acc_ref)

        queries, grad = stack(q_ref), stack(do_ref)
        delta = jnp.sum(grad.astype(F32) * stack(o_ref).astype(F32), axis=-1, keepdims=True)
        doc = jnp.concatenate([qd_ref[0]] * heads, axis=0)
        log_total = log_ref[0, 0]

        def body(block, grad_queries):
            first = pl.multiple_of(block * BLOCK, BLOCK)
            keys = kv_ref[0, pl.ds(first, BLOCK), :head_dim]
            values = kv_ref[0, pl.ds(first, BLOCK), head_dim:]
            scores = masked_scores(queries, keys, doc, kd_ref[0, :, pl.ds(first, BLOCK)], scale)
            probs = jnp.where(scores == NEG_FILL, 0.0, jnp.exp(scores - log_total))
            grad_probs = lax.dot_general(grad, values, (((1,), (1,)), ((), ())), preferred_element_type=F32)
            grad_scores = (probs * (grad_probs - delta)).astype(BF16)
            across = (((0,), (0,)), ((), ()))
            acc_ref[pl.ds(first, BLOCK), :head_dim] += (
                lax.dot_general(grad_scores, queries, across, preferred_element_type=F32) * scale
            )
            acc_ref[pl.ds(first, BLOCK), head_dim:] += lax.dot_general(
                probs.astype(BF16), grad, across, preferred_element_type=F32
            )
            return grad_queries + jnp.dot(grad_scores, keys, preferred_element_type=F32)

        grad_queries = lax.fori_loop(low, high, body, jnp.zeros((tall, head_dim), F32))
        grad_queries = (grad_queries * scale).astype(BF16)
        for h in range(heads):
            gq_ref[0, :, h * head_dim : (h + 1) * head_dim] = grad_queries[h * BLOCK : (h + 1) * BLOCK]

        @pl.when(pl.program_id(1) == blocks - 1)
        def _():
            gkv_ref[0] = acc_ref[...].astype(BF16)

    wide = pl.BlockSpec((1, BLOCK, heads * head_dim), lambda m, b, _: (m, b, 0))
    row = pl.BlockSpec((1, seq_len, 2 * head_dim), lambda m, b, _: (m, 0, 0))
    return pl.pallas_call(
        kernel,
        out_shape=[
            jax.ShapeDtypeStruct(queries.shape, BF16),
            jax.ShapeDtypeStruct(keys_vals.shape, BF16),
        ],
        grid_spec=pltpu.PrefetchScalarGridSpec(
            num_scalar_prefetch=1,
            grid=(micro_count, blocks),
            in_specs=[
                wide,
                row,
                wide,
                wide,
                pl.BlockSpec((1, 1, tall, 1), lambda m, b, _: (m, b, 0, 0)),
                pl.BlockSpec((1, BLOCK, 1), lambda m, b, _: (m, b, 0)),
                pl.BlockSpec((1, 1, seq_len), lambda m, b, _: (m, 0, 0)),
            ],
            out_specs=[wide, row],
            scratch_shapes=[pltpu.VMEM((seq_len, 2 * head_dim), F32)],
        ),
        compiler_params=pltpu.CompilerParams(vmem_limit_bytes=40 << 20),
        name="attend_backward",
    )(bounds, queries, keys_vals, mixed, grad_mixed, log_total, query_doc, key_doc)


def local(
    inputs,
    cotangent,
    doc_ids,
    attn_gain,
    attn_shift,
    w_query,
    w_keyval,
    w_attn_out,
    mlp_gain,
    mlp_shift,
    w_expand,
    w_reduce,
):
    nz = lax.axis_size("dp") // 2
    tensor_count = lax.axis_size("tensor")
    ny = tensor_count // 2
    ranks = 2 * tensor_count
    micro_count, own_rows, width = inputs.shape
    face_rows = own_rows * ranks
    tokens = micro_count * face_rows
    seq_len = doc_ids.shape[1]
    head_dim = w_keyval.shape[1] // 2
    heads = w_query.shape[1] // (2 * head_dim)
    z = lax.axis_index("dp") // 2
    swap = functools.partial(exchange, nz=nz, ny=ny)
    on = (nz, ny)

    def dot(a, b):
        return jnp.dot(a, b, preferred_element_type=F32)

    def dot_bt(a, b):
        return lax.dot_general(a, b, (((1,), (1,)), ((), ())), preferred_element_type=F32)

    def dot_at(a, b):
        return lax.dot_general(a, b, (((0,), (0,)), ((), ())), preferred_element_type=F32)

    norms = jnp.stack([attn_gain, attn_shift, mlp_gain, mlp_shift])
    norms = jnp.concatenate([norms, jnp.zeros((4, norms.shape[1]), BF16)])
    (face_in,), (wq, wo, wkv), (norms,) = swap(
        [
            FaceGather(inputs, *on),
            LineGather([w_query, w_attn_out, w_keyval], ["row", "col", "both"], *on),
            PlaneGather(norms, *on),
        ],
        collective_id=1,
        name="gather_attention",
    )
    norms = norms[:, :4].transpose(1, 0, 2).reshape(4, width).astype(F32)
    gain_one, shift_one, gain_two, shift_two = norms[0], norms[1], norms[2], norms[3]

    normed = layer_norm(face_in.astype(F32), gain_one, shift_one).astype(BF16).reshape(tokens, width)
    queries = dot(normed, wq).astype(BF16).reshape(micro_count, face_rows, heads * head_dim)
    keys_face = dot(normed, wkv).astype(BF16).reshape(micro_count, face_rows, 2 * head_dim)
    ((keys_vals,),) = swap([KeysGather(keys_face, *on)], collective_id=2, name="gather_keys")

    query_doc = lax.dynamic_slice_in_dim(doc_ids, z * face_rows, face_rows, axis=1)
    blocks = face_rows // BLOCK
    last_doc = doc_ids[:, BLOCK - 1 :: BLOCK]
    first_doc = query_doc[:, ::BLOCK]
    lows = jnp.sum((last_doc[:, None, :] < first_doc[:, :, None]).astype(jnp.int32), axis=-1)
    highs = jnp.broadcast_to(z * blocks + jnp.arange(blocks, dtype=jnp.int32) + 1, lows.shape)
    bounds = jnp.stack([lows, highs], axis=-1).reshape(-1)
    docs = (query_doc[:, :, None], doc_ids[:, None, :], bounds, heads, head_dim)
    mixed, log_total = attend_forward(queries, keys_vals, *docs)
    mixed_flat = mixed.reshape(tokens, heads * head_dim)

    branch = dot(mixed_flat, wo).astype(BF16).reshape(micro_count, face_rows, width)
    (branch,), (cot_face,), (wexp,) = swap(
        [FaceScatter(branch, *on), FaceGather(cotangent, *on), LineGather([w_expand], ["row"], *on)],
        collective_id=3,
        name="scatter_branch",
    )
    own_in = inputs.astype(F32)
    middle = own_in + branch
    normed_two_full, norm_pull_two = jax.vjp(layer_norm, middle, gain_two, shift_two)
    (normed_two,), (wred,) = swap(
        [FaceGather(normed_two_full.astype(BF16), *on), LineGather([w_reduce], ["col"], *on)],
        collective_id=4,
        name="gather_normed_two",
    )
    normed_two = normed_two.reshape(tokens, width)
    cot_flat = cot_face.reshape(tokens, width)
    gelu_value, gelu_pull = jax.vjp(gelu_tanh, dot(normed_two, wexp))
    active = gelu_value.astype(BF16)
    part_reduce = dot_at(active, cot_flat).astype(BF16)
    grad_hidden = gelu_pull(dot_bt(cot_flat, wred))[0].astype(BF16)
    grad_normed_two = dot_bt(grad_hidden, wexp).astype(BF16).reshape(micro_count, face_rows, width)
    part_expand = dot_at(normed_two, grad_hidden).astype(BF16)
    reduced = dot(active, wred).astype(BF16).reshape(micro_count, face_rows, width)
    (grad_normed_two,), (grad_reduce,) = swap(
        [FaceScatter(grad_normed_two, *on), LineScatter([part_reduce], ["col"], *on)],
        collective_id=5,
        name="scatter_normed_two",
    )
    grad_mid_norm, grad_gain_two, grad_shift_two = norm_pull_two(grad_normed_two)
    grad_middle = cotangent.astype(F32) + grad_mid_norm
    (grad_branch,), (reduced,), (grad_expand,) = swap(
        [
            FaceGather(grad_middle.astype(BF16), *on),
            FaceScatter(reduced, *on),
            LineScatter([part_expand], ["row"], *on),
        ],
        collective_id=6,
        name="gather_branch",
    )
    outputs = (middle + reduced).astype(BF16)
    grad_branch = grad_branch.reshape(tokens, width)
    part_attn_out = dot_at(mixed_flat, grad_branch).astype(BF16)
    grad_mixed = dot_bt(grad_branch, wo).astype(BF16).reshape(mixed.shape)
    grad_queries, grad_keys = attend_backward(queries, keys_vals, mixed, grad_mixed, log_total, *docs)
    grad_queries = grad_queries.reshape(tokens, heads * head_dim)
    part_query = dot_at(normed, grad_queries).astype(BF16)
    from_query = dot_bt(grad_queries, wq).astype(BF16).reshape(micro_count, face_rows, width)
    (from_query,), (grad_keys,), (grad_attn_out, grad_query) = swap(
        [
            FaceScatter(from_query, *on),
            WholeScatter(grad_keys.reshape(micro_count, nz, face_rows, 2 * head_dim), *on),
            LineScatter([part_attn_out, part_query], ["col", "row"], *on),
        ],
        collective_id=7,
        name="scatter_query",
    )
    grad_keys = grad_keys.astype(BF16).reshape(micro_count * own_rows, 2 * head_dim)
    normed_own, norm_pull_one = jax.vjp(layer_norm, own_in, gain_one, shift_one)
    grad_normed = from_query + dot_bt(grad_keys, wkv).reshape(from_query.shape)
    grad_tok_norm, grad_gain_one, grad_shift_one = norm_pull_one(grad_normed)
    part_keyval = dot_at(normed_own.astype(BF16).reshape(-1, width), grad_keys).astype(BF16)
    own_width = width // (nz * ranks)
    small = jnp.stack([grad_gain_one, grad_shift_one, grad_gain_two, grad_shift_two])
    small = small.reshape(4, nz, ranks, own_width).transpose(2, 1, 0, 3)
    small = jnp.pad(small, ((0, 0), (0, 0), (0, 4), (0, 128 - own_width)))
    (grad_keyval,), (small,) = swap(
        [WholeScatter(part_keyval.reshape(1, nz, width // nz, 2 * head_dim), *on), SmallScatter(small, *on)],
        collective_id=8,
        name="scatter_small",
    )
    small = small[:4, :own_width]

    def by_row(halves):
        return jnp.concatenate([halves[0], halves[1]], axis=1).astype(F32)

    def by_column(halves):
        return halves.reshape(-1, halves.shape[-1]).astype(F32)

    return (
        outputs,
        grad_middle + grad_tok_norm,
        small[0],
        small[1],
        by_row(grad_query),
        grad_keyval[0],
        by_column(grad_attn_out),
        small[2],
        small[3],
        by_row(grad_expand),
        by_column(grad_reduce),
    )


def solution(mesh):
    placed = (
        P(None, ("dp", "tensor"), None),
        P(None, ("dp", "tensor"), None),
        P(),
        P("dp"),
        P("dp"),
        P("dp", "tensor"),
        P("dp", None),
        P("tensor", "dp"),
        P("dp"),
        P("dp"),
        P("dp", "tensor"),
        P("tensor", "dp"),
    )
    return jax.shard_map(
        local,
        mesh=mesh,
        in_specs=placed,
        out_specs=(
            P(None, ("dp", "tensor"), None),
            P(None, ("dp", "tensor"), None),
            P(("dp", "tensor")),
            P(("dp", "tensor")),
            P("dp", "tensor"),
            P(("dp", "tensor"), None),
            P("tensor", "dp"),
            P(("dp", "tensor")),
            P(("dp", "tensor")),
            P("dp", "tensor"),
            P("tensor", "dp"),
        ),
        check_vma=False,
    )
```

```python
import functools
import math

import jax
import jax.numpy as jnp
from jax import lax
from jax.experimental import pallas as pl
from jax.experimental.pallas import tpu as pltpu
from jax.sharding import PartitionSpec as P

BLOCK = 256
EPSILON = 1e-05
NEG_FILL = -1e30
GELU_A = math.sqrt(2.0 / math.pi)
GELU_B = 0.044715
MESH = pl.DeviceIdType.MESH
ANY = pl.BlockSpec(memory_space=pl.ANY)
BF16 = jnp.bfloat16
F32 = jnp.float32


def layer_norm(values, gain, shift):
    center = jnp.mean(values, axis=-1, keepdims=True)
    centered = values - center
    variance = jnp.mean(centered * centered, axis=-1, keepdims=True)
    return centered * lax.rsqrt(variance + EPSILON) * gain + shift


def gelu_tanh(values):
    return jax.nn.gelu(values, approximate=True)


class Net:
    def __init__(self, nz, ny, send, recv, local):
        dp, tensor = lax.axis_index("dp"), lax.axis_index("tensor")
        self.nz, self.ny = nz, ny
        self.z, self.x = lax.div(dp, 2), lax.rem(dp, 2)
        self.y, self.c = lax.div(tensor, 2), lax.rem(tensor, 2)
        self.tensor = tensor
        self.send, self.recv, self.local = send, recv, local
        self.used = [0, 0]
        self.keys = {}

    def flip(self, value, by):
        return value + by - 2 * by * value if by else value

    def xy(self, dx, dy):
        return self.flip(self.x, dx), lax.rem(self.y + dy, self.ny) if dy else self.y

    def rank(self, dx=0, dy=0, dc=0):
        x, y = self.xy(dx, dy)
        return x * (2 * self.ny) + y * 2 + self.flip(self.c, dc)

    def device(self, dx=0, dy=0, dc=0, z=None):
        x, y = self.xy(dx, dy)
        return ((self.z if z is None else z) * 2 + x, y * 2 + self.flip(self.c, dc))

    def slot(self, key):
        if key not in self.keys:
            self.keys[key] = self.used[0]
            self.used[0] += 1
        return self.keys[key]

    def remote(self, key, src, dst, device):
        at = self.slot(key)
        return pltpu.make_async_remote_copy(
            src_ref=src,
            dst_ref=dst,
            send_sem=self.send.at[at],
            recv_sem=self.recv.at[at],
            device_id=device,
            device_id_type=MESH,
        )

    def copy(self, src, dst):
        at = self.used[1]
        self.used[1] += 1
        return pltpu.make_async_copy(src, dst, self.local.at[at])


def add_rows(dst, terms):
    lead, height, width = dst.shape
    rows = min(max(16, 32768 // width), height)
    steps = height // rows

    def body(step, carry):
        at, off = lax.div(step, steps), pl.multiple_of(lax.rem(step, steps) * rows, rows)
        total = terms[0][at, pl.ds(off, rows), :].astype(F32)
        for term in terms[1:]:
            total = total + term[at, pl.ds(off, rows), :].astype(F32)
        dst[at, pl.ds(off, rows), :] = total.astype(dst.dtype)
        return carry

    lax.fori_loop(0, lead * steps, body, 0)


class FaceGather:
    moves = ("x", "y", "c")

    def __init__(self, own, nz, ny, hold_x=False):
        self.ins, self.hold_x = [own], hold_x
        m, t, d = own.shape
        self.outs = [(jax.ShapeDtypeStruct((m, 4 * ny * t, d), own.dtype), ANY)]
        self.scratch = []
        self.half = t // 2
        self.remotes, self.locals = 8 * ny, 1

    def run(self, net, ins, outs, scratch):
        (own,), (out,), half = ins, outs, self.half
        dys = range(1, net.ny)

        def piece(dx, dy, h):
            return out.at[:, pl.ds(pl.multiple_of(net.rank(dx, dy) * 2 * half + h * half, half), half), :]

        mine = [own.at[:, pl.ds(h * half, half), :] for h in (0, 1)]
        keep = net.copy(own, out.at[:, pl.ds(pl.multiple_of(net.rank() * 2 * half, half), 2 * half), :])
        keep.start()
        sent = {}

        def send(key, src, dst, device):
            sent[key] = net.remote((id(self), key), src, dst, device)
            sent[key].start()

        if not self.hold_x:
            send(("x", 0), mine[0], piece(0, 0, 0), net.device(1, 0))
        for dy in dys:
            send(("y", dy, 1), mine[1], piece(0, 0, 1), net.device(0, dy))
        if not self.hold_x:
            send(("x", 1), mine[1], piece(0, 0, 1), net.device(1, 0))
        for dy in dys:
            send(("y", dy, 0), mine[0], piece(0, 0, 0), net.device(0, dy))
        for h in (0, 1):
            send(("c", h), mine[h], piece(0, 0, h), net.device(0, 0, 1))
        if self.hold_x:
            yield
            for h in (0, 1):
                send(("x", h), mine[h], piece(0, 0, h), net.device(1, 0))

        def share(key, dx, dy, h):
            send(("c",) + key, piece(dx, dy, h), piece(dx, dy, h), net.device(0, 0, 1))

        yield
        sent["x", 0].wait_recv()
        for dy in dys:
            send(("xy", dy), piece(1, 0, 0), piece(1, 0, 0), net.device(0, dy))
        share(("x", 0), 1, 0, 0)
        for dy in dys:
            yield
            sent["y", dy, 1].wait_recv()
            send(("yx", dy), piece(0, -dy % net.ny, 1), piece(0, -dy % net.ny, 1), net.device(1, 0))
            share(("y", dy, 1), 0, -dy % net.ny, 1)
        yield
        sent["x", 1].wait_recv()
        share(("x", 1), 1, 0, 1)
        for dy in dys:
            yield
            sent["y", dy, 0].wait_recv()
            share(("y", dy, 0), 0, -dy % net.ny, 0)
        for dy in dys:
            yield
            sent["xy", dy].wait_recv()
            share(("xy", dy), 1, -dy % net.ny, 0)
            yield
            sent["yx", dy].wait_recv()
            share(("yx", dy), 1, -dy % net.ny, 1)
        yield
        for key, copy in sent.items():
            if key[0] == "c":
                copy.wait_recv()
        for copy in sent.values():
            copy.wait_send()
        keep.wait()


class FaceScatter:
    moves = ("x", "y", "c")

    def __init__(self, part, nz, ny, resident=False):
        self.ins, self.resident = [part], resident
        m, rows, d = part.shape
        t = rows // (4 * ny)
        self.outs = [(jax.ShapeDtypeStruct((m, t, d), F32), pl.BlockSpec(memory_space=pltpu.VMEM))]
        half = t // 2
        self.half = half
        self.scratch = [
            pltpu.VMEM((2 * ny, m, t, d), BF16),
            pltpu.VMEM((ny - 1, m, half, d), BF16),
            pltpu.VMEM((ny - 1, m, half, d), BF16),
            pltpu.VMEM((2, m, half, d), BF16),
            pltpu.VMEM((2, ny - 1, m, half, d), BF16),
        ]
        if not resident:
            self.scratch.append(pltpu.VMEM((2 * ny, m, t, d), BF16))
        self.remotes, self.locals = 6 * ny + 4, 2 * ny

    def run(self, net, ins, outs, scratch):
        (part,), (out,), half = ins, outs, self.half
        from_core, x_diag, y_diag, x_in, y_in = scratch[:5]
        ny = net.ny
        dys = range(1, ny)
        order = [(1, dy) for dy in dys] + [(1, 0)] + [(0, dy) for dy in dys] + [(0, 0)]
        sent, loads = {}, {}

        def send(key, src, dst, device):
            sent[key] = net.remote((id(self), key), src, dst, device)
            sent[key].start()

        def rows(dx, dy, dc, first=0, size=2 * half):
            at = net.rank(dx, dy, dc) * 2 * half + first
            return part.at[:, pl.ds(pl.multiple_of(at, half), size), :]

        def work(dx, dy, first=0, size=2 * half):
            if self.resident:
                return rows(dx, dy, 0, first, size)
            return scratch[5].at[dx * ny + dy, :, pl.ds(first, size), :]

        for dx, dy in order:
            at = dx * ny + dy
            if not self.resident:
                loads[at] = net.copy(rows(dx, dy, 0), work(dx, dy))
                loads[at].start()
            send(("c", at), rows(dx, dy, 1), from_core.at[at], net.device(0, 0, 1))
        for dx, dy in order:
            at = dx * ny + dy
            yield
            if not self.resident:
                loads[at].wait()
            sent["c", at].wait_recv()
            add_rows(work(dx, dy), [work(dx, dy), from_core.at[at]])
            top, low = work(dx, dy, 0, half), work(dx, dy, half, half)
            if dx and dy:
                send(("xd", dy), top, x_diag.at[dy - 1], net.device(1, 0))
                send(("yd", dy), low, y_diag.at[dy - 1], net.device(0, dy))
            elif dx:
                send(("x", 0), top, x_in.at[0], net.device(1, 0))
            elif dy:
                send(("y", dy, 1), low, y_in.at[1, dy - 1], net.device(0, dy))
        for dy in dys:
            yield
            sent["xd", dy].wait_recv()
            top = work(0, dy, 0, half)
            add_rows(top, [top, x_diag.at[dy - 1]])
            send(("y", dy, 0), top, y_in.at[0, dy - 1], net.device(0, dy))
        low = work(1, 0, half, half)
        for dy in dys:
            yield
            sent["yd", dy].wait_recv()
            add_rows(low, [low, y_diag.at[dy - 1]])
        send(("x", 1), low, x_in.at[1], net.device(1, 0))
        for h in (0, 1):
            yield
            sent["x", h].wait_recv()
            for dy in dys:
                sent["y", dy, h].wait_recv()
            add_rows(
                out.at[:, pl.ds(h * half, half), :],
                [work(0, 0, h * half, half), x_in.at[h]] + [y_in.at[h, dy - 1] for dy in dys],
            )
        for copy in sent.values():
            copy.wait_send()


class LineGather:
    moves = ("x", "line", "c")

    def __init__(self, shards, kinds, nz, ny, share=(0, 1)):
        self.ins, self.kinds, self.share = list(shards), list(kinds), share
        self.outs, self.scratch = [], []
        for shard, kind in zip(shards, kinds):
            rows, columns = shard.shape
            if kind == "row":
                shape = (rows * 2 * nz, columns // 2 // share[1])
            elif kind == "col":
                shape = (rows // 2 // share[1], columns * 2 * nz)
            else:
                shape = (rows * 2 * nz, columns)
            self.outs.append((jax.ShapeDtypeStruct(shape, shard.dtype), ANY))
        count = len(self.ins)
        self.remotes = count * (1 + 4 * (nz - 1)) + kinds.count("both") * (1 + 4 * (nz - 1))
        self.locals = count

    def run(self, net, ins, outs, scratch):
        nz, z = net.nz, net.z
        sent, locals_, shared = [], [], []
        weights = []
        for at, (shard, out, kind) in enumerate(zip(ins, outs, self.kinds)):
            rows, columns = shard.shape

            if kind == "row":
                span = columns // 2 // self.share[1]

                def mine(dx, shard=shard, span=span):
                    first = (net.flip(net.x, dx) * self.share[1] + self.share[0]) * span
                    return shard.at[:, pl.ds(pl.multiple_of(first, span), span)]

                def block(line, dx, out=out, rows=rows):
                    first = (line * 2 + net.flip(net.x, dx)) * rows
                    return out.at[pl.ds(pl.multiple_of(first, rows), rows), :]

            elif kind == "col":
                span = rows // 2 // self.share[1]

                def mine(dx, shard=shard, span=span):
                    first = (net.flip(net.x, dx) * self.share[1] + self.share[0]) * span
                    return shard.at[pl.ds(pl.multiple_of(first, span), span), :]

                def block(line, dx, out=out, columns=columns):
                    first = (line * 2 + net.flip(net.x, dx)) * columns
                    return out.at[:, pl.ds(pl.multiple_of(first, columns), columns)]

            else:
                half = rows // 2

                def mine(dx, shard=shard, half=half):
                    return shard.at[pl.ds(pl.multiple_of(net.c * half, half), half), :]

                def block(line, dx, out=out, rows=rows, half=half):
                    first = (line * 2 + net.flip(net.x, dx)) * rows + net.c * half
                    return out.at[pl.ds(pl.multiple_of(first, half), half), :]

            weights.append((at, kind, mine, block))

        def hop(at, dx, step, up, block, src=None):
            origin = z - (step - 1) if up else z + (step - 1)
            there = z + 1 if up else z - 1
            copy = net.remote(
                (id(self), at, dx, step, up),
                block(origin, dx) if src is None else src,
                block(origin, dx),
                net.device(z=there),
            )
            fits = (origin >= 0) & (there < nz) if up else (origin < nz) & (there >= 0)
            return copy, fits

        def start(at, dx, step, up, block, src=None):
            copy, fits = hop(at, dx, step, up, block, src)
            pl.when(fits)(copy.start)
            sent.append((copy, fits))

        def arrived(at, dx, step, up, block, kind):
            copy, _ = hop(at, dx, step, up, block)
            origin = z - step if up else z + step
            fits = origin >= 0 if up else origin < nz
            pl.when(fits)(copy.wait_recv)
            if kind == "both":
                share = net.remote(
                    (id(self), "c", at, dx, step, up), block(origin, dx), block(origin, dx), net.device(0, 0, 1)
                )
                pl.when(fits)(share.start)
                shared.append((share, fits))

        swaps = {}
        for at, kind, mine, block in weights:
            swaps[at] = net.remote((id(self), at, "x"), mine(1), block(z, 0), net.device(1, 0))
            swaps[at].start()
            for up in (True, False):
                start(at, 0, 1, up, block, mine(0))
        for at, kind, mine, block in weights:
            if kind == "both":
                whole = ins[at].shape[0]
                into = outs[at].at[pl.ds(pl.multiple_of((z * 2 + net.x) * whole, whole), whole), :]
                locals_.append(net.copy(ins[at], into))
            else:
                locals_.append(net.copy(mine(0), block(z, 0)))
            locals_[-1].start()
        yield
        for copy in locals_:
            copy.wait()
        for at, kind, mine, block in weights:
            swaps[at].wait_recv()
            for up in (True, False):
                start(at, 1, 1, up, block)
            if kind == "both":
                share = net.remote((id(self), "c", at), block(z, 1), block(z, 1), net.device(0, 0, 1))
                share.start()
                shared.append((share, None))
        for step in range(1, nz):
            for at, kind, mine, block in weights:
                for dx in (0, 1):
                    yield
                    for up in (True, False):
                        arrived(at, dx, step, up, block, kind)
                        if step < nz - 1:
                            start(at, dx, step + 1, up, block)
        yield
        for copy, fits in shared:
            if fits is None:
                copy.wait()
            else:
                pl.when(fits)(copy.wait)
        for copy, fits in sent:
            pl.when(fits)(copy.wait_send)
        for copy in swaps.values():
            copy.wait_send()


class LineScatter:
    moves = ("x", "line")

    def __init__(self, parts, kinds, nz, ny, resident=False):
        self.ins, self.kinds, self.resident = list(parts), list(kinds), resident
        self.outs, self.scratch = [], []
        for part, kind in zip(parts, kinds):
            rows, columns = part.shape
            shape = (rows // (2 * nz), columns) if kind == "row" else (rows, columns // (2 * nz))
            self.outs.append((jax.ShapeDtypeStruct((2,) + shape, BF16), ANY))
            for lead in (nz - 1, nz - 1, 1) + (() if resident else (nz,)):
                self.scratch.append(pltpu.VMEM((lead, 2) + shape, BF16))
        count = len(self.ins)
        self.remotes = count * (1 + 4 * (nz - 1))
        self.locals = count * (2 * nz + 1)

    def run(self, net, ins, outs, scratch):
        nz, z = net.nz, net.z
        sent, loads, stores = [], {}, []
        grads = []
        each = 3 if self.resident else 4
        for at, (part, out, kind) in enumerate(zip(ins, outs, self.kinds)):
            down, up, mine = scratch[each * at : each * at + 3]
            _, _, rows, columns = mine.shape

            def block(line, dx, part=part, kind=kind, rows=rows, columns=columns):
                size = rows if kind == "row" else columns
                first = pl.ds(pl.multiple_of((line * 2 + net.flip(net.x, dx)) * size, size), size)
                return part.at[first, :] if kind == "row" else part.at[:, first]

            if self.resident:
                work = block
            else:

                def work(line, dx, at=at):
                    return scratch[each * at + 3].at[line, dx]

                order = []
                for k in range(nz):
                    order += [k, nz - 1 - k]
                for line in dict.fromkeys(order):
                    for dx in (1, 0):
                        loads[at, line, dx] = net.copy(block(line, dx), work(line, dx))
                        loads[at, line, dx].start()
            grads.append((at, out, work, down, up, mine))

        def inbox(slots, line, dx, toward):
            return slots.at[line if toward < 0 else line - 1, dx]

        for k in range(nz - 1):
            for dx in (1, 0):
                for at, out, work, down, up, mine in grads:
                    yield
                    for line, slots, toward in ((k, down, -1), (nz - 1 - k, up, 1)):
                        here, slot = work(line, dx), inbox(slots, line, dx, toward)
                        copy = net.remote((id(self), at, line, dx, toward), here, slot, net.device(z=z + toward))
                        first = z == (nz - 1 if toward < 0 else 0)
                        sends = z > line if toward < 0 else z < line

                        def step(copy=copy, here=here, slot=slot, first=first, load=loads.get((at, line, dx))):
                            if load is not None:
                                load.wait()

                            @pl.when(jnp.logical_not(first))
                            def _():
                                copy.wait_recv()
                                add_rows(_lead(here), [_lead(here), _lead(slot)])

                            copy.start()

                        pl.when(sends)(step)
                        sent.append((copy, sends))
        swaps = []
        for dx in (1, 0):
            for at, out, work, down, up, mine in grads:
                yield
                total = mine.at[0, dx]
                for line in range(nz):

                    @pl.when(z == line)
                    def _(line=line, at=at, total=total, work=work, down=down, up=up):
                        if not self.resident:
                            loads[at, line, dx].wait()
                        terms = [_lead(work(line, dx))]
                        for slots, toward in ((down, -1), (up, 1)):
                            if (line < nz - 1) if toward < 0 else (line > 0):
                                slot = inbox(slots, line, dx, toward)
                                key = (id(self), at, line, dx, toward)
                                net.remote(key, total, slot, net.device(z=z + toward)).wait_recv()
                                terms.append(_lead(slot))
                        add_rows(_lead(total), terms)

                if dx:
                    swaps.append(net.remote((id(self), at, "x"), total, out.at[net.x], net.device(1, 0)))
                    swaps[-1].start()
                else:
                    stores.append(net.copy(total, out.at[net.x]))
                    stores[-1].start()
        yield
        for copy, sends in sent:
            pl.when(sends)(copy.wait_send)
        for copy in swaps:
            copy.wait()
        for copy in stores:
            copy.wait()


def _lead(ref):
    return Lead(ref)


class Lead:
    def __init__(self, ref):
        self.ref, self.shape, self.dtype = ref, (1,) + tuple(ref.shape), ref.dtype

    def __getitem__(self, index):
        return self.ref[index[1], index[2]]

    def __setitem__(self, index, value):
        self.ref[index[1], index[2]] = value


class KeysGather:
    moves = ("x", "line", "c")

    def __init__(self, face, nz, ny):
        m, rows, width = face.shape
        self.ins = [face]
        self.outs = [(jax.ShapeDtypeStruct((m, nz * rows, width), face.dtype), ANY)]
        self.scratch = []
        self.remotes, self.locals = 4 * (nz - 1), 1

    def run(self, net, ins, outs, scratch):
        (face,), (out,) = ins, outs
        nz, z = net.nz, net.z
        _, rows, width = face.shape
        part, side = rows // 2, width // 2

        def block(line, dx, dc):
            first = pl.multiple_of(line * rows + net.flip(net.x, dx) * part, part)
            column = pl.multiple_of(net.flip(net.c, dc) * side, side)
            return out.at[:, pl.ds(first, part), pl.ds(column, side)]

        own = face.at[
            :,
            pl.ds(pl.multiple_of(net.x * part, part), part),
            pl.ds(pl.multiple_of(net.c * side, side), side),
        ]
        sent, shared = [], []

        def line_copy(step):
            origin = z - (step - 1)
            src = own if step == 1 else block(origin, 0, 0)
            return net.remote((id(self), step), src, block(origin, 0, 0), net.device(z=z + 1))

        def start(step):
            copy, fits = line_copy(step), (z - (step - 1) >= 0) & (z + 1 < nz)
            pl.when(fits)(copy.start)
            sent.append((copy, fits))

        start(1)
        keep = net.copy(face, out.at[:, pl.ds(pl.multiple_of(z * rows, rows), rows), :])
        keep.start()
        later = []
        for step in range(1, nz):
            yield
            fits = z - step >= 0
            pl.when(fits)(line_copy(step).wait_recv)
            if step < nz - 1:
                start(step + 1)
            here = block(z - step, 0, 0)
            across = net.remote((id(self), "x", step), here, here, net.device(1, 0))
            beside = net.remote((id(self), "c", step), here, here, net.device(0, 0, 1))
            for copy in (across, beside):
                pl.when(fits)(copy.start)
                sent.append((copy, fits))
            later.append((step, fits, across))
            shared.append((beside, fits))
        for step, fits, across in later:
            yield
            pl.when(fits)(across.wait_recv)
            there = block(z - step, 1, 0)
            beside = net.remote((id(self), "xc", step), there, there, net.device(0, 0, 1))
            pl.when(fits)(beside.start)
            sent.append((beside, fits))
            shared.append((beside, fits))
        yield
        for copy, fits in shared:
            pl.when(fits)(copy.wait_recv)
        for copy, fits in sent:
            pl.when(fits)(copy.wait_send)
        keep.wait()


class WholeScatter(FaceScatter):
    moves = ("x", "y", "c", "z")

    def __init__(self, part, nz, ny):
        m, _, rows, d = part.shape
        super().__init__(part.reshape(m * nz, rows, d), nz, ny)
        t = rows // (4 * ny)
        self.m, self.nz = m, nz
        self.outs = [(jax.ShapeDtypeStruct((m, t, d), F32), pl.BlockSpec(memory_space=pltpu.VMEM))]
        self.scratch = self.scratch + [pltpu.VMEM((m * nz, t, d), BF16), pltpu.VMEM((nz, m, t, d), BF16)]
        self.remotes = self.remotes + nz * m
        self.locals = self.locals + m

    def run(self, net, ins, outs, scratch):
        face, inbox = scratch[-2:]
        yield from super().run(net, ins, [face], scratch[:-2])
        nz, m = self.nz, self.m
        copies = []
        for far in range(1, nz):
            line = lax.rem(net.z + far, nz)
            for at in range(m):
                copies.append(
                    pltpu.make_async_remote_copy(
                        src_ref=face.at[at * nz + line],
                        dst_ref=inbox.at[far, at],
                        send_sem=net.send.at[net.slot((id(self), "z", far, at))],
                        recv_sem=net.recv.at[net.slot((id(self), "z", far, at))],
                        device_id=net.device(z=line),
                        device_id_type=MESH,
                    )
                )
                copies[-1].start()
        own = []
        for at in range(m):
            own.append(net.copy(face.at[at * nz + net.z], inbox.at[0, at]))
            own[-1].start()
        yield
        for copy in own:
            copy.wait()
        for copy in copies:
            copy.wait()
        add_rows(outs[0], [inbox.at[far] for far in range(nz)])


class PlaneGather:
    moves = ("plane",)

    def __init__(self, own, nz, ny):
        self.ins = [own]
        self.outs = [(jax.ShapeDtypeStruct((2 * nz,) + own.shape, own.dtype), ANY)]
        self.scratch = []
        self.remotes, self.locals = 2 * nz, 1

    def run(self, net, ins, outs, scratch):
        (own,), (out,) = ins, outs
        here = out.at[net.z * 2 + net.x]
        copies = []
        for far in range(net.nz):
            for dx in (0, 1):
                if far or dx:
                    line = lax.rem(net.z + far, net.nz)
                    copies.append(net.remote((id(self), far, dx), own, here, net.device(dx, z=line)))
                    copies[-1].start()
        keep = net.copy(own, here)
        keep.start()
        yield
        for copy in copies:
            copy.wait()
        keep.wait()


class SmallScatter:
    moves = ("face", "z")

    def __init__(self, part, nz, ny):
        ranks, _, rows, width = part.shape
        self.ins = [part]
        vmem = pl.BlockSpec(memory_space=pltpu.VMEM)
        self.outs = [(jax.ShapeDtypeStruct((rows, width), F32), vmem)]
        self.scratch = [
            pltpu.VMEM((ranks, nz, rows, width), F32),
            pltpu.VMEM((nz, rows, width), F32),
            pltpu.VMEM((nz, rows, width), F32),
        ]
        self.remotes, self.locals = ranks + nz, 2

    def run(self, net, ins, outs, scratch):
        (part,), (out,) = ins, outs
        inbox, total, line_in = scratch
        ny, nz = net.ny, net.nz
        copies = []
        for dx in (0, 1):
            for dy in range(ny):
                for dc in (0, 1):
                    if dx or dy or dc:
                        at = (dx * ny + dy) * 2 + dc
                        copies.append(
                            net.remote(
                                (id(self), at), part.at[net.rank(dx, dy, dc)], inbox.at[at], net.device(dx, dy, dc)
                            )
                        )
                        copies[-1].start()
        keep = net.copy(part.at[net.rank()], inbox.at[0])
        keep.start()
        yield
        keep.wait()
        for copy in copies:
            copy.wait()
        total[...] = jnp.sum(inbox[...], axis=0)
        lines = []
        for far in range(1, nz):
            line = lax.rem(net.z + far, nz)
            lines.append(net.remote((id(self), "z", far), total.at[line], line_in.at[far], net.device(z=line)))
            lines[-1].start()
        own = net.copy(total.at[net.z], line_in.at[0])
        own.start()
        yield
        own.wait()
        for copy in lines:
            copy.wait()
        out[...] = jnp.sum(line_in[...], axis=0)


def launch(body, ins, in_specs, outs, scratch, plans, nz, ny, collective_id, name, extra_locals=0, vmem=56):
    moves = set()
    for plan in plans:
        moves |= set(plan.moves)
    remotes = sum(plan.remotes for plan in plans)
    locals_ = max(1, extra_locals + sum(plan.locals for plan in plans))

    def kernel(*refs):
        in_refs, refs = refs[: len(ins)], refs[len(ins) :]
        out_refs, refs = refs[: len(outs)], refs[len(outs) :]
        scratch_refs, (send, recv, local) = refs[: len(scratch)], refs[len(scratch) :]
        net = Net(nz, ny, send, recv, local)
        peers = {}
        for far in range(nz):
            for dx in (0, 1):
                for dy in range(ny):
                    for dc in (0, 1):
                        kinds = set()
                        if not far:
                            kinds.add("face")
                            if dx and not dy and not dc:
                                kinds.add("x")
                            if dy and not dx and not dc:
                                kinds.add("y")
                            if dc and not dx and not dy:
                                kinds.add("c")
                        if far and not dx and not dy and not dc:
                            kinds.add("z")
                            if far in (1, nz - 1):
                                kinds.add("line")
                        if not dy and not dc:
                            kinds.add("plane")
                        if (far or dx or dy or dc) and kinds & moves:
                            line = lax.rem(net.z + far, nz) if far else None
                            peers[far, dx, dy, dc] = net.device(dx, dy, dc, line)
        barrier = pltpu.get_barrier_semaphore()
        for device in peers.values():
            pl.semaphore_signal(barrier, inc=1, device_id=device, device_id_type=MESH)
        pl.semaphore_wait(barrier, len(peers))
        body(net, in_refs, out_refs, scratch_refs)

    return list(
        pl.pallas_call(
            kernel,
            out_shape=[shape for shape, _ in outs],
            in_specs=in_specs,
            out_specs=[spec for _, spec in outs],
            scratch_shapes=list(scratch)
            + [
                pltpu.SemaphoreType.DMA((remotes,)),
                pltpu.SemaphoreType.DMA((remotes,)),
                pltpu.SemaphoreType.DMA((locals_,)),
            ],
            compiler_params=pltpu.CompilerParams(
                collective_id=collective_id, has_side_effects=True, vmem_limit_bytes=vmem << 20
            ),
            name=name,
        )(*ins)
    )


def exchange(plans, nz, ny, collective_id, name):
    ins = [array for plan in plans for array in plan.ins]
    outs = [out for plan in plans for out in plan.outs]
    scratch = [entry for plan in plans for entry in plan.scratch]

    def body(net, in_refs, out_refs, scratch_refs):
        running = []
        for plan in plans:
            mine = []
            for refs_of, count in ((in_refs, plan.ins), (out_refs, plan.outs), (scratch_refs, plan.scratch)):
                mine.append(list(refs_of[: len(count)]))
            in_refs = in_refs[len(plan.ins) :]
            out_refs = out_refs[len(plan.outs) :]
            scratch_refs = scratch_refs[len(plan.scratch) :]
            running.append(plan.run(net, *mine))
        while running:
            for steps in list(running):
                try:
                    next(steps)
                except StopIteration:
                    running.remove(steps)

    results = launch(body, ins, [ANY] * len(ins), outs, scratch, plans, nz, ny, collective_id, name)
    grouped = []
    for plan in plans:
        grouped.append(results[: len(plan.outs)])
        results = results[len(plan.outs) :]
    return grouped


def drive(steps, actions):
    actions = list(actions)
    for _ in steps:
        if actions:
            action = actions.pop(0)
            if action is not None:
                action()
    for action in actions:
        if action is not None:
            action()


def loop(count, body):
    def step(at, carry):
        body(at)
        return carry

    lax.fori_loop(0, count, step, 0)


def mlp_block(mixed, wo, inputs, cotangent, cot_face, norms, wexp_first, w_expand, w_reduce, nz, ny, collective_id):
    micro_count, own_rows, width = inputs.shape
    face_rows = cot_face.shape[1]
    tokens = micro_count * face_rows
    attn = mixed.shape[1]
    units = w_expand.shape[1] // 2
    half = units // 2
    tile = min(512, half)
    wide = 512
    part = jax.ShapeDtypeStruct((micro_count, face_rows, width), BF16)
    part_red = jax.ShapeDtypeStruct((units, width), BF16)
    own = (micro_count, own_rows, width)
    scatter_a, scatter_b = (FaceScatter(part, nz, ny, resident=True) for _ in range(2))
    gather = FaceGather(jax.ShapeDtypeStruct(own, BF16), nz, ny)
    line_e = LineGather([w_expand], ["row"], nz, ny, share=(1, 2))
    line_r = LineGather([w_reduce], ["col"], nz, ny)
    line_s = LineScatter([part_red], ["col"], nz, ny, resident=True)
    plans = [scatter_a, scatter_b, gather, line_e, line_r, line_s]
    vmem = pl.BlockSpec(memory_space=pltpu.VMEM)
    outs = [
        (jax.ShapeDtypeStruct(own, F32), ANY),
        (jax.ShapeDtypeStruct(own, F32), ANY),
        (jax.ShapeDtypeStruct(own, BF16), ANY),
        (jax.ShapeDtypeStruct((2, 16, width), F32), vmem),
        (jax.ShapeDtypeStruct((width, half), BF16), ANY),
        (jax.ShapeDtypeStruct((width, half), BF16), ANY),
        (part, ANY),
    ] + line_s.outs
    scratch = [
        pltpu.VMEM((micro_count, face_rows, width), BF16),
        pltpu.VMEM(own, F32),
        pltpu.VMEM(own, F32),
        pltpu.VMEM(own, BF16),
        pltpu.VMEM(own, BF16),
        pltpu.VMEM(own, BF16),
        pltpu.VMEM((micro_count, face_rows, width), BF16),
        pltpu.VMEM((micro_count, face_rows, width), BF16),
        pltpu.VMEM((width, half), BF16),
        pltpu.VMEM((width, half), BF16),
        pltpu.VMEM((units, width), BF16),
        pltpu.VMEM((tokens, units), BF16),
        pltpu.VMEM((tokens, units), BF16),
        pltpu.VMEM((units, width), BF16),
        pltpu.VMEM((tokens, attn), BF16),
        pltpu.VMEM((attn, width), BF16),
    ]
    shared = len(scratch)
    scratch += scatter_a.scratch + line_s.scratch

    def body(net, ins, outs, scratch):
        mixed_in, wo_in, own_in, cot_in, face_in, norms, first_in, expand_in, reduce_in = ins
        middle_out, grad_out, low_out, norm_out, expand_a, expand_b, reduced_out, reduce_out = outs
        p, branch, middle, own, cot_own, n_own, n_face, cot, we0, we1, wr, active, slope, pr, mixed, wo = scratch[:shared]
        we = (we0, we1)
        slots = list(scratch[shared : shared + len(scatter_a.scratch)])
        line_slots = list(scratch[shared + len(scatter_a.scratch) :])

        loads = [
            net.copy(*pair)
            for pair in (
                (mixed_in, mixed),
                (wo_in, wo),
                (own_in, own),
                (cot_in, cot_own),
                (first_in, we0),
                (face_in, cot),
            )
        ]
        e = line_e.run(net, [expand_in], [we1], [])
        r = line_r.run(net, [reduce_in], [wr], [])
        queue = []

        def tick(count=1):
            def act():
                for _ in range(count):
                    if queue:
                        next(queue.pop(0), None)

            return act

        next(e)
        for load in loads:
            load.start()
        queue += [e, r, e, e, r, e, e, r, r, e, e, r, r, r, r]
        loads[0].wait()
        loads[1].wait()

        def branch_tile(at):
            m, n = lax.div(at, width // wide), lax.rem(at, width // wide)
            columns = pl.ds(pl.multiple_of(n * wide, wide), wide)
            rows = pl.ds(pl.multiple_of(m * face_rows, face_rows), face_rows)
            p[m, :, columns] = jnp.dot(mixed[rows, :], wo[:, columns], preferred_element_type=F32).astype(BF16)

        loop(micro_count * (width // wide), branch_tile)
        tick(2)()
        drive(
            scatter_a.run(net, [p], [branch], slots),
            [None, None, None, None, tick(2), None, tick(1), None],
        )
        loads[2].wait()
        row_steps = own_rows // 16

        def own_rows_at(at):
            return lax.div(at, row_steps), pl.ds(pl.multiple_of(lax.rem(at, row_steps) * 16, 16), 16)

        def norm_rows(at):
            m, rows = own_rows_at(at)
            values = own[m, rows, :].astype(F32) + branch[m, rows, :]
            middle[m, rows, :] = values
            centered = values - jnp.mean(values, axis=-1, keepdims=True)
            spread = lax.rsqrt(jnp.mean(centered * centered, axis=-1, keepdims=True) + EPSILON)
            n_own[m, rows, :] = (centered * spread * norms[0:1, :] + norms[1:2, :]).astype(BF16)

        loop(micro_count * row_steps, norm_rows)
        keep_middle = net.copy(middle, middle_out)
        keep_middle.start()
        drive(
            gather.run(net, [n_own], [n_face], []),
            [tick(2), tick(1), tick(1), tick(2), None, None, None],
        )
        loads[4].wait()

        def hidden_tile(h):
            def tile_at(at):
                m, n = lax.div(at, half // tile), lax.rem(at, half // tile)
                rows = pl.ds(pl.multiple_of(m * face_rows, face_rows), face_rows)
                columns = pl.ds(pl.multiple_of(n * tile, tile), tile)
                into = pl.ds(pl.multiple_of(h * half + n * tile, tile), tile)
                hidden = jnp.dot(n_face[m], we[h][:, columns], preferred_element_type=F32)
                square = hidden * hidden
                bend = jnp.tanh(GELU_A * hidden * (1.0 + GELU_B * square))
                active[rows, into] = (0.5 * hidden * (1.0 + bend)).astype(BF16)
                slope[rows, into] = (
                    0.5 * (1.0 + bend)
                    + (0.5 * GELU_A) * hidden * (1.0 - bend * bend) * (1.0 + (3.0 * GELU_B) * square)
                ).astype(BF16)

            return tile_at

        across = (((0,), (0,)), ((), ()))
        along = (((1,), (1,)), ((), ()))
        loop(micro_count * (half // tile), hidden_tile(0))
        tick(1)()
        loop(micro_count * (half // tile), hidden_tile(1))
        tick(1)()
        loads[5].wait()

        def reduce_tile(first):
            def tile_at(at):
                f, n = lax.div(at, width // wide), lax.rem(at, width // wide)
                columns = pl.ds(pl.multiple_of(n * wide, wide), wide)
                rows = pl.ds(pl.multiple_of(first + f * tile, tile), tile)
                pr[rows, columns] = lax.dot_general(
                    active[:, rows],
                    cot[:, :, columns].reshape(tokens, wide),
                    across,
                    preferred_element_type=F32,
                ).astype(BF16)

            return tile_at

        loop((half // tile) * (width // wide), reduce_tile(0))
        tick(1)()
        loop((half // tile) * (width // wide), reduce_tile(half))
        s = line_s.run(net, [pr], [reduce_out], line_slots)
        tick(9)()
        queue.extend([s] * 40)
        tick(1)()

        def slope_tile(at):
            m, n = lax.div(at, units // tile), lax.rem(at, units // tile)
            rows = pl.ds(pl.multiple_of(m * face_rows, face_rows), face_rows)
            columns = pl.ds(pl.multiple_of(n * tile, tile), tile)
            grad = lax.dot_general(cot[m], wr[columns, :], along, preferred_element_type=F32)
            slope[rows, columns] = (grad * slope[rows, columns].astype(F32)).astype(BF16)

        def normed_tile(at):
            m, n = lax.div(at, width // wide), lax.rem(at, width // wide)
            rows = pl.ds(pl.multiple_of(m * face_rows, face_rows), face_rows)
            columns = pl.ds(pl.multiple_of(n * wide, wide), wide)
            grad = lax.dot_general(slope[rows, :half], we0[columns, :], along, preferred_element_type=F32)
            grad = grad + lax.dot_general(slope[rows, half:], we1[columns, :], along, preferred_element_type=F32)
            p[m, :, columns] = grad.astype(BF16)

        loop(micro_count * (units // tile), slope_tile)
        tick(1)()
        loop(micro_count * (width // wide), normed_tile)
        tick(1)()
        for steps in (e, r):
            for _ in steps:
                pass
        stores = []

        def reduced_tiles():
            def tile_at(at):
                m, n = lax.div(at, width // wide), lax.rem(at, width // wide)
                rows = pl.ds(pl.multiple_of(m * face_rows, face_rows), face_rows)
                columns = pl.ds(pl.multiple_of(n * wide, wide), wide)
                cot[m, :, columns] = jnp.dot(active[rows, :], wr[:, columns], preferred_element_type=F32).astype(BF16)

            loop(micro_count * (width // wide), tile_at)
            stores.append(net.copy(cot, reduced_out))
            stores[-1].start()

        def expand_tiles():
            for h in (0, 1):

                def tile_at(at, h=h):
                    k, n = lax.div(at, half // tile), lax.rem(at, half // tile)
                    rows = pl.ds(pl.multiple_of(k * wide, wide), wide)
                    columns = pl.ds(pl.multiple_of(n * tile, tile), tile)
                    grads = pl.ds(pl.multiple_of(h * half + n * tile, tile), tile)
                    we[h][rows, columns] = lax.dot_general(
                        n_face[:, :, rows].reshape(tokens, wide),
                        slope[:, grads],
                        across,
                        preferred_element_type=F32,
                    ).astype(BF16)

                loop((width // wide) * (half // tile), tile_at)
                stores.append(net.copy(we[h], (expand_a, expand_b)[h]))
                stores[-1].start()

        def do(*actions):
            def act():
                for action in actions:
                    action()

            return act

        drive(
            scatter_b.run(net, [p], [branch], slots),
            [None, None, None, None, expand_tiles, tick(1), do(tick(1), reduced_tiles, tick(1)), None],
        )
        loads[3].wait()
        keep_middle.wait()
        norm_out[...] = jnp.zeros_like(norm_out)

        def back_rows(at):
            m, rows = own_rows_at(at)
            values = middle[m, rows, :]
            centered = values - jnp.mean(values, axis=-1, keepdims=True)
            spread = lax.rsqrt(jnp.mean(centered * centered, axis=-1, keepdims=True) + EPSILON)
            unit = centered * spread
            grad = branch[m, rows, :]
            norm_out[0] += grad * unit
            norm_out[1] += grad
            turned = grad * norms[0:1, :]
            inner = jnp.mean(turned * unit, axis=-1, keepdims=True)
            total = cot_own[m, rows, :].astype(F32) + spread * (
                turned - jnp.mean(turned, axis=-1, keepdims=True) - unit * inner
            )
            middle[m, rows, :] = total
            n_own[m, rows, :] = total.astype(BF16)

        loop(micro_count * row_steps, back_rows)
        for pair in ((middle, grad_out), (n_own, low_out)):
            stores.append(net.copy(*pair))
            stores[-1].start()
        for _ in s:
            pass
        for store in stores:
            store.wait()

    ins = [mixed, wo, inputs, cotangent, cot_face, norms, wexp_first, w_expand, w_reduce]
    specs = [ANY] * 5 + [vmem] + [ANY] * 3
    return launch(
        body, ins, specs, outs, scratch, plans, nz, ny, collective_id, "mlp_block", extra_locals=12, vmem=62
    )


def masked_scores(queries, keys, query_doc, key_doc, scale):
    raw = lax.dot_general(queries, keys, (((1,), (1,)), ((), ())), preferred_element_type=F32) * scale
    return jnp.where(query_doc == key_doc, raw, NEG_FILL)


def attend_forward(queries, keys_vals, query_doc, key_doc, bounds, heads, head_dim):
    micro_count, rows, _ = queries.shape
    blocks = rows // BLOCK
    scale = 1.0 / math.sqrt(head_dim)
    tall = heads * BLOCK

    def kernel(bounds_ref, q_ref, kv_ref, qd_ref, kd_ref, out_ref, log_ref):
        at = pl.program_id(0) * blocks + pl.program_id(1)
        low, high = bounds_ref[2 * at], bounds_ref[2 * at + 1]
        queries = jnp.concatenate([q_ref[0, :, h * head_dim : (h + 1) * head_dim] for h in range(heads)], axis=0)
        doc = jnp.concatenate([qd_ref[0]] * heads, axis=0)

        def body(block, carry):
            top, total, mixed = carry
            first = pl.multiple_of(block * BLOCK, BLOCK)
            keys = kv_ref[0, pl.ds(first, BLOCK), :head_dim]
            values = kv_ref[0, pl.ds(first, BLOCK), head_dim:]
            scores = masked_scores(queries, keys, doc, kd_ref[0, :, pl.ds(first, BLOCK)], scale)
            new_top = jnp.maximum(top, jnp.max(scores, axis=-1, keepdims=True))
            weights = jnp.where(scores == NEG_FILL, 0.0, jnp.exp(scores - new_top))
            fade = jnp.exp(top - new_top)
            total = total * fade + jnp.sum(weights, axis=-1, keepdims=True)
            mixed = mixed * fade + jnp.dot(weights.astype(BF16), values, preferred_element_type=F32)
            return new_top, total, mixed

        top, total, mixed = lax.fori_loop(
            low,
            high,
            body,
            (
                jnp.full((tall, 1), NEG_FILL, F32),
                jnp.zeros((tall, 1), F32),
                jnp.zeros((tall, head_dim), F32),
            ),
        )
        mixed = (mixed / total).astype(BF16)
        for h in range(heads):
            out_ref[0, :, h * head_dim : (h + 1) * head_dim] = mixed[h * BLOCK : (h + 1) * BLOCK]
        log_ref[0, 0] = top + jnp.log(total)

    return pl.pallas_call(
        kernel,
        out_shape=[
            jax.ShapeDtypeStruct(queries.shape, BF16),
            jax.ShapeDtypeStruct((micro_count, blocks, tall, 1), F32),
        ],
        grid_spec=pltpu.PrefetchScalarGridSpec(
            num_scalar_prefetch=1,
            grid=(micro_count, blocks),
            in_specs=[
                pl.BlockSpec((1, BLOCK, heads * head_dim), lambda m, b, _: (m, b, 0)),
                pl.BlockSpec((1,) + keys_vals.shape[1:], lambda m, b, _: (m, 0, 0)),
                pl.BlockSpec((1, BLOCK, 1), lambda m, b, _: (m, b, 0)),
                pl.BlockSpec((1, 1, keys_vals.shape[1]), lambda m, b, _: (m, 0, 0)),
            ],
            out_specs=[
                pl.BlockSpec((1, BLOCK, heads * head_dim), lambda m, b, _: (m, b, 0)),
                pl.BlockSpec((1, 1, tall, 1), lambda m, b, _: (m, b, 0, 0)),
            ],
        ),
        compiler_params=pltpu.CompilerParams(vmem_limit_bytes=40 << 20),
        name="attend_forward",
    )(bounds, queries, keys_vals, query_doc, key_doc)


def attend_backward(queries, keys_vals, mixed, grad_mixed, log_total, query_doc, key_doc, bounds, heads, head_dim):
    micro_count, rows, _ = queries.shape
    blocks = rows // BLOCK
    seq_len = keys_vals.shape[1]
    scale = 1.0 / math.sqrt(head_dim)
    tall = heads * BLOCK

    def kernel(bounds_ref, q_ref, kv_ref, o_ref, do_ref, log_ref, qd_ref, kd_ref, gq_ref, gkv_ref, acc_ref):
        at = pl.program_id(0) * blocks + pl.program_id(1)
        low, high = bounds_ref[2 * at], bounds_ref[2 * at + 1]

        def stack(ref):
            return jnp.concatenate([ref[0, :, h * head_dim : (h + 1) * head_dim] for h in range(heads)], axis=0)

        @pl.when(pl.program_id(1) == 0)
        def _():
            acc_ref[...] = jnp.zeros_like(acc_ref)

        queries, grad = stack(q_ref), stack(do_ref)
        delta = jnp.sum(grad.astype(F32) * stack(o_ref).astype(F32), axis=-1, keepdims=True)
        doc = jnp.concatenate([qd_ref[0]] * heads, axis=0)
        log_total = log_ref[0, 0]

        def body(block, grad_queries):
            first = pl.multiple_of(block * BLOCK, BLOCK)
            keys = kv_ref[0, pl.ds(first, BLOCK), :head_dim]
            values = kv_ref[0, pl.ds(first, BLOCK), head_dim:]
            scores = masked_scores(queries, keys, doc, kd_ref[0, :, pl.ds(first, BLOCK)], scale)
            probs = jnp.where(scores == NEG_FILL, 0.0, jnp.exp(scores - log_total))
            grad_probs = lax.dot_general(grad, values, (((1,), (1,)), ((), ())), preferred_element_type=F32)
            grad_scores = (probs * (grad_probs - delta)).astype(BF16)
            across = (((0,), (0,)), ((), ()))
            acc_ref[pl.ds(first, BLOCK), :head_dim] += (
                lax.dot_general(grad_scores, queries, across, preferred_element_type=F32) * scale
            )
            acc_ref[pl.ds(first, BLOCK), head_dim:] += lax.dot_general(
                probs.astype(BF16), grad, across, preferred_element_type=F32
            )
            return grad_queries + jnp.dot(grad_scores, keys, preferred_element_type=F32)

        grad_queries = lax.fori_loop(low, high, body, jnp.zeros((tall, head_dim), F32))
        grad_queries = (grad_queries * scale).astype(BF16)
        for h in range(heads):
            gq_ref[0, :, h * head_dim : (h + 1) * head_dim] = grad_queries[h * BLOCK : (h + 1) * BLOCK]

        @pl.when(pl.program_id(1) == blocks - 1)
        def _():
            gkv_ref[0] = acc_ref[...].astype(BF16)

    wide = pl.BlockSpec((1, BLOCK, heads * head_dim), lambda m, b, _: (m, b, 0))
    row = pl.BlockSpec((1, seq_len, 2 * head_dim), lambda m, b, _: (m, 0, 0))
    return pl.pallas_call(
        kernel,
        out_shape=[
            jax.ShapeDtypeStruct(queries.shape, BF16),
            jax.ShapeDtypeStruct(keys_vals.shape, BF16),
        ],
        grid_spec=pltpu.PrefetchScalarGridSpec(
            num_scalar_prefetch=1,
            grid=(micro_count, blocks),
            in_specs=[
                wide,
                row,
                wide,
                wide,
                pl.BlockSpec((1, 1, tall, 1), lambda m, b, _: (m, b, 0, 0)),
                pl.BlockSpec((1, BLOCK, 1), lambda m, b, _: (m, b, 0)),
                pl.BlockSpec((1, 1, seq_len), lambda m, b, _: (m, 0, 0)),
            ],
            out_specs=[wide, row],
            scratch_shapes=[pltpu.VMEM((seq_len, 2 * head_dim), F32)],
        ),
        compiler_params=pltpu.CompilerParams(vmem_limit_bytes=40 << 20),
        name="attend_backward",
    )(bounds, queries, keys_vals, mixed, grad_mixed, log_total, query_doc, key_doc)


def local(
    inputs,
    cotangent,
    doc_ids,
    attn_gain,
    attn_shift,
    w_query,
    w_keyval,
    w_attn_out,
    mlp_gain,
    mlp_shift,
    w_expand,
    w_reduce,
):
    nz = lax.axis_size("dp") // 2
    tensor_count = lax.axis_size("tensor")
    ny = tensor_count // 2
    ranks = 2 * tensor_count
    micro_count, own_rows, width = inputs.shape
    face_rows = own_rows * ranks
    tokens = micro_count * face_rows
    seq_len = doc_ids.shape[1]
    head_dim = w_keyval.shape[1] // 2
    heads = w_query.shape[1] // (2 * head_dim)
    z = lax.axis_index("dp") // 2
    swap = functools.partial(exchange, nz=nz, ny=ny)
    on = (nz, ny)

    def dot(a, b):
        return jnp.dot(a, b, preferred_element_type=F32)

    def dot_bt(a, b):
        return lax.dot_general(a, b, (((1,), (1,)), ((), ())), preferred_element_type=F32)

    def dot_at(a, b):
        return lax.dot_general(a, b, (((0,), (0,)), ((), ())), preferred_element_type=F32)

    norms = jnp.stack([attn_gain, attn_shift, mlp_gain, mlp_shift])
    norms = jnp.concatenate([norms, jnp.zeros((4, norms.shape[1]), BF16)])
    (wq, wo, wkv), (norms,), (face_in,) = swap(
        [
            LineGather([w_query, w_attn_out, w_keyval], ["row", "col", "both"], *on),
            PlaneGather(norms, *on),
            FaceGather(inputs, *on, hold_x=True),
        ],
        collective_id=1,
        name="gather_attention",
    )
    norms = norms[:, :4].transpose(1, 0, 2).reshape(4, width).astype(F32)
    gain_one, shift_one = norms[0], norms[1]

    normed = layer_norm(face_in.astype(F32), gain_one, shift_one).astype(BF16).reshape(tokens, width)
    queries = dot(normed, wq).astype(BF16).reshape(micro_count, face_rows, heads * head_dim)
    keys_face = dot(normed, wkv).astype(BF16).reshape(micro_count, face_rows, 2 * head_dim)
    (keys_vals,), (wexp_first,), (cot_face,) = swap(
        [
            KeysGather(keys_face, *on),
            LineGather([w_expand], ["row"], *on, share=(0, 2)),
            FaceGather(cotangent, *on, hold_x=True),
        ],
        collective_id=2,
        name="gather_keys",
    )

    query_doc = lax.dynamic_slice_in_dim(doc_ids, z * face_rows, face_rows, axis=1)
    blocks = face_rows // BLOCK
    last_doc = doc_ids[:, BLOCK - 1 :: BLOCK]
    first_doc = query_doc[:, ::BLOCK]
    lows = jnp.sum((last_doc[:, None, :] < first_doc[:, :, None]).astype(jnp.int32), axis=-1)
    highs = jnp.broadcast_to(z * blocks + jnp.arange(blocks, dtype=jnp.int32) + 1, lows.shape)
    bounds = jnp.stack([lows, highs], axis=-1).reshape(-1)
    docs = (query_doc[:, :, None], doc_ids[:, None, :], bounds, heads, head_dim)
    mixed, log_total = attend_forward(queries, keys_vals, *docs)
    mixed_flat = mixed.reshape(tokens, heads * head_dim)

    own_in = inputs.astype(F32)
    middle, grad_middle, low_middle, grad_norm_two, part_expand_a, part_expand_b, reduced, grad_reduce = mlp_block(
        mixed_flat, wo, inputs, cotangent, cot_face, norms[2:], wexp_first, w_expand, w_reduce, *on, collective_id=3
    )
    grad_gain_two, grad_shift_two = jnp.sum(grad_norm_two, axis=1)
    (grad_branch,), (reduced,), (grad_expand_a, grad_expand_b) = swap(
        [
            FaceGather(low_middle, *on),
            FaceScatter(reduced, *on),
            LineScatter([part_expand_a, part_expand_b], ["row", "row"], *on),
        ],
        collective_id=6,
        name="gather_branch",
    )
    outputs = (middle + reduced).astype(BF16)
    grad_branch = grad_branch.reshape(tokens, width)
    part_attn_out = dot_at(mixed_flat, grad_branch).astype(BF16)
    grad_mixed = dot_bt(grad_branch, wo).astype(BF16).reshape(mixed.shape)
    grad_queries, grad_keys = attend_backward(queries, keys_vals, mixed, grad_mixed, log_total, *docs)
    grad_queries = grad_queries.reshape(tokens, heads * head_dim)
    part_query = dot_at(normed, grad_queries).astype(BF16)
    from_query = dot_bt(grad_queries, wq).astype(BF16).reshape(micro_count, face_rows, width)
    (from_query,), (grad_keys,), (grad_attn_out, grad_query) = swap(
        [
            FaceScatter(from_query, *on),
            WholeScatter(grad_keys.reshape(micro_count, nz, face_rows, 2 * head_dim), *on),
            LineScatter([part_attn_out, part_query], ["col", "row"], *on),
        ],
        collective_id=7,
        name="scatter_query",
    )
    grad_keys = grad_keys.astype(BF16).reshape(micro_count * own_rows, 2 * head_dim)
    normed_own, norm_pull_one = jax.vjp(layer_norm, own_in, gain_one, shift_one)
    grad_normed = from_query + dot_bt(grad_keys, wkv).reshape(from_query.shape)
    grad_tok_norm, grad_gain_one, grad_shift_one = norm_pull_one(grad_normed)
    part_keyval = dot_at(normed_own.astype(BF16).reshape(-1, width), grad_keys).astype(BF16)
    own_width = width // (nz * ranks)
    small = jnp.stack([grad_gain_one, grad_shift_one, grad_gain_two, grad_shift_two])
    small = small.reshape(4, nz, ranks, own_width).transpose(2, 1, 0, 3)
    small = jnp.pad(small, ((0, 0), (0, 0), (0, 4), (0, 128 - own_width)))
    (grad_keyval,), (small,) = swap(
        [WholeScatter(part_keyval.reshape(1, nz, width // nz, 2 * head_dim), *on), SmallScatter(small, *on)],
        collective_id=8,
        name="scatter_small",
    )
    small = small[:4, :own_width]

    def by_row(halves):
        return jnp.concatenate([halves[0], halves[1]], axis=1).astype(F32)

    def by_column(halves):
        return halves.reshape(-1, halves.shape[-1]).astype(F32)

    return (
        outputs,
        grad_middle + grad_tok_norm,
        small[0],
        small[1],
        by_row(grad_query),
        grad_keyval[0],
        by_column(grad_attn_out),
        small[2],
        small[3],
        by_row(jnp.concatenate([grad_expand_a, grad_expand_b], axis=2)),
        by_column(grad_reduce),
    )


def solution(mesh):
    placed = (
        P(None, ("dp", "tensor"), None),
        P(None, ("dp", "tensor"), None),
        P(),
        P("dp"),
        P("dp"),
        P("dp", "tensor"),
        P("dp", None),
        P("tensor", "dp"),
        P("dp"),
        P("dp"),
        P("dp", "tensor"),
        P("tensor", "dp"),
    )
    return jax.shard_map(
        local,
        mesh=mesh,
        in_specs=placed,
        out_specs=(
            P(None, ("dp", "tensor"), None),
            P(None, ("dp", "tensor"), None),
            P(("dp", "tensor")),
            P(("dp", "tensor")),
            P("dp", "tensor"),
            P(("dp", "tensor"), None),
            P("tensor", "dp"),
            P(("dp", "tensor")),
            P(("dp", "tensor")),
            P("dp", "tensor"),
            P("tensor", "dp"),
        ),
        check_vma=False,
    )
```

```python
import functools
import math

import jax
import jax.numpy as jnp
from jax import lax
from jax.experimental import pallas as pl
from jax.experimental.pallas import tpu as pltpu
from jax.sharding import PartitionSpec as P

BLOCK = 256
EPSILON = 1e-05
NEG_FILL = -1e30
GELU_A = math.sqrt(2.0 / math.pi)
GELU_B = 0.044715
LOG2_E = 1.0 / math.log(2.0)
K1_ORDER = (0, 2, 1, 2, 0, 2, 3, 0, 0, 0, 0, 0, 2, 0, 0, 2, 0, 1, 0, 0, 2, 2, 2, 0, 0, 0, 0, 0, 0, 2)
K2_ORDER = (0, 2, 2, 1, 0, 1, 1, 2, 2, 2, 0, 2, 0, 1, 2)
MESH = pl.DeviceIdType.MESH
ANY = pl.BlockSpec(memory_space=pl.ANY)
IN_VMEM = pl.BlockSpec(memory_space=pltpu.VMEM)
BF16 = jnp.bfloat16
F32 = jnp.float32


def layer_norm(values, gain, shift):
    center = jnp.mean(values, axis=-1, keepdims=True)
    centered = values - center
    variance = jnp.mean(centered * centered, axis=-1, keepdims=True)
    return centered * lax.rsqrt(variance + EPSILON) * gain + shift


def gelu_tanh(values):
    return jax.nn.gelu(values, approximate=True)


class Net:
    def __init__(self, nz, ny, send, recv, local):
        dp, tensor = lax.axis_index("dp"), lax.axis_index("tensor")
        self.nz, self.ny = nz, ny
        self.z, self.x = lax.div(dp, 2), lax.rem(dp, 2)
        self.y, self.c = lax.div(tensor, 2), lax.rem(tensor, 2)
        self.tensor = tensor
        self.send, self.recv, self.local = send, recv, local
        self.used = [0, 0]
        self.keys = {}

    def flip(self, value, by):
        return value + by - 2 * by * value if by else value

    def xy(self, dx, dy):
        return self.flip(self.x, dx), lax.rem(self.y + dy, self.ny) if dy else self.y

    def rank(self, dx=0, dy=0, dc=0):
        x, y = self.xy(dx, dy)
        return x * (2 * self.ny) + y * 2 + self.flip(self.c, dc)

    def device(self, dx=0, dy=0, dc=0, z=None):
        x, y = self.xy(dx, dy)
        return ((self.z if z is None else z) * 2 + x, y * 2 + self.flip(self.c, dc))

    def slot(self, key):
        if key not in self.keys:
            self.keys[key] = self.used[0]
            self.used[0] += 1
        return self.keys[key]

    def remote(self, key, src, dst, device):
        at = self.slot(key)
        return pltpu.make_async_remote_copy(
            src_ref=src,
            dst_ref=dst,
            send_sem=self.send.at[at],
            recv_sem=self.recv.at[at],
            device_id=device,
            device_id_type=MESH,
        )

    def take_locals(self, count):
        first = self.used[1]
        self.used[1] += count
        return first

    def copy_at(self, at, src, dst):
        return pltpu.make_async_copy(src, dst, self.local.at[at])

    def copy(self, src, dst):
        return self.copy_at(self.take_locals(1), src, dst)


def add_rows(dst, terms):
    lead, height, width = dst.shape
    rows = min(max(16, 32768 // width), height)
    steps = height // rows

    def body(step, carry):
        at, off = lax.div(step, steps), pl.multiple_of(lax.rem(step, steps) * rows, rows)
        total = terms[0][at, pl.ds(off, rows), :].astype(F32)
        for term in terms[1:]:
            total = total + term[at, pl.ds(off, rows), :].astype(F32)
        dst[at, pl.ds(off, rows), :] = total.astype(dst.dtype)
        return carry

    lax.fori_loop(0, lead * steps, body, 0)


class FaceGather:
    moves = ("x", "y", "c")
    in_spec = IN_VMEM

    def __init__(self, own, nz, ny, hold_x=False):
        self.ins, self.hold_x = [own], hold_x
        m, t, d = own.shape
        self.outs = [(jax.ShapeDtypeStruct((m, 4 * ny * t, d), own.dtype), ANY)]
        self.scratch = []
        self.half = t // 2
        self.remotes, self.locals = 8 * ny, 1

    def run(self, net, ins, outs, scratch):
        (own,), (out,), half = ins, outs, self.half
        dys = range(1, net.ny)

        def piece(dx, dy, h):
            return out.at[:, pl.ds(pl.multiple_of(net.rank(dx, dy) * 2 * half + h * half, half), half), :]

        mine = [own.at[:, pl.ds(h * half, half), :] for h in (0, 1)]
        keep = net.copy(own, out.at[:, pl.ds(pl.multiple_of(net.rank() * 2 * half, half), 2 * half), :])
        keep.start()
        sent = {}

        def send(key, src, dst, device):
            sent[key] = net.remote((id(self), key), src, dst, device)
            sent[key].start()

        if not self.hold_x:
            send(("x", 0), mine[0], piece(0, 0, 0), net.device(1, 0))
        for dy in dys:
            send(("y", dy, 1), mine[1], piece(0, 0, 1), net.device(0, dy))
        if not self.hold_x:
            send(("x", 1), mine[1], piece(0, 0, 1), net.device(1, 0))
        for dy in dys:
            send(("y", dy, 0), mine[0], piece(0, 0, 0), net.device(0, dy))
        for h in (0, 1):
            send(("c", h), mine[h], piece(0, 0, h), net.device(0, 0, 1))
        if self.hold_x:
            yield
            for h in (0, 1):
                send(("x", h), mine[h], piece(0, 0, h), net.device(1, 0))

        def share(key, dx, dy, h):
            send(("c",) + key, piece(dx, dy, h), piece(dx, dy, h), net.device(0, 0, 1))

        def from_x(h):
            sent["x", h].wait_recv()
            if not h:
                for dy in dys:
                    send(("xy", dy), piece(1, 0, 0), piece(1, 0, 0), net.device(0, dy))
            share(("x", h), 1, 0, h)

        def from_y(dy, h):
            sent["y", dy, h].wait_recv()
            if h:
                send(("yx", dy), piece(0, -dy % net.ny, 1), piece(0, -dy % net.ny, 1), net.device(1, 0))
            share(("y", dy, h), 0, -dy % net.ny, h)

        arrivals = []
        for first in (True, False):
            on_x = [functools.partial(from_x, 0 if first else 1)]
            on_y = [functools.partial(from_y, dy, 1 if first else 0) for dy in dys]
            arrivals.append(on_x + on_y)
        if self.hold_x:
            arrivals = [arrivals[0][1:], arrivals[1][1:], arrivals[0][:1], arrivals[1][:1]]
        for group in arrivals:
            for arrive in group:
                yield
                arrive()
        for dy in dys:
            yield
            sent["xy", dy].wait_recv()
            share(("xy", dy), 1, -dy % net.ny, 0)
            yield
            sent["yx", dy].wait_recv()
            share(("yx", dy), 1, -dy % net.ny, 1)
        yield
        for key, copy in sent.items():
            if key[0] == "c":
                copy.wait_recv()
        for copy in sent.values():
            copy.wait_send()
        keep.wait()


class FaceScatter:
    moves = ("x", "y", "c")

    def __init__(self, part, nz, ny, resident=False):
        self.ins, self.resident = [part], resident
        m, rows, d = part.shape
        t = rows // (4 * ny)
        self.outs = [(jax.ShapeDtypeStruct((m, t, d), F32), pl.BlockSpec(memory_space=pltpu.VMEM))]
        half = t // 2
        self.half = half
        self.scratch = [
            pltpu.VMEM((2 * ny, m, t, d), BF16),
            pltpu.VMEM((ny - 1, m, half, d), BF16),
            pltpu.VMEM((ny - 1, m, half, d), BF16),
            pltpu.VMEM((2, m, half, d), BF16),
            pltpu.VMEM((2, ny - 1, m, half, d), BF16),
        ]
        if not resident:
            self.scratch.append(pltpu.VMEM((2 * ny, m, t, d), BF16))
        self.remotes, self.locals = 6 * ny + 4, 2 * ny

    def run(self, net, ins, outs, scratch):
        (part,), (out,), half = ins, outs, self.half
        from_core, x_diag, y_diag, x_in, y_in = scratch[:5]
        ny = net.ny
        dys = range(1, ny)
        order = [(1, dy) for dy in dys] + [(1, 0)] + [(0, dy) for dy in dys] + [(0, 0)]
        sent, loads = {}, {}

        def send(key, src, dst, device):
            sent[key] = net.remote((id(self), key), src, dst, device)
            sent[key].start()

        def rows(dx, dy, dc, first=0, size=2 * half):
            at = net.rank(dx, dy, dc) * 2 * half + first
            return part.at[:, pl.ds(pl.multiple_of(at, half), size), :]

        def work(dx, dy, first=0, size=2 * half):
            if self.resident:
                return rows(dx, dy, 0, first, size)
            return scratch[5].at[dx * ny + dy, :, pl.ds(first, size), :]

        for dx, dy in order:
            at = dx * ny + dy
            if not self.resident:
                loads[at] = net.copy(rows(dx, dy, 0), work(dx, dy))
                loads[at].start()
            send(("c", at), rows(dx, dy, 1), from_core.at[at], net.device(0, 0, 1))
        for dx, dy in order:
            at = dx * ny + dy
            yield
            if not self.resident:
                loads[at].wait()
            sent["c", at].wait_recv()
            add_rows(work(dx, dy), [work(dx, dy), from_core.at[at]])
            top, low = work(dx, dy, 0, half), work(dx, dy, half, half)
            if dx and dy:
                send(("xd", dy), top, x_diag.at[dy - 1], net.device(1, 0))
                send(("yd", dy), low, y_diag.at[dy - 1], net.device(0, dy))
            elif dx:
                send(("x", 0), top, x_in.at[0], net.device(1, 0))
            elif dy:
                send(("y", dy, 1), low, y_in.at[1, dy - 1], net.device(0, dy))
        for dy in dys:
            yield
            sent["xd", dy].wait_recv()
            top = work(0, dy, 0, half)
            add_rows(top, [top, x_diag.at[dy - 1]])
            send(("y", dy, 0), top, y_in.at[0, dy - 1], net.device(0, dy))
        low = work(1, 0, half, half)
        for dy in dys:
            yield
            sent["yd", dy].wait_recv()
            add_rows(low, [low, y_diag.at[dy - 1]])
        send(("x", 1), low, x_in.at[1], net.device(1, 0))
        for h in (0, 1):
            yield
            sent["x", h].wait_recv()
            for dy in dys:
                sent["y", dy, h].wait_recv()
            add_rows(
                out.at[:, pl.ds(h * half, half), :],
                [work(0, 0, h * half, half), x_in.at[h]] + [y_in.at[h, dy - 1] for dy in dys],
            )
        for copy in sent.values():
            copy.wait_send()


class LineGather:
    moves = ("x", "line", "c")
    in_spec = IN_VMEM

    def __init__(self, shards, kinds, nz, ny, share=(0, 1), given=()):
        self.ins, self.kinds, self.share = list(shards) + list(given), list(kinds), share
        self.outs, self.scratch = [], []
        for shard, kind in zip(shards, kinds):
            rows, columns = shard.shape
            if kind == "row":
                shape = (rows * 2 * nz, columns // 2 // share[1])
            elif kind == "col":
                shape = (rows // 2 // share[1], columns * 2 * nz)
            else:
                shape = (rows * 2 * nz, columns)
            self.outs.append((jax.ShapeDtypeStruct(shape, shard.dtype), ANY))
        count = len(self.kinds)
        self.remotes = count * (1 + 4 * (nz - 1)) + kinds.count("both") * (1 + 4 * (nz - 1))
        self.locals = 2 * count

    def run(self, net, ins, outs, scratch):
        nz, z = net.nz, net.z
        sent, locals_, shared = [], [], []
        weights = []
        given = ins[len(self.kinds) :]
        for at, (shard, out, kind) in enumerate(zip(ins, outs, self.kinds)):
            rows, columns = shard.shape

            if kind == "row":
                span = columns // 2 // self.share[1]

                def mine(dx, shard=shard, span=span):
                    first = (net.flip(net.x, dx) * self.share[1] + self.share[0]) * span
                    return shard.at[:, pl.ds(pl.multiple_of(first, span), span)]

                def block(line, dx, out=out, rows=rows):
                    first = (line * 2 + net.flip(net.x, dx)) * rows
                    return out.at[pl.ds(pl.multiple_of(first, rows), rows), :]

            elif kind == "col":
                span = rows // 2 // self.share[1]

                def mine(dx, shard=shard, span=span):
                    first = (net.flip(net.x, dx) * self.share[1] + self.share[0]) * span
                    return shard.at[pl.ds(pl.multiple_of(first, span), span), :]

                def block(line, dx, out=out, columns=columns):
                    first = (line * 2 + net.flip(net.x, dx)) * columns
                    return out.at[:, pl.ds(pl.multiple_of(first, columns), columns)]

            else:
                half = rows // 2

                def mine(dx, shard=shard, half=half):
                    return shard.at[pl.ds(pl.multiple_of(net.c * half, half), half), :]

                def block(line, dx, out=out, rows=rows, half=half):
                    first = (line * 2 + net.flip(net.x, dx)) * rows + net.c * half
                    return out.at[pl.ds(pl.multiple_of(first, half), half), :]

            weights.append((at, kind, mine, block))

        def hop(at, dx, step, up, block, src=None):
            origin = z - (step - 1) if up else z + (step - 1)
            there = z + 1 if up else z - 1
            copy = net.remote(
                (id(self), at, dx, step, up),
                block(origin, dx) if src is None else src,
                block(origin, dx),
                net.device(z=there),
            )
            fits = (origin >= 0) & (there < nz) if up else (origin < nz) & (there >= 0)
            return copy, fits

        def start(at, dx, step, up, block, src=None):
            copy, fits = hop(at, dx, step, up, block, src)
            pl.when(fits)(copy.start)
            sent.append((copy, fits))

        def arrived(at, dx, step, up, block, kind):
            copy, _ = hop(at, dx, step, up, block)
            origin = z - step if up else z + step
            fits = origin >= 0 if up else origin < nz
            pl.when(fits)(copy.wait_recv)
            if kind == "both":
                share = net.remote(
                    (id(self), "c", at, dx, step, up), block(origin, dx), block(origin, dx), net.device(0, 0, 1)
                )
                pl.when(fits)(share.start)
                shared.append((share, fits))

        swaps = {}
        for at, kind, mine, block in weights:
            if not given:
                swaps[at] = net.remote((id(self), at, "x"), mine(1), block(z, 0), net.device(1, 0))
                swaps[at].start()
            for up in (True, False):
                start(at, 0, 1, up, block, mine(0))
        for at, kind, mine, block in weights:
            if kind == "both":
                whole = ins[at].shape[0]
                into = outs[at].at[pl.ds(pl.multiple_of((z * 2 + net.x) * whole, whole), whole), :]
                locals_.append(net.copy(ins[at], into))
            else:
                locals_.append(net.copy(mine(0), block(z, 0)))
            locals_[-1].start()
        for (at, kind, mine, block), other in zip(weights, given):
            span = pl.ds(self.share[0] * other.shape[kind == "row"] // self.share[1], other.shape[kind == "row"] // self.share[1])
            other = other.at[:, span] if kind == "row" else other.at[span, :]
            locals_.append(net.copy(other, block(z, 1)))
            locals_[-1].start()
            for up in (True, False):
                start(at, 1, 1, up, block, other)
        yield
        for copy in locals_:
            copy.wait()
        for at, kind, mine, block in weights:
            if given:
                continue
            swaps[at].wait_recv()
            for up in (True, False):
                start(at, 1, 1, up, block)
            if kind == "both":
                share = net.remote((id(self), "c", at), block(z, 1), block(z, 1), net.device(0, 0, 1))
                share.start()
                shared.append((share, None))
        for step in range(1, nz):
            for at, kind, mine, block in weights:
                for dx in (0, 1):
                    yield
                    for up in (True, False):
                        arrived(at, dx, step, up, block, kind)
                        if step < nz - 1:
                            start(at, dx, step + 1, up, block)
        yield
        for copy, fits in shared:
            if fits is None:
                copy.wait()
            else:
                pl.when(fits)(copy.wait)
        for copy, fits in sent:
            pl.when(fits)(copy.wait_send)
        for copy in swaps.values():
            copy.wait_send()


class HalfSwap:
    moves = ("x",)

    def __init__(self, shards, kinds, nz, ny):
        self.ins, self.kinds = list(shards), list(kinds)
        self.outs, self.scratch = [], []
        for shard, kind in zip(shards, kinds):
            rows, columns = shard.shape
            shape = (rows, columns // 2) if kind == "row" else (rows // 2, columns)
            self.outs.append((jax.ShapeDtypeStruct(shape, shard.dtype), ANY))
        self.remotes, self.locals = len(self.ins), 0

    def run(self, net, ins, outs, scratch):
        copies = []
        for at, (shard, out, kind) in enumerate(zip(ins, outs, self.kinds)):
            span = out.shape[kind == "row"]
            there = pl.ds(pl.multiple_of((1 - net.x) * span, span), span)
            src = shard.at[:, there] if kind == "row" else shard.at[there, :]
            copies.append(net.remote((id(self), at), src, out, net.device(1, 0)))
            copies[-1].start()
        yield
        for copy in copies:
            copy.wait()


class LineScatter:
    moves = ("x", "line")

    def __init__(self, parts, kinds, nz, ny, resident=False):
        self.ins, self.kinds, self.resident = list(parts), list(kinds), resident
        self.outs, self.scratch = [], []
        for part, kind in zip(parts, kinds):
            rows, columns = part.shape
            shape = (rows // (2 * nz), columns) if kind == "row" else (rows, columns // (2 * nz))
            self.outs.append((jax.ShapeDtypeStruct((2,) + shape, BF16), ANY))
            for lead in (nz - 1, nz - 1, 1) + (() if resident else (nz,)):
                self.scratch.append(pltpu.VMEM((lead, 2) + shape, BF16))
        count = len(self.ins)
        self.remotes = count * (1 + 4 * nz)
        self.locals = count * (2 * nz + 1)

    def run(self, net, ins, outs, scratch):
        nz, z = net.nz, net.z
        loads, grads = {}, []
        each = 3 if self.resident else 4
        for at, (part, out, kind) in enumerate(zip(ins, outs, self.kinds)):
            down, up, mine = scratch[each * at : each * at + 3]
            _, _, rows, columns = mine.shape

            def block(line, dx, part=part, kind=kind, rows=rows, columns=columns):
                size = rows if kind == "row" else columns
                first = pl.ds(pl.multiple_of((line * 2 + net.flip(net.x, dx)) * size, size), size)
                return part.at[first, :] if kind == "row" else part.at[:, first]

            if self.resident:
                work = block
            else:

                def work(line, dx, at=at):
                    return scratch[each * at + 3].at[line, dx]

                order = []
                for k in range(nz):
                    order += [k, nz - 1 - k]
                for line in dict.fromkeys(order):
                    for dx in (1, 0):
                        loads[at, line, dx] = net.copy(block(line, dx), work(line, dx))
                        loads[at, line, dx].start()
            grads.append((at, out, work, down, up, mine))

        def inbox(slots, line, dx, toward):
            return slots.at[line if toward < 0 else line - 1, dx]

        pieces = [(grad, dx) for dx in (1, 0) for grad in grads]
        each_line = len(pieces)

        for at, *_ in grads:
            net.slot((id(self), at, "x"))
            for dx in (0, 1):
                for line in range(nz):
                    for toward in (-1, 1):
                        net.slot((id(self), at, line, dx, toward))

        def chain(grad, dx, line, toward):
            at, out, work, down, up, mine = grad
            slot = inbox(down if toward < 0 else up, line, dx, toward)
            copy = net.remote((id(self), at, line, dx, toward), work(line, dx), slot, net.device(z=z + toward))
            return copy, slot

        def forward(place, grad, dx, line, toward):
            at, out, work, down, up, mine = grad
            copy, slot = chain(grad, dx, line, toward)
            if not self.resident:
                loads[at, line, dx].wait()
            if place != (nz - 1 if toward < 0 else 0):
                copy.wait_recv()
                add_rows(_lead(work(line, dx)), [_lead(work(line, dx)), _lead(slot)])
            copy.start()

        def finish(place, grad, dx):
            at, out, work, down, up, mine = grad
            if not self.resident:
                loads[at, place, dx].wait()
            terms = [_lead(work(place, dx))]
            for toward in (-1, 1):
                if (place < nz - 1) if toward < 0 else (place > 0):
                    copy, slot = chain(grad, dx, place, toward)
                    copy.wait_recv()
                    terms.append(_lead(slot))
            total = mine.at[0, dx]
            add_rows(_lead(total), terms)
            if dx:
                net.remote((id(self), at, "x"), total, out.at[net.x], net.device(1, 0)).start()
            else:
                net.copy_at(self.first_local + at, total, out.at[net.x]).start()

        plan = {}
        for place in range(nz):
            waits_up, waits_down = place, nz - 1 - place
            todo = []
            for toward, waits, lines in (
                (1, waits_up, range(nz - 1, place, -1)),
                (-1, waits_down, range(place)),
            ):
                order = [(line, piece) for line in lines for piece in pieces]
                for j, (line, (grad, dx)) in enumerate(order):
                    todo.append((waits + j if waits else 0, waits, (forward, grad, dx, line, toward)))
            for q, (grad, dx) in enumerate(pieces):
                times = []
                if waits_up:
                    times.append(waits_up + each_line * (nz - 1 - place) + q)
                if waits_down:
                    times.append(waits_down + each_line * place + q)
                todo.append((max(times), nz, (finish, grad, dx)))
            for time, waits, item in sorted(todo, key=lambda entry: entry[:2]):
                plan.setdefault(time, {}).setdefault(place, []).append(item)
        self.first_local = net.take_locals(len(grads))
        for time in range(max(plan) + 1):
            if time:
                yield
            for place, items in sorted(plan.get(time, {}).items()):

                def act(place=place, items=items):
                    for item in items:
                        item[0](place, *item[1:])

                pl.when(z == place)(act)
        sent = [
            (chain(grad, dx, line, toward)[0], (z > line) if toward < 0 else (z < line))
            for grad, dx in pieces
            for toward, lines in ((-1, range(nz - 1)), (1, range(1, nz)))
            for line in lines
        ]
        swaps = [net.remote((id(self), at, "x"), mine.at[0, 1], out.at[net.x], net.device(1, 0)) for at, out, _, _, _, mine in grads]
        stores = [net.copy_at(self.first_local + at, mine.at[0, 0], out.at[net.x]) for at, out, _, _, _, mine in grads]
        yield
        for copy, sends in sent:
            pl.when(sends)(copy.wait_send)
        for copy in swaps:
            copy.wait()
        for copy in stores:
            copy.wait()


def _lead(ref):
    return Lead(ref)


class Lead:
    def __init__(self, ref):
        self.ref, self.shape, self.dtype = ref, (1,) + tuple(ref.shape), ref.dtype

    def __getitem__(self, index):
        return self.ref[index[1], index[2]]

    def __setitem__(self, index, value):
        self.ref[index[1], index[2]] = value


class KeysGather:
    moves = ("x", "line", "c")
    in_spec = IN_VMEM

    def __init__(self, face, nz, ny):
        m, rows, width = face.shape
        self.ins = [face]
        self.outs = [(jax.ShapeDtypeStruct((m, nz * rows, width), face.dtype), ANY)]
        self.scratch = []
        self.remotes, self.locals = 4 * (nz - 1), 1

    def run(self, net, ins, outs, scratch):
        (face,), (out,) = ins, outs
        nz, z = net.nz, net.z
        _, rows, width = face.shape
        part, side = rows // 2, width // 2

        def block(line, dx, dc):
            first = pl.multiple_of(line * rows + net.flip(net.x, dx) * part, part)
            column = pl.multiple_of(net.flip(net.c, dc) * side, side)
            return out.at[:, pl.ds(first, part), pl.ds(column, side)]

        own = face.at[
            :,
            pl.ds(pl.multiple_of(net.x * part, part), part),
            pl.ds(pl.multiple_of(net.c * side, side), side),
        ]
        sent, shared = [], []

        def line_copy(step):
            origin = z - (step - 1)
            src = own if step == 1 else block(origin, 0, 0)
            return net.remote((id(self), step), src, block(origin, 0, 0), net.device(z=z + 1))

        def start(step):
            copy, fits = line_copy(step), (z - (step - 1) >= 0) & (z + 1 < nz)
            pl.when(fits)(copy.start)
            sent.append((copy, fits))

        start(1)
        keep = net.copy(face, out.at[:, pl.ds(pl.multiple_of(z * rows, rows), rows), :])
        keep.start()
        later = []
        for step in range(1, nz):
            yield
            fits = z - step >= 0
            pl.when(fits)(line_copy(step).wait_recv)
            if step < nz - 1:
                start(step + 1)
            here = block(z - step, 0, 0)
            across = net.remote((id(self), "x", step), here, here, net.device(1, 0))
            beside = net.remote((id(self), "c", step), here, here, net.device(0, 0, 1))
            for copy in (across, beside):
                pl.when(fits)(copy.start)
                sent.append((copy, fits))
            later.append((step, fits, across))
            shared.append((beside, fits))
        for step, fits, across in later:
            yield
            pl.when(fits)(across.wait_recv)
            there = block(z - step, 1, 0)
            beside = net.remote((id(self), "xc", step), there, there, net.device(0, 0, 1))
            pl.when(fits)(beside.start)
            sent.append((beside, fits))
            shared.append((beside, fits))
        yield
        for copy, fits in shared:
            pl.when(fits)(copy.wait_recv)
        for copy, fits in sent:
            pl.when(fits)(copy.wait_send)
        keep.wait()


class WholeScatter(FaceScatter):
    moves = ("x", "y", "c", "z")

    def __init__(self, part, nz, ny):
        m, _, rows, d = part.shape
        super().__init__(part.reshape(m * nz, rows, d), nz, ny)
        t = rows // (4 * ny)
        self.m, self.nz = m, nz
        self.outs = [(jax.ShapeDtypeStruct((m, t, d), F32), pl.BlockSpec(memory_space=pltpu.VMEM))]
        self.scratch = self.scratch + [pltpu.VMEM((m * nz, t, d), BF16), pltpu.VMEM((nz, m, t, d), BF16)]
        self.remotes = self.remotes + nz * m
        self.locals = self.locals + m

    def run(self, net, ins, outs, scratch):
        face, inbox = scratch[-2:]
        yield from super().run(net, ins, [face], scratch[:-2])
        nz, m = self.nz, self.m
        copies = []
        for far in range(1, nz):
            line = lax.rem(net.z + far, nz)
            for at in range(m):
                copies.append(
                    pltpu.make_async_remote_copy(
                        src_ref=face.at[at * nz + line],
                        dst_ref=inbox.at[far, at],
                        send_sem=net.send.at[net.slot((id(self), "z", far, at))],
                        recv_sem=net.recv.at[net.slot((id(self), "z", far, at))],
                        device_id=net.device(z=line),
                        device_id_type=MESH,
                    )
                )
                copies[-1].start()
        own = []
        for at in range(m):
            own.append(net.copy(face.at[at * nz + net.z], inbox.at[0, at]))
            own[-1].start()
        yield
        for copy in own:
            copy.wait()
        for copy in copies:
            copy.wait()
        add_rows(outs[0], [inbox.at[far] for far in range(nz)])


class PlaneGather:
    moves = ("plane",)
    in_spec = IN_VMEM

    def __init__(self, own, nz, ny):
        self.ins = [own]
        self.outs = [(jax.ShapeDtypeStruct((2 * nz,) + own.shape, own.dtype), ANY)]
        self.scratch = []
        self.remotes, self.locals = 2 * nz, 1

    def run(self, net, ins, outs, scratch):
        (own,), (out,) = ins, outs
        here = out.at[net.z * 2 + net.x]
        copies = []
        for far in range(net.nz):
            for dx in (0, 1):
                if far or dx:
                    line = lax.rem(net.z + far, net.nz)
                    copies.append(net.remote((id(self), far, dx), own, here, net.device(dx, z=line)))
                    copies[-1].start()
        keep = net.copy(own, here)
        keep.start()
        yield
        for copy in copies:
            copy.wait()
        keep.wait()


class SmallScatter:
    moves = ("face", "z")

    def __init__(self, part, nz, ny):
        ranks, _, rows, width = part.shape
        self.ins = [part]
        vmem = pl.BlockSpec(memory_space=pltpu.VMEM)
        self.outs = [(jax.ShapeDtypeStruct((rows, width), F32), vmem)]
        self.scratch = [
            pltpu.VMEM((ranks, nz, rows, width), F32),
            pltpu.VMEM((nz, rows, width), F32),
            pltpu.VMEM((nz, rows, width), F32),
        ]
        self.remotes, self.locals = ranks + nz, 2

    def run(self, net, ins, outs, scratch):
        (part,), (out,) = ins, outs
        inbox, total, line_in = scratch
        ny, nz = net.ny, net.nz
        copies = []
        for dx in (0, 1):
            for dy in range(ny):
                for dc in (0, 1):
                    if dx or dy or dc:
                        at = (dx * ny + dy) * 2 + dc
                        copies.append(
                            net.remote(
                                (id(self), at), part.at[net.rank(dx, dy, dc)], inbox.at[at], net.device(dx, dy, dc)
                            )
                        )
                        copies[-1].start()
        keep = net.copy(part.at[net.rank()], inbox.at[0])
        keep.start()
        yield
        keep.wait()
        for copy in copies:
            copy.wait()
        total[...] = jnp.sum(inbox[...], axis=0)
        lines = []
        for far in range(1, nz):
            line = lax.rem(net.z + far, nz)
            lines.append(net.remote((id(self), "z", far), total.at[line], line_in.at[far], net.device(z=line)))
            lines[-1].start()
        own = net.copy(total.at[net.z], line_in.at[0])
        own.start()
        yield
        own.wait()
        for copy in lines:
            copy.wait()
        out[...] = jnp.sum(line_in[...], axis=0)


def launch(body, ins, in_specs, outs, scratch, plans, nz, ny, collective_id, name, extra_locals=0, vmem=56):
    moves = set()
    for plan in plans:
        moves |= set(plan.moves)
    remotes = sum(plan.remotes for plan in plans)
    locals_ = max(1, extra_locals + sum(plan.locals for plan in plans))

    def kernel(*refs):
        in_refs, refs = refs[: len(ins)], refs[len(ins) :]
        out_refs, refs = refs[: len(outs)], refs[len(outs) :]
        scratch_refs, (send, recv, local) = refs[: len(scratch)], refs[len(scratch) :]
        net = Net(nz, ny, send, recv, local)
        peers = {}
        for far in range(nz):
            for dx in (0, 1):
                for dy in range(ny):
                    for dc in (0, 1):
                        kinds = set()
                        if not far:
                            kinds.add("face")
                            if dx and not dy and not dc:
                                kinds.add("x")
                            if dy and not dx and not dc:
                                kinds.add("y")
                            if dc and not dx and not dy:
                                kinds.add("c")
                        if far and not dx and not dy and not dc:
                            kinds.add("z")
                            if far in (1, nz - 1):
                                kinds.add("line")
                        if not dy and not dc:
                            kinds.add("plane")
                        if (far or dx or dy or dc) and kinds & moves:
                            line = lax.rem(net.z + far, nz) if far else None
                            peers[far, dx, dy, dc] = net.device(dx, dy, dc, line)
        barrier = pltpu.get_barrier_semaphore()
        for device in peers.values():
            pl.semaphore_signal(barrier, inc=1, device_id=device, device_id_type=MESH)
        pl.semaphore_wait(barrier, len(peers))
        body(net, in_refs, out_refs, scratch_refs)

    return list(
        pl.pallas_call(
            kernel,
            out_shape=[shape for shape, _ in outs],
            in_specs=in_specs,
            out_specs=[spec for _, spec in outs],
            scratch_shapes=list(scratch)
            + [
                pltpu.SemaphoreType.DMA((remotes,)),
                pltpu.SemaphoreType.DMA((remotes,)),
                pltpu.SemaphoreType.DMA((locals_,)),
            ],
            compiler_params=pltpu.CompilerParams(
                collective_id=collective_id, has_side_effects=True, vmem_limit_bytes=vmem << 20
            ),
            name=name,
        )(*ins)
    )


def exchange(plans, nz, ny, collective_id, name, order=()):
    ins = [array for plan in plans for array in plan.ins]
    outs = [out for plan in plans for out in plan.outs]
    scratch = [entry for plan in plans for entry in plan.scratch]

    def body(net, in_refs, out_refs, scratch_refs):
        running = []
        for plan in plans:
            mine = []
            for refs_of, count in ((in_refs, plan.ins), (out_refs, plan.outs), (scratch_refs, plan.scratch)):
                mine.append(list(refs_of[: len(count)]))
            in_refs = in_refs[len(plan.ins) :]
            out_refs = out_refs[len(plan.outs) :]
            scratch_refs = scratch_refs[len(plan.scratch) :]
            running.append(plan.run(net, *mine))
        for at in order:
            next(running[at], None)
        while running:
            for steps in list(running):
                try:
                    next(steps)
                except StopIteration:
                    running.remove(steps)

    specs = [getattr(plan, "in_spec", ANY) for plan in plans for _ in plan.ins]
    results = launch(body, ins, specs, outs, scratch, plans, nz, ny, collective_id, name)
    grouped = []
    for plan in plans:
        grouped.append(results[: len(plan.outs)])
        results = results[len(plan.outs) :]
    return grouped


def drive(steps, actions):
    actions = list(actions)
    for _ in steps:
        if actions:
            action = actions.pop(0)
            if action is not None:
                action()
    for action in actions:
        if action is not None:
            action()


def loop(count, body):
    def step(at, carry):
        body(at)
        return carry

    lax.fori_loop(0, count, step, 0)


def mlp_block(mixed, wo, inputs, cotangent, cot_face, norms, wexp_first, w_expand, w_reduce, nz, ny, collective_id):
    micro_count, own_rows, width = inputs.shape
    face_rows = cot_face.shape[1]
    tokens = micro_count * face_rows
    attn = mixed.shape[1]
    units = w_expand[0].shape[1] // 2
    half = units // 2
    tile = min(512, half)
    wide = 512
    part = jax.ShapeDtypeStruct((micro_count, face_rows, width), BF16)
    part_red = jax.ShapeDtypeStruct((units, width), BF16)
    own = (micro_count, own_rows, width)
    scatter_a, scatter_b = (FaceScatter(part, nz, ny, resident=True) for _ in range(2))
    gather = FaceGather(jax.ShapeDtypeStruct(own, BF16), nz, ny)
    line_e = LineGather(w_expand[:1], ["row"], nz, ny, share=(1, 2), given=w_expand[1:])
    line_r = LineGather(w_reduce[:1], ["col"], nz, ny, given=w_reduce[1:])
    line_s = LineScatter([part_red], ["col"], nz, ny, resident=True)
    plans = [scatter_a, scatter_b, gather, line_e, line_r, line_s]
    vmem = pl.BlockSpec(memory_space=pltpu.VMEM)
    outs = [
        (jax.ShapeDtypeStruct(own, F32), ANY),
        (jax.ShapeDtypeStruct(own, F32), ANY),
        (jax.ShapeDtypeStruct(own, BF16), ANY),
        (jax.ShapeDtypeStruct((2, 16, width), F32), vmem),
        (jax.ShapeDtypeStruct((width, half), BF16), ANY),
        (jax.ShapeDtypeStruct((width, half), BF16), ANY),
        (part, ANY),
    ] + line_s.outs
    scratch = [
        pltpu.VMEM((micro_count, face_rows, width), BF16),
        pltpu.VMEM(own, F32),
        pltpu.VMEM(own, F32),
        pltpu.VMEM(own, BF16),
        pltpu.VMEM(own, BF16),
        pltpu.VMEM(own, BF16),
        pltpu.VMEM((micro_count, face_rows, width), BF16),
        pltpu.VMEM((micro_count, face_rows, width), BF16),
        pltpu.VMEM((width, half), BF16),
        pltpu.VMEM((width, half), BF16),
        pltpu.VMEM((units, width), BF16),
        pltpu.VMEM((tokens, units), BF16),
        pltpu.VMEM((tokens, units), BF16),
        pltpu.VMEM((units, width), BF16),
        pltpu.VMEM((tokens, attn), BF16),
        pltpu.VMEM((attn, width), BF16),
    ]
    shared = len(scratch)
    scratch += scatter_a.scratch + line_s.scratch

    def body(net, ins, outs, scratch):
        mixed_in, wo_in, own_in, cot_in, face_in, norms, first_in, *weights_in = ins
        middle_out, grad_out, low_out, norm_out, expand_a, expand_b, reduced_out, reduce_out = outs
        p, branch, middle, own, cot_own, n_own, n_face, cot, we0, we1, wr, active, slope, pr, mixed, wo = scratch[:shared]
        we = (we0, we1)
        slots = list(scratch[shared : shared + len(scatter_a.scratch)])
        line_slots = list(scratch[shared + len(scatter_a.scratch) :])

        loads = [
            net.copy(*pair)
            for pair in (
                (mixed_in, mixed),
                (wo_in, wo),
                (own_in, own),
                (cot_in, cot_own),
                (first_in, we0),
                (face_in, cot),
            )
        ]
        e = line_e.run(net, weights_in[:2], [we1], [])
        r = line_r.run(net, weights_in[2:], [wr], [])
        queue = []

        def tick(count=1):
            def act():
                for _ in range(count):
                    if queue:
                        next(queue.pop(0), None)

            return act

        next(e)
        next(r)
        for load in loads:
            load.start()
        queue += [e, e, e, r, e, e, r, r, e, e, r, r, r, r]
        loads[0].wait()
        loads[1].wait()

        def branch_tile(at):
            m, n = lax.div(at, width // wide), lax.rem(at, width // wide)
            columns = pl.ds(pl.multiple_of(n * wide, wide), wide)
            rows = pl.ds(pl.multiple_of(m * face_rows, face_rows), face_rows)
            p[m, :, columns] = jnp.dot(mixed[rows, :], wo[:, columns], preferred_element_type=F32).astype(BF16)

        loop(micro_count * (width // wide), branch_tile)
        tick(1)()
        drive(
            scatter_a.run(net, [p], [branch], slots),
            [None, None, None, None, tick(2), None, tick(1), None],
        )
        loads[2].wait()
        row_steps = own_rows // 16

        def own_rows_at(at):
            return lax.div(at, row_steps), pl.ds(pl.multiple_of(lax.rem(at, row_steps) * 16, 16), 16)

        def norm_rows(at):
            m, rows = own_rows_at(at)
            values = own[m, rows, :].astype(F32) + branch[m, rows, :]
            middle[m, rows, :] = values
            centered = values - jnp.mean(values, axis=-1, keepdims=True)
            spread = lax.rsqrt(jnp.mean(centered * centered, axis=-1, keepdims=True) + EPSILON)
            n_own[m, rows, :] = (centered * spread * norms[0:1, :] + norms[1:2, :]).astype(BF16)

        loop(micro_count * row_steps, norm_rows)
        keep_middle = net.copy(middle, middle_out)
        keep_middle.start()
        drive(
            gather.run(net, [n_own], [n_face], []),
            [tick(2), tick(1), tick(1), tick(2), None, None, None],
        )
        loads[4].wait()

        def hidden_tile(h):
            def tile_at(at):
                m, n = lax.div(at, half // tile), lax.rem(at, half // tile)
                rows = pl.ds(pl.multiple_of(m * face_rows, face_rows), face_rows)
                columns = pl.ds(pl.multiple_of(n * tile, tile), tile)
                into = pl.ds(pl.multiple_of(h * half + n * tile, tile), tile)
                hidden = jnp.dot(n_face[m], we[h][:, columns], preferred_element_type=F32)
                square = hidden * hidden
                bend = jnp.tanh(GELU_A * hidden * (1.0 + GELU_B * square))
                active[rows, into] = (0.5 * hidden * (1.0 + bend)).astype(BF16)
                slope[rows, into] = (
                    0.5 * (1.0 + bend)
                    + (0.5 * GELU_A) * hidden * (1.0 - bend * bend) * (1.0 + (3.0 * GELU_B) * square)
                ).astype(BF16)

            return tile_at

        across = (((0,), (0,)), ((), ()))
        along = (((1,), (1,)), ((), ()))
        loop(micro_count * (half // tile), hidden_tile(0))
        tick(1)()
        loop(micro_count * (half // tile), hidden_tile(1))
        tick(1)()
        loads[5].wait()

        def reduce_tile(first):
            def tile_at(at):
                f, n = lax.div(at, width // wide), lax.rem(at, width // wide)
                columns = pl.ds(pl.multiple_of(n * wide, wide), wide)
                rows = pl.ds(pl.multiple_of(first + f * tile, tile), tile)
                pr[rows, columns] = lax.dot_general(
                    active[:, rows],
                    cot[:, :, columns].reshape(tokens, wide),
                    across,
                    preferred_element_type=F32,
                ).astype(BF16)

            return tile_at

        loop((half // tile) * (width // wide), reduce_tile(0))
        tick(1)()
        loop((half // tile) * (width // wide), reduce_tile(half))
        s = line_s.run(net, [pr], [reduce_out], line_slots)
        next(s)
        tick(9)()
        queue.extend([s] * 40)

        def slope_tile(at):
            m, n = lax.div(at, units // tile), lax.rem(at, units // tile)
            rows = pl.ds(pl.multiple_of(m * face_rows, face_rows), face_rows)
            columns = pl.ds(pl.multiple_of(n * tile, tile), tile)
            grad = lax.dot_general(cot[m], wr[columns, :], along, preferred_element_type=F32)
            slope[rows, columns] = (grad * slope[rows, columns].astype(F32)).astype(BF16)

        def normed_tile(at):
            m, n = lax.div(at, width // wide), lax.rem(at, width // wide)
            rows = pl.ds(pl.multiple_of(m * face_rows, face_rows), face_rows)
            columns = pl.ds(pl.multiple_of(n * wide, wide), wide)
            grad = lax.dot_general(slope[rows, :half], we0[columns, :], along, preferred_element_type=F32)
            grad = grad + lax.dot_general(slope[rows, half:], we1[columns, :], along, preferred_element_type=F32)
            p[m, :, columns] = grad.astype(BF16)

        loop(micro_count * (units // tile), slope_tile)
        tick(1)()
        loop(micro_count * (width // wide), normed_tile)
        tick(1)()
        for steps in (e, r):
            for _ in steps:
                pass
        stores = []

        def reduced_tiles(m):
            def tile_at(n):
                rows = pl.ds(m * face_rows, face_rows)
                columns = pl.ds(pl.multiple_of(n * wide, wide), wide)
                cot[m, :, columns] = jnp.dot(active[rows, :], wr[:, columns], preferred_element_type=F32).astype(BF16)

            def act():
                loop(width // wide, tile_at)
                stores.append(net.copy(cot.at[m], reduced_out.at[m]))
                stores[-1].start()

            return act

        def expand_tiles(h):
            def tile_at(at):
                k, n = lax.div(at, half // tile), lax.rem(at, half // tile)
                rows = pl.ds(pl.multiple_of(k * wide, wide), wide)
                columns = pl.ds(pl.multiple_of(n * tile, tile), tile)
                grads = pl.ds(pl.multiple_of(h * half + n * tile, tile), tile)
                we[h][rows, columns] = lax.dot_general(
                    n_face[:, :, rows].reshape(tokens, wide),
                    slope[:, grads],
                    across,
                    preferred_element_type=F32,
                ).astype(BF16)

            def act():
                loop((width // wide) * (half // tile), tile_at)
                stores.append(net.copy(we[h], (expand_a, expand_b)[h]))
                stores[-1].start()

            return act

        def do(*actions):
            def act():
                for action in actions:
                    action()

            return act

        drive(
            scatter_b.run(net, [p], [branch], slots),
            [
                None,
                None,
                None,
                None,
                do(tick(1), expand_tiles(0)),
                do(expand_tiles(1), tick(1)),
                do(*[reduced_tiles(m) for m in range(micro_count)], tick(1)),
                None,
            ],
        )
        loads[3].wait()
        keep_middle.wait()
        norm_out[...] = jnp.zeros_like(norm_out)

        def back_rows(at):
            m, rows = own_rows_at(at)
            values = middle[m, rows, :]
            centered = values - jnp.mean(values, axis=-1, keepdims=True)
            spread = lax.rsqrt(jnp.mean(centered * centered, axis=-1, keepdims=True) + EPSILON)
            unit = centered * spread
            grad = branch[m, rows, :]
            norm_out[0] += grad * unit
            norm_out[1] += grad
            turned = grad * norms[0:1, :]
            inner = jnp.mean(turned * unit, axis=-1, keepdims=True)
            total = cot_own[m, rows, :].astype(F32) + spread * (
                turned - jnp.mean(turned, axis=-1, keepdims=True) - unit * inner
            )
            middle[m, rows, :] = total
            n_own[m, rows, :] = total.astype(BF16)

        loop(micro_count * row_steps, back_rows)
        for pair in ((middle, grad_out), (n_own, low_out)):
            stores.append(net.copy(*pair))
            stores[-1].start()
        for _ in s:
            pass
        for store in stores:
            store.wait()

    ins = [mixed, wo, inputs, cotangent, cot_face, norms, wexp_first, *w_expand, *w_reduce]
    specs = [ANY] * 5 + [vmem] + [ANY] * (len(ins) - 6)
    return launch(
        body, ins, specs, outs, scratch, plans, nz, ny, collective_id, "mlp_block", extra_locals=12, vmem=62
    )


def stack_heads(ref, heads, head_dim):
    return jnp.concatenate([ref[0, :, h * head_dim : (h + 1) * head_dim] for h in range(heads)], axis=0)


def masked_scores(queries, keys, query_doc, key_doc, head_dim):
    raw = lax.dot_general(keys, queries, (((1,), (1,)), ((), ())), preferred_element_type=F32)
    key_doc = jnp.concatenate([key_doc] * (raw.shape[1] // key_doc.shape[1]), axis=1)
    return jnp.where(query_doc == key_doc, raw * (LOG2_E / math.sqrt(head_dim)), NEG_FILL)


def attend_forward(queries, keys_vals, query_doc, key_doc, bounds, heads, head_dim):
    micro_count, rows, _ = queries.shape
    blocks = rows // BLOCK
    tall = heads * BLOCK

    def kernel(bounds_ref, q_ref, kv_ref, qd_ref, kd_ref, out_ref, log_ref):
        at = pl.program_id(0) * blocks + pl.program_id(1)
        low, high = bounds_ref[2 * at], bounds_ref[2 * at + 1]
        queries = stack_heads(q_ref, heads, head_dim)
        doc = jnp.concatenate([qd_ref[0, 0]] * heads, axis=1)

        def body(block, carry):
            top, total, mixed = carry
            first = pl.multiple_of(block * BLOCK, BLOCK)
            keys = kv_ref[0, pl.ds(first, BLOCK), :head_dim]
            values = kv_ref[0, pl.ds(first, BLOCK), head_dim:]
            scores = masked_scores(queries, keys, doc, kd_ref[0, pl.ds(first, BLOCK), :], head_dim)
            new_top = jnp.maximum(top, jnp.max(scores, axis=0, keepdims=True))
            weights = jnp.exp2(scores - new_top)
            fade = jnp.exp2(top - new_top)
            total = total * fade + jnp.sum(weights, axis=0, keepdims=True)
            mixed = mixed * fade + lax.dot_general(
                values, weights.astype(BF16), (((0,), (0,)), ((), ())), preferred_element_type=F32
            )
            return new_top, total, mixed

        top, total, mixed = lax.fori_loop(
            low,
            high,
            body,
            (
                jnp.full((1, tall), NEG_FILL, F32),
                jnp.zeros((1, tall), F32),
                jnp.zeros((head_dim, tall), F32),
            ),
        )
        mixed = jnp.transpose(mixed / total).astype(BF16)
        for h in range(heads):
            out_ref[0, :, h * head_dim : (h + 1) * head_dim] = mixed[h * BLOCK : (h + 1) * BLOCK]
        log_ref[0, 0] = top + jnp.log2(total)

    return pl.pallas_call(
        kernel,
        out_shape=[
            jax.ShapeDtypeStruct(queries.shape, BF16),
            jax.ShapeDtypeStruct((micro_count, blocks, 1, tall), F32),
        ],
        grid_spec=pltpu.PrefetchScalarGridSpec(
            num_scalar_prefetch=1,
            grid=(micro_count, blocks),
            in_specs=[
                pl.BlockSpec((1, BLOCK, heads * head_dim), lambda m, b, _: (m, b, 0)),
                pl.BlockSpec((1,) + keys_vals.shape[1:], lambda m, b, _: (m, 0, 0)),
                pl.BlockSpec((1, 1, 1, BLOCK), lambda m, b, _: (m, b, 0, 0)),
                pl.BlockSpec((1,) + key_doc.shape[1:], lambda m, b, _: (m, 0, 0)),
            ],
            out_specs=[
                pl.BlockSpec((1, BLOCK, heads * head_dim), lambda m, b, _: (m, b, 0)),
                pl.BlockSpec((1, 1, 1, tall), lambda m, b, _: (m, b, 0, 0)),
            ],
        ),
        compiler_params=pltpu.CompilerParams(vmem_limit_bytes=40 << 20),
        name="attend_forward",
    )(bounds, queries, keys_vals, query_doc, key_doc)


def attend_backward(queries, keys_vals, mixed, grad_mixed, log_total, query_doc, key_doc, bounds, heads, head_dim):
    micro_count, rows, _ = queries.shape
    blocks = rows // BLOCK
    seq_len = keys_vals.shape[1]
    scale = 1.0 / math.sqrt(head_dim)
    tall = heads * BLOCK

    def kernel(bounds_ref, q_ref, kv_ref, o_ref, do_ref, log_ref, qd_ref, kd_ref, gq_ref, gkv_ref, acc_ref):
        at = pl.program_id(0) * blocks + pl.program_id(1)
        low, high = bounds_ref[2 * at], bounds_ref[2 * at + 1]

        @pl.when(pl.program_id(1) == 0)
        def _():
            acc_ref[...] = jnp.zeros_like(acc_ref)

        queries, grad = stack_heads(q_ref, heads, head_dim), stack_heads(do_ref, heads, head_dim)
        products = grad.astype(F32) * stack_heads(o_ref, heads, head_dim).astype(F32)
        delta = jnp.sum(jnp.transpose(products), axis=0, keepdims=True)
        doc = jnp.concatenate([qd_ref[0, 0]] * heads, axis=1)
        log_total = log_ref[0, 0]

        def body(block, grad_queries):
            first = pl.multiple_of(block * BLOCK, BLOCK)
            keys = kv_ref[0, pl.ds(first, BLOCK), :head_dim]
            values = kv_ref[0, pl.ds(first, BLOCK), head_dim:]
            scores = masked_scores(queries, keys, doc, kd_ref[0, pl.ds(first, BLOCK), :], head_dim)
            probs = jnp.exp2(scores - log_total)
            grad_probs = lax.dot_general(values, grad, (((1,), (1,)), ((), ())), preferred_element_type=F32)
            grad_scores = (probs * (grad_probs - delta)).astype(BF16)
            acc_ref[pl.ds(first, BLOCK), :head_dim] += (
                jnp.dot(grad_scores, queries, preferred_element_type=F32) * scale
            )
            acc_ref[pl.ds(first, BLOCK), head_dim:] += jnp.dot(probs.astype(BF16), grad, preferred_element_type=F32)
            return grad_queries + lax.dot_general(
                keys, grad_scores, (((0,), (0,)), ((), ())), preferred_element_type=F32
            )

        grad_queries = lax.fori_loop(low, high, body, jnp.zeros((head_dim, tall), F32))
        grad_queries = jnp.transpose(grad_queries * scale).astype(BF16)
        for h in range(heads):
            gq_ref[0, :, h * head_dim : (h + 1) * head_dim] = grad_queries[h * BLOCK : (h + 1) * BLOCK]

        @pl.when(pl.program_id(1) == blocks - 1)
        def _():
            gkv_ref[0] = acc_ref[...].astype(BF16)

    wide = pl.BlockSpec((1, BLOCK, heads * head_dim), lambda m, b, _: (m, b, 0))
    row = pl.BlockSpec((1, seq_len, 2 * head_dim), lambda m, b, _: (m, 0, 0))
    return pl.pallas_call(
        kernel,
        out_shape=[
            jax.ShapeDtypeStruct(queries.shape, BF16),
            jax.ShapeDtypeStruct(keys_vals.shape, BF16),
        ],
        grid_spec=pltpu.PrefetchScalarGridSpec(
            num_scalar_prefetch=1,
            grid=(micro_count, blocks),
            in_specs=[
                wide,
                row,
                wide,
                wide,
                pl.BlockSpec((1, 1, 1, tall), lambda m, b, _: (m, b, 0, 0)),
                pl.BlockSpec((1, 1, 1, BLOCK), lambda m, b, _: (m, b, 0, 0)),
                pl.BlockSpec((1,) + key_doc.shape[1:], lambda m, b, _: (m, 0, 0)),
            ],
            out_specs=[wide, row],
            scratch_shapes=[pltpu.VMEM((seq_len, 2 * head_dim), F32)],
        ),
        compiler_params=pltpu.CompilerParams(vmem_limit_bytes=40 << 20),
        name="attend_backward",
    )(bounds, queries, keys_vals, mixed, grad_mixed, log_total, query_doc, key_doc)


def local(
    inputs,
    cotangent,
    doc_ids,
    attn_gain,
    attn_shift,
    w_query,
    w_keyval,
    w_attn_out,
    mlp_gain,
    mlp_shift,
    w_expand,
    w_reduce,
):
    nz = lax.axis_size("dp") // 2
    tensor_count = lax.axis_size("tensor")
    ny = tensor_count // 2
    ranks = 2 * tensor_count
    micro_count, own_rows, width = inputs.shape
    face_rows = own_rows * ranks
    tokens = micro_count * face_rows
    seq_len = doc_ids.shape[1]
    head_dim = w_keyval.shape[1] // 2
    heads = w_query.shape[1] // (2 * head_dim)
    z = lax.axis_index("dp") // 2
    swap = functools.partial(exchange, nz=nz, ny=ny)
    on = (nz, ny)

    def dot(a, b):
        return jnp.dot(a, b, preferred_element_type=F32)

    def dot_bt(a, b):
        return lax.dot_general(a, b, (((1,), (1,)), ((), ())), preferred_element_type=F32)

    def dot_at(a, b):
        return lax.dot_general(a, b, (((0,), (0,)), ((), ())), preferred_element_type=F32)

    norms = jnp.stack([attn_gain, attn_shift, mlp_gain, mlp_shift])
    norms = jnp.concatenate([norms, jnp.zeros((4, norms.shape[1]), BF16)])
    (wq, wo, wkv), (norms,), (face_in,), (expand_given,) = swap(
        [
            LineGather([w_query, w_attn_out, w_keyval], ["row", "col", "both"], *on),
            PlaneGather(norms, *on),
            FaceGather(inputs, *on, hold_x=True),
            HalfSwap([w_expand], ["row"], *on),
        ],
        collective_id=1,
        name="gather_attention",
        order=K1_ORDER,
    )
    norms = norms[:, :4].transpose(1, 0, 2).reshape(4, width).astype(F32)
    gain_one, shift_one = norms[0], norms[1]

    normed = layer_norm(face_in.astype(F32), gain_one, shift_one).astype(BF16).reshape(tokens, width)
    queries = dot(normed, wq).astype(BF16).reshape(micro_count, face_rows, heads * head_dim)
    keys_face = dot(normed, wkv).astype(BF16).reshape(micro_count, face_rows, 2 * head_dim)
    (keys_vals,), (wexp_first,), (cot_face,) = swap(
        [
            KeysGather(keys_face, *on),
            LineGather([w_expand], ["row"], *on, share=(0, 2), given=[expand_given]),
            FaceGather(cotangent, *on, hold_x=True),
        ],
        collective_id=2,
        name="gather_keys",
        order=K2_ORDER,
    )

    query_doc = lax.dynamic_slice_in_dim(doc_ids, z * face_rows, face_rows, axis=1)
    blocks = face_rows // BLOCK
    last_doc = doc_ids[:, BLOCK - 1 :: BLOCK]
    first_doc = query_doc[:, ::BLOCK]
    lows = jnp.sum((last_doc[:, None, :] < first_doc[:, :, None]).astype(jnp.int32), axis=-1)
    highs = jnp.broadcast_to(z * blocks + jnp.arange(blocks, dtype=jnp.int32) + 1, lows.shape)
    bounds = jnp.stack([lows, highs], axis=-1).reshape(-1)
    docs = (
        query_doc.reshape(micro_count, blocks, 1, BLOCK),
        jnp.broadcast_to(doc_ids[:, :, None], doc_ids.shape + (128,)),
        bounds,
        heads,
        head_dim,
    )
    mixed, log_total = attend_forward(queries, keys_vals, *docs)
    mixed_flat = mixed.reshape(tokens, heads * head_dim)

    own_in = inputs.astype(F32)
    middle, grad_middle, low_middle, grad_norm_two, part_expand_a, part_expand_b, reduced, grad_reduce = mlp_block(
        mixed_flat, wo, inputs, cotangent, cot_face, norms[2:], wexp_first, (w_expand, expand_given), (w_reduce,), *on, collective_id=3
    )
    grad_gain_two, grad_shift_two = jnp.sum(grad_norm_two, axis=1)
    (grad_branch,), (reduced,), (grad_expand_a, grad_expand_b) = swap(
        [
            FaceGather(low_middle, *on),
            FaceScatter(reduced, *on),
            LineScatter([part_expand_a, part_expand_b], ["row", "row"], *on),
        ],
        collective_id=6,
        name="gather_branch",
    )
    outputs = (middle + reduced).astype(BF16)
    grad_branch = grad_branch.reshape(tokens, width)
    part_attn_out = dot_at(mixed_flat, grad_branch).astype(BF16)
    grad_mixed = dot_bt(grad_branch, wo).astype(BF16).reshape(mixed.shape)
    grad_queries, grad_keys = attend_backward(queries, keys_vals, mixed, grad_mixed, log_total, *docs)
    grad_queries = grad_queries.reshape(tokens, heads * head_dim)
    part_query = dot_at(normed, grad_queries).astype(BF16)
    from_query = dot_bt(grad_queries, wq).astype(BF16).reshape(micro_count, face_rows, width)
    (from_query,), (grad_keys,), (grad_attn_out, grad_query) = swap(
        [
            FaceScatter(from_query, *on),
            WholeScatter(grad_keys.reshape(micro_count, nz, face_rows, 2 * head_dim), *on),
            LineScatter([part_attn_out, part_query], ["col", "row"], *on),
        ],
        collective_id=7,
        name="scatter_query",
    )
    grad_keys = grad_keys.astype(BF16).reshape(micro_count * own_rows, 2 * head_dim)
    normed_own, norm_pull_one = jax.vjp(layer_norm, own_in, gain_one, shift_one)
    grad_normed = from_query + dot_bt(grad_keys, wkv).reshape(from_query.shape)
    grad_tok_norm, grad_gain_one, grad_shift_one = norm_pull_one(grad_normed)
    part_keyval = dot_at(normed_own.astype(BF16).reshape(-1, width), grad_keys).astype(BF16)
    own_width = width // (nz * ranks)
    small = jnp.stack([grad_gain_one, grad_shift_one, grad_gain_two, grad_shift_two])
    small = small.reshape(4, nz, ranks, own_width).transpose(2, 1, 0, 3)
    small = jnp.pad(small, ((0, 0), (0, 0), (0, 4), (0, 128 - own_width)))
    (grad_keyval,), (small,) = swap(
        [WholeScatter(part_keyval.reshape(1, nz, width // nz, 2 * head_dim), *on), SmallScatter(small, *on)],
        collective_id=8,
        name="scatter_small",
    )
    small = small[:4, :own_width]

    def by_row(halves):
        return jnp.concatenate([halves[0], halves[1]], axis=1).astype(F32)

    def by_column(halves):
        return halves.reshape(-1, halves.shape[-1]).astype(F32)

    return (
        outputs,
        grad_middle + grad_tok_norm,
        small[0],
        small[1],
        by_row(grad_query),
        grad_keyval[0],
        by_column(grad_attn_out),
        small[2],
        small[3],
        by_row(jnp.concatenate([grad_expand_a, grad_expand_b], axis=2)),
        by_column(grad_reduce),
    )


def solution(mesh):
    placed = (
        P(None, ("dp", "tensor"), None),
        P(None, ("dp", "tensor"), None),
        P(),
        P("dp"),
        P("dp"),
        P("dp", "tensor"),
        P("dp", None),
        P("tensor", "dp"),
        P("dp"),
        P("dp"),
        P("dp", "tensor"),
        P("tensor", "dp"),
    )
    return jax.shard_map(
        local,
        mesh=mesh,
        in_specs=placed,
        out_specs=(
            P(None, ("dp", "tensor"), None),
            P(None, ("dp", "tensor"), None),
            P(("dp", "tensor")),
            P(("dp", "tensor")),
            P("dp", "tensor"),
            P(("dp", "tensor"), None),
            P("tensor", "dp"),
            P(("dp", "tensor")),
            P(("dp", "tensor")),
            P("dp", "tensor"),
            P("tensor", "dp"),
        ),
        check_vma=False,
    )
```

```python
import functools
import math

import jax
import jax.numpy as jnp
from jax import lax
from jax.experimental import pallas as pl
from jax.experimental.pallas import tpu as pltpu
from jax.sharding import PartitionSpec as P

BLOCK = 256
EPSILON = 1e-05
NEG_FILL = -1e30
GELU_A = math.sqrt(2.0 / math.pi)
GELU_B = 0.044715
LOG2_E = 1.0 / math.log(2.0)
MLP_ORDER = ("mmmmmeeemmmeerrmmmrmmmrmmmrmmmmsmsmmxxmm", "mmsxxsxsmm",)
BACK_ORDER = ("mrmerrmrrmmmemmemmrreemwwwqwqqaewrawrqaa", "eaqwqwaaw",)
K1_ORDER = (0, 2, 1, 2, 0, 2, 3, 0, 0, 0, 0, 0, 2, 0, 0, 2, 0, 1, 0, 0, 2, 2, 2, 0, 0, 0, 0, 0, 0, 2)
K2_ORDER = (0, 2, 2, 1, 0, 1, 1, 2, 2, 2, 0, 2, 0, 1, 2)
MESH = pl.DeviceIdType.MESH
ANY = pl.BlockSpec(memory_space=pl.ANY)
IN_VMEM = pl.BlockSpec(memory_space=pltpu.VMEM)
BF16 = jnp.bfloat16
F32 = jnp.float32


def layer_norm(values, gain, shift):
    center = jnp.mean(values, axis=-1, keepdims=True)
    centered = values - center
    variance = jnp.mean(centered * centered, axis=-1, keepdims=True)
    return centered * lax.rsqrt(variance + EPSILON) * gain + shift


def gelu_tanh(values):
    return jax.nn.gelu(values, approximate=True)


class Net:
    def __init__(self, nz, ny, send, recv, local):
        dp, tensor = lax.axis_index("dp"), lax.axis_index("tensor")
        self.nz, self.ny = nz, ny
        self.z, self.x = lax.div(dp, 2), lax.rem(dp, 2)
        self.y, self.c = lax.div(tensor, 2), lax.rem(tensor, 2)
        self.tensor = tensor
        self.send, self.recv, self.local = send, recv, local
        self.used = [0, 0]
        self.keys = {}

    def flip(self, value, by):
        return value + by - 2 * by * value if by else value

    def xy(self, dx, dy):
        return self.flip(self.x, dx), lax.rem(self.y + dy, self.ny) if dy else self.y

    def rank(self, dx=0, dy=0, dc=0):
        x, y = self.xy(dx, dy)
        return x * (2 * self.ny) + y * 2 + self.flip(self.c, dc)

    def device(self, dx=0, dy=0, dc=0, z=None):
        x, y = self.xy(dx, dy)
        return ((self.z if z is None else z) * 2 + x, y * 2 + self.flip(self.c, dc))

    def slot(self, key):
        if key not in self.keys:
            self.keys[key] = self.used[0]
            self.used[0] += 1
        return self.keys[key]

    def remote(self, key, src, dst, device):
        at = self.slot(key)
        return pltpu.make_async_remote_copy(
            src_ref=src,
            dst_ref=dst,
            send_sem=self.send.at[at],
            recv_sem=self.recv.at[at],
            device_id=device,
            device_id_type=MESH,
        )

    def take_locals(self, count):
        first = self.used[1]
        self.used[1] += count
        return first

    def copy_at(self, at, src, dst):
        return pltpu.make_async_copy(src, dst, self.local.at[at])

    def copy(self, src, dst):
        return self.copy_at(self.take_locals(1), src, dst)


def add_rows(dst, terms):
    lead, height, width = dst.shape
    rows = min(max(16, 32768 // width), height)
    steps = height // rows

    def body(step, carry):
        at, off = lax.div(step, steps), pl.multiple_of(lax.rem(step, steps) * rows, rows)
        total = terms[0][at, pl.ds(off, rows), :].astype(F32)
        for term in terms[1:]:
            total = total + term[at, pl.ds(off, rows), :].astype(F32)
        dst[at, pl.ds(off, rows), :] = total.astype(dst.dtype)
        return carry

    lax.fori_loop(0, lead * steps, body, 0)


class FaceGather:
    moves = ("x", "y", "c")
    in_spec = IN_VMEM

    def __init__(self, own, nz, ny, hold_x=False):
        self.ins, self.hold_x = [own], hold_x
        m, t, d = own.shape
        self.outs = [(jax.ShapeDtypeStruct((m, 4 * ny * t, d), own.dtype), ANY)]
        self.scratch = []
        self.half = t // 2
        self.remotes, self.locals = 8 * ny, 1

    def run(self, net, ins, outs, scratch):
        (own,), (out,), half = ins, outs, self.half
        dys = range(1, net.ny)

        def piece(dx, dy, h):
            return out.at[:, pl.ds(pl.multiple_of(net.rank(dx, dy) * 2 * half + h * half, half), half), :]

        mine = [own.at[:, pl.ds(h * half, half), :] for h in (0, 1)]
        keep = net.copy(own, out.at[:, pl.ds(pl.multiple_of(net.rank() * 2 * half, half), 2 * half), :])
        keep.start()
        sent = {}

        def send(key, src, dst, device):
            sent[key] = net.remote((id(self), key), src, dst, device)
            sent[key].start()

        if not self.hold_x:
            send(("x", 0), mine[0], piece(0, 0, 0), net.device(1, 0))
        for dy in dys:
            send(("y", dy, 1), mine[1], piece(0, 0, 1), net.device(0, dy))
        if not self.hold_x:
            send(("x", 1), mine[1], piece(0, 0, 1), net.device(1, 0))
        for dy in dys:
            send(("y", dy, 0), mine[0], piece(0, 0, 0), net.device(0, dy))
        for h in (0, 1):
            send(("c", h), mine[h], piece(0, 0, h), net.device(0, 0, 1))
        if self.hold_x:
            yield
            for h in (0, 1):
                send(("x", h), mine[h], piece(0, 0, h), net.device(1, 0))

        def share(key, dx, dy, h):
            send(("c",) + key, piece(dx, dy, h), piece(dx, dy, h), net.device(0, 0, 1))

        def from_x(h):
            sent["x", h].wait_recv()
            if not h:
                for dy in dys:
                    send(("xy", dy), piece(1, 0, 0), piece(1, 0, 0), net.device(0, dy))
            share(("x", h), 1, 0, h)

        def from_y(dy, h):
            sent["y", dy, h].wait_recv()
            if h:
                send(("yx", dy), piece(0, -dy % net.ny, 1), piece(0, -dy % net.ny, 1), net.device(1, 0))
            share(("y", dy, h), 0, -dy % net.ny, h)

        arrivals = []
        for first in (True, False):
            on_x = [functools.partial(from_x, 0 if first else 1)]
            on_y = [functools.partial(from_y, dy, 1 if first else 0) for dy in dys]
            arrivals.append(on_x + on_y)
        if self.hold_x:
            arrivals = [arrivals[0][1:], arrivals[1][1:], arrivals[0][:1], arrivals[1][:1]]
        for group in arrivals:
            for arrive in group:
                yield
                arrive()
        for dy in dys:
            yield
            sent["xy", dy].wait_recv()
            share(("xy", dy), 1, -dy % net.ny, 0)
            yield
            sent["yx", dy].wait_recv()
            share(("yx", dy), 1, -dy % net.ny, 1)
        yield
        for key, copy in sent.items():
            if key[0] == "c":
                copy.wait_recv()
        for copy in sent.values():
            copy.wait_send()
        keep.wait()


class FaceScatter:
    moves = ("x", "y", "c")

    def __init__(self, part, nz, ny, resident=False):
        self.ins, self.resident = [part], resident
        m, rows, d = part.shape
        t = rows // (4 * ny)
        self.outs = [(jax.ShapeDtypeStruct((m, t, d), F32), pl.BlockSpec(memory_space=pltpu.VMEM))]
        half = t // 2
        self.half = half
        self.scratch = [
            pltpu.VMEM((2 * ny, m, t, d), BF16),
            pltpu.VMEM((ny - 1, m, half, d), BF16),
            pltpu.VMEM((ny - 1, m, half, d), BF16),
            pltpu.VMEM((2, m, half, d), BF16),
            pltpu.VMEM((2, ny - 1, m, half, d), BF16),
        ]
        if not resident:
            self.scratch.append(pltpu.VMEM((2 * ny, m, t, d), BF16))
        self.remotes, self.locals = 6 * ny + 4, 2 * ny

    def run(self, net, ins, outs, scratch):
        (part,), (out,), half = ins, outs, self.half
        from_core, x_diag, y_diag, x_in, y_in = scratch[:5]
        ny = net.ny
        dys = range(1, ny)
        order = [(1, dy) for dy in dys] + [(1, 0)] + [(0, dy) for dy in dys] + [(0, 0)]
        sent, loads = {}, {}

        def send(key, src, dst, device):
            sent[key] = net.remote((id(self), key), src, dst, device)
            sent[key].start()

        def rows(dx, dy, dc, first=0, size=2 * half):
            at = net.rank(dx, dy, dc) * 2 * half + first
            return part.at[:, pl.ds(pl.multiple_of(at, half), size), :]

        def work(dx, dy, first=0, size=2 * half):
            if self.resident:
                return rows(dx, dy, 0, first, size)
            return scratch[5].at[dx * ny + dy, :, pl.ds(first, size), :]

        for dx, dy in order:
            at = dx * ny + dy
            if not self.resident:
                loads[at] = net.copy(rows(dx, dy, 0), work(dx, dy))
                loads[at].start()
            send(("c", at), rows(dx, dy, 1), from_core.at[at], net.device(0, 0, 1))
        for dx, dy in order:
            at = dx * ny + dy
            yield
            if not self.resident:
                loads[at].wait()
            sent["c", at].wait_recv()
            add_rows(work(dx, dy), [work(dx, dy), from_core.at[at]])
            top, low = work(dx, dy, 0, half), work(dx, dy, half, half)
            if dx and dy:
                send(("xd", dy), top, x_diag.at[dy - 1], net.device(1, 0))
                send(("yd", dy), low, y_diag.at[dy - 1], net.device(0, dy))
            elif dx:
                send(("x", 0), top, x_in.at[0], net.device(1, 0))
            elif dy:
                send(("y", dy, 1), low, y_in.at[1, dy - 1], net.device(0, dy))
        for dy in dys:
            yield
            sent["xd", dy].wait_recv()
            top = work(0, dy, 0, half)
            add_rows(top, [top, x_diag.at[dy - 1]])
            send(("y", dy, 0), top, y_in.at[0, dy - 1], net.device(0, dy))
        low = work(1, 0, half, half)
        for dy in dys:
            yield
            sent["yd", dy].wait_recv()
            add_rows(low, [low, y_diag.at[dy - 1]])
        send(("x", 1), low, x_in.at[1], net.device(1, 0))
        for h in (0, 1):
            yield
            sent["x", h].wait_recv()
            for dy in dys:
                sent["y", dy, h].wait_recv()
            add_rows(
                out.at[:, pl.ds(h * half, half), :],
                [work(0, 0, h * half, half), x_in.at[h]] + [y_in.at[h, dy - 1] for dy in dys],
            )
        for copy in sent.values():
            copy.wait_send()


class LineGather:
    moves = ("x", "line", "c")
    in_spec = IN_VMEM

    def __init__(self, shards, kinds, nz, ny, share=(0, 1), given=()):
        self.ins, self.kinds, self.share = list(shards) + list(given), list(kinds), share
        self.outs, self.scratch = [], []
        for shard, kind in zip(shards, kinds):
            rows, columns = shard.shape
            if kind == "row":
                shape = (rows * 2 * nz, columns // 2 // share[1])
            elif kind == "col":
                shape = (rows // 2 // share[1], columns * 2 * nz)
            else:
                shape = (rows * 2 * nz, columns)
            self.outs.append((jax.ShapeDtypeStruct(shape, shard.dtype), ANY))
        count = len(self.kinds)
        self.remotes = count * (1 + 4 * (nz - 1)) + kinds.count("both") * (1 + 4 * (nz - 1))
        self.locals = 2 * count

    def run(self, net, ins, outs, scratch):
        nz, z = net.nz, net.z
        sent, locals_, shared = [], [], []
        weights = []
        given = ins[len(self.kinds) :]
        for at, (shard, out, kind) in enumerate(zip(ins, outs, self.kinds)):
            rows, columns = shard.shape

            if kind == "row":
                span = columns // 2 // self.share[1]

                def mine(dx, shard=shard, span=span):
                    first = (net.flip(net.x, dx) * self.share[1] + self.share[0]) * span
                    return shard.at[:, pl.ds(pl.multiple_of(first, span), span)]

                def block(line, dx, out=out, rows=rows):
                    first = (line * 2 + net.flip(net.x, dx)) * rows
                    return out.at[pl.ds(pl.multiple_of(first, rows), rows), :]

            elif kind == "col":
                span = rows // 2 // self.share[1]

                def mine(dx, shard=shard, span=span):
                    first = (net.flip(net.x, dx) * self.share[1] + self.share[0]) * span
                    return shard.at[pl.ds(pl.multiple_of(first, span), span), :]

                def block(line, dx, out=out, columns=columns):
                    first = (line * 2 + net.flip(net.x, dx)) * columns
                    return out.at[:, pl.ds(pl.multiple_of(first, columns), columns)]

            else:
                half = rows // 2

                def mine(dx, shard=shard, half=half):
                    return shard.at[pl.ds(pl.multiple_of(net.c * half, half), half), :]

                def block(line, dx, out=out, rows=rows, half=half):
                    first = (line * 2 + net.flip(net.x, dx)) * rows + net.c * half
                    return out.at[pl.ds(pl.multiple_of(first, half), half), :]

            weights.append((at, kind, mine, block))

        def hop(at, dx, step, up, block, src=None):
            origin = z - (step - 1) if up else z + (step - 1)
            there = z + 1 if up else z - 1
            copy = net.remote(
                (id(self), at, dx, step, up),
                block(origin, dx) if src is None else src,
                block(origin, dx),
                net.device(z=there),
            )
            fits = (origin >= 0) & (there < nz) if up else (origin < nz) & (there >= 0)
            return copy, fits

        def start(at, dx, step, up, block, src=None):
            copy, fits = hop(at, dx, step, up, block, src)
            pl.when(fits)(copy.start)
            sent.append((copy, fits))

        def arrived(at, dx, step, up, block, kind):
            copy, _ = hop(at, dx, step, up, block)
            origin = z - step if up else z + step
            fits = origin >= 0 if up else origin < nz
            pl.when(fits)(copy.wait_recv)
            if kind == "both":
                share = net.remote(
                    (id(self), "c", at, dx, step, up), block(origin, dx), block(origin, dx), net.device(0, 0, 1)
                )
                pl.when(fits)(share.start)
                shared.append((share, fits))

        swaps = {}
        for at, kind, mine, block in weights:
            if not given:
                swaps[at] = net.remote((id(self), at, "x"), mine(1), block(z, 0), net.device(1, 0))
                swaps[at].start()
            for up in (True, False):
                start(at, 0, 1, up, block, mine(0))
        for at, kind, mine, block in weights:
            if kind == "both":
                whole = ins[at].shape[0]
                into = outs[at].at[pl.ds(pl.multiple_of((z * 2 + net.x) * whole, whole), whole), :]
                locals_.append(net.copy(ins[at], into))
            else:
                locals_.append(net.copy(mine(0), block(z, 0)))
            locals_[-1].start()
        for (at, kind, mine, block), other in zip(weights, given):
            span = pl.ds(self.share[0] * other.shape[kind == "row"] // self.share[1], other.shape[kind == "row"] // self.share[1])
            other = other.at[:, span] if kind == "row" else other.at[span, :]
            locals_.append(net.copy(other, block(z, 1)))
            locals_[-1].start()
            for up in (True, False):
                start(at, 1, 1, up, block, other)
        yield
        for copy in locals_:
            copy.wait()
        for at, kind, mine, block in weights:
            if given:
                continue
            swaps[at].wait_recv()
            for up in (True, False):
                start(at, 1, 1, up, block)
            if kind == "both":
                share = net.remote((id(self), "c", at), block(z, 1), block(z, 1), net.device(0, 0, 1))
                share.start()
                shared.append((share, None))
        for step in range(1, nz):
            for at, kind, mine, block in weights:
                for dx in (0, 1):
                    yield
                    for up in (True, False):
                        arrived(at, dx, step, up, block, kind)
                        if step < nz - 1:
                            start(at, dx, step + 1, up, block)
        yield
        for copy, fits in shared:
            if fits is None:
                copy.wait()
            else:
                pl.when(fits)(copy.wait)
        for copy, fits in sent:
            pl.when(fits)(copy.wait_send)
        for copy in swaps.values():
            copy.wait_send()


class HalfSwap:
    moves = ("x",)

    def __init__(self, shards, kinds, nz, ny):
        self.ins, self.kinds = list(shards), list(kinds)
        self.outs, self.scratch = [], []
        for shard, kind in zip(shards, kinds):
            rows, columns = shard.shape
            shape = (rows, columns // 2) if kind == "row" else (rows // 2, columns)
            self.outs.append((jax.ShapeDtypeStruct(shape, shard.dtype), ANY))
        self.remotes, self.locals = len(self.ins), 0

    def run(self, net, ins, outs, scratch):
        copies = []
        for at, (shard, out, kind) in enumerate(zip(ins, outs, self.kinds)):
            span = out.shape[kind == "row"]
            there = pl.ds(pl.multiple_of((1 - net.x) * span, span), span)
            src = shard.at[:, there] if kind == "row" else shard.at[there, :]
            copies.append(net.remote((id(self), at), src, out, net.device(1, 0)))
            copies[-1].start()
        yield
        for copy in copies:
            copy.wait()


class LineScatter:
    moves = ("x", "line")

    def __init__(self, parts, kinds, nz, ny, resident=False):
        self.ins, self.kinds, self.resident = list(parts), list(kinds), resident
        self.outs, self.scratch = [], []
        for part, kind in zip(parts, kinds):
            rows, columns = part.shape
            shape = (rows // (2 * nz), columns) if kind == "row" else (rows, columns // (2 * nz))
            self.outs.append((jax.ShapeDtypeStruct((2,) + shape, BF16), ANY))
            for lead in (nz - 1, nz - 1, 1) + (() if resident else (nz,)):
                self.scratch.append(pltpu.VMEM((lead, 2) + shape, BF16))
        count = len(self.ins)
        self.remotes = count * (1 + 4 * nz)
        self.locals = count * (2 * nz + 1)

    def run(self, net, ins, outs, scratch):
        nz, z = net.nz, net.z
        loads, grads = {}, []
        each = 3 if self.resident else 4
        for at, (part, out, kind) in enumerate(zip(ins, outs, self.kinds)):
            down, up, mine = scratch[each * at : each * at + 3]
            _, _, rows, columns = mine.shape

            def block(line, dx, part=part, kind=kind, rows=rows, columns=columns):
                size = rows if kind == "row" else columns
                first = pl.ds(pl.multiple_of((line * 2 + net.flip(net.x, dx)) * size, size), size)
                return part.at[first, :] if kind == "row" else part.at[:, first]

            if self.resident:
                work = block
            else:

                def work(line, dx, at=at):
                    return scratch[each * at + 3].at[line, dx]

                order = []
                for k in range(nz):
                    order += [k, nz - 1 - k]
                for line in dict.fromkeys(order):
                    for dx in (1, 0):
                        loads[at, line, dx] = net.copy(block(line, dx), work(line, dx))
                        loads[at, line, dx].start()
            grads.append((at, out, work, down, up, mine))

        def inbox(slots, line, dx, toward):
            return slots.at[line if toward < 0 else line - 1, dx]

        pieces = (1, 0)
        each_line = len(pieces)

        for at, *_ in grads:
            net.slot((id(self), at, "x"))
            for dx in (0, 1):
                for line in range(nz):
                    for toward in (-1, 1):
                        net.slot((id(self), at, line, dx, toward))

        def chain(grad, dx, line, toward):
            at, out, work, down, up, mine = grad
            slot = inbox(down if toward < 0 else up, line, dx, toward)
            copy = net.remote((id(self), at, line, dx, toward), work(line, dx), slot, net.device(z=z + toward))
            return copy, slot

        def forward(place, grad, dx, line, toward):
            at, out, work, down, up, mine = grad
            copy, slot = chain(grad, dx, line, toward)
            if not self.resident:
                loads[at, line, dx].wait()
            if place != (nz - 1 if toward < 0 else 0):
                copy.wait_recv()
                add_rows(_lead(work(line, dx)), [_lead(work(line, dx)), _lead(slot)])
            copy.start()

        def finish(place, grad, dx):
            at, out, work, down, up, mine = grad
            if not self.resident:
                loads[at, place, dx].wait()
            terms = [_lead(work(place, dx))]
            for toward in (-1, 1):
                if (place < nz - 1) if toward < 0 else (place > 0):
                    copy, slot = chain(grad, dx, place, toward)
                    copy.wait_recv()
                    terms.append(_lead(slot))
            total = mine.at[0, dx]
            add_rows(_lead(total), terms)
            if dx:
                net.remote((id(self), at, "x"), total, out.at[net.x], net.device(1, 0)).start()
            else:
                net.copy_at(self.first_local + at, total, out.at[net.x]).start()

        plan = {}
        for place in range(nz):
            waits_up, waits_down = place, nz - 1 - place
            todo = []
            for toward, waits, lines in (
                (1, waits_up, range(nz - 1, place, -1)),
                (-1, waits_down, range(place)),
            ):
                order = [(line, dx) for line in lines for dx in pieces]
                for j, (line, dx) in enumerate(order):
                    for grad in grads:
                        todo.append((waits + j if waits else 0, waits, (forward, grad, dx, line, toward)))
            for q, dx in enumerate(pieces):
                times = []
                if waits_up:
                    times.append(waits_up + each_line * (nz - 1 - place) + q)
                if waits_down:
                    times.append(waits_down + each_line * place + q)
                for grad in grads:
                    todo.append((max(times), nz, (finish, grad, dx)))
            for time, waits, item in sorted(todo, key=lambda entry: entry[:2]):
                plan.setdefault(time, {}).setdefault(place, []).append(item)
        self.first_local = net.take_locals(len(grads))
        for time in range(max(plan) + 1):
            if time:
                yield
            for place, items in sorted(plan.get(time, {}).items()):

                def act(place=place, items=items):
                    for item in items:
                        item[0](place, *item[1:])

                pl.when(z == place)(act)
        sent = [
            (chain(grad, dx, line, toward)[0], (z > line) if toward < 0 else (z < line))
            for grad in grads
            for dx in pieces
            for toward, lines in ((-1, range(nz - 1)), (1, range(1, nz)))
            for line in lines
        ]
        swaps = [net.remote((id(self), at, "x"), mine.at[0, 1], out.at[net.x], net.device(1, 0)) for at, out, _, _, _, mine in grads]
        stores = [net.copy_at(self.first_local + at, mine.at[0, 0], out.at[net.x]) for at, out, _, _, _, mine in grads]
        yield
        for copy, sends in sent:
            pl.when(sends)(copy.wait_send)
        for copy in swaps:
            copy.wait()
        for copy in stores:
            copy.wait()


def _lead(ref):
    return Lead(ref)


class Lead:
    def __init__(self, ref):
        self.ref, self.shape, self.dtype = ref, (1,) + tuple(ref.shape), ref.dtype

    def __getitem__(self, index):
        return self.ref[index[1], index[2]]

    def __setitem__(self, index, value):
        self.ref[index[1], index[2]] = value


class KeysGather:
    moves = ("x", "line", "c")
    in_spec = IN_VMEM

    def __init__(self, face, nz, ny):
        m, rows, width = face.shape
        self.ins = [face]
        self.outs = [(jax.ShapeDtypeStruct((m, nz * rows, width), face.dtype), ANY)]
        self.scratch = []
        self.remotes, self.locals = 4 * (nz - 1), 1

    def run(self, net, ins, outs, scratch):
        (face,), (out,) = ins, outs
        nz, z = net.nz, net.z
        _, rows, width = face.shape
        part, side = rows // 2, width // 2

        def block(line, dx, dc):
            first = pl.multiple_of(line * rows + net.flip(net.x, dx) * part, part)
            column = pl.multiple_of(net.flip(net.c, dc) * side, side)
            return out.at[:, pl.ds(first, part), pl.ds(column, side)]

        own = face.at[
            :,
            pl.ds(pl.multiple_of(net.x * part, part), part),
            pl.ds(pl.multiple_of(net.c * side, side), side),
        ]
        sent, shared = [], []

        def line_copy(step):
            origin = z - (step - 1)
            src = own if step == 1 else block(origin, 0, 0)
            return net.remote((id(self), step), src, block(origin, 0, 0), net.device(z=z + 1))

        def start(step):
            copy, fits = line_copy(step), (z - (step - 1) >= 0) & (z + 1 < nz)
            pl.when(fits)(copy.start)
            sent.append((copy, fits))

        start(1)
        keep = net.copy(face, out.at[:, pl.ds(pl.multiple_of(z * rows, rows), rows), :])
        keep.start()
        later = []
        for step in range(1, nz):
            yield
            fits = z - step >= 0
            pl.when(fits)(line_copy(step).wait_recv)
            if step < nz - 1:
                start(step + 1)
            here = block(z - step, 0, 0)
            across = net.remote((id(self), "x", step), here, here, net.device(1, 0))
            beside = net.remote((id(self), "c", step), here, here, net.device(0, 0, 1))
            for copy in (across, beside):
                pl.when(fits)(copy.start)
                sent.append((copy, fits))
            later.append((step, fits, across))
            shared.append((beside, fits))
        for step, fits, across in later:
            yield
            pl.when(fits)(across.wait_recv)
            there = block(z - step, 1, 0)
            beside = net.remote((id(self), "xc", step), there, there, net.device(0, 0, 1))
            pl.when(fits)(beside.start)
            sent.append((beside, fits))
            shared.append((beside, fits))
        yield
        for copy, fits in shared:
            pl.when(fits)(copy.wait_recv)
        for copy, fits in sent:
            pl.when(fits)(copy.wait_send)
        keep.wait()


class WholeScatter(FaceScatter):
    moves = ("x", "y", "c", "z")

    def __init__(self, part, nz, ny, resident=False):
        m, _, rows, d = part.shape
        merged = jax.ShapeDtypeStruct((m * nz, rows, d), part.dtype) if resident else part.reshape(m * nz, rows, d)
        super().__init__(merged, nz, ny, resident)
        t = rows // (4 * ny)
        self.m, self.nz = m, nz
        self.outs = [(jax.ShapeDtypeStruct((m, t, d), F32), pl.BlockSpec(memory_space=pltpu.VMEM))]
        self.scratch = self.scratch + [pltpu.VMEM((m * nz, t, d), BF16), pltpu.VMEM((nz, m, t, d), BF16)]
        self.remotes = self.remotes + nz * m
        self.locals = self.locals + m

    def run(self, net, ins, outs, scratch):
        face, inbox = scratch[-2:]
        yield from super().run(net, ins, [face], scratch[:-2])
        nz, m = self.nz, self.m
        copies = []
        for far in range(1, nz):
            line = lax.rem(net.z + far, nz)
            for at in range(m):
                copies.append(
                    pltpu.make_async_remote_copy(
                        src_ref=face.at[at * nz + line],
                        dst_ref=inbox.at[far, at],
                        send_sem=net.send.at[net.slot((id(self), "z", far, at))],
                        recv_sem=net.recv.at[net.slot((id(self), "z", far, at))],
                        device_id=net.device(z=line),
                        device_id_type=MESH,
                    )
                )
                copies[-1].start()
        own = []
        for at in range(m):
            own.append(net.copy(face.at[at * nz + net.z], inbox.at[0, at]))
            own[-1].start()
        yield
        for copy in own:
            copy.wait()
        for copy in copies:
            copy.wait()
        add_rows(outs[0], [inbox.at[far] for far in range(nz)])


class QuickScatter:
    moves = ("c", "same", "z")

    def __init__(self, part, nz, ny):
        _, rows, d = part.shape
        t = rows // (4 * ny)
        self.ins, self.t = [part], t
        self.outs = [(jax.ShapeDtypeStruct((t, d), F32), pl.BlockSpec(memory_space=pltpu.VMEM))]
        self.scratch = [
            pltpu.VMEM((2 * ny, nz, t, d), BF16),
            pltpu.VMEM((2 * ny, nz, t, d), BF16),
            pltpu.VMEM((2 * ny, nz, t, d), BF16),
            pltpu.VMEM((nz, t, d), BF16),
            pltpu.VMEM((nz, 1, t, d), BF16),
        ]
        self.remotes, self.locals = 4 * ny + nz, 2 * ny + 1

    def run(self, net, ins, outs, scratch):
        (part,), (out,), t = ins, outs, self.t
        work, from_core, inbox, face, line_in = scratch
        ny, nz = net.ny, net.nz
        order = [(dx, dy) for dx in (1, 0) for dy in reversed(range(ny))]
        cores, loads, copies = {}, {}, {}

        def rows(dx, dy, dc):
            return part.at[:, pl.ds(pl.multiple_of(net.rank(dx, dy, dc) * t, t), t), :]

        for dx, dy in order:
            at = dx * ny + dy
            loads[at] = net.copy(rows(dx, dy, 0), work.at[at])
            loads[at].start()
            cores[at] = net.remote((id(self), "c", at), rows(dx, dy, 1), from_core.at[at], net.device(0, 0, 1))
            cores[at].start()
        for dx, dy in order:
            at = dx * ny + dy
            yield
            loads[at].wait()
            cores[at].wait_recv()
            add_rows(work.at[at], [work.at[at], from_core.at[at]])
            if at:
                copies[at] = net.remote((id(self), at), work.at[at], inbox.at[at], net.device(dx, dy))
                copies[at].start()
        yield
        for copy in copies.values():
            copy.wait_recv()
        add_rows(face, [work.at[0]] + [inbox.at[at] for at in copies])
        lines = []
        for far in range(1, nz):
            line = lax.rem(net.z + far, nz)
            lines.append(
                net.remote((id(self), "z", far), face.at[pl.ds(line, 1)], line_in.at[far], net.device(z=line))
            )
            lines[-1].start()
        own = net.copy(face.at[pl.ds(net.z, 1)], line_in.at[0])
        own.start()
        yield
        own.wait()
        for copy in lines:
            copy.wait_recv()
        add_rows(_lead(out), [line_in.at[far] for far in range(nz)])
        for copy in list(cores.values()) + list(copies.values()) + lines:
            copy.wait_send()


class PlaneGather:
    moves = ("plane",)
    in_spec = IN_VMEM

    def __init__(self, own, nz, ny):
        self.ins = [own]
        self.outs = [(jax.ShapeDtypeStruct((2 * nz,) + own.shape, own.dtype), ANY)]
        self.scratch = []
        self.remotes, self.locals = 2 * nz, 1

    def run(self, net, ins, outs, scratch):
        (own,), (out,) = ins, outs
        here = out.at[net.z * 2 + net.x]
        copies = []
        for far in range(net.nz):
            for dx in (0, 1):
                if far or dx:
                    line = lax.rem(net.z + far, net.nz)
                    copies.append(net.remote((id(self), far, dx), own, here, net.device(dx, z=line)))
                    copies[-1].start()
        keep = net.copy(own, here)
        keep.start()
        yield
        for copy in copies:
            copy.wait()
        keep.wait()


class SmallScatter:
    moves = ("face", "z")

    def __init__(self, part, nz, ny):
        ranks, _, rows, width = part.shape
        self.ins = [part]
        vmem = pl.BlockSpec(memory_space=pltpu.VMEM)
        self.outs = [(jax.ShapeDtypeStruct((rows, width), F32), vmem)]
        self.scratch = [
            pltpu.VMEM((ranks, nz, rows, width), F32),
            pltpu.VMEM((nz, rows, width), F32),
            pltpu.VMEM((nz, rows, width), F32),
        ]
        self.remotes, self.locals = ranks + nz, 2

    def run(self, net, ins, outs, scratch):
        (part,), (out,) = ins, outs
        inbox, total, line_in = scratch
        ny, nz = net.ny, net.nz
        copies = []
        for dx in (0, 1):
            for dy in range(ny):
                for dc in (0, 1):
                    if dx or dy or dc:
                        at = (dx * ny + dy) * 2 + dc
                        copies.append(
                            net.remote(
                                (id(self), at), part.at[net.rank(dx, dy, dc)], inbox.at[at], net.device(dx, dy, dc)
                            )
                        )
                        copies[-1].start()
        keep = net.copy(part.at[net.rank()], inbox.at[0])
        keep.start()
        yield
        keep.wait()
        for copy in copies:
            copy.wait()
        total[...] = jnp.sum(inbox[...], axis=0)
        lines = []
        for far in range(1, nz):
            line = lax.rem(net.z + far, nz)
            lines.append(net.remote((id(self), "z", far), total.at[line], line_in.at[far], net.device(z=line)))
            lines[-1].start()
        own = net.copy(total.at[net.z], line_in.at[0])
        own.start()
        yield
        own.wait()
        for copy in lines:
            copy.wait()
        out[...] = jnp.sum(line_in[...], axis=0)


def launch(body, ins, in_specs, outs, scratch, plans, nz, ny, collective_id, name, extra_locals=0, vmem=56):
    moves = set()
    for plan in plans:
        moves |= set(plan.moves)
    remotes = sum(plan.remotes for plan in plans)
    locals_ = max(1, extra_locals + sum(plan.locals for plan in plans))

    def kernel(*refs):
        in_refs, refs = refs[: len(ins)], refs[len(ins) :]
        out_refs, refs = refs[: len(outs)], refs[len(outs) :]
        scratch_refs, (send, recv, local) = refs[: len(scratch)], refs[len(scratch) :]
        net = Net(nz, ny, send, recv, local)
        peers = {}
        for far in range(nz):
            for dx in (0, 1):
                for dy in range(ny):
                    for dc in (0, 1):
                        kinds = set()
                        if not far:
                            kinds.add("face")
                            if dx and not dy and not dc:
                                kinds.add("x")
                            if dy and not dx and not dc:
                                kinds.add("y")
                            if dc and not dx and not dy:
                                kinds.add("c")
                            if not dc:
                                kinds.add("same")
                        if far and not dx and not dy and not dc:
                            kinds.add("z")
                            if far in (1, nz - 1):
                                kinds.add("line")
                        if not dy and not dc:
                            kinds.add("plane")
                        if (far or dx or dy or dc) and kinds & moves:
                            line = lax.rem(net.z + far, nz) if far else None
                            peers[far, dx, dy, dc] = net.device(dx, dy, dc, line)
        barrier = pltpu.get_barrier_semaphore()
        for device in peers.values():
            pl.semaphore_signal(barrier, inc=1, device_id=device, device_id_type=MESH)
        pl.semaphore_wait(barrier, len(peers))
        body(net, in_refs, out_refs, scratch_refs)

    return list(
        pl.pallas_call(
            kernel,
            out_shape=[shape for shape, _ in outs],
            in_specs=in_specs,
            out_specs=[spec for _, spec in outs],
            scratch_shapes=list(scratch)
            + [
                pltpu.SemaphoreType.DMA((remotes,)),
                pltpu.SemaphoreType.DMA((remotes,)),
                pltpu.SemaphoreType.DMA((locals_,)),
            ],
            compiler_params=pltpu.CompilerParams(
                collective_id=collective_id, has_side_effects=True, vmem_limit_bytes=vmem << 20
            ),
            name=name,
        )(*ins)
    )


def exchange(plans, nz, ny, collective_id, name, order=()):
    ins = [array for plan in plans for array in plan.ins]
    outs = [out for plan in plans for out in plan.outs]
    scratch = [entry for plan in plans for entry in plan.scratch]

    def body(net, in_refs, out_refs, scratch_refs):
        running = []
        for plan in plans:
            mine = []
            for refs_of, count in ((in_refs, plan.ins), (out_refs, plan.outs), (scratch_refs, plan.scratch)):
                mine.append(list(refs_of[: len(count)]))
            in_refs = in_refs[len(plan.ins) :]
            out_refs = out_refs[len(plan.outs) :]
            scratch_refs = scratch_refs[len(plan.scratch) :]
            running.append(plan.run(net, *mine))
        for at in order:
            next(running[at], None)
        while running:
            for steps in list(running):
                try:
                    next(steps)
                except StopIteration:
                    running.remove(steps)

    specs = [getattr(plan, "in_spec", ANY) for plan in plans for _ in plan.ins]
    results = launch(body, ins, specs, outs, scratch, plans, nz, ny, collective_id, name)
    grouped = []
    for plan in plans:
        grouped.append(results[: len(plan.outs)])
        results = results[len(plan.outs) :]
    return grouped


class Weave:
    def __init__(self):
        self.plans = {}

    def add(self, name, steps):
        self.plans[name] = steps

    def step(self, name):
        steps = self.plans.get(name)
        if steps is not None and next(steps, self) is self:
            del self.plans[name]

    def finish(self, name):
        while name in self.plans:
            self.step(name)


def loop(count, body):
    def step(at, carry):
        body(at)
        return carry

    lax.fori_loop(0, count, step, 0)


def mlp_block(mixed, wo, inputs, cotangent, cot_face, norms, wexp_first, w_expand, w_reduce, nz, ny, collective_id):
    micro_count, own_rows, width = inputs.shape
    face_rows = cot_face.shape[1]
    tokens = micro_count * face_rows
    attn = mixed.shape[1]
    units = w_expand[0].shape[1] // 2
    half = units // 2
    tile = min(512, half)
    wide = 512
    part = jax.ShapeDtypeStruct((micro_count, face_rows, width), BF16)
    part_red = jax.ShapeDtypeStruct((units, width), BF16)
    own = (micro_count, own_rows, width)
    scatter_a, scatter_b = (FaceScatter(part, nz, ny, resident=True) for _ in range(2))
    gather = FaceGather(jax.ShapeDtypeStruct(own, BF16), nz, ny)
    line_e = LineGather(w_expand[:1], ["row"], nz, ny, share=(1, 2), given=w_expand[1:])
    line_r = LineGather(w_reduce[:1], ["col"], nz, ny, given=w_reduce[1:])
    line_s = LineScatter([part_red], ["col"], nz, ny, resident=True)
    plans = [scatter_a, scatter_b, gather, line_e, line_r, line_s]
    vmem = pl.BlockSpec(memory_space=pltpu.VMEM)
    outs = [
        (jax.ShapeDtypeStruct(own, F32), ANY),
        (jax.ShapeDtypeStruct(own, F32), ANY),
        (jax.ShapeDtypeStruct(own, BF16), ANY),
        (jax.ShapeDtypeStruct((2, 16, width), F32), vmem),
        (jax.ShapeDtypeStruct((width, half), BF16), ANY),
        (jax.ShapeDtypeStruct((width, half), BF16), ANY),
        (part, ANY),
    ] + line_s.outs
    scratch = [
        pltpu.VMEM((micro_count, face_rows, width), BF16),
        pltpu.VMEM(own, F32),
        pltpu.VMEM(own, F32),
        pltpu.VMEM(own, BF16),
        pltpu.VMEM(own, BF16),
        pltpu.VMEM(own, BF16),
        pltpu.VMEM((micro_count, face_rows, width), BF16),
        pltpu.VMEM((micro_count, face_rows, width), BF16),
        pltpu.VMEM((width, half), BF16),
        pltpu.VMEM((width, half), BF16),
        pltpu.VMEM((units, width), BF16),
        pltpu.VMEM((tokens, units), BF16),
        pltpu.VMEM((tokens, units), BF16),
        pltpu.VMEM((units, width), BF16),
        pltpu.VMEM((tokens, attn), BF16),
        pltpu.VMEM((attn, width), BF16),
    ]
    shared = len(scratch)
    scratch += scatter_a.scratch + line_s.scratch

    def body(net, ins, outs, scratch):
        mixed_in, wo_in, own_in, cot_in, face_in, norms, first_in, *weights_in = ins
        middle_out, grad_out, low_out, norm_out, expand_a, expand_b, reduced_out, reduce_out = outs
        p, branch, middle, own, cot_own, n_own, n_face, cot, we0, we1, wr, active, slope, pr, mixed, wo = scratch[:shared]
        we = (we0, we1)
        slots = list(scratch[shared : shared + len(scatter_a.scratch)])
        line_slots = list(scratch[shared + len(scatter_a.scratch) :])

        loads = [
            net.copy(*pair)
            for pair in (
                (mixed_in, mixed),
                (wo_in, wo),
                (own_in, own),
                (cot_in, cot_own),
                (first_in, we0),
                (face_in, cot),
            )
        ]
        weave = Weave()
        stores = []
        weave.add("e", line_e.run(net, weights_in[:2], [we1], []))
        weave.step("e")
        weave.add("r", line_r.run(net, weights_in[2:], [wr], []))
        weave.step("r")
        for load in loads:
            load.start()

        def branch_tile(at):
            m, n = lax.div(at, width // wide), lax.rem(at, width // wide)
            columns = pl.ds(pl.multiple_of(n * wide, wide), wide)
            rows = pl.ds(pl.multiple_of(m * face_rows, face_rows), face_rows)
            p[m, :, columns] = jnp.dot(mixed[rows, :], wo[:, columns], preferred_element_type=F32).astype(BF16)

        row_steps = own_rows // 16

        def own_rows_at(at):
            return lax.div(at, row_steps), pl.ds(pl.multiple_of(lax.rem(at, row_steps) * 16, 16), 16)

        def norm_rows(at):
            m, rows = own_rows_at(at)
            values = own[m, rows, :].astype(F32) + branch[m, rows, :]
            middle[m, rows, :] = values
            centered = values - jnp.mean(values, axis=-1, keepdims=True)
            spread = lax.rsqrt(jnp.mean(centered * centered, axis=-1, keepdims=True) + EPSILON)
            n_own[m, rows, :] = (centered * spread * norms[0:1, :] + norms[1:2, :]).astype(BF16)

        def hidden_tile(h):
            def tile_at(at):
                m, n = lax.div(at, half // tile), lax.rem(at, half // tile)
                rows = pl.ds(pl.multiple_of(m * face_rows, face_rows), face_rows)
                columns = pl.ds(pl.multiple_of(n * tile, tile), tile)
                into = pl.ds(pl.multiple_of(h * half + n * tile, tile), tile)
                hidden = jnp.dot(n_face[m], we[h][:, columns], preferred_element_type=F32)
                square = hidden * hidden
                bend = jnp.tanh(GELU_A * hidden * (1.0 + GELU_B * square))
                active[rows, into] = (0.5 * hidden * (1.0 + bend)).astype(BF16)
                slope[rows, into] = (
                    0.5 * (1.0 + bend)
                    + (0.5 * GELU_A) * hidden * (1.0 - bend * bend) * (1.0 + (3.0 * GELU_B) * square)
                ).astype(BF16)

            return tile_at

        across = (((0,), (0,)), ((), ()))
        along = (((1,), (1,)), ((), ()))
        def reduce_tile(first):
            def tile_at(at):
                f, n = lax.div(at, width // wide), lax.rem(at, width // wide)
                columns = pl.ds(pl.multiple_of(n * wide, wide), wide)
                rows = pl.ds(pl.multiple_of(first + f * tile, tile), tile)
                pr[rows, columns] = lax.dot_general(
                    active[:, rows],
                    cot[:, :, columns].reshape(tokens, wide),
                    across,
                    preferred_element_type=F32,
                ).astype(BF16)

            return tile_at

        def slope_tile(at):
            m, n = lax.div(at, units // tile), lax.rem(at, units // tile)
            rows = pl.ds(pl.multiple_of(m * face_rows, face_rows), face_rows)
            columns = pl.ds(pl.multiple_of(n * tile, tile), tile)
            grad = lax.dot_general(cot[m], wr[columns, :], along, preferred_element_type=F32)
            slope[rows, columns] = (grad * slope[rows, columns].astype(F32)).astype(BF16)

        def normed_tile(at):
            m, n = lax.div(at, width // wide), lax.rem(at, width // wide)
            rows = pl.ds(pl.multiple_of(m * face_rows, face_rows), face_rows)
            columns = pl.ds(pl.multiple_of(n * wide, wide), wide)
            grad = lax.dot_general(slope[rows, :half], we0[columns, :], along, preferred_element_type=F32)
            grad = grad + lax.dot_general(slope[rows, half:], we1[columns, :], along, preferred_element_type=F32)
            p[m, :, columns] = grad.astype(BF16)

        def reduced_tiles(m):
            def tile_at(n):
                rows = pl.ds(m * face_rows, face_rows)
                columns = pl.ds(pl.multiple_of(n * wide, wide), wide)
                cot[m, :, columns] = jnp.dot(active[rows, :], wr[:, columns], preferred_element_type=F32).astype(BF16)

            def act():
                loop(width // wide, tile_at)
                stores.append(net.copy(cot.at[m], reduced_out.at[m]))
                stores[-1].start()

            return act

        def expand_tiles(h):
            def tile_at(at):
                k, n = lax.div(at, half // tile), lax.rem(at, half // tile)
                rows = pl.ds(pl.multiple_of(k * wide, wide), wide)
                columns = pl.ds(pl.multiple_of(n * tile, tile), tile)
                grads = pl.ds(pl.multiple_of(h * half + n * tile, tile), tile)
                we[h][rows, columns] = lax.dot_general(
                    n_face[:, :, rows].reshape(tokens, wide),
                    slope[:, grads],
                    across,
                    preferred_element_type=F32,
                ).astype(BF16)

            def act():
                loop((width // wide) * (half // tile), tile_at)
                stores.append(net.copy(we[h], (expand_a, expand_b)[h]))
                stores[-1].start()

            return act

        def back_rows(at):
            m, rows = own_rows_at(at)
            values = middle[m, rows, :]
            centered = values - jnp.mean(values, axis=-1, keepdims=True)
            spread = lax.rsqrt(jnp.mean(centered * centered, axis=-1, keepdims=True) + EPSILON)
            unit = centered * spread
            grad = branch[m, rows, :]
            norm_out[0] += grad * unit
            norm_out[1] += grad
            turned = grad * norms[0:1, :]
            inner = jnp.mean(turned * unit, axis=-1, keepdims=True)
            total = cot_own[m, rows, :].astype(F32) + spread * (
                turned - jnp.mean(turned, axis=-1, keepdims=True) - unit * inner
            )
            middle[m, rows, :] = total
            n_own[m, rows, :] = total.astype(BF16)

        def later():
            for h in (0, 1):
                expand_tiles(h)()
                yield
            for m in range(micro_count):
                reduced_tiles(m)()
                yield

        def main():
            loads[0].wait()
            loads[1].wait()
            loop(micro_count * (width // wide), branch_tile)
            yield
            yield from scatter_a.run(net, [p], [branch], slots)
            loads[2].wait()
            loop(micro_count * row_steps, norm_rows)
            keep_middle = net.copy(middle, middle_out)
            keep_middle.start()
            yield from gather.run(net, [n_own], [n_face], [])
            loads[4].wait()
            loop(micro_count * (half // tile), hidden_tile(0))
            yield
            weave.finish("e")
            loop(micro_count * (half // tile), hidden_tile(1))
            yield
            loads[5].wait()
            loop((half // tile) * (width // wide), reduce_tile(0))
            yield
            loop((half // tile) * (width // wide), reduce_tile(half))
            weave.add("s", line_s.run(net, [pr], [reduce_out], line_slots))
            weave.step("s")
            yield
            weave.finish("r")
            loop(micro_count * (units // tile), slope_tile)
            yield
            loop(micro_count * (width // wide), normed_tile)
            weave.add("x", later())
            yield from scatter_b.run(net, [p], [branch], slots)
            loads[3].wait()
            keep_middle.wait()
            norm_out[...] = jnp.zeros_like(norm_out)
            loop(micro_count * row_steps, back_rows)
            for pair in ((middle, grad_out), (n_own, low_out)):
                stores.append(net.copy(*pair))
                stores[-1].start()

        weave.add("m", main())
        for name in "".join(MLP_ORDER):
            weave.step(name)
        for name in "mxsre":
            weave.finish(name)
        for store in stores:
            store.wait()

    ins = [mixed, wo, inputs, cotangent, cot_face, norms, wexp_first, *w_expand, *w_reduce]
    specs = [ANY] * 5 + [vmem] + [ANY] * (len(ins) - 6)
    return launch(
        body, ins, specs, outs, scratch, plans, nz, ny, collective_id, "mlp_block", extra_locals=12, vmem=62
    )


def stack_heads(ref, heads, head_dim):
    return jnp.concatenate([ref[0, :, h * head_dim : (h + 1) * head_dim] for h in range(heads)], axis=0)


def masked_scores(queries, keys, query_doc, key_doc, head_dim):
    raw = lax.dot_general(keys, queries, (((1,), (1,)), ((), ())), preferred_element_type=F32)
    key_doc = jnp.concatenate([key_doc] * (raw.shape[1] // key_doc.shape[1]), axis=1)
    return jnp.where(query_doc == key_doc, raw * (LOG2_E / math.sqrt(head_dim)), NEG_FILL)


def attend_forward(queries, keys_vals, query_doc, key_doc, bounds, heads, head_dim):
    micro_count, rows, _ = queries.shape
    blocks = rows // BLOCK
    tall = heads * BLOCK

    def kernel(bounds_ref, q_ref, kv_ref, qd_ref, kd_ref, out_ref, log_ref):
        at = pl.program_id(0) * blocks + pl.program_id(1)
        low, high = bounds_ref[2 * at], bounds_ref[2 * at + 1]
        queries = stack_heads(q_ref, heads, head_dim)
        doc = jnp.concatenate([qd_ref[0, 0]] * heads, axis=1)

        def body(block, carry):
            top, total, mixed = carry
            first = pl.multiple_of(block * BLOCK, BLOCK)
            keys = kv_ref[0, pl.ds(first, BLOCK), :head_dim]
            values = kv_ref[0, pl.ds(first, BLOCK), head_dim:]
            scores = masked_scores(queries, keys, doc, kd_ref[0, pl.ds(first, BLOCK), :], head_dim)
            new_top = jnp.maximum(top, jnp.max(scores, axis=0, keepdims=True))
            weights = jnp.exp2(scores - new_top)
            fade = jnp.exp2(top - new_top)
            total = total * fade + jnp.sum(weights, axis=0, keepdims=True)
            mixed = mixed * fade + lax.dot_general(
                values, weights.astype(BF16), (((0,), (0,)), ((), ())), preferred_element_type=F32
            )
            return new_top, total, mixed

        top, total, mixed = lax.fori_loop(
            low,
            high,
            body,
            (
                jnp.full((1, tall), NEG_FILL, F32),
                jnp.zeros((1, tall), F32),
                jnp.zeros((head_dim, tall), F32),
            ),
        )
        mixed = jnp.transpose(mixed / total).astype(BF16)
        for h in range(heads):
            out_ref[0, :, h * head_dim : (h + 1) * head_dim] = mixed[h * BLOCK : (h + 1) * BLOCK]
        log_ref[0, 0] = top + jnp.log2(total)

    return pl.pallas_call(
        kernel,
        out_shape=[
            jax.ShapeDtypeStruct(queries.shape, BF16),
            jax.ShapeDtypeStruct((micro_count, blocks, 1, tall), F32),
        ],
        grid_spec=pltpu.PrefetchScalarGridSpec(
            num_scalar_prefetch=1,
            grid=(micro_count, blocks),
            in_specs=[
                pl.BlockSpec((1, BLOCK, heads * head_dim), lambda m, b, _: (m, b, 0)),
                pl.BlockSpec((1,) + keys_vals.shape[1:], lambda m, b, _: (m, 0, 0)),
                pl.BlockSpec((1, 1, 1, BLOCK), lambda m, b, _: (m, b, 0, 0)),
                pl.BlockSpec((1,) + key_doc.shape[1:], lambda m, b, _: (m, 0, 0)),
            ],
            out_specs=[
                pl.BlockSpec((1, BLOCK, heads * head_dim), lambda m, b, _: (m, b, 0)),
                pl.BlockSpec((1, 1, 1, tall), lambda m, b, _: (m, b, 0, 0)),
            ],
        ),
        compiler_params=pltpu.CompilerParams(vmem_limit_bytes=40 << 20),
        name="attend_forward",
    )(bounds, queries, keys_vals, query_doc, key_doc)


def attend_backward(queries, keys_vals, mixed, grad_mixed, log_total, query_doc, key_doc, bounds, heads, head_dim):
    micro_count, rows, _ = queries.shape
    blocks = rows // BLOCK
    seq_len = keys_vals.shape[1]
    scale = 1.0 / math.sqrt(head_dim)
    tall = heads * BLOCK

    def kernel(bounds_ref, q_ref, kv_ref, o_ref, do_ref, log_ref, qd_ref, kd_ref, gq_ref, gkv_ref, acc_ref):
        at = pl.program_id(0) * blocks + pl.program_id(1)
        low, high = bounds_ref[2 * at], bounds_ref[2 * at + 1]

        @pl.when(pl.program_id(1) == 0)
        def _():
            acc_ref[...] = jnp.zeros_like(acc_ref)

        queries, grad = stack_heads(q_ref, heads, head_dim), stack_heads(do_ref, heads, head_dim)
        products = grad.astype(F32) * stack_heads(o_ref, heads, head_dim).astype(F32)
        delta = jnp.sum(jnp.transpose(products), axis=0, keepdims=True)
        doc = jnp.concatenate([qd_ref[0, 0]] * heads, axis=1)
        log_total = log_ref[0, 0]

        def body(block, grad_queries):
            first = pl.multiple_of(block * BLOCK, BLOCK)
            keys = kv_ref[0, pl.ds(first, BLOCK), :head_dim]
            values = kv_ref[0, pl.ds(first, BLOCK), head_dim:]
            scores = masked_scores(queries, keys, doc, kd_ref[0, pl.ds(first, BLOCK), :], head_dim)
            probs = jnp.exp2(scores - log_total)
            grad_probs = lax.dot_general(values, grad, (((1,), (1,)), ((), ())), preferred_element_type=F32)
            grad_scores = (probs * (grad_probs - delta)).astype(BF16)
            acc_ref[pl.ds(first, BLOCK), :head_dim] += (
                jnp.dot(grad_scores, queries, preferred_element_type=F32) * scale
            )
            acc_ref[pl.ds(first, BLOCK), head_dim:] += jnp.dot(probs.astype(BF16), grad, preferred_element_type=F32)
            return grad_queries + lax.dot_general(
                keys, grad_scores, (((0,), (0,)), ((), ())), preferred_element_type=F32
            )

        grad_queries = lax.fori_loop(low, high, body, jnp.zeros((head_dim, tall), F32))
        grad_queries = jnp.transpose(grad_queries * scale).astype(BF16)
        for h in range(heads):
            gq_ref[0, :, h * head_dim : (h + 1) * head_dim] = grad_queries[h * BLOCK : (h + 1) * BLOCK]

        @pl.when(pl.program_id(1) == blocks - 1)
        def _():
            gkv_ref[0] = acc_ref[...].astype(BF16)

    wide = pl.BlockSpec((1, BLOCK, heads * head_dim), lambda m, b, _: (m, b, 0))
    row = pl.BlockSpec((1, seq_len, 2 * head_dim), lambda m, b, _: (m, 0, 0))
    return pl.pallas_call(
        kernel,
        out_shape=[
            jax.ShapeDtypeStruct(queries.shape, BF16),
            jax.ShapeDtypeStruct(keys_vals.shape, BF16),
        ],
        grid_spec=pltpu.PrefetchScalarGridSpec(
            num_scalar_prefetch=1,
            grid=(micro_count, blocks),
            in_specs=[
                wide,
                row,
                wide,
                wide,
                pl.BlockSpec((1, 1, 1, tall), lambda m, b, _: (m, b, 0, 0)),
                pl.BlockSpec((1, 1, 1, BLOCK), lambda m, b, _: (m, b, 0, 0)),
                pl.BlockSpec((1,) + key_doc.shape[1:], lambda m, b, _: (m, 0, 0)),
            ],
            out_specs=[wide, row],
            scratch_shapes=[pltpu.VMEM((seq_len, 2 * head_dim), F32)],
        ),
        compiler_params=pltpu.CompilerParams(vmem_limit_bytes=40 << 20),
        name="attend_backward",
    )(bounds, queries, keys_vals, mixed, grad_mixed, log_total, query_doc, key_doc)


def back_block(low, reduced, parts, mixed, wo, wq, normed, queries, keys_vals, logs, limits, nz, ny, collective_id, head_dim):
    micro_count, own_rows, width = low.shape
    face_rows, attn = queries.shape[1:]
    seq_len = keys_vals.shape[1]
    tokens = micro_count * face_rows
    blocks = face_rows // BLOCK
    heads = attn // head_dim
    tall = heads * BLOCK
    scale = 1.0 / math.sqrt(head_dim)
    wide = 512
    half = parts[0].shape[1]
    part = jax.ShapeDtypeStruct((micro_count, face_rows, width), BF16)
    gather = FaceGather(low, nz, ny)
    scatter_r = FaceScatter(reduced, nz, ny)
    scatter_q = FaceScatter(part, nz, ny, resident=True)
    whole = WholeScatter(jax.ShapeDtypeStruct((micro_count, nz, face_rows, 2 * head_dim), BF16), nz, ny, resident=True)
    line_e = LineScatter(parts, ["row", "row"], nz, ny, resident=True)
    attn_parts = [jax.ShapeDtypeStruct((attn, width), BF16), jax.ShapeDtypeStruct((width, attn), BF16)]
    line_a = LineScatter(attn_parts, ["col", "row"], nz, ny, resident=True)
    plans = [gather, scatter_r, scatter_q, whole, line_e, line_a]
    groups = [scatter_r, scatter_q, whole, line_e, line_a]
    outs = scatter_r.outs + scatter_q.outs + whole.outs + line_e.outs + line_a.outs
    normed = normed.reshape(micro_count, face_rows, width)
    given = [mixed, wo, wq, queries, keys_vals, logs, limits, *parts]
    scratch = [pltpu.VMEM(entry.shape, entry.dtype) for entry in given] + [
        pltpu.VMEM(part.shape, BF16),
        pltpu.VMEM(queries.shape, BF16),
        pltpu.VMEM(queries.shape, BF16),
        pltpu.VMEM((seq_len, 2 * head_dim), F32),
        pltpu.VMEM((micro_count * nz, face_rows, 2 * head_dim), BF16),
        pltpu.VMEM((attn, width), BF16),
        pltpu.VMEM((width, attn), BF16),
        pltpu.VMEM((2, micro_count, face_rows, wide), BF16),
    ]
    shared = len(scratch)
    for plan in groups:
        scratch = scratch + plan.scratch

    def body(net, ins, outs, scratch):
        low, reduced_in, normed_in, *given_in = ins
        reduced_out, from_out, keys_out, *line_outs = outs
        mixed, wo, wq, queries, keys_vals, logs, limits, *expand = scratch[: len(given)]
        face, grad_mixed, grad_queries, acc, grad_keys, part_out, part_query, normed = scratch[len(given) : shared]
        slots, first = {}, shared
        for name, plan in zip("rqwea", groups):
            slots[name] = list(scratch[first : first + len(plan.scratch)])
            first += len(plan.scratch)
        loads = [net.copy(*pair) for pair in zip(given_in, scratch)]
        order = [len(given) - 2, len(given) - 1] + list(range(len(given) - 2))
        weave = Weave()
        along = (((1,), (1,)), ((), ()))
        across = (((0,), (0,)), ((), ()))

        def mix_tile(m):
            grad_mixed[m] = lax.dot_general(face[m], wo[...], along, preferred_element_type=F32).astype(BF16)

        def attn_out_tile(n):
            columns = pl.ds(pl.multiple_of(n * wide, wide), wide)
            part_out[:, columns] = lax.dot_general(
                mixed[...].reshape(tokens, attn),
                face[:, :, columns].reshape(tokens, wide),
                across,
                preferred_element_type=F32,
            ).astype(BF16)

        def attn_tile(m):
            def tile_at(b):
                rows = pl.ds(pl.multiple_of(b * BLOCK, BLOCK), BLOCK)

                def stack(ref):
                    return jnp.concatenate(
                        [ref[m, rows, h * head_dim : (h + 1) * head_dim] for h in range(heads)], axis=0
                    )

                query, grad = stack(queries), stack(grad_mixed)
                products = grad.astype(F32) * stack(mixed).astype(F32)
                delta = jnp.sum(jnp.transpose(products), axis=0, keepdims=True)
                starts = jnp.concatenate([limits[m, b, 0:1, :]] * heads, axis=1)
                ends = jnp.concatenate([limits[m, b, 1:2, :]] * heads, axis=1)
                log_total = logs[m, b]
                place = lax.broadcasted_iota(jnp.int32, (BLOCK, tall), 0)

                def body(block, grad_query):
                    first = pl.multiple_of(block * BLOCK, BLOCK)
                    keys = keys_vals[m, pl.ds(first, BLOCK), :head_dim]
                    values = keys_vals[m, pl.ds(first, BLOCK), head_dim:]
                    raw = lax.dot_general(keys, query, along, preferred_element_type=F32)
                    allowed = (place >= starts - first) & (place < ends - first)
                    probs = jnp.where(allowed, jnp.exp2(raw * (LOG2_E * scale) - log_total), 0.0)
                    grad_probs = lax.dot_general(values, grad, along, preferred_element_type=F32)
                    grad_scores = (probs * (grad_probs - delta)).astype(BF16)
                    acc[pl.ds(first, BLOCK), :head_dim] += (
                        jnp.dot(grad_scores, query, preferred_element_type=F32) * scale
                    )
                    acc[pl.ds(first, BLOCK), head_dim:] += jnp.dot(
                        probs.astype(BF16), grad, preferred_element_type=F32
                    )
                    return grad_query + lax.dot_general(keys, grad_scores, across, preferred_element_type=F32)

                grad_query = lax.fori_loop(
                    0, net.z * blocks + b + 1, body, jnp.zeros((head_dim, tall), F32)
                )
                grad_query = jnp.transpose(grad_query * scale).astype(BF16)
                for h in range(heads):
                    grad_queries[m, rows, h * head_dim : (h + 1) * head_dim] = grad_query[h * BLOCK : (h + 1) * BLOCK]

            return tile_at

        def from_tile(at):
            m, n = lax.div(at, width // wide), lax.rem(at, width // wide)
            columns = pl.ds(pl.multiple_of(n * wide, wide), wide)
            face[m, :, columns] = lax.dot_general(
                grad_queries[m], wq[columns, :], along, preferred_element_type=F32
            ).astype(BF16)

        columns_in = [
            net.copy(normed_in.at[:, :, pl.ds(n * wide, wide)], normed.at[n % 2]) for n in range(width // wide)
        ]

        def query_tile(n):
            columns_in[n].wait()

            def tile_at(_):
                part_query[n * wide : (n + 1) * wide, :] = lax.dot_general(
                    normed[n % 2].reshape(tokens, wide),
                    grad_queries[...].reshape(tokens, attn),
                    across,
                    preferred_element_type=F32,
                ).astype(BF16)

            loop(1, tile_at)
            if n + 2 < width // wide:
                columns_in[n + 2].start()

        def main():
            yield from gather.run(net, [low], [face], [])
            for at in order[2:]:
                loads[at].wait()
            loop(micro_count, mix_tile)
            yield
            for m in range(micro_count):
                acc[...] = jnp.zeros_like(acc)
                loop(blocks, attn_tile(m))
                for k in range(nz):
                    grad_keys[m * nz + k] = acc[k * face_rows : (k + 1) * face_rows, :].astype(BF16)
                yield
            loop(width // wide, attn_out_tile)
            weave.add("w", whole.run(net, [grad_keys], [keys_out], slots["w"]))
            weave.step("w")
            loop(micro_count * (width // wide), from_tile)
            weave.add("q", scatter_q.run(net, [face], [from_out], slots["q"]))
            weave.step("q")
            for n in range(width // wide):
                query_tile(n)
            weave.add("a", line_a.run(net, [part_out, part_query], line_outs[2:], slots["a"]))
            weave.step("a")

        weave.add("m", main())
        weave.step("m")
        for at in order:
            loads[at].start()
        for copy in columns_in[:2]:
            copy.start()
        for at in order[:2]:
            loads[at].wait()
        weave.add("e", line_e.run(net, expand, line_outs[:2], slots["e"]))
        weave.step("e")
        weave.add("r", scatter_r.run(net, [reduced_in], [reduced_out], slots["r"]))
        for name in "".join(BACK_ORDER):
            weave.step(name)
        for name in "mwqrea":
            weave.finish(name)

    ins = [low, reduced, normed, *given]
    specs = [IN_VMEM] + [ANY] * (len(ins) - 1)
    return launch(
        body, ins, specs, outs, scratch, plans, nz, ny, collective_id, "back_block", extra_locals=len(given) + width // wide, vmem=62
    )


def local(
    inputs,
    cotangent,
    doc_ids,
    attn_gain,
    attn_shift,
    w_query,
    w_keyval,
    w_attn_out,
    mlp_gain,
    mlp_shift,
    w_expand,
    w_reduce,
):
    nz = lax.axis_size("dp") // 2
    tensor_count = lax.axis_size("tensor")
    ny = tensor_count // 2
    ranks = 2 * tensor_count
    micro_count, own_rows, width = inputs.shape
    face_rows = own_rows * ranks
    tokens = micro_count * face_rows
    seq_len = doc_ids.shape[1]
    head_dim = w_keyval.shape[1] // 2
    heads = w_query.shape[1] // (2 * head_dim)
    z = lax.axis_index("dp") // 2
    swap = functools.partial(exchange, nz=nz, ny=ny)
    on = (nz, ny)

    def dot(a, b):
        return jnp.dot(a, b, preferred_element_type=F32)

    def dot_bt(a, b):
        return lax.dot_general(a, b, (((1,), (1,)), ((), ())), preferred_element_type=F32)

    def dot_at(a, b):
        return lax.dot_general(a, b, (((0,), (0,)), ((), ())), preferred_element_type=F32)

    norms = jnp.stack([attn_gain, attn_shift, mlp_gain, mlp_shift])
    norms = jnp.concatenate([norms, jnp.zeros((4, norms.shape[1]), BF16)])
    (wq, wo, wkv), (norms,), (face_in,), (expand_given,) = swap(
        [
            LineGather([w_query, w_attn_out, w_keyval], ["row", "col", "both"], *on),
            PlaneGather(norms, *on),
            FaceGather(inputs, *on, hold_x=True),
            HalfSwap([w_expand], ["row"], *on),
        ],
        collective_id=1,
        name="gather_attention",
        order=K1_ORDER,
    )
    norms = norms[:, :4].transpose(1, 0, 2).reshape(4, width).astype(F32)
    gain_one, shift_one = norms[0], norms[1]

    normed = layer_norm(face_in.astype(F32), gain_one, shift_one).astype(BF16).reshape(tokens, width)
    queries = dot(normed, wq).astype(BF16).reshape(micro_count, face_rows, heads * head_dim)
    keys_face = dot(normed, wkv).astype(BF16).reshape(micro_count, face_rows, 2 * head_dim)
    (keys_vals,), (wexp_first,), (cot_face,) = swap(
        [
            KeysGather(keys_face, *on),
            LineGather([w_expand], ["row"], *on, share=(0, 2), given=[expand_given]),
            FaceGather(cotangent, *on, hold_x=True),
        ],
        collective_id=2,
        name="gather_keys",
        order=K2_ORDER,
    )

    query_doc = lax.dynamic_slice_in_dim(doc_ids, z * face_rows, face_rows, axis=1)
    blocks = face_rows // BLOCK
    last_doc = doc_ids[:, BLOCK - 1 :: BLOCK]
    first_doc = query_doc[:, ::BLOCK]
    lows = jnp.sum((last_doc[:, None, :] < first_doc[:, :, None]).astype(jnp.int32), axis=-1)
    highs = jnp.broadcast_to(z * blocks + jnp.arange(blocks, dtype=jnp.int32) + 1, lows.shape)
    bounds = jnp.stack([lows, highs], axis=-1).reshape(-1)
    docs = (
        query_doc.reshape(micro_count, blocks, 1, BLOCK),
        jnp.broadcast_to(doc_ids[:, :, None], doc_ids.shape + (128,)),
        bounds,
        heads,
        head_dim,
    )
    mixed, log_total = attend_forward(queries, keys_vals, *docs)
    mixed_flat = mixed.reshape(tokens, heads * head_dim)

    own_in = inputs.astype(F32)
    middle, grad_middle, low_middle, grad_norm_two, part_expand_a, part_expand_b, reduced, grad_reduce = mlp_block(
        mixed_flat, wo, inputs, cotangent, cot_face, norms[2:], wexp_first, (w_expand, expand_given), (w_reduce,), *on, collective_id=3
    )
    grad_gain_two, grad_shift_two = jnp.sum(grad_norm_two, axis=1)
    same = doc_ids[:, None, :]
    starts = jnp.sum((same < query_doc[:, :, None]).astype(jnp.int32), axis=-1)
    ends = jnp.sum((same <= query_doc[:, :, None]).astype(jnp.int32), axis=-1)
    limits = jnp.stack([starts, ends], axis=1).reshape(micro_count, 2, blocks, BLOCK).transpose(0, 2, 1, 3)
    reduced, from_query, grad_keys, grad_expand_a, grad_expand_b, grad_attn_out, grad_query = back_block(
        low_middle,
        reduced,
        [part_expand_a, part_expand_b],
        mixed,
        wo,
        wq,
        normed,
        queries,
        keys_vals,
        log_total,
        limits,
        *on,
        collective_id=6,
        head_dim=head_dim,
    )
    outputs = (middle + reduced).astype(BF16)
    grad_keys = grad_keys.astype(BF16).reshape(micro_count * own_rows, 2 * head_dim)
    normed_own, norm_pull_one = jax.vjp(layer_norm, own_in, gain_one, shift_one)
    grad_normed = from_query + dot_bt(grad_keys, wkv).reshape(from_query.shape)
    grad_tok_norm, grad_gain_one, grad_shift_one = norm_pull_one(grad_normed)
    part_keyval = dot_at(normed_own.astype(BF16).reshape(-1, width), grad_keys).astype(BF16)
    own_width = width // (nz * ranks)
    small = jnp.stack([grad_gain_one, grad_shift_one, grad_gain_two, grad_shift_two])
    small = small.reshape(4, nz, ranks, own_width).transpose(2, 1, 0, 3)
    small = jnp.pad(small, ((0, 0), (0, 0), (0, 4), (0, 128 - own_width)))
    (grad_keyval,), (small,) = swap(
        [QuickScatter(part_keyval.reshape(nz, width // nz, 2 * head_dim), *on), SmallScatter(small, *on)],
        collective_id=8,
        name="scatter_small",
    )
    small = small[:4, :own_width]

    def by_row(halves):
        return jnp.concatenate([halves[0], halves[1]], axis=1).astype(F32)

    def by_column(halves):
        return halves.reshape(-1, halves.shape[-1]).astype(F32)

    return (
        outputs,
        grad_middle + grad_tok_norm,
        small[0],
        small[1],
        by_row(grad_query),
        grad_keyval,
        by_column(grad_attn_out),
        small[2],
        small[3],
        by_row(jnp.concatenate([grad_expand_a, grad_expand_b], axis=2)),
        by_column(grad_reduce),
    )


def solution(mesh):
    placed = (
        P(None, ("dp", "tensor"), None),
        P(None, ("dp", "tensor"), None),
        P(),
        P("dp"),
        P("dp"),
        P("dp", "tensor"),
        P("dp", None),
        P("tensor", "dp"),
        P("dp"),
        P("dp"),
        P("dp", "tensor"),
        P("tensor", "dp"),
    )
    return jax.shard_map(
        local,
        mesh=mesh,
        in_specs=placed,
        out_specs=(
            P(None, ("dp", "tensor"), None),
            P(None, ("dp", "tensor"), None),
            P(("dp", "tensor")),
            P(("dp", "tensor")),
            P("dp", "tensor"),
            P(("dp", "tensor"), None),
            P("tensor", "dp"),
            P(("dp", "tensor")),
            P(("dp", "tensor")),
            P("dp", "tensor"),
            P("tensor", "dp"),
        ),
        check_vma=False,
    )
```

```python
import functools
import math

import jax
import jax.numpy as jnp
from jax import lax
from jax.experimental import pallas as pl
from jax.experimental.pallas import tpu as pltpu
from jax.sharding import PartitionSpec as P

BLOCK = 256
EPSILON = 1e-05
NEG_FILL = -1e30
GELU_A = math.sqrt(2.0 / math.pi)
GELU_B = 0.044715
LOG2_E = 1.0 / math.log(2.0)
MLP_ORDER = ("mmmmmeeemmmeerrmmmrmmmrmmmrmmmmsmsmmxmmm", "msxxsxs",)
BACK_ORDER = ("mrmerrmrrmmmemmemmrreemwwwqwqqaewrawrqaa", "eaqwqwaa",)
FRONT_ORDER = ("omoaaaamaaaaamcoaammhaommaommokkmekcooeh", "kookcacemecmkecmcemcec",)
MESH = pl.DeviceIdType.MESH
ANY = pl.BlockSpec(memory_space=pl.ANY)
READY = "ready"
IN_VMEM = pl.BlockSpec(memory_space=pltpu.VMEM)
BF16 = jnp.bfloat16
F32 = jnp.float32


def layer_norm(values, gain, shift):
    center = jnp.mean(values, axis=-1, keepdims=True)
    centered = values - center
    variance = jnp.mean(centered * centered, axis=-1, keepdims=True)
    return centered * lax.rsqrt(variance + EPSILON) * gain + shift


def gelu_tanh(values):
    return jax.nn.gelu(values, approximate=True)


class Net:
    def __init__(self, nz, ny, send, recv, local):
        dp, tensor = lax.axis_index("dp"), lax.axis_index("tensor")
        self.nz, self.ny = nz, ny
        self.z, self.x = lax.div(dp, 2), lax.rem(dp, 2)
        self.y, self.c = lax.div(tensor, 2), lax.rem(tensor, 2)
        self.tensor = tensor
        self.send, self.recv, self.local = send, recv, local
        self.used = [0, 0]
        self.keys = {}

    def flip(self, value, by):
        return value + by - 2 * by * value if by else value

    def xy(self, dx, dy):
        return self.flip(self.x, dx), lax.rem(self.y + dy, self.ny) if dy else self.y

    def rank(self, dx=0, dy=0, dc=0):
        x, y = self.xy(dx, dy)
        return x * (2 * self.ny) + y * 2 + self.flip(self.c, dc)

    def device(self, dx=0, dy=0, dc=0, z=None):
        x, y = self.xy(dx, dy)
        return ((self.z if z is None else z) * 2 + x, y * 2 + self.flip(self.c, dc))

    def slot(self, key):
        if key not in self.keys:
            self.keys[key] = self.used[0]
            self.used[0] += 1
        return self.keys[key]

    def remote(self, key, src, dst, device):
        at = self.slot(key)
        return pltpu.make_async_remote_copy(
            src_ref=src,
            dst_ref=dst,
            send_sem=self.send.at[at],
            recv_sem=self.recv.at[at],
            device_id=device,
            device_id_type=MESH,
        )

    def take_locals(self, count):
        first = self.used[1]
        self.used[1] += count
        return first

    def copy_at(self, at, src, dst):
        return pltpu.make_async_copy(src, dst, self.local.at[at])

    def copy(self, src, dst):
        return self.copy_at(self.take_locals(1), src, dst)


def add_rows(dst, terms):
    lead, height, width = dst.shape
    rows = min(max(16, 32768 // width), height)
    steps = height // rows

    def body(step, carry):
        at, off = lax.div(step, steps), pl.multiple_of(lax.rem(step, steps) * rows, rows)
        total = terms[0][at, pl.ds(off, rows), :].astype(F32)
        for term in terms[1:]:
            total = total + term[at, pl.ds(off, rows), :].astype(F32)
        dst[at, pl.ds(off, rows), :] = total.astype(dst.dtype)
        return carry

    lax.fori_loop(0, lead * steps, body, 0)


class FaceGather:
    moves = ("x", "y", "c")
    in_spec = IN_VMEM

    def __init__(self, own, nz, ny, hold_x=False):
        self.ins, self.hold_x = [own], hold_x
        m, t, d = own.shape
        self.outs = [(jax.ShapeDtypeStruct((m, 4 * ny * t, d), own.dtype), ANY)]
        self.scratch = []
        self.half = t // 2
        self.remotes, self.locals = 8 * ny, 1

    def run(self, net, ins, outs, scratch):
        (own,), (out,), half = ins, outs, self.half
        dys = range(1, net.ny)

        def piece(dx, dy, h):
            return out.at[:, pl.ds(pl.multiple_of(net.rank(dx, dy) * 2 * half + h * half, half), half), :]

        mine = [own.at[:, pl.ds(h * half, half), :] for h in (0, 1)]
        keep = net.copy(own, out.at[:, pl.ds(pl.multiple_of(net.rank() * 2 * half, half), 2 * half), :])
        keep.start()
        sent = {}

        def send(key, src, dst, device):
            sent[key] = net.remote((id(self), key), src, dst, device)
            sent[key].start()

        if not self.hold_x:
            send(("x", 0), mine[0], piece(0, 0, 0), net.device(1, 0))
        for dy in dys:
            send(("y", dy, 1), mine[1], piece(0, 0, 1), net.device(0, dy))
        if not self.hold_x:
            send(("x", 1), mine[1], piece(0, 0, 1), net.device(1, 0))
        for dy in dys:
            send(("y", dy, 0), mine[0], piece(0, 0, 0), net.device(0, dy))
        for h in (0, 1):
            send(("c", h), mine[h], piece(0, 0, h), net.device(0, 0, 1))
        if self.hold_x:
            yield
            for h in (0, 1):
                send(("x", h), mine[h], piece(0, 0, h), net.device(1, 0))

        def share(key, dx, dy, h):
            send(("c",) + key, piece(dx, dy, h), piece(dx, dy, h), net.device(0, 0, 1))

        def from_x(h):
            sent["x", h].wait_recv()
            if not h:
                for dy in dys:
                    send(("xy", dy), piece(1, 0, 0), piece(1, 0, 0), net.device(0, dy))
            share(("x", h), 1, 0, h)

        def from_y(dy, h):
            sent["y", dy, h].wait_recv()
            if h:
                send(("yx", dy), piece(0, -dy % net.ny, 1), piece(0, -dy % net.ny, 1), net.device(1, 0))
            share(("y", dy, h), 0, -dy % net.ny, h)

        arrivals = []
        for first in (True, False):
            on_x = [functools.partial(from_x, 0 if first else 1)]
            on_y = [functools.partial(from_y, dy, 1 if first else 0) for dy in dys]
            arrivals.append(on_x + on_y)
        if self.hold_x:
            arrivals = [arrivals[0][1:], arrivals[1][1:], arrivals[0][:1], arrivals[1][:1]]
        for group in arrivals:
            for arrive in group:
                yield
                arrive()
        for dy in dys:
            yield
            sent["xy", dy].wait_recv()
            share(("xy", dy), 1, -dy % net.ny, 0)
            yield
            sent["yx", dy].wait_recv()
            share(("yx", dy), 1, -dy % net.ny, 1)
        yield
        for key, copy in sent.items():
            if key[0] == "c":
                copy.wait_recv()
        for copy in sent.values():
            copy.wait_send()
        keep.wait()


class FaceScatter:
    moves = ("x", "y", "c")

    def __init__(self, part, nz, ny, resident=False):
        self.ins, self.resident = [part], resident
        m, rows, d = part.shape
        t = rows // (4 * ny)
        self.outs = [(jax.ShapeDtypeStruct((m, t, d), F32), pl.BlockSpec(memory_space=pltpu.VMEM))]
        half = t // 2
        self.half = half
        self.scratch = [
            pltpu.VMEM((2 * ny, m, t, d), BF16),
            pltpu.VMEM((ny - 1, m, half, d), BF16),
            pltpu.VMEM((ny - 1, m, half, d), BF16),
            pltpu.VMEM((2, m, half, d), BF16),
            pltpu.VMEM((2, ny - 1, m, half, d), BF16),
        ]
        if not resident:
            self.scratch.append(pltpu.VMEM((2 * ny, m, t, d), BF16))
        self.remotes, self.locals = 6 * ny + 4, 2 * ny

    def run(self, net, ins, outs, scratch):
        (part,), (out,), half = ins, outs, self.half
        from_core, x_diag, y_diag, x_in, y_in = scratch[:5]
        ny = net.ny
        dys = range(1, ny)
        order = [(1, dy) for dy in dys] + [(1, 0)] + [(0, dy) for dy in dys] + [(0, 0)]
        sent, loads = {}, {}

        def send(key, src, dst, device):
            sent[key] = net.remote((id(self), key), src, dst, device)
            sent[key].start()

        def rows(dx, dy, dc, first=0, size=2 * half):
            at = net.rank(dx, dy, dc) * 2 * half + first
            return part.at[:, pl.ds(pl.multiple_of(at, half), size), :]

        def work(dx, dy, first=0, size=2 * half):
            if self.resident:
                return rows(dx, dy, 0, first, size)
            return scratch[5].at[dx * ny + dy, :, pl.ds(first, size), :]

        for dx, dy in order:
            at = dx * ny + dy
            if not self.resident:
                loads[at] = net.copy(rows(dx, dy, 0), work(dx, dy))
                loads[at].start()
            send(("c", at), rows(dx, dy, 1), from_core.at[at], net.device(0, 0, 1))
        for dx, dy in order:
            at = dx * ny + dy
            yield
            if not self.resident:
                loads[at].wait()
            sent["c", at].wait_recv()
            add_rows(work(dx, dy), [work(dx, dy), from_core.at[at]])
            top, low = work(dx, dy, 0, half), work(dx, dy, half, half)
            if dx and dy:
                send(("xd", dy), top, x_diag.at[dy - 1], net.device(1, 0))
                send(("yd", dy), low, y_diag.at[dy - 1], net.device(0, dy))
            elif dx:
                send(("x", 0), top, x_in.at[0], net.device(1, 0))
            elif dy:
                send(("y", dy, 1), low, y_in.at[1, dy - 1], net.device(0, dy))
        for dy in dys:
            yield
            sent["xd", dy].wait_recv()
            top = work(0, dy, 0, half)
            add_rows(top, [top, x_diag.at[dy - 1]])
            send(("y", dy, 0), top, y_in.at[0, dy - 1], net.device(0, dy))
        low = work(1, 0, half, half)
        for dy in dys:
            yield
            sent["yd", dy].wait_recv()
            add_rows(low, [low, y_diag.at[dy - 1]])
        send(("x", 1), low, x_in.at[1], net.device(1, 0))
        for h in (0, 1):
            yield
            sent["x", h].wait_recv()
            for dy in dys:
                sent["y", dy, h].wait_recv()
            add_rows(
                out.at[:, pl.ds(h * half, half), :],
                [work(0, 0, h * half, half), x_in.at[h]] + [y_in.at[h, dy - 1] for dy in dys],
            )
        for copy in sent.values():
            copy.wait_send()


class LineGather:
    moves = ("x", "line", "c")
    in_spec = IN_VMEM

    def __init__(self, shards, kinds, nz, ny, share=(0, 1), given=()):
        self.ins, self.kinds, self.share = list(shards) + list(given), list(kinds), share
        self.outs, self.scratch = [], []
        for shard, kind in zip(shards, kinds):
            rows, columns = shard.shape
            if kind == "row":
                shape = (rows * 2 * nz, columns // 2 // share[1])
            elif kind == "col":
                shape = (rows // 2 // share[1], columns * 2 * nz)
            else:
                shape = (rows * 2 * nz, columns)
            self.outs.append((jax.ShapeDtypeStruct(shape, shard.dtype), ANY))
        count = len(self.kinds)
        self.remotes = count * (1 + 4 * (nz - 1)) + kinds.count("both") * (1 + 4 * (nz - 1))
        self.locals = 2 * count

    def run(self, net, ins, outs, scratch):
        nz, z = net.nz, net.z
        sent, locals_, shared = [], [], []
        weights = []
        given = ins[len(self.kinds) :]
        for at, (shard, out, kind) in enumerate(zip(ins, outs, self.kinds)):
            rows, columns = shard.shape

            if kind == "row":
                span = columns // 2 // self.share[1]

                def mine(dx, shard=shard, span=span):
                    first = (net.flip(net.x, dx) * self.share[1] + self.share[0]) * span
                    return shard.at[:, pl.ds(pl.multiple_of(first, span), span)]

                def block(line, dx, out=out, rows=rows):
                    first = (line * 2 + net.flip(net.x, dx)) * rows
                    return out.at[pl.ds(pl.multiple_of(first, rows), rows), :]

            elif kind == "col":
                span = rows // 2 // self.share[1]

                def mine(dx, shard=shard, span=span):
                    first = (net.flip(net.x, dx) * self.share[1] + self.share[0]) * span
                    return shard.at[pl.ds(pl.multiple_of(first, span), span), :]

                def block(line, dx, out=out, columns=columns):
                    first = (line * 2 + net.flip(net.x, dx)) * columns
                    return out.at[:, pl.ds(pl.multiple_of(first, columns), columns)]

            else:
                half = rows // 2

                def mine(dx, shard=shard, half=half):
                    return shard.at[pl.ds(pl.multiple_of(net.c * half, half), half), :]

                def block(line, dx, out=out, rows=rows, half=half):
                    first = (line * 2 + net.flip(net.x, dx)) * rows + net.c * half
                    return out.at[pl.ds(pl.multiple_of(first, half), half), :]

            weights.append((at, kind, mine, block))

        def hop(at, dx, step, up, block, src=None):
            origin = z - (step - 1) if up else z + (step - 1)
            there = z + 1 if up else z - 1
            copy = net.remote(
                (id(self), at, dx, step, up),
                block(origin, dx) if src is None else src,
                block(origin, dx),
                net.device(z=there),
            )
            fits = (origin >= 0) & (there < nz) if up else (origin < nz) & (there >= 0)
            return copy, fits

        def start(at, dx, step, up, block, src=None):
            copy, fits = hop(at, dx, step, up, block, src)
            pl.when(fits)(copy.start)
            sent.append((copy, fits))

        def arrived(at, dx, step, up, block, kind):
            copy, _ = hop(at, dx, step, up, block)
            origin = z - step if up else z + step
            fits = origin >= 0 if up else origin < nz
            pl.when(fits)(copy.wait_recv)
            if kind == "both":
                share = net.remote(
                    (id(self), "c", at, dx, step, up), block(origin, dx), block(origin, dx), net.device(0, 0, 1)
                )
                pl.when(fits)(share.start)
                shared.append((share, fits))

        swaps = {}
        for at, kind, mine, block in weights:
            if not given:
                swaps[at] = net.remote((id(self), at, "x"), mine(1), block(z, 0), net.device(1, 0))
                swaps[at].start()
            for up in (True, False):
                start(at, 0, 1, up, block, mine(0))
        for at, kind, mine, block in weights:
            if kind == "both":
                whole = ins[at].shape[0]
                into = outs[at].at[pl.ds(pl.multiple_of((z * 2 + net.x) * whole, whole), whole), :]
                locals_.append(net.copy(ins[at], into))
            else:
                locals_.append(net.copy(mine(0), block(z, 0)))
            locals_[-1].start()
        for (at, kind, mine, block), other in zip(weights, given):
            span = pl.ds(self.share[0] * other.shape[kind == "row"] // self.share[1], other.shape[kind == "row"] // self.share[1])
            other = other.at[:, span] if kind == "row" else other.at[span, :]
            locals_.append(net.copy(other, block(z, 1)))
            locals_[-1].start()
            for up in (True, False):
                start(at, 1, 1, up, block, other)
        yield
        for copy in locals_:
            copy.wait()
        for at, kind, mine, block in weights:
            if given:
                continue
            swaps[at].wait_recv()
            for up in (True, False):
                start(at, 1, 1, up, block)
            if kind == "both":
                share = net.remote((id(self), "c", at), block(z, 1), block(z, 1), net.device(0, 0, 1))
                share.start()
                shared.append((share, None))
        for step in range(1, nz):
            for at, kind, mine, block in weights:
                for dx in (0, 1):
                    yield
                    for up in (True, False):
                        arrived(at, dx, step, up, block, kind)
                        if step < nz - 1:
                            start(at, dx, step + 1, up, block)
        yield
        for copy, fits in shared:
            if fits is None:
                copy.wait_recv()
            else:
                pl.when(fits)(copy.wait_recv)
        yield READY
        for copy, fits in shared:
            if fits is None:
                copy.wait_send()
            else:
                pl.when(fits)(copy.wait_send)
        for copy, fits in sent:
            pl.when(fits)(copy.wait_send)
        for copy in swaps.values():
            copy.wait_send()


class HalfSwap:
    moves = ("x",)

    def __init__(self, shards, kinds, nz, ny):
        self.ins, self.kinds = list(shards), list(kinds)
        self.outs, self.scratch = [], []
        for shard, kind in zip(shards, kinds):
            rows, columns = shard.shape
            shape = (rows, columns // 2) if kind == "row" else (rows // 2, columns)
            self.outs.append((jax.ShapeDtypeStruct(shape, shard.dtype), ANY))
        self.remotes, self.locals = len(self.ins), 0

    def run(self, net, ins, outs, scratch):
        copies = []
        for at, (shard, out, kind) in enumerate(zip(ins, outs, self.kinds)):
            span = out.shape[kind == "row"]
            there = pl.ds(pl.multiple_of((1 - net.x) * span, span), span)
            src = shard.at[:, there] if kind == "row" else shard.at[there, :]
            copies.append(net.remote((id(self), at), src, out, net.device(1, 0)))
            copies[-1].start()
        yield
        for copy in copies:
            copy.wait_recv()
        yield READY
        for copy in copies:
            copy.wait_send()


class LineScatter:
    moves = ("x", "line")

    def __init__(self, parts, kinds, nz, ny, resident=False):
        self.ins, self.kinds, self.resident = list(parts), list(kinds), resident
        self.outs, self.scratch = [], []
        for part, kind in zip(parts, kinds):
            rows, columns = part.shape
            shape = (rows // (2 * nz), columns) if kind == "row" else (rows, columns // (2 * nz))
            self.outs.append((jax.ShapeDtypeStruct((2,) + shape, BF16), ANY))
            for lead in (nz - 1, nz - 1, 1) + (() if resident else (nz,)):
                self.scratch.append(pltpu.VMEM((lead, 2) + shape, BF16))
        count = len(self.ins)
        self.remotes = count * (1 + 4 * nz)
        self.locals = count * (2 * nz + 1)

    def run(self, net, ins, outs, scratch):
        nz, z = net.nz, net.z
        loads, grads = {}, []
        each = 3 if self.resident else 4
        for at, (part, out, kind) in enumerate(zip(ins, outs, self.kinds)):
            down, up, mine = scratch[each * at : each * at + 3]
            _, _, rows, columns = mine.shape

            def block(line, dx, part=part, kind=kind, rows=rows, columns=columns):
                size = rows if kind == "row" else columns
                first = pl.ds(pl.multiple_of((line * 2 + net.flip(net.x, dx)) * size, size), size)
                return part.at[first, :] if kind == "row" else part.at[:, first]

            if self.resident:
                work = block
            else:

                def work(line, dx, at=at):
                    return scratch[each * at + 3].at[line, dx]

                order = []
                for k in range(nz):
                    order += [k, nz - 1 - k]
                for line in dict.fromkeys(order):
                    for dx in (1, 0):
                        loads[at, line, dx] = net.copy(block(line, dx), work(line, dx))
                        loads[at, line, dx].start()
            grads.append((at, out, work, down, up, mine))

        def inbox(slots, line, dx, toward):
            return slots.at[line if toward < 0 else line - 1, dx]

        pieces = (1, 0)
        each_line = len(pieces)

        for at, *_ in grads:
            net.slot((id(self), at, "x"))
            for dx in (0, 1):
                for line in range(nz):
                    for toward in (-1, 1):
                        net.slot((id(self), at, line, dx, toward))

        def chain(grad, dx, line, toward):
            at, out, work, down, up, mine = grad
            slot = inbox(down if toward < 0 else up, line, dx, toward)
            copy = net.remote((id(self), at, line, dx, toward), work(line, dx), slot, net.device(z=z + toward))
            return copy, slot

        def forward(place, grad, dx, line, toward):
            at, out, work, down, up, mine = grad
            copy, slot = chain(grad, dx, line, toward)
            if not self.resident:
                loads[at, line, dx].wait()
            if place != (nz - 1 if toward < 0 else 0):
                copy.wait_recv()
                add_rows(_lead(work(line, dx)), [_lead(work(line, dx)), _lead(slot)])
            copy.start()

        def finish(place, grad, dx):
            at, out, work, down, up, mine = grad
            if not self.resident:
                loads[at, place, dx].wait()
            terms = [_lead(work(place, dx))]
            for toward in (-1, 1):
                if (place < nz - 1) if toward < 0 else (place > 0):
                    copy, slot = chain(grad, dx, place, toward)
                    copy.wait_recv()
                    terms.append(_lead(slot))
            total = mine.at[0, dx]
            add_rows(_lead(total), terms)
            if dx:
                net.remote((id(self), at, "x"), total, out.at[net.x], net.device(1, 0)).start()
            else:
                net.copy_at(self.first_local + at, total, out.at[net.x]).start()

        plan = {}
        for place in range(nz):
            waits_up, waits_down = place, nz - 1 - place
            todo = []
            for toward, waits, lines in (
                (1, waits_up, range(nz - 1, place, -1)),
                (-1, waits_down, range(place)),
            ):
                order = [(line, dx) for line in lines for dx in pieces]
                for j, (line, dx) in enumerate(order):
                    for grad in grads:
                        todo.append((waits + j if waits else 0, waits, (forward, grad, dx, line, toward)))
            for q, dx in enumerate(pieces):
                times = []
                if waits_up:
                    times.append(waits_up + each_line * (nz - 1 - place) + q)
                if waits_down:
                    times.append(waits_down + each_line * place + q)
                for grad in grads:
                    todo.append((max(times), nz, (finish, grad, dx)))
            for time, waits, item in sorted(todo, key=lambda entry: entry[:2]):
                plan.setdefault(time, {}).setdefault(place, []).append(item)
        self.first_local = net.take_locals(len(grads))
        for time in range(max(plan) + 1):
            if time:
                yield
            for place, items in sorted(plan.get(time, {}).items()):

                def act(place=place, items=items):
                    for item in items:
                        item[0](place, *item[1:])

                pl.when(z == place)(act)
        sent = [
            (chain(grad, dx, line, toward)[0], (z > line) if toward < 0 else (z < line))
            for grad in grads
            for dx in pieces
            for toward, lines in ((-1, range(nz - 1)), (1, range(1, nz)))
            for line in lines
        ]
        swaps = [net.remote((id(self), at, "x"), mine.at[0, 1], out.at[net.x], net.device(1, 0)) for at, out, _, _, _, mine in grads]
        stores = [net.copy_at(self.first_local + at, mine.at[0, 0], out.at[net.x]) for at, out, _, _, _, mine in grads]
        yield
        for copy, sends in sent:
            pl.when(sends)(copy.wait_send)
        for copy in swaps:
            copy.wait()
        for copy in stores:
            copy.wait()


def _lead(ref):
    return Lead(ref)


class Lead:
    def __init__(self, ref):
        self.ref, self.shape, self.dtype = ref, (1,) + tuple(ref.shape), ref.dtype

    def __getitem__(self, index):
        return self.ref[index[1], index[2]]

    def __setitem__(self, index, value):
        self.ref[index[1], index[2]] = value


class KeysGather:
    moves = ("x", "line", "c")
    in_spec = IN_VMEM

    def __init__(self, face, nz, ny):
        m, rows, width = face.shape
        self.ins = [face]
        self.outs = [(jax.ShapeDtypeStruct((m, nz * rows, width), face.dtype), ANY)]
        self.scratch = []
        self.remotes, self.locals = 4 * (nz - 1), 1

    def run(self, net, ins, outs, scratch):
        (face,), (out,) = ins, outs
        nz, z = net.nz, net.z
        _, rows, width = face.shape
        part, side = rows // 2, width // 2

        def block(line, dx, dc):
            first = pl.multiple_of(line * rows + net.flip(net.x, dx) * part, part)
            column = pl.multiple_of(net.flip(net.c, dc) * side, side)
            return out.at[:, pl.ds(first, part), pl.ds(column, side)]

        own = face.at[
            :,
            pl.ds(pl.multiple_of(net.x * part, part), part),
            pl.ds(pl.multiple_of(net.c * side, side), side),
        ]
        sent, shared = [], []

        def line_copy(step):
            origin = z - (step - 1)
            src = own if step == 1 else block(origin, 0, 0)
            return net.remote((id(self), step), src, block(origin, 0, 0), net.device(z=z + 1))

        def start(step):
            copy, fits = line_copy(step), (z - (step - 1) >= 0) & (z + 1 < nz)
            pl.when(fits)(copy.start)
            sent.append((copy, fits))

        start(1)
        keep = net.copy(face, out.at[:, pl.ds(pl.multiple_of(z * rows, rows), rows), :])
        keep.start()
        later = []
        for step in range(1, nz):
            yield
            fits = z - step >= 0
            pl.when(fits)(line_copy(step).wait_recv)
            if step < nz - 1:
                start(step + 1)
            here = block(z - step, 0, 0)
            across = net.remote((id(self), "x", step), here, here, net.device(1, 0))
            beside = net.remote((id(self), "c", step), here, here, net.device(0, 0, 1))
            for copy in (across, beside):
                pl.when(fits)(copy.start)
                sent.append((copy, fits))
            later.append((step, fits, across))
            shared.append((beside, fits))
        for step, fits, across in later:
            yield
            pl.when(fits)(across.wait_recv)
            there = block(z - step, 1, 0)
            beside = net.remote((id(self), "xc", step), there, there, net.device(0, 0, 1))
            pl.when(fits)(beside.start)
            sent.append((beside, fits))
            shared.append((beside, fits))
        yield
        for copy, fits in shared:
            pl.when(fits)(copy.wait_recv)
        keep.wait()
        yield READY
        for copy, fits in sent:
            pl.when(fits)(copy.wait_send)


class WholeScatter(FaceScatter):
    moves = ("x", "y", "c", "z")

    def __init__(self, part, nz, ny, resident=False):
        m, _, rows, d = part.shape
        merged = jax.ShapeDtypeStruct((m * nz, rows, d), part.dtype) if resident else part.reshape(m * nz, rows, d)
        super().__init__(merged, nz, ny, resident)
        t = rows // (4 * ny)
        self.m, self.nz = m, nz
        self.outs = [(jax.ShapeDtypeStruct((m, t, d), F32), pl.BlockSpec(memory_space=pltpu.VMEM))]
        self.scratch = self.scratch + [pltpu.VMEM((m * nz, t, d), BF16), pltpu.VMEM((nz, m, t, d), BF16)]
        self.remotes = self.remotes + nz * m
        self.locals = self.locals + m

    def run(self, net, ins, outs, scratch):
        face, inbox = scratch[-2:]
        yield from super().run(net, ins, [face], scratch[:-2])
        nz, m = self.nz, self.m
        copies = []
        for far in range(1, nz):
            line = lax.rem(net.z + far, nz)
            for at in range(m):
                copies.append(
                    pltpu.make_async_remote_copy(
                        src_ref=face.at[at * nz + line],
                        dst_ref=inbox.at[far, at],
                        send_sem=net.send.at[net.slot((id(self), "z", far, at))],
                        recv_sem=net.recv.at[net.slot((id(self), "z", far, at))],
                        device_id=net.device(z=line),
                        device_id_type=MESH,
                    )
                )
                copies[-1].start()
        own = []
        for at in range(m):
            own.append(net.copy(face.at[at * nz + net.z], inbox.at[0, at]))
            own[-1].start()
        yield
        for copy in own:
            copy.wait()
        for copy in copies:
            copy.wait()
        add_rows(outs[0], [inbox.at[far] for far in range(nz)])


class QuickScatter:
    moves = ("c", "same", "z")

    def __init__(self, part, nz, ny):
        _, rows, d = part.shape
        t = rows // (4 * ny)
        self.ins, self.t = [part], t
        self.outs = [(jax.ShapeDtypeStruct((t, d), F32), pl.BlockSpec(memory_space=pltpu.VMEM))]
        self.scratch = [
            pltpu.VMEM((2 * ny, nz, t, d), BF16),
            pltpu.VMEM((2 * ny, nz, t, d), BF16),
            pltpu.VMEM((2 * ny, nz, t, d), BF16),
            pltpu.VMEM((nz, t, d), BF16),
            pltpu.VMEM((nz, 1, t, d), BF16),
        ]
        self.remotes, self.locals = 4 * ny + nz, 2 * ny + 1

    def run(self, net, ins, outs, scratch):
        (part,), (out,), t = ins, outs, self.t
        work, from_core, inbox, face, line_in = scratch
        ny, nz = net.ny, net.nz
        order = [(dx, dy) for dx in (1, 0) for dy in reversed(range(ny))]
        cores, loads, copies = {}, {}, {}

        def rows(dx, dy, dc):
            return part.at[:, pl.ds(pl.multiple_of(net.rank(dx, dy, dc) * t, t), t), :]

        for dx, dy in order:
            at = dx * ny + dy
            loads[at] = net.copy(rows(dx, dy, 0), work.at[at])
            loads[at].start()
            cores[at] = net.remote((id(self), "c", at), rows(dx, dy, 1), from_core.at[at], net.device(0, 0, 1))
            cores[at].start()
        for dx, dy in order:
            at = dx * ny + dy
            yield
            loads[at].wait()
            cores[at].wait_recv()
            add_rows(work.at[at], [work.at[at], from_core.at[at]])
            if at:
                copies[at] = net.remote((id(self), at), work.at[at], inbox.at[at], net.device(dx, dy))
                copies[at].start()
        yield
        for copy in copies.values():
            copy.wait_recv()
        add_rows(face, [work.at[0]] + [inbox.at[at] for at in copies])
        lines = []
        for far in range(1, nz):
            line = lax.rem(net.z + far, nz)
            lines.append(
                net.remote((id(self), "z", far), face.at[pl.ds(line, 1)], line_in.at[far], net.device(z=line))
            )
            lines[-1].start()
        own = net.copy(face.at[pl.ds(net.z, 1)], line_in.at[0])
        own.start()
        yield
        own.wait()
        for copy in lines:
            copy.wait_recv()
        add_rows(_lead(out), [line_in.at[far] for far in range(nz)])
        for copy in list(cores.values()) + list(copies.values()) + lines:
            copy.wait_send()


class PlaneGather:
    moves = ("plane",)
    in_spec = IN_VMEM

    def __init__(self, own, nz, ny):
        self.ins = [own]
        self.outs = [(jax.ShapeDtypeStruct((2 * nz,) + own.shape, own.dtype), ANY)]
        self.scratch = []
        self.remotes, self.locals = 2 * nz, 1

    def run(self, net, ins, outs, scratch):
        (own,), (out,) = ins, outs
        here = out.at[net.z * 2 + net.x]
        copies = []
        for far in range(net.nz):
            for dx in (0, 1):
                if far or dx:
                    line = lax.rem(net.z + far, net.nz)
                    copies.append(net.remote((id(self), far, dx), own, here, net.device(dx, z=line)))
                    copies[-1].start()
        keep = net.copy(own, here)
        keep.start()
        yield
        for copy in copies:
            copy.wait()
        keep.wait()


class SmallScatter:
    moves = ("face", "z")

    def __init__(self, part, nz, ny):
        ranks, _, rows, width = part.shape
        self.ins = [part]
        vmem = pl.BlockSpec(memory_space=pltpu.VMEM)
        self.outs = [(jax.ShapeDtypeStruct((rows, width), F32), vmem)]
        self.scratch = [
            pltpu.VMEM((ranks, nz, rows, width), F32),
            pltpu.VMEM((nz, rows, width), F32),
            pltpu.VMEM((nz, rows, width), F32),
        ]
        self.remotes, self.locals = ranks + nz, 2

    def run(self, net, ins, outs, scratch):
        (part,), (out,) = ins, outs
        inbox, total, line_in = scratch
        ny, nz = net.ny, net.nz
        copies = []
        for dx in (0, 1):
            for dy in range(ny):
                for dc in (0, 1):
                    if dx or dy or dc:
                        at = (dx * ny + dy) * 2 + dc
                        copies.append(
                            net.remote(
                                (id(self), at), part.at[net.rank(dx, dy, dc)], inbox.at[at], net.device(dx, dy, dc)
                            )
                        )
                        copies[-1].start()
        keep = net.copy(part.at[net.rank()], inbox.at[0])
        keep.start()
        yield
        keep.wait()
        for copy in copies:
            copy.wait()
        total[...] = jnp.sum(inbox[...], axis=0)
        lines = []
        for far in range(1, nz):
            line = lax.rem(net.z + far, nz)
            lines.append(net.remote((id(self), "z", far), total.at[line], line_in.at[far], net.device(z=line)))
            lines[-1].start()
        own = net.copy(total.at[net.z], line_in.at[0])
        own.start()
        yield
        own.wait()
        for copy in lines:
            copy.wait()
        out[...] = jnp.sum(line_in[...], axis=0)


def launch(body, ins, in_specs, outs, scratch, plans, nz, ny, collective_id, name, extra_locals=0, vmem=56):
    moves = set()
    for plan in plans:
        moves |= set(plan.moves)
    remotes = sum(plan.remotes for plan in plans)
    locals_ = max(1, extra_locals + sum(plan.locals for plan in plans))

    def kernel(*refs):
        in_refs, refs = refs[: len(ins)], refs[len(ins) :]
        out_refs, refs = refs[: len(outs)], refs[len(outs) :]
        scratch_refs, (send, recv, local) = refs[: len(scratch)], refs[len(scratch) :]
        net = Net(nz, ny, send, recv, local)
        peers = {}
        for far in range(nz):
            for dx in (0, 1):
                for dy in range(ny):
                    for dc in (0, 1):
                        kinds = set()
                        if not far:
                            kinds.add("face")
                            if dx and not dy and not dc:
                                kinds.add("x")
                            if dy and not dx and not dc:
                                kinds.add("y")
                            if dc and not dx and not dy:
                                kinds.add("c")
                            if not dc:
                                kinds.add("same")
                        if far and not dx and not dy and not dc:
                            kinds.add("z")
                            if far in (1, nz - 1):
                                kinds.add("line")
                        if not dy and not dc:
                            kinds.add("plane")
                        if (far or dx or dy or dc) and kinds & moves:
                            line = lax.rem(net.z + far, nz) if far else None
                            peers[far, dx, dy, dc] = net.device(dx, dy, dc, line)
        barrier = pltpu.get_barrier_semaphore()
        for device in peers.values():
            pl.semaphore_signal(barrier, inc=1, device_id=device, device_id_type=MESH)
        pl.semaphore_wait(barrier, len(peers))
        body(net, in_refs, out_refs, scratch_refs)

    return list(
        pl.pallas_call(
            kernel,
            out_shape=[shape for shape, _ in outs],
            in_specs=in_specs,
            out_specs=[spec for _, spec in outs],
            scratch_shapes=list(scratch)
            + [
                pltpu.SemaphoreType.DMA((remotes,)),
                pltpu.SemaphoreType.DMA((remotes,)),
                pltpu.SemaphoreType.DMA((locals_,)),
            ],
            compiler_params=pltpu.CompilerParams(
                collective_id=collective_id, has_side_effects=True, vmem_limit_bytes=vmem << 20
            ),
            name=name,
        )(*ins)
    )


def exchange(plans, nz, ny, collective_id, name, order=()):
    ins = [array for plan in plans for array in plan.ins]
    outs = [out for plan in plans for out in plan.outs]
    scratch = [entry for plan in plans for entry in plan.scratch]

    def body(net, in_refs, out_refs, scratch_refs):
        running = []
        for plan in plans:
            mine = []
            for refs_of, count in ((in_refs, plan.ins), (out_refs, plan.outs), (scratch_refs, plan.scratch)):
                mine.append(list(refs_of[: len(count)]))
            in_refs = in_refs[len(plan.ins) :]
            out_refs = out_refs[len(plan.outs) :]
            scratch_refs = scratch_refs[len(plan.scratch) :]
            running.append(plan.run(net, *mine))
        for at in order:
            next(running[at], None)
        while running:
            for steps in list(running):
                try:
                    next(steps)
                except StopIteration:
                    running.remove(steps)

    specs = [getattr(plan, "in_spec", ANY) for plan in plans for _ in plan.ins]
    results = launch(body, ins, specs, outs, scratch, plans, nz, ny, collective_id, name)
    grouped = []
    for plan in plans:
        grouped.append(results[: len(plan.outs)])
        results = results[len(plan.outs) :]
    return grouped


class Weave:
    def __init__(self):
        self.plans, self.ready = {}, set()

    def add(self, name, steps):
        self.plans[name] = steps

    def step(self, name):
        steps = self.plans.get(name)
        if steps is not None:
            state = next(steps, self)
            if state is self:
                del self.plans[name]
            elif state == READY:
                self.ready.add(name)

    def need(self, name):
        while name in self.plans and name not in self.ready:
            self.step(name)

    def finish(self, name):
        while name in self.plans:
            self.step(name)


def loop(count, body):
    def step(at, carry):
        body(at)
        return carry

    lax.fori_loop(0, count, step, 0)


def mlp_block(mixed, wo, inputs, cotangent, cot_face, norms, wexp_first, w_expand, w_reduce, nz, ny, collective_id):
    micro_count, own_rows, width = inputs.shape
    face_rows = cot_face.shape[1]
    tokens = micro_count * face_rows
    attn = mixed.shape[1]
    units = w_expand[0].shape[1] // 2
    half = units // 2
    tile = min(512, half)
    wide = 512
    part = jax.ShapeDtypeStruct((micro_count, face_rows, width), BF16)
    part_red = jax.ShapeDtypeStruct((units, width), BF16)
    own = (micro_count, own_rows, width)
    scatter_a, scatter_b = (FaceScatter(part, nz, ny, resident=True) for _ in range(2))
    gather = FaceGather(jax.ShapeDtypeStruct(own, BF16), nz, ny)
    line_e = LineGather(w_expand[:1], ["row"], nz, ny, share=(1, 2), given=w_expand[1:])
    line_r = LineGather(w_reduce[:1], ["col"], nz, ny, given=w_reduce[1:])
    line_s = LineScatter([part_red], ["col"], nz, ny, resident=True)
    plans = [scatter_a, scatter_b, gather, line_e, line_r, line_s]
    vmem = pl.BlockSpec(memory_space=pltpu.VMEM)
    outs = [
        (jax.ShapeDtypeStruct(own, F32), ANY),
        (jax.ShapeDtypeStruct(own, F32), ANY),
        (jax.ShapeDtypeStruct(own, BF16), ANY),
        (jax.ShapeDtypeStruct((2, 16, width), F32), vmem),
        (jax.ShapeDtypeStruct((width, half), BF16), ANY),
        (jax.ShapeDtypeStruct((width, half), BF16), ANY),
        (part, ANY),
    ] + line_s.outs
    scratch = [
        pltpu.VMEM((micro_count, face_rows, width), BF16),
        pltpu.VMEM(own, F32),
        pltpu.VMEM(own, F32),
        pltpu.VMEM(own, BF16),
        pltpu.VMEM(own, BF16),
        pltpu.VMEM(own, BF16),
        pltpu.VMEM((micro_count, face_rows, width), BF16),
        pltpu.VMEM((micro_count, face_rows, width), BF16),
        pltpu.VMEM((width, half), BF16),
        pltpu.VMEM((width, half), BF16),
        pltpu.VMEM((units, width), BF16),
        pltpu.VMEM((tokens, units), BF16),
        pltpu.VMEM((tokens, units), BF16),
        pltpu.VMEM((units, width), BF16),
        pltpu.VMEM((tokens, attn), BF16),
        pltpu.VMEM((attn, width), BF16),
    ]
    shared = len(scratch)
    scratch += scatter_a.scratch + line_s.scratch

    def body(net, ins, outs, scratch):
        mixed_in, wo_in, own_in, cot_in, face_in, norms, first_in, *weights_in = ins
        middle_out, grad_out, low_out, norm_out, expand_a, expand_b, reduced_out, reduce_out = outs
        p, branch, middle, own, cot_own, n_own, n_face, cot, we0, we1, wr, active, slope, pr, mixed, wo = scratch[:shared]
        we = (we0, we1)
        slots = list(scratch[shared : shared + len(scatter_a.scratch)])
        line_slots = list(scratch[shared + len(scatter_a.scratch) :])

        loads = [
            net.copy(*pair)
            for pair in (
                (mixed_in, mixed),
                (wo_in, wo),
                (own_in, own),
                (cot_in, cot_own),
                (first_in, we0),
                (face_in, cot),
            )
        ]
        weave = Weave()
        stores = []
        weave.add("e", line_e.run(net, weights_in[:2], [we1], []))
        weave.step("e")
        weave.add("r", line_r.run(net, weights_in[2:], [wr], []))
        weave.step("r")
        for load in loads:
            load.start()

        def branch_tile(at):
            m, n = lax.div(at, width // wide), lax.rem(at, width // wide)
            columns = pl.ds(pl.multiple_of(n * wide, wide), wide)
            rows = pl.ds(pl.multiple_of(m * face_rows, face_rows), face_rows)
            p[m, :, columns] = jnp.dot(mixed[rows, :], wo[:, columns], preferred_element_type=F32).astype(BF16)

        row_steps = own_rows // 16

        def own_rows_at(at):
            return lax.div(at, row_steps), pl.ds(pl.multiple_of(lax.rem(at, row_steps) * 16, 16), 16)

        def norm_rows(at):
            m, rows = own_rows_at(at)
            values = own[m, rows, :].astype(F32) + branch[m, rows, :]
            middle[m, rows, :] = values
            centered = values - jnp.mean(values, axis=-1, keepdims=True)
            spread = lax.rsqrt(jnp.mean(centered * centered, axis=-1, keepdims=True) + EPSILON)
            n_own[m, rows, :] = (centered * spread * norms[0:1, :] + norms[1:2, :]).astype(BF16)

        def hidden_tile(h):
            def tile_at(at):
                m, n = lax.div(at, half // tile), lax.rem(at, half // tile)
                rows = pl.ds(pl.multiple_of(m * face_rows, face_rows), face_rows)
                columns = pl.ds(pl.multiple_of(n * tile, tile), tile)
                into = pl.ds(pl.multiple_of(h * half + n * tile, tile), tile)
                hidden = jnp.dot(n_face[m], we[h][:, columns], preferred_element_type=F32)
                square = hidden * hidden
                bend = jnp.tanh(GELU_A * hidden * (1.0 + GELU_B * square))
                active[rows, into] = (0.5 * hidden * (1.0 + bend)).astype(BF16)
                slope[rows, into] = (
                    0.5 * (1.0 + bend)
                    + (0.5 * GELU_A) * hidden * (1.0 - bend * bend) * (1.0 + (3.0 * GELU_B) * square)
                ).astype(BF16)

            return tile_at

        across = (((0,), (0,)), ((), ()))
        along = (((1,), (1,)), ((), ()))
        def reduce_tile(first):
            def tile_at(at):
                f, n = lax.div(at, width // wide), lax.rem(at, width // wide)
                columns = pl.ds(pl.multiple_of(n * wide, wide), wide)
                rows = pl.ds(pl.multiple_of(first + f * tile, tile), tile)
                pr[rows, columns] = lax.dot_general(
                    active[:, rows],
                    cot[:, :, columns].reshape(tokens, wide),
                    across,
                    preferred_element_type=F32,
                ).astype(BF16)

            return tile_at

        def slope_tile(at):
            m, n = lax.div(at, units // tile), lax.rem(at, units // tile)
            rows = pl.ds(pl.multiple_of(m * face_rows, face_rows), face_rows)
            columns = pl.ds(pl.multiple_of(n * tile, tile), tile)
            grad = lax.dot_general(cot[m], wr[columns, :], along, preferred_element_type=F32)
            slope[rows, columns] = (grad * slope[rows, columns].astype(F32)).astype(BF16)

        def normed_tile(at):
            m, n = lax.div(at, width // wide), lax.rem(at, width // wide)
            rows = pl.ds(pl.multiple_of(m * face_rows, face_rows), face_rows)
            columns = pl.ds(pl.multiple_of(n * wide, wide), wide)
            grad = lax.dot_general(slope[rows, :half], we0[columns, :], along, preferred_element_type=F32)
            grad = grad + lax.dot_general(slope[rows, half:], we1[columns, :], along, preferred_element_type=F32)
            p[m, :, columns] = grad.astype(BF16)

        def reduced_tiles(m):
            def tile_at(n):
                rows = pl.ds(m * face_rows, face_rows)
                columns = pl.ds(pl.multiple_of(n * wide, wide), wide)
                cot[m, :, columns] = jnp.dot(active[rows, :], wr[:, columns], preferred_element_type=F32).astype(BF16)

            def act():
                loop(width // wide, tile_at)
                stores.append(net.copy(cot.at[m], reduced_out.at[m]))
                stores[-1].start()

            return act

        def expand_tiles(h):
            def tile_at(at):
                k, n = lax.div(at, half // tile), lax.rem(at, half // tile)
                rows = pl.ds(pl.multiple_of(k * wide, wide), wide)
                columns = pl.ds(pl.multiple_of(n * tile, tile), tile)
                grads = pl.ds(pl.multiple_of(h * half + n * tile, tile), tile)
                we[h][rows, columns] = lax.dot_general(
                    n_face[:, :, rows].reshape(tokens, wide),
                    slope[:, grads],
                    across,
                    preferred_element_type=F32,
                ).astype(BF16)

            def act():
                loop((width // wide) * (half // tile), tile_at)
                stores.append(net.copy(we[h], (expand_a, expand_b)[h]))
                stores[-1].start()

            return act

        def back_rows(at):
            m, rows = own_rows_at(at)
            values = middle[m, rows, :]
            centered = values - jnp.mean(values, axis=-1, keepdims=True)
            spread = lax.rsqrt(jnp.mean(centered * centered, axis=-1, keepdims=True) + EPSILON)
            unit = centered * spread
            grad = branch[m, rows, :]
            norm_out[0] += grad * unit
            norm_out[1] += grad
            turned = grad * norms[0:1, :]
            inner = jnp.mean(turned * unit, axis=-1, keepdims=True)
            total = cot_own[m, rows, :].astype(F32) + spread * (
                turned - jnp.mean(turned, axis=-1, keepdims=True) - unit * inner
            )
            middle[m, rows, :] = total
            n_own[m, rows, :] = total.astype(BF16)

        def later():
            weave.finish("e")
            for h in (0, 1):
                expand_tiles(h)()
                yield
            for m in range(micro_count):
                reduced_tiles(m)()
                yield

        def main():
            loads[0].wait()
            loads[1].wait()
            loop(micro_count * (width // wide), branch_tile)
            yield
            yield from scatter_a.run(net, [p], [branch], slots)
            loads[2].wait()
            loop(micro_count * row_steps, norm_rows)
            keep_middle = net.copy(middle, middle_out)
            keep_middle.start()
            yield from gather.run(net, [n_own], [n_face], [])
            loads[4].wait()
            loop(micro_count * (half // tile), hidden_tile(0))
            yield
            weave.need("e")
            loop(micro_count * (half // tile), hidden_tile(1))
            yield
            loads[5].wait()
            loop((half // tile) * (width // wide), reduce_tile(0))
            yield
            loop((half // tile) * (width // wide), reduce_tile(half))
            weave.add("s", line_s.run(net, [pr], [reduce_out], line_slots))
            weave.step("s")
            yield
            weave.need("r")
            loop(micro_count * (units // tile), slope_tile)
            yield
            loop(micro_count * (width // wide), normed_tile)
            weave.add("x", later())
            yield from scatter_b.run(net, [p], [branch], slots)
            loads[3].wait()
            keep_middle.wait()
            norm_out[...] = jnp.zeros_like(norm_out)
            loop(micro_count * row_steps, back_rows)
            for pair in ((middle, grad_out), (n_own, low_out)):
                stores.append(net.copy(*pair))
                stores[-1].start()

        weave.add("m", main())
        for name in "".join(MLP_ORDER):
            weave.step(name)
        for name in "mxsre":
            weave.finish(name)
        for store in stores:
            store.wait()

    ins = [mixed, wo, inputs, cotangent, cot_face, norms, wexp_first, *w_expand, *w_reduce]
    specs = [ANY] * 5 + [vmem] + [ANY] * (len(ins) - 6)
    return launch(
        body, ins, specs, outs, scratch, plans, nz, ny, collective_id, "mlp_block", extra_locals=12, vmem=62
    )


def front_block(inputs, cotangent, w_query, w_attn_out, w_keyval, w_expand, norms, limits, nz, ny, collective_id, head_dim):
    micro_count, own_rows, width = inputs.shape
    face_rows = own_rows * 4 * ny
    attn = w_query.shape[1] // 2
    seq_len = nz * face_rows
    blocks = face_rows // BLOCK
    heads = attn // head_dim
    tall = heads * BLOCK
    own = jax.ShapeDtypeStruct(inputs.shape, BF16)
    keys_face = jax.ShapeDtypeStruct((micro_count, face_rows, 2 * head_dim), BF16)
    plane = PlaneGather(norms, nz, ny)
    gather = FaceGather(own, nz, ny)
    gather_c = FaceGather(cotangent, nz, ny, hold_x=True)
    swap_e = HalfSwap([w_expand], ["row"], nz, ny)
    line_a = LineGather([w_keyval, w_query], ["both", "row"], nz, ny)
    line_o = LineGather([w_attn_out], ["col"], nz, ny)
    given = jax.ShapeDtypeStruct((w_expand.shape[0], w_expand.shape[1] // 2), BF16)
    line_e = LineGather([w_expand], ["row"], nz, ny, share=(0, 2), given=[given])
    keys = KeysGather(keys_face, nz, ny)
    plans = [plane, gather, gather_c, swap_e, line_a, line_o, line_e, keys]
    kept = [
        jax.ShapeDtypeStruct((micro_count, face_rows, width), BF16),
        line_a.outs[0][0],
        line_a.outs[1][0],
        given,
        jax.ShapeDtypeStruct((micro_count, face_rows, attn), BF16),
        keys.outs[0][0],
        jax.ShapeDtypeStruct((micro_count, face_rows, attn), BF16),
        jax.ShapeDtypeStruct((micro_count, blocks, 1, tall), F32),
    ]
    outs = [(shape, ANY) for shape in kept] + [
        (plane.outs[0][0], IN_VMEM),
        gather_c.outs[0],
        line_o.outs[0],
        line_e.outs[0],
    ]
    scratch = [pltpu.VMEM(shape.shape, shape.dtype) for shape in kept] + [
        pltpu.VMEM(inputs.shape, BF16),
        pltpu.VMEM(keys_face.shape, BF16),
    ]

    def body(net, ins, outs, scratch):
        inputs, cotangent, w_query, w_attn_out, w_keyval, w_expand, norms, limits = ins
        norms_out, cot_out, wo_out, first_out = outs[len(kept) :]
        normed, wkv, wq, given, queries, keys_vals, mixed, logs, n_own, keys_face = scratch
        stores = [net.copy(*pair) for pair in zip(scratch, outs[: len(kept)])]
        weave = Weave()
        weave.add("p", plane.run(net, [norms], [norms_out], []))
        weave.step("p")
        weave.add("a", line_a.run(net, [w_keyval, w_query], [wkv, wq], []))
        weave.step("a")
        weave.add("h", swap_e.run(net, [w_expand], [given], []))
        weave.add("o", line_o.run(net, [w_attn_out], [wo_out], []))
        weave.add("c", gather_c.run(net, [cotangent], [cot_out], []))

        def line_first():
            weave.need("h")
            yield from line_e.run(net, [w_expand, given], [first_out], [])

        weave.add("e", line_first())
        along = (((1,), (1,)), ((), ()))
        across = (((0,), (0,)), ((), ()))
        step = min(32, own_rows)

        def own_norm(at):
            m = lax.div(at, own_rows // step)
            rows = pl.ds(pl.multiple_of(lax.rem(at, own_rows // step) * step, step), step)
            gain, shift = (
                jnp.concatenate([norms_out[d].astype(F32)[k : k + 1] for d in range(2 * nz)], axis=1) for k in (0, 1)
            )
            values = inputs[m, rows, :].astype(F32)
            centered = values - jnp.mean(values, axis=-1, keepdims=True)
            spread = lax.rsqrt(jnp.mean(centered * centered, axis=-1, keepdims=True) + EPSILON)
            n_own[m, rows, :] = (centered * spread * gain + shift).astype(BF16)

        def keys_tile(m):
            keys_face[m] = jnp.dot(normed[m], wkv[...], preferred_element_type=F32).astype(BF16)

        def queries_tile(m):
            queries[m] = jnp.dot(normed[m], wq[...], preferred_element_type=F32).astype(BF16)

        def mixed_tile(m):
            def tile_at(b):
                rows = pl.ds(pl.multiple_of(b * BLOCK, BLOCK), BLOCK)
                query = jnp.concatenate(
                    [queries[m, rows, h * head_dim : (h + 1) * head_dim] for h in range(heads)], axis=0
                )
                starts = jnp.concatenate([limits[m, b, 0:1, :]] * heads, axis=1)
                ends = jnp.concatenate([limits[m, b, 1:2, :]] * heads, axis=1)
                place = lax.broadcasted_iota(jnp.int32, (BLOCK, tall), 0)

                def body(block, carry):
                    top, total, out = carry
                    first = pl.multiple_of(block * BLOCK, BLOCK)
                    keys = keys_vals[m, pl.ds(first, BLOCK), :head_dim]
                    values = keys_vals[m, pl.ds(first, BLOCK), head_dim:]
                    raw = lax.dot_general(keys, query, along, preferred_element_type=F32)
                    allowed = (place >= starts - first) & (place < ends - first)
                    scores = jnp.where(allowed, raw * (LOG2_E / math.sqrt(head_dim)), NEG_FILL)
                    new_top = jnp.maximum(top, jnp.max(scores, axis=0, keepdims=True))
                    weights = jnp.exp2(scores - new_top)
                    fade = jnp.exp2(top - new_top)
                    total = total * fade + jnp.sum(weights, axis=0, keepdims=True)
                    out = out * fade + lax.dot_general(
                        values, weights.astype(BF16), across, preferred_element_type=F32
                    )
                    return new_top, total, out

                top, total, out = lax.fori_loop(
                    0,
                    net.z * blocks + b + 1,
                    body,
                    (
                        jnp.full((1, tall), NEG_FILL, F32),
                        jnp.zeros((1, tall), F32),
                        jnp.zeros((head_dim, tall), F32),
                    ),
                )
                out = jnp.transpose(out / total).astype(BF16)
                for h in range(heads):
                    mixed[m, rows, h * head_dim : (h + 1) * head_dim] = out[h * BLOCK : (h + 1) * BLOCK]
                logs[m, b] = top + jnp.log2(total)

            return tile_at

        def main():
            weave.finish("p")
            loop(micro_count * (own_rows // step), own_norm)
            yield from gather.run(net, [n_own], [normed], [])
            stores[0].start()
            yield
            weave.need("a")
            loop(micro_count, keys_tile)
            weave.add("k", keys.run(net, [keys_face], [keys_vals], []))
            weave.step("k")
            yield
            for at in (1, 2):
                stores[at].start()
            loop(micro_count, queries_tile)
            stores[4].start()
            yield
            weave.need("k")
            stores[5].start()
            for m in range(micro_count):
                loop(blocks, mixed_tile(m))
                yield
            for at in (6, 7):
                stores[at].start()

        weave.add("m", main())
        for name in "".join(FRONT_ORDER):
            weave.step(name)
        for name in "mhcoeak":
            weave.finish(name)
        stores[3].start()
        for store in stores:
            store.wait()

    ins = [inputs, cotangent, w_query, w_attn_out, w_keyval, w_expand, norms, limits]
    return launch(
        body, ins, [IN_VMEM] * len(ins), outs, scratch, plans, nz, ny, collective_id, "front_block", extra_locals=len(kept)
    )


def back_block(low, reduced, parts, mixed, wo, wq, normed, queries, keys_vals, logs, limits, nz, ny, collective_id, head_dim):
    micro_count, own_rows, width = low.shape
    face_rows, attn = queries.shape[1:]
    seq_len = keys_vals.shape[1]
    tokens = micro_count * face_rows
    blocks = face_rows // BLOCK
    heads = attn // head_dim
    tall = heads * BLOCK
    scale = 1.0 / math.sqrt(head_dim)
    wide = 512
    half = parts[0].shape[1]
    part = jax.ShapeDtypeStruct((micro_count, face_rows, width), BF16)
    gather = FaceGather(low, nz, ny)
    scatter_r = FaceScatter(reduced, nz, ny)
    scatter_q = FaceScatter(part, nz, ny, resident=True)
    whole = WholeScatter(jax.ShapeDtypeStruct((micro_count, nz, face_rows, 2 * head_dim), BF16), nz, ny, resident=True)
    line_e = LineScatter(parts, ["row", "row"], nz, ny, resident=True)
    attn_parts = [jax.ShapeDtypeStruct((attn, width), BF16), jax.ShapeDtypeStruct((width, attn), BF16)]
    line_a = LineScatter(attn_parts, ["col", "row"], nz, ny, resident=True)
    plans = [gather, scatter_r, scatter_q, whole, line_e, line_a]
    groups = [scatter_r, scatter_q, whole, line_e, line_a]
    outs = scatter_r.outs + scatter_q.outs + whole.outs + line_e.outs + line_a.outs
    normed = normed.reshape(micro_count, face_rows, width)
    given = [mixed, wo, wq, queries, keys_vals, logs, limits, *parts]
    scratch = [pltpu.VMEM(entry.shape, entry.dtype) for entry in given] + [
        pltpu.VMEM(part.shape, BF16),
        pltpu.VMEM(queries.shape, BF16),
        pltpu.VMEM(queries.shape, BF16),
        pltpu.VMEM((seq_len, 2 * head_dim), F32),
        pltpu.VMEM((micro_count * nz, face_rows, 2 * head_dim), BF16),
        pltpu.VMEM((attn, width), BF16),
        pltpu.VMEM((width, attn), BF16),
        pltpu.VMEM((2, micro_count, face_rows, wide), BF16),
    ]
    shared = len(scratch)
    for plan in groups:
        scratch = scratch + plan.scratch

    def body(net, ins, outs, scratch):
        low, reduced_in, normed_in, *given_in = ins
        reduced_out, from_out, keys_out, *line_outs = outs
        mixed, wo, wq, queries, keys_vals, logs, limits, *expand = scratch[: len(given)]
        face, grad_mixed, grad_queries, acc, grad_keys, part_out, part_query, normed = scratch[len(given) : shared]
        slots, first = {}, shared
        for name, plan in zip("rqwea", groups):
            slots[name] = list(scratch[first : first + len(plan.scratch)])
            first += len(plan.scratch)
        loads = [net.copy(*pair) for pair in zip(given_in, scratch)]
        order = [len(given) - 2, len(given) - 1] + list(range(len(given) - 2))
        weave = Weave()
        along = (((1,), (1,)), ((), ()))
        across = (((0,), (0,)), ((), ()))

        def mix_tile(m):
            grad_mixed[m] = lax.dot_general(face[m], wo[...], along, preferred_element_type=F32).astype(BF16)

        def attn_out_tile(n):
            columns = pl.ds(pl.multiple_of(n * wide, wide), wide)
            part_out[:, columns] = lax.dot_general(
                mixed[...].reshape(tokens, attn),
                face[:, :, columns].reshape(tokens, wide),
                across,
                preferred_element_type=F32,
            ).astype(BF16)

        def attn_tile(m):
            def tile_at(b):
                rows = pl.ds(pl.multiple_of(b * BLOCK, BLOCK), BLOCK)

                def stack(ref):
                    return jnp.concatenate(
                        [ref[m, rows, h * head_dim : (h + 1) * head_dim] for h in range(heads)], axis=0
                    )

                query, grad = stack(queries), stack(grad_mixed)
                products = grad.astype(F32) * stack(mixed).astype(F32)
                delta = jnp.sum(jnp.transpose(products), axis=0, keepdims=True)
                starts = jnp.concatenate([limits[m, b, 0:1, :]] * heads, axis=1)
                ends = jnp.concatenate([limits[m, b, 1:2, :]] * heads, axis=1)
                log_total = logs[m, b]
                place = lax.broadcasted_iota(jnp.int32, (BLOCK, tall), 0)

                def body(block, grad_query):
                    first = pl.multiple_of(block * BLOCK, BLOCK)
                    keys = keys_vals[m, pl.ds(first, BLOCK), :head_dim]
                    values = keys_vals[m, pl.ds(first, BLOCK), head_dim:]
                    raw = lax.dot_general(keys, query, along, preferred_element_type=F32)
                    allowed = (place >= starts - first) & (place < ends - first)
                    probs = jnp.where(allowed, jnp.exp2(raw * (LOG2_E * scale) - log_total), 0.0)
                    grad_probs = lax.dot_general(values, grad, along, preferred_element_type=F32)
                    grad_scores = (probs * (grad_probs - delta)).astype(BF16)
                    acc[pl.ds(first, BLOCK), :head_dim] += (
                        jnp.dot(grad_scores, query, preferred_element_type=F32) * scale
                    )
                    acc[pl.ds(first, BLOCK), head_dim:] += jnp.dot(
                        probs.astype(BF16), grad, preferred_element_type=F32
                    )
                    return grad_query + lax.dot_general(keys, grad_scores, across, preferred_element_type=F32)

                grad_query = lax.fori_loop(
                    0, net.z * blocks + b + 1, body, jnp.zeros((head_dim, tall), F32)
                )
                grad_query = jnp.transpose(grad_query * scale).astype(BF16)
                for h in range(heads):
                    grad_queries[m, rows, h * head_dim : (h + 1) * head_dim] = grad_query[h * BLOCK : (h + 1) * BLOCK]

            return tile_at

        def from_tile(at):
            m, n = lax.div(at, width // wide), lax.rem(at, width // wide)
            columns = pl.ds(pl.multiple_of(n * wide, wide), wide)
            face[m, :, columns] = lax.dot_general(
                grad_queries[m], wq[columns, :], along, preferred_element_type=F32
            ).astype(BF16)

        columns_in = [
            net.copy(normed_in.at[:, :, pl.ds(n * wide, wide)], normed.at[n % 2]) for n in range(width // wide)
        ]

        def query_tile(n):
            columns_in[n].wait()

            def tile_at(_):
                part_query[n * wide : (n + 1) * wide, :] = lax.dot_general(
                    normed[n % 2].reshape(tokens, wide),
                    grad_queries[...].reshape(tokens, attn),
                    across,
                    preferred_element_type=F32,
                ).astype(BF16)

            loop(1, tile_at)
            if n + 2 < width // wide:
                columns_in[n + 2].start()

        def main():
            yield from gather.run(net, [low], [face], [])
            for at in order[2:]:
                loads[at].wait()
            loop(micro_count, mix_tile)
            yield
            for m in range(micro_count):
                acc[...] = jnp.zeros_like(acc)
                loop(blocks, attn_tile(m))
                for k in range(nz):
                    grad_keys[m * nz + k] = acc[k * face_rows : (k + 1) * face_rows, :].astype(BF16)
                yield
            loop(width // wide, attn_out_tile)
            weave.add("w", whole.run(net, [grad_keys], [keys_out], slots["w"]))
            weave.step("w")
            loop(micro_count * (width // wide), from_tile)
            weave.add("q", scatter_q.run(net, [face], [from_out], slots["q"]))
            weave.step("q")
            for n in range(width // wide):
                query_tile(n)
            weave.add("a", line_a.run(net, [part_out, part_query], line_outs[2:], slots["a"]))
            weave.step("a")

        weave.add("m", main())
        weave.step("m")
        for at in order:
            loads[at].start()
        for copy in columns_in[:2]:
            copy.start()
        for at in order[:2]:
            loads[at].wait()
        weave.add("e", line_e.run(net, expand, line_outs[:2], slots["e"]))
        weave.step("e")
        weave.add("r", scatter_r.run(net, [reduced_in], [reduced_out], slots["r"]))
        for name in "".join(BACK_ORDER):
            weave.step(name)
        for name in "mwqrea":
            weave.finish(name)

    ins = [low, reduced, normed, *given]
    specs = [IN_VMEM] + [ANY] * (len(ins) - 1)
    return launch(
        body, ins, specs, outs, scratch, plans, nz, ny, collective_id, "back_block", extra_locals=len(given) + width // wide, vmem=62
    )


def end_block(inputs, grad_middle, from_query, grad_keys, wkv, norms, grad_norm_two, nz, ny, collective_id):
    micro_count, own_rows, width = inputs.shape
    rows_all = micro_count * own_rows
    side = grad_keys.shape[-1]
    ranks = 4 * ny
    own_width = width // (nz * ranks)
    step = min(32, own_rows)
    part = jax.ShapeDtypeStruct((nz, width // nz, side), BF16)
    small = jax.ShapeDtypeStruct((ranks, nz, 8, 128), F32)
    quick, tiny = QuickScatter(part, nz, ny), SmallScatter(small, nz, ny)
    plans = [quick, tiny]
    outs = [(jax.ShapeDtypeStruct(inputs.shape, F32), IN_VMEM)] + quick.outs + tiny.outs
    scratch = [
        pltpu.VMEM((rows_all, width), BF16),
        pltpu.VMEM((rows_all, side), BF16),
        pltpu.VMEM(part.shape, BF16),
        pltpu.VMEM(small.shape, F32),
        pltpu.VMEM((2, step, width), F32),
    ] + quick.scratch + tiny.scratch

    def body(net, ins, outs, scratch):
        inputs, grad_middle, from_query, grad_keys, wkv, norms, grad_norm_two = ins
        grad_out, keyval_out, small_out = outs
        n_own, low_keys, part, small, sums, *slots = scratch
        weave = Weave()

        def place(at):
            m, first = lax.div(at, own_rows // step), lax.rem(at, own_rows // step) * step
            rows = pl.ds(pl.multiple_of(first, step), step)
            return m, rows, pl.ds(pl.multiple_of(at * step, step), step)

        def unit_rows(m, rows):
            values = inputs[m, rows, :].astype(F32)
            centered = values - jnp.mean(values, axis=-1, keepdims=True)
            spread = lax.rsqrt(jnp.mean(centered * centered, axis=-1, keepdims=True) + EPSILON)
            return centered * spread, spread

        def first_rows(at):
            m, rows, flat = place(at)
            unit, _ = unit_rows(m, rows)
            n_own[flat, :] = (unit * norms[0:1, :] + norms[1:2, :]).astype(BF16)
            low_keys[flat, :] = grad_keys[m, rows, :].astype(BF16)

        def keyval_tile(k):
            columns = pl.ds(pl.multiple_of(k * (width // nz), width // nz), width // nz)
            part[k] = lax.dot_general(
                n_own[:, columns], low_keys[...], (((0,), (0,)), ((), ())), preferred_element_type=F32
            ).astype(BF16)

        def last_rows(at):
            m, rows, flat = place(at)
            unit, spread = unit_rows(m, rows)
            grad = from_query[m, rows, :] + lax.dot_general(
                low_keys[flat, :], wkv[...], (((1,), (1,)), ((), ())), preferred_element_type=F32
            )
            sums[0] += grad * unit
            sums[1] += grad
            turned = grad * norms[0:1, :]
            inner = jnp.mean(turned * unit, axis=-1, keepdims=True)
            grad_out[m, rows, :] = grad_middle[m, rows, :] + spread * (
                turned - jnp.mean(turned, axis=-1, keepdims=True) - unit * inner
            )

        count = rows_all // step
        loop(count, first_rows)
        loop(nz, keyval_tile)
        weave.add("q", quick.run(net, [part], [keyval_out], slots[: len(quick.scratch)]))
        for _ in range(2 * ny + 1):
            weave.step("q")
        sums[...] = jnp.zeros_like(sums)
        loop(count, last_rows)
        rows = [jnp.sum(sums[k], axis=0, keepdims=True) for k in (0, 1)]
        rows += [jnp.sum(grad_norm_two[k], axis=0, keepdims=True) for k in (0, 1)]
        rows = jnp.concatenate(rows + [jnp.zeros((4, width), F32)], axis=0)
        for line in range(nz):
            for rank in range(ranks):
                first = (line * ranks + rank) * own_width // 128 * 128
                small[rank, line] = rows[:, first : first + 128]
        weave.add("s", tiny.run(net, [small], [small_out], slots[len(quick.scratch) :]))
        for name in "sqsqs":
            weave.step(name)
        for name in "qs":
            weave.finish(name)

    ins = [inputs, grad_middle, from_query, grad_keys, wkv, norms, grad_norm_two]
    return launch(body, ins, [IN_VMEM] * len(ins), outs, scratch, plans, nz, ny, collective_id, "end_block")


def local(
    inputs,
    cotangent,
    doc_ids,
    attn_gain,
    attn_shift,
    w_query,
    w_keyval,
    w_attn_out,
    mlp_gain,
    mlp_shift,
    w_expand,
    w_reduce,
):
    nz = lax.axis_size("dp") // 2
    tensor_count = lax.axis_size("tensor")
    ny = tensor_count // 2
    ranks = 2 * tensor_count
    micro_count, own_rows, width = inputs.shape
    face_rows = own_rows * ranks
    tokens = micro_count * face_rows
    seq_len = doc_ids.shape[1]
    head_dim = w_keyval.shape[1] // 2
    heads = w_query.shape[1] // (2 * head_dim)
    z = lax.axis_index("dp") // 2
    on = (nz, ny)

    norms = jnp.stack([attn_gain, attn_shift, mlp_gain, mlp_shift])
    norms = jnp.concatenate([norms, jnp.zeros((4, norms.shape[1]), BF16)])
    query_doc = lax.dynamic_slice_in_dim(doc_ids, z * face_rows, face_rows, axis=1)
    blocks = face_rows // BLOCK
    same = doc_ids[:, None, :]
    starts = jnp.sum((same < query_doc[:, :, None]).astype(jnp.int32), axis=-1)
    ends = jnp.sum((same <= query_doc[:, :, None]).astype(jnp.int32), axis=-1)
    limits = jnp.stack([starts, ends], axis=1).reshape(micro_count, 2, blocks, BLOCK).transpose(0, 2, 1, 3)
    normed, wkv, wq, expand_given, queries, keys_vals, mixed, log_total, norms, cot_face, wo, wexp_first = front_block(
        inputs,
        cotangent,
        w_query,
        w_attn_out,
        w_keyval,
        w_expand,
        norms,
        limits,
        *on,
        collective_id=1,
        head_dim=head_dim,
    )
    norms = norms[:, :4].transpose(1, 0, 2).reshape(4, width).astype(F32)
    mixed_flat = mixed.reshape(tokens, heads * head_dim)
    middle, grad_middle, low_middle, grad_norm_two, part_expand_a, part_expand_b, reduced, grad_reduce = mlp_block(
        mixed_flat, wo, inputs, cotangent, cot_face, norms[2:], wexp_first, (w_expand, expand_given), (w_reduce,), *on, collective_id=3
    )
    reduced, from_query, grad_keys, grad_expand_a, grad_expand_b, grad_attn_out, grad_query = back_block(
        low_middle,
        reduced,
        [part_expand_a, part_expand_b],
        mixed,
        wo,
        wq,
        normed,
        queries,
        keys_vals,
        log_total,
        limits,
        *on,
        collective_id=6,
        head_dim=head_dim,
    )
    outputs = (middle + reduced).astype(BF16)
    grad_inputs, grad_keyval, small = end_block(
        inputs, grad_middle, from_query, grad_keys, wkv, norms[:2], grad_norm_two, *on, collective_id=8
    )
    own_width = width // (nz * ranks)
    device = lax.axis_index("dp") * tensor_count + lax.axis_index("tensor")
    small = lax.dynamic_slice_in_dim(small[:4], device * own_width % 128, own_width, axis=1)

    def by_row(halves):
        return jnp.concatenate([halves[0], halves[1]], axis=1).astype(F32)

    def by_column(halves):
        return halves.reshape(-1, halves.shape[-1]).astype(F32)

    return (
        outputs,
        grad_inputs,
        small[0],
        small[1],
        by_row(grad_query),
        grad_keyval,
        by_column(grad_attn_out),
        small[2],
        small[3],
        by_row(jnp.concatenate([grad_expand_a, grad_expand_b], axis=2)),
        by_column(grad_reduce),
    )


def solution(mesh):
    placed = (
        P(None, ("dp", "tensor"), None),
        P(None, ("dp", "tensor"), None),
        P(),
        P("dp"),
        P("dp"),
        P("dp", "tensor"),
        P("dp", None),
        P("tensor", "dp"),
        P("dp"),
        P("dp"),
        P("dp", "tensor"),
        P("tensor", "dp"),
    )
    return jax.shard_map(
        local,
        mesh=mesh,
        in_specs=placed,
        out_specs=(
            P(None, ("dp", "tensor"), None),
            P(None, ("dp", "tensor"), None),
            P(("dp", "tensor")),
            P(("dp", "tensor")),
            P("dp", "tensor"),
            P(("dp", "tensor"), None),
            P("tensor", "dp"),
            P(("dp", "tensor")),
            P(("dp", "tensor")),
            P("dp", "tensor"),
            P("tensor", "dp"),
        ),
        check_vma=False,
    )
```

```python
import functools
import math

import jax
import jax.numpy as jnp
from jax import lax
from jax.experimental import pallas as pl
from jax.experimental.pallas import tpu as pltpu
from jax.sharding import PartitionSpec as P

BLOCK = 256
EPSILON = 1e-05
NEG_FILL = -1e30
GELU_A = math.sqrt(2.0 / math.pi)
GELU_B = 0.044715
LOG2_E = 1.0 / math.log(2.0)
MLP_ORDER = ("mmmmmmmrmrmemeemememermmmeeermmrmmmmsmmx", "rmsmmxmxsxss",)
BACK_ORDER = ("rmmemrrmrmermmmremrmeemwwawqaqqwaqawrwqr", "qeaae",)
FRONT_ORDER = ("omaoaaamaaamcoaammhaaommommokkmekecaceme", "ckceme",)
MESH = pl.DeviceIdType.MESH
ANY = pl.BlockSpec(memory_space=pl.ANY)
READY = "ready"
IN_VMEM = pl.BlockSpec(memory_space=pltpu.VMEM)
BF16 = jnp.bfloat16
F32 = jnp.float32


def layer_norm(values, gain, shift):
    center = jnp.mean(values, axis=-1, keepdims=True)
    centered = values - center
    variance = jnp.mean(centered * centered, axis=-1, keepdims=True)
    return centered * lax.rsqrt(variance + EPSILON) * gain + shift


def gelu_tanh(values):
    return jax.nn.gelu(values, approximate=True)


class Net:
    def __init__(self, nz, ny, send, recv, local):
        dp, tensor = lax.axis_index("dp"), lax.axis_index("tensor")
        self.nz, self.ny = nz, ny
        self.z, self.x = lax.div(dp, 2), lax.rem(dp, 2)
        self.y, self.c = lax.div(tensor, 2), lax.rem(tensor, 2)
        self.tensor = tensor
        self.send, self.recv, self.local = send, recv, local
        self.used = [0, 0]
        self.keys = {}

    def flip(self, value, by):
        return value + by - 2 * by * value if by else value

    def xy(self, dx, dy):
        return self.flip(self.x, dx), lax.rem(self.y + dy, self.ny) if dy else self.y

    def rank(self, dx=0, dy=0, dc=0):
        x, y = self.xy(dx, dy)
        return x * (2 * self.ny) + y * 2 + self.flip(self.c, dc)

    def device(self, dx=0, dy=0, dc=0, z=None):
        x, y = self.xy(dx, dy)
        return ((self.z if z is None else z) * 2 + x, y * 2 + self.flip(self.c, dc))

    def slot(self, key):
        if key not in self.keys:
            self.keys[key] = self.used[0]
            self.used[0] += 1
        return self.keys[key]

    def remote(self, key, src, dst, device):
        at = self.slot(key)
        return pltpu.make_async_remote_copy(
            src_ref=src,
            dst_ref=dst,
            send_sem=self.send.at[at],
            recv_sem=self.recv.at[at],
            device_id=device,
            device_id_type=MESH,
        )

    def take_locals(self, count):
        first = self.used[1]
        self.used[1] += count
        return first

    def copy_at(self, at, src, dst):
        return pltpu.make_async_copy(src, dst, self.local.at[at])

    def copy(self, src, dst):
        return self.copy_at(self.take_locals(1), src, dst)


def add_rows(dst, terms):
    lead, height, width = dst.shape
    rows = min(max(16, 32768 // width), height)
    steps = height // rows

    def body(step, carry):
        at, off = lax.div(step, steps), pl.multiple_of(lax.rem(step, steps) * rows, rows)
        total = terms[0][at, pl.ds(off, rows), :].astype(F32)
        for term in terms[1:]:
            total = total + term[at, pl.ds(off, rows), :].astype(F32)
        dst[at, pl.ds(off, rows), :] = total.astype(dst.dtype)
        return carry

    lax.fori_loop(0, lead * steps, body, 0)


class FaceGather:
    moves = ("x", "y", "c")
    in_spec = IN_VMEM

    def __init__(self, own, nz, ny, hold_x=False):
        self.ins, self.hold_x = [own], hold_x
        m, t, d = own.shape
        self.outs = [(jax.ShapeDtypeStruct((m, 4 * ny * t, d), own.dtype), ANY)]
        self.scratch = []
        self.half = t // 2
        self.remotes, self.locals = 8 * ny, 1

    def run(self, net, ins, outs, scratch):
        (own,), (out,), half = ins, outs, self.half
        dys = range(1, net.ny)

        def piece(dx, dy, h):
            return out.at[:, pl.ds(pl.multiple_of(net.rank(dx, dy) * 2 * half + h * half, half), half), :]

        mine = [own.at[:, pl.ds(h * half, half), :] for h in (0, 1)]
        keep = net.copy(own, out.at[:, pl.ds(pl.multiple_of(net.rank() * 2 * half, half), 2 * half), :])
        keep.start()
        sent = {}

        def send(key, src, dst, device):
            sent[key] = net.remote((id(self), key), src, dst, device)
            sent[key].start()

        if not self.hold_x:
            send(("x", 0), mine[0], piece(0, 0, 0), net.device(1, 0))
        for dy in dys:
            send(("y", dy, 1), mine[1], piece(0, 0, 1), net.device(0, dy))
        if not self.hold_x:
            send(("x", 1), mine[1], piece(0, 0, 1), net.device(1, 0))
        for dy in dys:
            send(("y", dy, 0), mine[0], piece(0, 0, 0), net.device(0, dy))
        for h in (0, 1):
            send(("c", h), mine[h], piece(0, 0, h), net.device(0, 0, 1))
        if self.hold_x:
            yield
            for h in (0, 1):
                send(("x", h), mine[h], piece(0, 0, h), net.device(1, 0))

        def share(key, dx, dy, h):
            send(("c",) + key, piece(dx, dy, h), piece(dx, dy, h), net.device(0, 0, 1))

        def from_x(h):
            sent["x", h].wait_recv()
            if not h:
                for dy in dys:
                    send(("xy", dy), piece(1, 0, 0), piece(1, 0, 0), net.device(0, dy))
            share(("x", h), 1, 0, h)

        def from_y(dy, h):
            sent["y", dy, h].wait_recv()
            if h:
                send(("yx", dy), piece(0, -dy % net.ny, 1), piece(0, -dy % net.ny, 1), net.device(1, 0))
            share(("y", dy, h), 0, -dy % net.ny, h)

        arrivals = []
        for first in (True, False):
            on_x = [functools.partial(from_x, 0 if first else 1)]
            on_y = [functools.partial(from_y, dy, 1 if first else 0) for dy in dys]
            arrivals.append(on_x + on_y)
        if self.hold_x:
            arrivals = [arrivals[0][1:], arrivals[1][1:], arrivals[0][:1], arrivals[1][:1]]
        for group in arrivals:
            for arrive in group:
                yield
                arrive()
        for dy in dys:
            yield
            sent["xy", dy].wait_recv()
            share(("xy", dy), 1, -dy % net.ny, 0)
            yield
            sent["yx", dy].wait_recv()
            share(("yx", dy), 1, -dy % net.ny, 1)
        yield
        for key, copy in sent.items():
            if key[0] == "c":
                copy.wait_recv()
        for copy in sent.values():
            copy.wait_send()
        keep.wait()


class FaceScatter:
    moves = ("x", "y", "c")

    def __init__(self, part, nz, ny, resident=False):
        self.ins, self.resident = [part], resident
        m, rows, d = part.shape
        t = rows // (4 * ny)
        self.outs = [(jax.ShapeDtypeStruct((m, t, d), F32), pl.BlockSpec(memory_space=pltpu.VMEM))]
        half = t // 2
        self.half = half
        self.scratch = [
            pltpu.VMEM((2 * ny, m, t, d), BF16),
            pltpu.VMEM((ny - 1, m, half, d), BF16),
            pltpu.VMEM((ny - 1, m, half, d), BF16),
            pltpu.VMEM((2, m, half, d), BF16),
            pltpu.VMEM((2, ny - 1, m, half, d), BF16),
        ]
        if not resident:
            self.scratch.append(pltpu.VMEM((2 * ny, m, t, d), BF16))
        self.remotes, self.locals = 6 * ny + 4, 2 * ny

    def run(self, net, ins, outs, scratch):
        (part,), (out,), half = ins, outs, self.half
        from_core, x_diag, y_diag, x_in, y_in = scratch[:5]
        ny = net.ny
        dys = range(1, ny)
        order = [(1, dy) for dy in dys] + [(1, 0)] + [(0, dy) for dy in dys] + [(0, 0)]
        sent, loads = {}, {}

        def send(key, src, dst, device):
            sent[key] = net.remote((id(self), key), src, dst, device)
            sent[key].start()

        def rows(dx, dy, dc, first=0, size=2 * half):
            at = net.rank(dx, dy, dc) * 2 * half + first
            return part.at[:, pl.ds(pl.multiple_of(at, half), size), :]

        def work(dx, dy, first=0, size=2 * half):
            if self.resident:
                return rows(dx, dy, 0, first, size)
            return scratch[5].at[dx * ny + dy, :, pl.ds(first, size), :]

        for dx, dy in order:
            at = dx * ny + dy
            if not self.resident:
                loads[at] = net.copy(rows(dx, dy, 0), work(dx, dy))
                loads[at].start()
            send(("c", at), rows(dx, dy, 1), from_core.at[at], net.device(0, 0, 1))
        for dx, dy in order:
            at = dx * ny + dy
            yield
            if not self.resident:
                loads[at].wait()
            sent["c", at].wait_recv()
            add_rows(work(dx, dy), [work(dx, dy), from_core.at[at]])
            top, low = work(dx, dy, 0, half), work(dx, dy, half, half)
            if dx and dy:
                send(("xd", dy), top, x_diag.at[dy - 1], net.device(1, 0))
                send(("yd", dy), low, y_diag.at[dy - 1], net.device(0, dy))
            elif dx:
                send(("x", 0), top, x_in.at[0], net.device(1, 0))
            elif dy:
                send(("y", dy, 1), low, y_in.at[1, dy - 1], net.device(0, dy))
        for dy in dys:
            yield
            sent["xd", dy].wait_recv()
            top = work(0, dy, 0, half)
            add_rows(top, [top, x_diag.at[dy - 1]])
            send(("y", dy, 0), top, y_in.at[0, dy - 1], net.device(0, dy))
        low = work(1, 0, half, half)
        for dy in dys:
            yield
            sent["yd", dy].wait_recv()
            add_rows(low, [low, y_diag.at[dy - 1]])
        send(("x", 1), low, x_in.at[1], net.device(1, 0))
        for h in (0, 1):
            yield
            sent["x", h].wait_recv()
            for dy in dys:
                sent["y", dy, h].wait_recv()
            add_rows(
                out.at[:, pl.ds(h * half, half), :],
                [work(0, 0, h * half, half), x_in.at[h]] + [y_in.at[h, dy - 1] for dy in dys],
            )
        for copy in sent.values():
            copy.wait_send()


class LineGather:
    moves = ("x", "line", "c")
    in_spec = IN_VMEM

    def __init__(self, shards, kinds, nz, ny, share=(0, 1), given=()):
        self.ins, self.kinds, self.share = list(shards) + list(given), list(kinds), share
        self.outs, self.scratch = [], []
        for shard, kind in zip(shards, kinds):
            rows, columns = shard.shape
            if kind == "row":
                shape = (rows * 2 * nz, columns // 2 // share[1])
            elif kind == "col":
                shape = (rows // 2 // share[1], columns * 2 * nz)
            else:
                shape = (rows * 2 * nz, columns)
            self.outs.append((jax.ShapeDtypeStruct(shape, shard.dtype), ANY))
        count = len(self.kinds)
        self.remotes = count * (1 + 4 * (nz - 1)) + kinds.count("both") * (1 + 4 * (nz - 1))
        self.locals = 2 * count

    def run(self, net, ins, outs, scratch):
        nz, z = net.nz, net.z
        sent, locals_, shared = [], [], []
        weights = []
        given = ins[len(self.kinds) :]
        for at, (shard, out, kind) in enumerate(zip(ins, outs, self.kinds)):
            rows, columns = shard.shape

            if kind == "row":
                span = columns // 2 // self.share[1]

                def mine(dx, shard=shard, span=span):
                    first = (net.flip(net.x, dx) * self.share[1] + self.share[0]) * span
                    return shard.at[:, pl.ds(pl.multiple_of(first, span), span)]

                def block(line, dx, out=out, rows=rows):
                    first = (line * 2 + net.flip(net.x, dx)) * rows
                    return out.at[pl.ds(pl.multiple_of(first, rows), rows), :]

            elif kind == "col":
                span = rows // 2 // self.share[1]

                def mine(dx, shard=shard, span=span):
                    first = (net.flip(net.x, dx) * self.share[1] + self.share[0]) * span
                    return shard.at[pl.ds(pl.multiple_of(first, span), span), :]

                def block(line, dx, out=out, columns=columns):
                    first = (line * 2 + net.flip(net.x, dx)) * columns
                    return out.at[:, pl.ds(pl.multiple_of(first, columns), columns)]

            else:
                half = rows // 2

                def mine(dx, shard=shard, half=half):
                    return shard.at[pl.ds(pl.multiple_of(net.c * half, half), half), :]

                def block(line, dx, out=out, rows=rows, half=half):
                    first = (line * 2 + net.flip(net.x, dx)) * rows + net.c * half
                    return out.at[pl.ds(pl.multiple_of(first, half), half), :]

            weights.append((at, kind, mine, block))

        def hop(at, dx, step, up, block, src=None):
            origin = z - (step - 1) if up else z + (step - 1)
            there = z + 1 if up else z - 1
            copy = net.remote(
                (id(self), at, dx, step, up),
                block(origin, dx) if src is None else src,
                block(origin, dx),
                net.device(z=there),
            )
            fits = (origin >= 0) & (there < nz) if up else (origin < nz) & (there >= 0)
            return copy, fits

        def start(at, dx, step, up, block, src=None):
            copy, fits = hop(at, dx, step, up, block, src)
            pl.when(fits)(copy.start)
            sent.append((copy, fits))

        def arrived(at, dx, step, up, block, kind):
            copy, _ = hop(at, dx, step, up, block)
            origin = z - step if up else z + step
            fits = origin >= 0 if up else origin < nz
            pl.when(fits)(copy.wait_recv)
            if kind == "both":
                share = net.remote(
                    (id(self), "c", at, dx, step, up), block(origin, dx), block(origin, dx), net.device(0, 0, 1)
                )
                pl.when(fits)(share.start)
                shared.append((share, fits))

        swaps = {}
        for at, kind, mine, block in weights:
            if not given:
                swaps[at] = net.remote((id(self), at, "x"), mine(1), block(z, 0), net.device(1, 0))
                swaps[at].start()
            for up in (True, False):
                start(at, 0, 1, up, block, mine(0))
        for at, kind, mine, block in weights:
            if kind == "both":
                whole = ins[at].shape[0]
                into = outs[at].at[pl.ds(pl.multiple_of((z * 2 + net.x) * whole, whole), whole), :]
                locals_.append(net.copy(ins[at], into))
            else:
                locals_.append(net.copy(mine(0), block(z, 0)))
            locals_[-1].start()
        for (at, kind, mine, block), other in zip(weights, given):
            span = pl.ds(self.share[0] * other.shape[kind == "row"] // self.share[1], other.shape[kind == "row"] // self.share[1])
            other = other.at[:, span] if kind == "row" else other.at[span, :]
            locals_.append(net.copy(other, block(z, 1)))
            locals_[-1].start()
            for up in (True, False):
                start(at, 1, 1, up, block, other)
        yield
        for copy in locals_:
            copy.wait()
        for at, kind, mine, block in weights:
            if given:
                continue
            swaps[at].wait_recv()
            for up in (True, False):
                start(at, 1, 1, up, block)
            if kind == "both":
                share = net.remote((id(self), "c", at), block(z, 1), block(z, 1), net.device(0, 0, 1))
                share.start()
                shared.append((share, None))
        for step in range(1, nz):
            for at, kind, mine, block in weights:
                for dx in (0, 1):
                    yield
                    for up in (True, False):
                        arrived(at, dx, step, up, block, kind)
                        if step < nz - 1:
                            start(at, dx, step + 1, up, block)
        yield
        for copy, fits in shared:
            if fits is None:
                copy.wait_recv()
            else:
                pl.when(fits)(copy.wait_recv)
        yield READY
        for copy, fits in shared:
            if fits is None:
                copy.wait_send()
            else:
                pl.when(fits)(copy.wait_send)
        for copy, fits in sent:
            pl.when(fits)(copy.wait_send)
        for copy in swaps.values():
            copy.wait_send()


class HalfSwap:
    moves = ("x",)

    def __init__(self, shards, kinds, nz, ny):
        self.ins, self.kinds = list(shards), list(kinds)
        self.outs, self.scratch = [], []
        for shard, kind in zip(shards, kinds):
            rows, columns = shard.shape
            shape = (rows, columns // 2) if kind == "row" else (rows // 2, columns)
            self.outs.append((jax.ShapeDtypeStruct(shape, shard.dtype), ANY))
        self.remotes, self.locals = len(self.ins), 0

    def run(self, net, ins, outs, scratch):
        copies = []
        for at, (shard, out, kind) in enumerate(zip(ins, outs, self.kinds)):
            span = out.shape[kind == "row"]
            there = pl.ds(pl.multiple_of((1 - net.x) * span, span), span)
            src = shard.at[:, there] if kind == "row" else shard.at[there, :]
            copies.append(net.remote((id(self), at), src, out, net.device(1, 0)))
            copies[-1].start()
        yield
        for copy in copies:
            copy.wait_recv()
        yield READY
        for copy in copies:
            copy.wait_send()


class LineScatter:
    moves = ("x", "line")

    def __init__(self, parts, kinds, nz, ny, resident=False, joined=False):
        self.ins, self.kinds, self.resident, self.joined = list(parts), list(kinds), resident, joined
        self.outs, self.scratch = [], []
        for part, kind in zip(parts, kinds):
            rows, columns = part.shape
            shape = (rows // (2 * nz), columns) if kind == "row" else (rows, columns // (2 * nz))
            times = 2 * (len(parts) if joined else 1)
            whole = (shape[0], shape[1] * times) if kind == "row" else (shape[0] * times, shape[1])
            if not (joined and self.outs):
                self.outs.append((jax.ShapeDtypeStruct(whole, BF16), ANY))
            for lead in (nz - 1, nz - 1, 1) + (() if resident else (nz,)):
                self.scratch.append(pltpu.VMEM((lead, 2) + shape, BF16))
        count = len(self.ins)
        self.remotes = count * (1 + 4 * nz)
        self.locals = count * (2 * nz + 1)

    def run(self, net, ins, outs, scratch):
        nz, z = net.nz, net.z
        loads, grads = {}, []
        each = 3 if self.resident else 4
        outs = list(outs) * len(ins) if self.joined else outs

        def spot(at, out):
            rows, columns = scratch[each * at + 2].shape[2:]
            kind = self.kinds[at]
            size = columns if kind == "row" else rows
            first = (net.x * len(ins) + at) * size if self.joined else net.x * size
            span = pl.ds(pl.multiple_of(first, size), size)
            return out.at[:, span] if kind == "row" else out.at[span, :]

        for at, (part, out, kind) in enumerate(zip(ins, outs, self.kinds)):
            down, up, mine = scratch[each * at : each * at + 3]
            _, _, rows, columns = mine.shape

            def block(line, dx, part=part, kind=kind, rows=rows, columns=columns):
                size = rows if kind == "row" else columns
                first = pl.ds(pl.multiple_of((line * 2 + net.flip(net.x, dx)) * size, size), size)
                return part.at[first, :] if kind == "row" else part.at[:, first]

            if self.resident:
                work = block
            else:

                def work(line, dx, at=at):
                    return scratch[each * at + 3].at[line, dx]

                order = []
                for k in range(nz):
                    order += [k, nz - 1 - k]
                for line in dict.fromkeys(order):
                    for dx in (1, 0):
                        loads[at, line, dx] = net.copy(block(line, dx), work(line, dx))
                        loads[at, line, dx].start()
            grads.append((at, out, work, down, up, mine))

        def inbox(slots, line, dx, toward):
            return slots.at[line if toward < 0 else line - 1, dx]

        pieces = (1, 0)
        each_line = len(pieces)

        for at, *_ in grads:
            net.slot((id(self), at, "x"))
            for dx in (0, 1):
                for line in range(nz):
                    for toward in (-1, 1):
                        net.slot((id(self), at, line, dx, toward))

        def chain(grad, dx, line, toward):
            at, out, work, down, up, mine = grad
            slot = inbox(down if toward < 0 else up, line, dx, toward)
            copy = net.remote((id(self), at, line, dx, toward), work(line, dx), slot, net.device(z=z + toward))
            return copy, slot

        def forward(place, grad, dx, line, toward):
            at, out, work, down, up, mine = grad
            copy, slot = chain(grad, dx, line, toward)
            if not self.resident:
                loads[at, line, dx].wait()
            if place != (nz - 1 if toward < 0 else 0):
                copy.wait_recv()
                add_rows(_lead(work(line, dx)), [_lead(work(line, dx)), _lead(slot)])
            copy.start()

        def finish(place, grad, dx):
            at, out, work, down, up, mine = grad
            if not self.resident:
                loads[at, place, dx].wait()
            terms = [_lead(work(place, dx))]
            for toward in (-1, 1):
                if (place < nz - 1) if toward < 0 else (place > 0):
                    copy, slot = chain(grad, dx, place, toward)
                    copy.wait_recv()
                    terms.append(_lead(slot))
            total = mine.at[0, dx]
            add_rows(_lead(total), terms)
            if dx:
                net.remote((id(self), at, "x"), total, spot(at, out), net.device(1, 0)).start()
            else:
                net.copy_at(self.first_local + at, total, spot(at, out)).start()

        plan = {}
        for place in range(nz):
            waits_up, waits_down = place, nz - 1 - place
            todo = []
            for toward, waits, lines in (
                (1, waits_up, range(nz - 1, place, -1)),
                (-1, waits_down, range(place)),
            ):
                order = [(line, dx) for line in lines for dx in pieces]
                for j, (line, dx) in enumerate(order):
                    for grad in grads:
                        todo.append((waits + j if waits else 0, waits, (forward, grad, dx, line, toward)))
            for q, dx in enumerate(pieces):
                times = []
                if waits_up:
                    times.append(waits_up + each_line * (nz - 1 - place) + q)
                if waits_down:
                    times.append(waits_down + each_line * place + q)
                for grad in grads:
                    todo.append((max(times), nz, (finish, grad, dx)))
            for time, waits, item in sorted(todo, key=lambda entry: entry[:2]):
                plan.setdefault(time, {}).setdefault(place, []).append(item)
        self.first_local = net.take_locals(len(grads))
        for time in range(max(plan) + 1):
            if time:
                yield
            for place, items in sorted(plan.get(time, {}).items()):

                def act(place=place, items=items):
                    for item in items:
                        item[0](place, *item[1:])

                pl.when(z == place)(act)
        sent = [
            (chain(grad, dx, line, toward)[0], (z > line) if toward < 0 else (z < line))
            for grad in grads
            for dx in pieces
            for toward, lines in ((-1, range(nz - 1)), (1, range(1, nz)))
            for line in lines
        ]
        swaps, stores = [], []
        for at, out, _, _, _, mine in grads:
            swaps.append(net.remote((id(self), at, "x"), mine.at[0, 1], spot(at, out), net.device(1, 0)))
            stores.append(net.copy_at(self.first_local + at, mine.at[0, 0], spot(at, out)))
        yield
        for copy, sends in sent:
            pl.when(sends)(copy.wait_send)
        for copy in swaps:
            copy.wait()
        for copy in stores:
            copy.wait()


def _lead(ref):
    return Lead(ref)


class Lead:
    def __init__(self, ref):
        self.ref, self.shape, self.dtype = ref, (1,) + tuple(ref.shape), ref.dtype

    def __getitem__(self, index):
        return self.ref[index[1], index[2]]

    def __setitem__(self, index, value):
        self.ref[index[1], index[2]] = value


class KeysGather:
    moves = ("x", "line", "c")
    in_spec = IN_VMEM

    def __init__(self, face, nz, ny):
        m, rows, width = face.shape
        self.ins = [face]
        self.outs = [(jax.ShapeDtypeStruct((m, nz * rows, width), face.dtype), ANY)]
        self.scratch = []
        self.remotes, self.locals = 4 * (nz - 1), 1

    def run(self, net, ins, outs, scratch):
        (face,), (out,) = ins, outs
        nz, z = net.nz, net.z
        _, rows, width = face.shape
        part, side = rows // 2, width // 2

        def block(line, dx, dc):
            first = pl.multiple_of(line * rows + net.flip(net.x, dx) * part, part)
            column = pl.multiple_of(net.flip(net.c, dc) * side, side)
            return out.at[:, pl.ds(first, part), pl.ds(column, side)]

        own = face.at[
            :,
            pl.ds(pl.multiple_of(net.x * part, part), part),
            pl.ds(pl.multiple_of(net.c * side, side), side),
        ]
        sent, shared = [], []

        def line_copy(step):
            origin = z - (step - 1)
            src = own if step == 1 else block(origin, 0, 0)
            return net.remote((id(self), step), src, block(origin, 0, 0), net.device(z=z + 1))

        def start(step):
            copy, fits = line_copy(step), (z - (step - 1) >= 0) & (z + 1 < nz)
            pl.when(fits)(copy.start)
            sent.append((copy, fits))

        start(1)
        keep = net.copy(face, out.at[:, pl.ds(pl.multiple_of(z * rows, rows), rows), :])
        keep.start()
        later = []
        for step in range(1, nz):
            yield
            fits = z - step >= 0
            pl.when(fits)(line_copy(step).wait_recv)
            if step < nz - 1:
                start(step + 1)
            here = block(z - step, 0, 0)
            across = net.remote((id(self), "x", step), here, here, net.device(1, 0))
            beside = net.remote((id(self), "c", step), here, here, net.device(0, 0, 1))
            for copy in (across, beside):
                pl.when(fits)(copy.start)
                sent.append((copy, fits))
            later.append((step, fits, across))
            shared.append((beside, fits))
        for step, fits, across in later:
            yield
            pl.when(fits)(across.wait_recv)
            there = block(z - step, 1, 0)
            beside = net.remote((id(self), "xc", step), there, there, net.device(0, 0, 1))
            pl.when(fits)(beside.start)
            sent.append((beside, fits))
            shared.append((beside, fits))
        yield
        for copy, fits in shared:
            pl.when(fits)(copy.wait_recv)
        keep.wait()
        yield READY
        for copy, fits in sent:
            pl.when(fits)(copy.wait_send)


class WholeScatter(FaceScatter):
    moves = ("x", "y", "c", "z")

    def __init__(self, part, nz, ny, resident=False):
        m, _, rows, d = part.shape
        merged = jax.ShapeDtypeStruct((m * nz, rows, d), part.dtype) if resident else part.reshape(m * nz, rows, d)
        super().__init__(merged, nz, ny, resident)
        t = rows // (4 * ny)
        self.m, self.nz = m, nz
        self.outs = [(jax.ShapeDtypeStruct((m, t, d), F32), pl.BlockSpec(memory_space=pltpu.VMEM))]
        self.scratch = self.scratch + [pltpu.VMEM((m * nz, t, d), BF16), pltpu.VMEM((nz, m, t, d), BF16)]
        self.remotes = self.remotes + nz * m
        self.locals = self.locals + m

    def run(self, net, ins, outs, scratch):
        face, inbox = scratch[-2:]
        yield from super().run(net, ins, [face], scratch[:-2])
        nz, m = self.nz, self.m
        copies = []
        for far in range(1, nz):
            line = lax.rem(net.z + far, nz)
            for at in range(m):
                copies.append(
                    pltpu.make_async_remote_copy(
                        src_ref=face.at[at * nz + line],
                        dst_ref=inbox.at[far, at],
                        send_sem=net.send.at[net.slot((id(self), "z", far, at))],
                        recv_sem=net.recv.at[net.slot((id(self), "z", far, at))],
                        device_id=net.device(z=line),
                        device_id_type=MESH,
                    )
                )
                copies[-1].start()
        own = []
        for at in range(m):
            own.append(net.copy(face.at[at * nz + net.z], inbox.at[0, at]))
            own[-1].start()
        yield
        for copy in own:
            copy.wait()
        for copy in copies:
            copy.wait()
        add_rows(outs[0], [inbox.at[far] for far in range(nz)])


class QuickScatter:
    moves = ("c", "same", "z")

    def __init__(self, part, nz, ny):
        _, rows, d = part.shape
        t = rows // (4 * ny)
        self.ins, self.t = [part], t
        self.outs = [(jax.ShapeDtypeStruct((t, d), F32), pl.BlockSpec(memory_space=pltpu.VMEM))]
        self.scratch = [
            pltpu.VMEM((2 * ny, nz, t, d), BF16),
            pltpu.VMEM((2 * ny, nz, t, d), BF16),
            pltpu.VMEM((2 * ny, nz, t, d), BF16),
            pltpu.VMEM((nz, t, d), BF16),
            pltpu.VMEM((nz, 1, t, d), BF16),
        ]
        self.remotes, self.locals = 4 * ny + nz, 2 * ny + 1

    def run(self, net, ins, outs, scratch):
        (part,), (out,), t = ins, outs, self.t
        work, from_core, inbox, face, line_in = scratch
        ny, nz = net.ny, net.nz
        order = [(dx, dy) for dx in (1, 0) for dy in reversed(range(ny))]
        cores, loads, copies = {}, {}, {}

        def rows(dx, dy, dc):
            return part.at[:, pl.ds(pl.multiple_of(net.rank(dx, dy, dc) * t, t), t), :]

        for dx, dy in order:
            at = dx * ny + dy
            loads[at] = net.copy(rows(dx, dy, 0), work.at[at])
            loads[at].start()
            cores[at] = net.remote((id(self), "c", at), rows(dx, dy, 1), from_core.at[at], net.device(0, 0, 1))
            cores[at].start()
        for dx, dy in order:
            at = dx * ny + dy
            yield
            loads[at].wait()
            cores[at].wait_recv()
            add_rows(work.at[at], [work.at[at], from_core.at[at]])
            if at:
                copies[at] = net.remote((id(self), at), work.at[at], inbox.at[at], net.device(dx, dy))
                copies[at].start()
        yield
        for copy in copies.values():
            copy.wait_recv()
        add_rows(face, [work.at[0]] + [inbox.at[at] for at in copies])
        lines = []
        for far in range(1, nz):
            line = lax.rem(net.z + far, nz)
            lines.append(
                net.remote((id(self), "z", far), face.at[pl.ds(line, 1)], line_in.at[far], net.device(z=line))
            )
            lines[-1].start()
        own = net.copy(face.at[pl.ds(net.z, 1)], line_in.at[0])
        own.start()
        yield
        own.wait()
        for copy in lines:
            copy.wait_recv()
        add_rows(_lead(out), [line_in.at[far] for far in range(nz)])
        for copy in list(cores.values()) + list(copies.values()) + lines:
            copy.wait_send()


class PlaneGather:
    moves = ("plane",)
    in_spec = IN_VMEM

    def __init__(self, own, nz, ny):
        self.ins = [own]
        self.outs = [(jax.ShapeDtypeStruct((2 * nz,) + own.shape, own.dtype), ANY)]
        self.scratch = []
        self.remotes, self.locals = 2 * nz, 1

    def run(self, net, ins, outs, scratch):
        (own,), (out,) = ins, outs
        here = out.at[net.z * 2 + net.x]
        copies = []
        for far in range(net.nz):
            for dx in (0, 1):
                if far or dx:
                    line = lax.rem(net.z + far, net.nz)
                    copies.append(net.remote((id(self), far, dx), own, here, net.device(dx, z=line)))
                    copies[-1].start()
        keep = net.copy(own, here)
        keep.start()
        yield
        for copy in copies:
            copy.wait()
        keep.wait()


class SmallScatter:
    moves = ("face", "z")

    def __init__(self, part, nz, ny):
        ranks, _, rows, width = part.shape
        self.ins = [part]
        vmem = pl.BlockSpec(memory_space=pltpu.VMEM)
        self.outs = [(jax.ShapeDtypeStruct((rows, width), F32), vmem)]
        self.scratch = [
            pltpu.VMEM((ranks, nz, rows, width), F32),
            pltpu.VMEM((nz, rows, width), F32),
            pltpu.VMEM((nz, rows, width), F32),
        ]
        self.remotes, self.locals = ranks + nz, 2

    def run(self, net, ins, outs, scratch):
        (part,), (out,) = ins, outs
        inbox, total, line_in = scratch
        ny, nz = net.ny, net.nz
        copies = []
        for dx in (0, 1):
            for dy in range(ny):
                for dc in (0, 1):
                    if dx or dy or dc:
                        at = (dx * ny + dy) * 2 + dc
                        copies.append(
                            net.remote(
                                (id(self), at), part.at[net.rank(dx, dy, dc)], inbox.at[at], net.device(dx, dy, dc)
                            )
                        )
                        copies[-1].start()
        keep = net.copy(part.at[net.rank()], inbox.at[0])
        keep.start()
        yield
        keep.wait()
        for copy in copies:
            copy.wait()
        total[...] = jnp.sum(inbox[...], axis=0)
        lines = []
        for far in range(1, nz):
            line = lax.rem(net.z + far, nz)
            lines.append(net.remote((id(self), "z", far), total.at[line], line_in.at[far], net.device(z=line)))
            lines[-1].start()
        own = net.copy(total.at[net.z], line_in.at[0])
        own.start()
        yield
        own.wait()
        for copy in lines:
            copy.wait()
        out[...] = jnp.sum(line_in[...], axis=0)


def launch(body, ins, in_specs, outs, scratch, plans, nz, ny, collective_id, name, extra_locals=0, vmem=56):
    moves = set()
    for plan in plans:
        moves |= set(plan.moves)
    remotes = sum(plan.remotes for plan in plans)
    locals_ = max(1, extra_locals + sum(plan.locals for plan in plans))

    def kernel(*refs):
        in_refs, refs = refs[: len(ins)], refs[len(ins) :]
        out_refs, refs = refs[: len(outs)], refs[len(outs) :]
        scratch_refs, (send, recv, local) = refs[: len(scratch)], refs[len(scratch) :]
        net = Net(nz, ny, send, recv, local)
        peers = {}
        for far in range(nz):
            for dx in (0, 1):
                for dy in range(ny):
                    for dc in (0, 1):
                        kinds = set()
                        if not far:
                            kinds.add("face")
                            if dx and not dy and not dc:
                                kinds.add("x")
                            if dy and not dx and not dc:
                                kinds.add("y")
                            if dc and not dx and not dy:
                                kinds.add("c")
                            if not dc:
                                kinds.add("same")
                        if far and not dx and not dy and not dc:
                            kinds.add("z")
                            if far in (1, nz - 1):
                                kinds.add("line")
                        if not dy and not dc:
                            kinds.add("plane")
                        if (far or dx or dy or dc) and kinds & moves:
                            line = lax.rem(net.z + far, nz) if far else None
                            peers[far, dx, dy, dc] = net.device(dx, dy, dc, line)
        barrier = pltpu.get_barrier_semaphore()
        for device in peers.values():
            pl.semaphore_signal(barrier, inc=1, device_id=device, device_id_type=MESH)
        pl.semaphore_wait(barrier, len(peers))
        body(net, in_refs, out_refs, scratch_refs)

    return list(
        pl.pallas_call(
            kernel,
            out_shape=[shape for shape, _ in outs],
            in_specs=in_specs,
            out_specs=[spec for _, spec in outs],
            scratch_shapes=list(scratch)
            + [
                pltpu.SemaphoreType.DMA((remotes,)),
                pltpu.SemaphoreType.DMA((remotes,)),
                pltpu.SemaphoreType.DMA((locals_,)),
            ],
            compiler_params=pltpu.CompilerParams(
                collective_id=collective_id, has_side_effects=True, vmem_limit_bytes=vmem << 20
            ),
            name=name,
        )(*ins)
    )


def exchange(plans, nz, ny, collective_id, name, order=()):
    ins = [array for plan in plans for array in plan.ins]
    outs = [out for plan in plans for out in plan.outs]
    scratch = [entry for plan in plans for entry in plan.scratch]

    def body(net, in_refs, out_refs, scratch_refs):
        running = []
        for plan in plans:
            mine = []
            for refs_of, count in ((in_refs, plan.ins), (out_refs, plan.outs), (scratch_refs, plan.scratch)):
                mine.append(list(refs_of[: len(count)]))
            in_refs = in_refs[len(plan.ins) :]
            out_refs = out_refs[len(plan.outs) :]
            scratch_refs = scratch_refs[len(plan.scratch) :]
            running.append(plan.run(net, *mine))
        for at in order:
            next(running[at], None)
        while running:
            for steps in list(running):
                try:
                    next(steps)
                except StopIteration:
                    running.remove(steps)

    specs = [getattr(plan, "in_spec", ANY) for plan in plans for _ in plan.ins]
    results = launch(body, ins, specs, outs, scratch, plans, nz, ny, collective_id, name)
    grouped = []
    for plan in plans:
        grouped.append(results[: len(plan.outs)])
        results = results[len(plan.outs) :]
    return grouped


class Weave:
    def __init__(self):
        self.plans, self.ready = {}, set()

    def add(self, name, steps):
        self.plans[name] = steps

    def step(self, name):
        steps = self.plans.get(name)
        if steps is not None:
            state = next(steps, self)
            if state is self:
                del self.plans[name]
            elif state == READY:
                self.ready.add(name)

    def need(self, name):
        while name in self.plans and name not in self.ready:
            self.step(name)

    def finish(self, name):
        while name in self.plans:
            self.step(name)


def first_block(block, seq_len):
    longest = seq_len // 2 + BLOCK
    return jnp.maximum(block - (longest - 1 + BLOCK - 1) // BLOCK, 0)


def loop(count, body):
    def step(at, carry):
        body(at)
        return carry

    lax.fori_loop(0, count, step, 0)


def mlp_block(mixed, wo, inputs, cotangent, cot_face, norms, wexp_first, w_expand, w_reduce, nz, ny, collective_id):
    micro_count, own_rows, width = inputs.shape
    face_rows = cot_face.shape[1]
    tokens = micro_count * face_rows
    attn = mixed.shape[1]
    units = w_expand[0].shape[1] // 2
    half = units // 2
    tile = min(512, half)
    wide = 512
    part = jax.ShapeDtypeStruct((micro_count, face_rows, width), BF16)
    part_red = jax.ShapeDtypeStruct((units, width), BF16)
    own = (micro_count, own_rows, width)
    scatter_a, scatter_b = (FaceScatter(part, nz, ny, resident=True) for _ in range(2))
    gather = FaceGather(jax.ShapeDtypeStruct(own, BF16), nz, ny)
    line_e = LineGather(w_expand[:1], ["row"], nz, ny, share=(1, 2), given=w_expand[1:])
    line_r = LineGather(w_reduce[:1], ["col"], nz, ny, given=w_reduce[1:])
    line_s = LineScatter([part_red], ["col"], nz, ny, resident=True)
    plans = [scatter_a, scatter_b, gather, line_e, line_r, line_s]
    vmem = pl.BlockSpec(memory_space=pltpu.VMEM)
    outs = [
        (jax.ShapeDtypeStruct(own, F32), ANY),
        (jax.ShapeDtypeStruct(own, F32), ANY),
        (jax.ShapeDtypeStruct(own, BF16), ANY),
        (jax.ShapeDtypeStruct((2, 16, width), F32), vmem),
        (jax.ShapeDtypeStruct((width, half), BF16), ANY),
        (jax.ShapeDtypeStruct((width, half), BF16), ANY),
        (part, ANY),
    ] + line_s.outs
    scratch = [
        pltpu.VMEM((micro_count, face_rows, width), BF16),
        pltpu.VMEM(own, F32),
        pltpu.VMEM(own, F32),
        pltpu.VMEM(own, BF16),
        pltpu.VMEM(own, BF16),
        pltpu.VMEM(own, BF16),
        pltpu.VMEM((micro_count, face_rows, width), BF16),
        pltpu.VMEM((micro_count, face_rows, width), BF16),
        pltpu.VMEM((width, half), BF16),
        pltpu.VMEM((width, half), BF16),
        pltpu.VMEM((units, width), BF16),
        pltpu.VMEM((tokens, units), BF16),
        pltpu.VMEM((tokens, units), BF16),
        pltpu.VMEM((units, width), BF16),
        pltpu.VMEM((tokens, attn), BF16),
        pltpu.VMEM((attn, width), BF16),
    ]
    shared = len(scratch)
    scratch += scatter_a.scratch + line_s.scratch

    def body(net, ins, outs, scratch):
        mixed_in, wo_in, own_in, cot_in, face_in, norms, first_in, *weights_in = ins
        middle_out, grad_out, low_out, norm_out, expand_a, expand_b, reduced_out, reduce_out = outs
        p, branch, middle, own, cot_own, n_own, n_face, cot, we0, we1, wr, active, slope, pr, mixed, wo = scratch[:shared]
        we = (we0, we1)
        slots = list(scratch[shared : shared + len(scatter_a.scratch)])
        line_slots = list(scratch[shared + len(scatter_a.scratch) :])

        loads = [
            net.copy(*pair)
            for pair in (
                (mixed_in, mixed),
                (wo_in, wo),
                (own_in, own),
                (cot_in, cot_own),
                (first_in, we0),
                (face_in, cot),
            )
        ]
        weave = Weave()
        stores = []
        weave.add("e", line_e.run(net, weights_in[:2], [we1], []))
        weave.step("e")
        weave.add("r", line_r.run(net, weights_in[2:], [wr], []))
        weave.step("r")
        for load in loads:
            load.start()

        def branch_tile(at):
            m, n = lax.div(at, width // wide), lax.rem(at, width // wide)
            columns = pl.ds(pl.multiple_of(n * wide, wide), wide)
            rows = pl.ds(pl.multiple_of(m * face_rows, face_rows), face_rows)
            p[m, :, columns] = jnp.dot(mixed[rows, :], wo[:, columns], preferred_element_type=F32).astype(BF16)

        row_steps = own_rows // 16

        def own_rows_at(at):
            return lax.div(at, row_steps), pl.ds(pl.multiple_of(lax.rem(at, row_steps) * 16, 16), 16)

        def norm_rows(at):
            m, rows = own_rows_at(at)
            values = own[m, rows, :].astype(F32) + branch[m, rows, :]
            middle[m, rows, :] = values
            centered = values - jnp.mean(values, axis=-1, keepdims=True)
            spread = lax.rsqrt(jnp.mean(centered * centered, axis=-1, keepdims=True) + EPSILON)
            n_own[m, rows, :] = (centered * spread * norms[2:3, :] + norms[3:4, :]).astype(BF16)

        def hidden_tile(h):
            def tile_at(at):
                m, n = lax.div(at, half // tile), lax.rem(at, half // tile)
                rows = pl.ds(pl.multiple_of(m * face_rows, face_rows), face_rows)
                columns = pl.ds(pl.multiple_of(n * tile, tile), tile)
                into = pl.ds(pl.multiple_of(h * half + n * tile, tile), tile)
                hidden = jnp.dot(n_face[m], we[h][:, columns], preferred_element_type=F32)
                square = hidden * hidden
                bend = jnp.tanh(GELU_A * hidden * (1.0 + GELU_B * square))
                active[rows, into] = (0.5 * hidden * (1.0 + bend)).astype(BF16)
                slope[rows, into] = (
                    0.5 * (1.0 + bend)
                    + (0.5 * GELU_A) * hidden * (1.0 - bend * bend) * (1.0 + (3.0 * GELU_B) * square)
                ).astype(BF16)

            return tile_at

        across = (((0,), (0,)), ((), ()))
        along = (((1,), (1,)), ((), ()))
        def reduce_tile(first):
            def tile_at(at):
                f, n = lax.div(at, width // wide), lax.rem(at, width // wide)
                columns = pl.ds(pl.multiple_of(n * wide, wide), wide)
                rows = pl.ds(pl.multiple_of(first + f * tile, tile), tile)
                pr[rows, columns] = lax.dot_general(
                    active[:, rows],
                    cot[:, :, columns].reshape(tokens, wide),
                    across,
                    preferred_element_type=F32,
                ).astype(BF16)

            return tile_at

        def slope_tile(at):
            m, n = lax.div(at, units // tile), lax.rem(at, units // tile)
            rows = pl.ds(pl.multiple_of(m * face_rows, face_rows), face_rows)
            columns = pl.ds(pl.multiple_of(n * tile, tile), tile)
            grad = lax.dot_general(cot[m], wr[columns, :], along, preferred_element_type=F32)
            slope[rows, columns] = (grad * slope[rows, columns].astype(F32)).astype(BF16)

        def normed_tile(at):
            m, n = lax.div(at, width // wide), lax.rem(at, width // wide)
            rows = pl.ds(pl.multiple_of(m * face_rows, face_rows), face_rows)
            columns = pl.ds(pl.multiple_of(n * wide, wide), wide)
            grad = lax.dot_general(slope[rows, :half], we0[columns, :], along, preferred_element_type=F32)
            grad = grad + lax.dot_general(slope[rows, half:], we1[columns, :], along, preferred_element_type=F32)
            p[m, :, columns] = grad.astype(BF16)

        def reduced_tiles(m):
            def tile_at(n):
                rows = pl.ds(m * face_rows, face_rows)
                columns = pl.ds(pl.multiple_of(n * wide, wide), wide)
                cot[m, :, columns] = jnp.dot(active[rows, :], wr[:, columns], preferred_element_type=F32).astype(BF16)

            def act():
                loop(width // wide, tile_at)
                stores.append(net.copy(cot.at[m], reduced_out.at[m]))
                stores[-1].start()

            return act

        def expand_tiles(h):
            def tile_at(at):
                k, n = lax.div(at, half // tile), lax.rem(at, half // tile)
                rows = pl.ds(pl.multiple_of(k * wide, wide), wide)
                columns = pl.ds(pl.multiple_of(n * tile, tile), tile)
                grads = pl.ds(pl.multiple_of(h * half + n * tile, tile), tile)
                we[h][rows, columns] = lax.dot_general(
                    n_face[:, :, rows].reshape(tokens, wide),
                    slope[:, grads],
                    across,
                    preferred_element_type=F32,
                ).astype(BF16)

            def act():
                loop((width // wide) * (half // tile), tile_at)
                stores.append(net.copy(we[h], (expand_a, expand_b)[h]))
                stores[-1].start()

            return act

        def back_rows(at):
            m, rows = own_rows_at(at)
            values = middle[m, rows, :]
            centered = values - jnp.mean(values, axis=-1, keepdims=True)
            spread = lax.rsqrt(jnp.mean(centered * centered, axis=-1, keepdims=True) + EPSILON)
            unit = centered * spread
            grad = branch[m, rows, :]
            norm_out[0] += grad * unit
            norm_out[1] += grad
            turned = grad * norms[2:3, :]
            inner = jnp.mean(turned * unit, axis=-1, keepdims=True)
            total = cot_own[m, rows, :].astype(F32) + spread * (
                turned - jnp.mean(turned, axis=-1, keepdims=True) - unit * inner
            )
            middle[m, rows, :] = total
            n_own[m, rows, :] = total.astype(BF16)

        def later():
            weave.finish("e")
            for h in (0, 1):
                expand_tiles(h)()
                yield
            for m in range(micro_count):
                reduced_tiles(m)()
                yield

        def main():
            loads[0].wait()
            loads[1].wait()
            loop(micro_count * (width // wide), branch_tile)
            yield
            yield from scatter_a.run(net, [p], [branch], slots)
            loads[2].wait()
            loop(micro_count * row_steps, norm_rows)
            keep_middle = net.copy(middle, middle_out)
            keep_middle.start()
            yield from gather.run(net, [n_own], [n_face], [])
            loads[4].wait()
            loop(micro_count * (half // tile), hidden_tile(0))
            yield
            weave.need("e")
            loop(micro_count * (half // tile), hidden_tile(1))
            yield
            loads[5].wait()
            loop((half // tile) * (width // wide), reduce_tile(0))
            yield
            loop((half // tile) * (width // wide), reduce_tile(half))
            weave.add("s", line_s.run(net, [pr], [reduce_out], line_slots))
            weave.step("s")
            yield
            weave.need("r")
            loop(micro_count * (units // tile), slope_tile)
            yield
            loop(micro_count * (width // wide), normed_tile)
            weave.add("x", later())
            yield from scatter_b.run(net, [p], [branch], slots)
            loads[3].wait()
            keep_middle.wait()
            norm_out[...] = jnp.zeros_like(norm_out)
            loop(micro_count * row_steps, back_rows)
            for pair in ((middle, grad_out), (n_own, low_out)):
                stores.append(net.copy(*pair))
                stores[-1].start()

        weave.add("m", main())
        for name in "".join(MLP_ORDER):
            weave.step(name)
        for name in "mxsre":
            weave.finish(name)
        for store in stores:
            store.wait()

    ins = [mixed, wo, inputs, cotangent, cot_face, norms, wexp_first, *w_expand, *w_reduce]
    specs = [ANY] * 5 + [vmem] + [ANY] * (len(ins) - 6)
    return launch(
        body, ins, specs, outs, scratch, plans, nz, ny, collective_id, "mlp_block", extra_locals=12, vmem=62
    )


def front_block(inputs, cotangent, w_query, w_attn_out, w_keyval, w_expand, norms, doc_ids, nz, ny, collective_id, head_dim):
    micro_count, own_rows, width = inputs.shape
    face_rows = own_rows * 4 * ny
    attn = w_query.shape[1] // 2
    seq_len = nz * face_rows
    blocks = face_rows // BLOCK
    heads = attn // head_dim
    tall = heads * BLOCK
    own = jax.ShapeDtypeStruct(inputs.shape, BF16)
    keys_face = jax.ShapeDtypeStruct((micro_count, face_rows, 2 * head_dim), BF16)
    shard = norms.shape[1] // 4
    norms_own = jax.ShapeDtypeStruct((8, shard), F32)
    plane = PlaneGather(norms_own, nz, ny)
    gather = FaceGather(own, nz, ny)
    gather_c = FaceGather(cotangent, nz, ny, hold_x=True)
    swap_e = HalfSwap([w_expand], ["row"], nz, ny)
    line_a = LineGather([w_keyval, w_query], ["both", "row"], nz, ny)
    line_o = LineGather([w_attn_out], ["col"], nz, ny)
    given = jax.ShapeDtypeStruct((w_expand.shape[0], w_expand.shape[1] // 2), BF16)
    line_e = LineGather([w_expand], ["row"], nz, ny, share=(0, 2), given=[given])
    keys = KeysGather(keys_face, nz, ny)
    plans = [plane, gather, gather_c, swap_e, line_a, line_o, line_e, keys]
    kept = [
        jax.ShapeDtypeStruct((micro_count, face_rows, width), BF16),
        line_a.outs[0][0],
        line_a.outs[1][0],
        given,
        jax.ShapeDtypeStruct((micro_count, face_rows, attn), BF16),
        keys.outs[0][0],
        jax.ShapeDtypeStruct((micro_count, face_rows, attn), BF16),
        jax.ShapeDtypeStruct((micro_count, blocks, 1, tall), F32),
        jax.ShapeDtypeStruct((micro_count, blocks, 2, BLOCK), jnp.int32),
        own,
    ]
    outs = [(shape, ANY) for shape in kept] + [
        (jax.ShapeDtypeStruct((8, width), F32), IN_VMEM),
        gather_c.outs[0],
        line_o.outs[0],
        line_e.outs[0],
    ]
    scratch = [pltpu.VMEM(shape.shape, shape.dtype) for shape in kept] + [
        pltpu.VMEM(keys_face.shape, BF16),
        pltpu.VMEM((8, shard), F32),
        pltpu.VMEM((2 * nz, 8, shard), F32),
    ]

    def body(net, ins, outs, scratch):
        inputs, cotangent, w_query, w_attn_out, w_keyval, w_expand, doc_ids, norms_in = ins
        norm_rows, cot_out, wo_out, first_out = outs[len(kept) :]
        normed, wkv, wq, given, queries, keys_vals, mixed, logs, limits, n_own, keys_face, norms, norms_out = scratch
        norms[...] = jnp.zeros_like(norms)
        for k in range(4):
            norms[k : k + 1, :] = norms_in[:, k * shard : (k + 1) * shard].astype(F32)
        stores = [net.copy(*pair) for pair in zip(scratch, outs[: len(kept)])]
        weave = Weave()
        weave.add("p", plane.run(net, [norms], [norms_out], []))
        weave.step("p")
        weave.add("a", line_a.run(net, [w_keyval, w_query], [wkv, wq], []))
        weave.step("a")
        weave.add("h", swap_e.run(net, [w_expand], [given], []))
        weave.add("o", line_o.run(net, [w_attn_out], [wo_out], []))
        weave.add("c", gather_c.run(net, [cotangent], [cot_out], []))

        def line_first():
            weave.need("h")
            yield from line_e.run(net, [w_expand, given], [first_out], [])

        weave.add("e", line_first())
        along = (((1,), (1,)), ((), ()))
        across = (((0,), (0,)), ((), ()))
        step = min(32, own_rows)

        def own_norm(at):
            m = lax.div(at, own_rows // step)
            rows = pl.ds(pl.multiple_of(lax.rem(at, own_rows // step) * step, step), step)
            gain, shift = norm_rows[0:1, :], norm_rows[1:2, :]
            values = inputs[m, rows, :].astype(F32)
            centered = values - jnp.mean(values, axis=-1, keepdims=True)
            spread = lax.rsqrt(jnp.mean(centered * centered, axis=-1, keepdims=True) + EPSILON)
            n_own[m, rows, :] = (centered * spread * gain + shift).astype(BF16)

        def keys_tile(m):
            keys_face[m] = jnp.dot(normed[m], wkv[...], preferred_element_type=F32).astype(BF16)

        def queries_tile(m):
            queries[m] = jnp.dot(normed[m], wq[...], preferred_element_type=F32).astype(BF16)

        def mixed_tile(m):
            def tile_at(b):
                rows = pl.ds(pl.multiple_of(b * BLOCK, BLOCK), BLOCK)
                query = jnp.concatenate(
                    [queries[m, rows, h * head_dim : (h + 1) * head_dim] for h in range(heads)], axis=0
                )
                starts = jnp.concatenate([limits[m, b, 0:1, :]] * heads, axis=1)
                ends = jnp.concatenate([limits[m, b, 1:2, :]] * heads, axis=1)
                place = lax.broadcasted_iota(jnp.int32, (BLOCK, tall), 0)

                def body(block, carry):
                    top, total, out = carry
                    first = pl.multiple_of(block * BLOCK, BLOCK)
                    keys = keys_vals[m, pl.ds(first, BLOCK), :head_dim]
                    values = keys_vals[m, pl.ds(first, BLOCK), head_dim:]
                    raw = lax.dot_general(keys, query, along, preferred_element_type=F32)
                    allowed = (place >= starts - first) & (place < ends - first)
                    scores = jnp.where(allowed, raw * (LOG2_E / math.sqrt(head_dim)), NEG_FILL)
                    new_top = jnp.maximum(top, jnp.max(scores, axis=0, keepdims=True))
                    weights = jnp.exp2(scores - new_top)
                    fade = jnp.exp2(top - new_top)
                    total = total * fade + jnp.sum(weights, axis=0, keepdims=True)
                    out = out * fade + lax.dot_general(
                        values, weights.astype(BF16), across, preferred_element_type=F32
                    )
                    return new_top, total, out

                top, total, out = lax.fori_loop(
                    first_block(net.z * blocks + b, seq_len),
                    net.z * blocks + b + 1,
                    body,
                    (
                        jnp.full((1, tall), NEG_FILL, F32),
                        jnp.zeros((1, tall), F32),
                        jnp.zeros((head_dim, tall), F32),
                    ),
                )
                out = jnp.transpose(out / total).astype(BF16)
                for h in range(heads):
                    mixed[m, rows, h * head_dim : (h + 1) * head_dim] = out[h * BLOCK : (h + 1) * BLOCK]
                logs[m, b] = top + jnp.log2(total)

            return tile_at

        def limits_tile(m):
            kinds = lax.broadcasted_iota(jnp.int32, (32, 1), 0)
            counts = jnp.sum((doc_ids[m : m + 1, :] == kinds).astype(F32), axis=1, keepdims=True)
            for b in range(blocks):
                first = pl.multiple_of(net.z * face_rows + b * BLOCK, BLOCK)
                docs = doc_ids[m : m + 1, pl.ds(first, BLOCK)]
                starts = jnp.sum(jnp.where(kinds < docs, counts, 0.0), axis=0, keepdims=True)
                ends = jnp.sum(jnp.where(kinds <= docs, counts, 0.0), axis=0, keepdims=True)
                limits[m, b, 0:1, :] = starts.astype(jnp.int32)
                limits[m, b, 1:2, :] = ends.astype(jnp.int32)

        def main():
            weave.finish("p")
            norm_rows[...] = jnp.concatenate([norms_out[d] for d in range(2 * nz)], axis=1)
            loop(micro_count * (own_rows // step), own_norm)
            stores[9].start()
            yield from gather.run(net, [n_own], [normed], [])
            stores[0].start()
            for m in range(micro_count):
                limits_tile(m)
            stores[8].start()
            yield
            weave.need("a")
            loop(micro_count, keys_tile)
            weave.add("k", keys.run(net, [keys_face], [keys_vals], []))
            weave.step("k")
            yield
            for at in (1, 2):
                stores[at].start()
            loop(micro_count, queries_tile)
            stores[4].start()
            yield
            weave.need("k")
            stores[5].start()
            for m in range(micro_count):
                loop(blocks, mixed_tile(m))
                yield
            for at in (6, 7):
                stores[at].start()

        weave.add("m", main())
        for name in "".join(FRONT_ORDER):
            weave.step(name)
        for name in "mhcoeak":
            weave.finish(name)
        stores[3].start()
        for store in stores:
            store.wait()

    ins = [inputs, cotangent, w_query, w_attn_out, w_keyval, w_expand, doc_ids, norms]
    results = launch(
        body, ins, [IN_VMEM] * len(ins), outs, scratch, plans, nz, ny, collective_id, "front_block", extra_locals=len(kept)
    )
    return results[: len(kept)], results[len(kept) :]


def back_block(low, reduced, parts, mixed, wo, wq, normed, queries, keys_vals, logs, limits, nz, ny, collective_id, head_dim):
    micro_count, own_rows, width = low.shape
    face_rows, attn = queries.shape[1:]
    seq_len = keys_vals.shape[1]
    tokens = micro_count * face_rows
    blocks = face_rows // BLOCK
    heads = attn // head_dim
    tall = heads * BLOCK
    scale = 1.0 / math.sqrt(head_dim)
    wide = 512
    half = parts[0].shape[1]
    part = jax.ShapeDtypeStruct((micro_count, face_rows, width), BF16)
    gather = FaceGather(low, nz, ny)
    scatter_r = FaceScatter(reduced, nz, ny)
    scatter_q = FaceScatter(part, nz, ny, resident=True)
    whole = WholeScatter(jax.ShapeDtypeStruct((micro_count, nz, face_rows, 2 * head_dim), BF16), nz, ny, resident=True)
    line_e = LineScatter(parts, ["row", "row"], nz, ny, resident=True, joined=True)
    attn_parts = [jax.ShapeDtypeStruct((attn, width), BF16), jax.ShapeDtypeStruct((width, attn), BF16)]
    line_a = LineScatter(attn_parts, ["col", "row"], nz, ny, resident=True)
    plans = [gather, scatter_r, scatter_q, whole, line_e, line_a]
    groups = [scatter_r, scatter_q, whole, line_e, line_a]
    outs = scatter_r.outs + scatter_q.outs + whole.outs + line_e.outs + line_a.outs
    normed = normed.reshape(micro_count, face_rows, width)
    given = [mixed, wo, wq, queries, keys_vals, logs, limits, *parts]
    scratch = [pltpu.VMEM(entry.shape, entry.dtype) for entry in given] + [
        pltpu.VMEM(part.shape, BF16),
        pltpu.VMEM(queries.shape, BF16),
        pltpu.VMEM(queries.shape, BF16),
        pltpu.VMEM((seq_len, 2 * head_dim), F32),
        pltpu.VMEM((micro_count * nz, face_rows, 2 * head_dim), BF16),
        pltpu.VMEM((attn, width), BF16),
        pltpu.VMEM((width, attn), BF16),
        pltpu.VMEM((2, micro_count, face_rows, wide), BF16),
    ]
    shared = len(scratch)
    for plan in groups:
        scratch = scratch + plan.scratch

    def body(net, ins, outs, scratch):
        low, reduced_in, normed_in, *given_in = ins
        reduced_out, from_out, keys_out, *line_outs = outs
        mixed, wo, wq, queries, keys_vals, logs, limits, *expand = scratch[: len(given)]
        face, grad_mixed, grad_queries, acc, grad_keys, part_out, part_query, normed = scratch[len(given) : shared]
        slots, first = {}, shared
        for name, plan in zip("rqwea", groups):
            slots[name] = list(scratch[first : first + len(plan.scratch)])
            first += len(plan.scratch)
        loads = [net.copy(*pair) for pair in zip(given_in, scratch)]
        order = [len(given) - 2, len(given) - 1] + list(range(len(given) - 2))
        weave = Weave()
        along = (((1,), (1,)), ((), ()))
        across = (((0,), (0,)), ((), ()))

        def mix_tile(m):
            grad_mixed[m] = lax.dot_general(face[m], wo[...], along, preferred_element_type=F32).astype(BF16)

        def attn_out_tile(n):
            columns = pl.ds(pl.multiple_of(n * wide, wide), wide)
            part_out[:, columns] = lax.dot_general(
                mixed[...].reshape(tokens, attn),
                face[:, :, columns].reshape(tokens, wide),
                across,
                preferred_element_type=F32,
            ).astype(BF16)

        def attn_tile(m):
            def tile_at(b):
                rows = pl.ds(pl.multiple_of(b * BLOCK, BLOCK), BLOCK)

                def stack(ref):
                    return jnp.concatenate(
                        [ref[m, rows, h * head_dim : (h + 1) * head_dim] for h in range(heads)], axis=0
                    )

                query, grad = stack(queries), stack(grad_mixed)
                products = grad.astype(F32) * stack(mixed).astype(F32)
                delta = jnp.sum(jnp.transpose(products), axis=0, keepdims=True)
                starts = jnp.concatenate([limits[m, b, 0:1, :]] * heads, axis=1)
                ends = jnp.concatenate([limits[m, b, 1:2, :]] * heads, axis=1)
                log_total = logs[m, b]
                place = lax.broadcasted_iota(jnp.int32, (BLOCK, tall), 0)

                def body(block, grad_query):
                    first = pl.multiple_of(block * BLOCK, BLOCK)
                    keys = keys_vals[m, pl.ds(first, BLOCK), :head_dim]
                    values = keys_vals[m, pl.ds(first, BLOCK), head_dim:]
                    raw = lax.dot_general(keys, query, along, preferred_element_type=F32)
                    allowed = (place >= starts - first) & (place < ends - first)
                    probs = jnp.where(allowed, jnp.exp2(raw * (LOG2_E * scale) - log_total), 0.0)
                    grad_probs = lax.dot_general(values, grad, along, preferred_element_type=F32)
                    grad_scores = (probs * (grad_probs - delta)).astype(BF16)
                    acc[pl.ds(first, BLOCK), :head_dim] += (
                        jnp.dot(grad_scores, query, preferred_element_type=F32) * scale
                    )
                    acc[pl.ds(first, BLOCK), head_dim:] += jnp.dot(
                        probs.astype(BF16), grad, preferred_element_type=F32
                    )
                    return grad_query + lax.dot_general(keys, grad_scores, across, preferred_element_type=F32)

                grad_query = lax.fori_loop(
                    first_block(net.z * blocks + b, seq_len),
                    net.z * blocks + b + 1,
                    body,
                    jnp.zeros((head_dim, tall), F32),
                )
                grad_query = jnp.transpose(grad_query * scale).astype(BF16)
                for h in range(heads):
                    grad_queries[m, rows, h * head_dim : (h + 1) * head_dim] = grad_query[h * BLOCK : (h + 1) * BLOCK]

            return tile_at

        def from_tile(at):
            m, n = lax.div(at, width // wide), lax.rem(at, width // wide)
            columns = pl.ds(pl.multiple_of(n * wide, wide), wide)
            face[m, :, columns] = lax.dot_general(
                grad_queries[m], wq[columns, :], along, preferred_element_type=F32
            ).astype(BF16)

        columns_in = [
            net.copy(normed_in.at[:, :, pl.ds(n * wide, wide)], normed.at[n % 2]) for n in range(width // wide)
        ]

        def query_tile(n):
            columns_in[n].wait()

            def tile_at(_):
                part_query[n * wide : (n + 1) * wide, :] = lax.dot_general(
                    normed[n % 2].reshape(tokens, wide),
                    grad_queries[...].reshape(tokens, attn),
                    across,
                    preferred_element_type=F32,
                ).astype(BF16)

            loop(1, tile_at)
            if n + 2 < width // wide:
                columns_in[n + 2].start()

        def main():
            yield from gather.run(net, [low], [face], [])
            for at in order[2:]:
                loads[at].wait()
            loop(micro_count, mix_tile)
            yield
            for m in range(micro_count):
                acc[...] = jnp.zeros_like(acc)
                loop(blocks, attn_tile(m))
                for k in range(nz):
                    grad_keys[m * nz + k] = acc[k * face_rows : (k + 1) * face_rows, :].astype(BF16)
                yield
            loop(width // wide, attn_out_tile)
            weave.add("w", whole.run(net, [grad_keys], [keys_out], slots["w"]))
            weave.step("w")
            loop(micro_count * (width // wide), from_tile)
            weave.add("q", scatter_q.run(net, [face], [from_out], slots["q"]))
            weave.step("q")
            for n in range(width // wide):
                query_tile(n)
            weave.add("a", line_a.run(net, [part_out, part_query], line_outs[1:], slots["a"]))
            weave.step("a")

        weave.add("m", main())
        weave.step("m")
        for at in order:
            loads[at].start()
        for copy in columns_in[:2]:
            copy.start()
        for at in order[:2]:
            loads[at].wait()
        weave.add("e", line_e.run(net, expand, line_outs[:1], slots["e"]))
        weave.step("e")
        weave.add("r", scatter_r.run(net, [reduced_in], [reduced_out], slots["r"]))
        for name in "".join(BACK_ORDER):
            weave.step(name)
        for name in "mwqrea":
            weave.finish(name)

    ins = [low, reduced, normed, *given]
    specs = [IN_VMEM] + [ANY] * (len(ins) - 1)
    return launch(
        body, ins, specs, outs, scratch, plans, nz, ny, collective_id, "back_block", extra_locals=len(given) + width // wide, vmem=62
    )


def end_block(inputs, normed_own, grad_middle, from_query, grad_keys, wkv, norms, grad_norm_two, nz, ny, collective_id):
    micro_count, own_rows, width = inputs.shape
    rows_all = micro_count * own_rows
    side = grad_keys.shape[-1]
    ranks = 4 * ny
    own_width = width // (nz * ranks)
    step = min(32, own_rows)
    part = jax.ShapeDtypeStruct((nz, width // nz, side), BF16)
    small = jax.ShapeDtypeStruct((ranks, nz, 8, 128), F32)
    quick, tiny = QuickScatter(part, nz, ny), SmallScatter(small, nz, ny)
    plans = [quick, tiny]
    outs = [(jax.ShapeDtypeStruct(inputs.shape, F32), IN_VMEM)] + quick.outs + tiny.outs
    scratch = [
        pltpu.VMEM((rows_all, side), BF16),
        pltpu.VMEM(part.shape, BF16),
        pltpu.VMEM(small.shape, F32),
        pltpu.VMEM((2, step, width), F32),
    ] + quick.scratch + tiny.scratch

    def body(net, ins, outs, scratch):
        inputs, n_own, grad_middle, from_query, grad_keys, wkv, norms, grad_norm_two = ins
        grad_out, keyval_out, small_out = outs
        low_keys, part, small, sums, *slots = scratch
        weave = Weave()

        def place(at):
            m, first = lax.div(at, own_rows // step), lax.rem(at, own_rows // step) * step
            rows = pl.ds(pl.multiple_of(first, step), step)
            return m, rows, pl.ds(pl.multiple_of(at * step, step), step)

        def unit_rows(m, rows):
            values = inputs[m, rows, :].astype(F32)
            centered = values - jnp.mean(values, axis=-1, keepdims=True)
            spread = lax.rsqrt(jnp.mean(centered * centered, axis=-1, keepdims=True) + EPSILON)
            return centered * spread, spread

        def first_rows(at):
            m, rows, flat = place(at)
            low_keys[flat, :] = grad_keys[m, rows, :].astype(BF16)

        def keyval_tile(k):
            columns = pl.ds(pl.multiple_of(k * (width // nz), width // nz), width // nz)
            part[k] = lax.dot_general(
                n_own[:, :, columns].reshape(rows_all, width // nz),
                low_keys[...],
                (((0,), (0,)), ((), ())),
                preferred_element_type=F32,
            ).astype(BF16)

        def last_rows(at):
            m, rows, flat = place(at)
            unit, spread = unit_rows(m, rows)
            grad = from_query[m, rows, :] + lax.dot_general(
                low_keys[flat, :], wkv[...], (((1,), (1,)), ((), ())), preferred_element_type=F32
            )
            sums[0] += grad * unit
            sums[1] += grad
            turned = grad * norms[0:1, :]
            inner = jnp.mean(turned * unit, axis=-1, keepdims=True)
            grad_out[m, rows, :] = grad_middle[m, rows, :] + spread * (
                turned - jnp.mean(turned, axis=-1, keepdims=True) - unit * inner
            )

        count = rows_all // step
        loop(count, first_rows)
        loop(nz, keyval_tile)
        weave.add("q", quick.run(net, [part], [keyval_out], slots[: len(quick.scratch)]))
        for _ in range(2 * ny + 1):
            weave.step("q")
        sums[...] = jnp.zeros_like(sums)
        loop(count, last_rows)
        rows = [jnp.sum(sums[k], axis=0, keepdims=True) for k in (0, 1)]
        rows += [jnp.sum(grad_norm_two[k], axis=0, keepdims=True) for k in (0, 1)]
        rows = jnp.concatenate(rows + [jnp.zeros((4, width), F32)], axis=0)
        for line in range(nz):
            for rank in range(ranks):
                first = (line * ranks + rank) * own_width // 128 * 128
                small[rank, line] = rows[:, first : first + 128]
        weave.add("s", tiny.run(net, [small], [small_out], slots[len(quick.scratch) :]))
        for name in "sqsqs":
            weave.step(name)
        for name in "qs":
            weave.finish(name)

    ins = [inputs, normed_own, grad_middle, from_query, grad_keys, wkv, norms, grad_norm_two]
    return launch(body, ins, [IN_VMEM] * len(ins), outs, scratch, plans, nz, ny, collective_id, "end_block")


def local(
    inputs,
    cotangent,
    doc_ids,
    attn_gain,
    attn_shift,
    w_query,
    w_keyval,
    w_attn_out,
    mlp_gain,
    mlp_shift,
    w_expand,
    w_reduce,
):
    nz = lax.axis_size("dp") // 2
    tensor_count = lax.axis_size("tensor")
    ny = tensor_count // 2
    ranks = 2 * tensor_count
    micro_count, own_rows, width = inputs.shape
    face_rows = own_rows * ranks
    tokens = micro_count * face_rows
    seq_len = doc_ids.shape[1]
    head_dim = w_keyval.shape[1] // 2
    heads = w_query.shape[1] // (2 * head_dim)
    on = (nz, ny)

    gains = jnp.concatenate([attn_gain, attn_shift, mlp_gain, mlp_shift])[None, :]
    kept, rest = front_block(
        inputs,
        cotangent,
        w_query,
        w_attn_out,
        w_keyval,
        w_expand,
        gains,
        doc_ids,
        *on,
        collective_id=1,
        head_dim=head_dim,
    )
    normed, wkv, wq, expand_given, queries, keys_vals, mixed, log_total, limits, normed_own = kept
    norms, cot_face, wo, wexp_first = rest
    mixed_flat = mixed.reshape(tokens, heads * head_dim)
    middle, grad_middle, low_middle, grad_norm_two, part_expand_a, part_expand_b, reduced, grad_reduce = mlp_block(
        mixed_flat, wo, inputs, cotangent, cot_face, norms, wexp_first, (w_expand, expand_given), (w_reduce,), *on, collective_id=3
    )
    reduced, from_query, grad_keys, grad_expand, grad_attn_out, grad_query = back_block(
        low_middle,
        reduced,
        [part_expand_a, part_expand_b],
        mixed,
        wo,
        wq,
        normed,
        queries,
        keys_vals,
        log_total,
        limits,
        *on,
        collective_id=6,
        head_dim=head_dim,
    )
    outputs = (middle + reduced).astype(BF16)
    grad_inputs, grad_keyval, small = end_block(
        inputs, normed_own, grad_middle, from_query, grad_keys, wkv, norms, grad_norm_two, *on, collective_id=8
    )
    own_width = width // (nz * ranks)
    device = lax.axis_index("dp") * tensor_count + lax.axis_index("tensor")
    small = lax.dynamic_slice_in_dim(small[:4], device * own_width % 128, own_width, axis=1)

    return (
        outputs,
        grad_inputs,
        small[0],
        small[1],
        grad_query.astype(F32),
        grad_keyval,
        grad_attn_out.astype(F32),
        small[2],
        small[3],
        grad_expand.astype(F32),
        grad_reduce.astype(F32),
    )


def solution(mesh):
    placed = (
        P(None, ("dp", "tensor"), None),
        P(None, ("dp", "tensor"), None),
        P(),
        P("dp"),
        P("dp"),
        P("dp", "tensor"),
        P("dp", None),
        P("tensor", "dp"),
        P("dp"),
        P("dp"),
        P("dp", "tensor"),
        P("tensor", "dp"),
    )
    return jax.shard_map(
        local,
        mesh=mesh,
        in_specs=placed,
        out_specs=(
            P(None, ("dp", "tensor"), None),
            P(None, ("dp", "tensor"), None),
            P(("dp", "tensor")),
            P(("dp", "tensor")),
            P("dp", "tensor"),
            P(("dp", "tensor"), None),
            P("tensor", "dp"),
            P(("dp", "tensor")),
            P(("dp", "tensor")),
            P("dp", "tensor"),
            P("tensor", "dp"),
        ),
        check_vma=False,
    )
```

```python
import functools
import math

import jax
import jax.numpy as jnp
from jax import lax
from jax.experimental import pallas as pl
from jax.experimental.pallas import tpu as pltpu
from jax.sharding import PartitionSpec as P

BLOCK = 256
EPSILON = 1e-05
NEG_FILL = -1e30
GELU_A = math.sqrt(2.0 / math.pi)
GELU_B = 0.044715
LOG2_E = 1.0 / math.log(2.0)
MLP_ORDER = ("memmmmeemmrmememmmrmmmmrmmrmmmmmmemmmsxs", "mmmmxxsxxrmm",)
BACK_ORDER = ("mremmmrrrrmemmmerrmmeemwqqwaawwwqqaqqwaa", "qwearwaerw",)
FRONT_ORDER = ("omaoaaamaaamcoaammhaaommommokkmekecaceme", "ckceme",)
MESH = pl.DeviceIdType.MESH
ANY = pl.BlockSpec(memory_space=pl.ANY)
READY = "ready"
IN_VMEM = pl.BlockSpec(memory_space=pltpu.VMEM)
BF16 = jnp.bfloat16
F32 = jnp.float32


def layer_norm(values, gain, shift):
    center = jnp.mean(values, axis=-1, keepdims=True)
    centered = values - center
    variance = jnp.mean(centered * centered, axis=-1, keepdims=True)
    return centered * lax.rsqrt(variance + EPSILON) * gain + shift


def gelu_tanh(values):
    return jax.nn.gelu(values, approximate=True)


class Net:
    def __init__(self, nz, ny, send, recv, local):
        dp, tensor = lax.axis_index("dp"), lax.axis_index("tensor")
        self.nz, self.ny = nz, ny
        self.z, self.x = lax.div(dp, 2), lax.rem(dp, 2)
        self.y, self.c = lax.div(tensor, 2), lax.rem(tensor, 2)
        self.tensor = tensor
        self.send, self.recv, self.local = send, recv, local
        self.used = [0, 0]
        self.keys = {}

    def flip(self, value, by):
        return value + by - 2 * by * value if by else value

    def xy(self, dx, dy):
        return self.flip(self.x, dx), lax.rem(self.y + dy, self.ny) if dy else self.y

    def rank(self, dx=0, dy=0, dc=0):
        x, y = self.xy(dx, dy)
        return x * (2 * self.ny) + y * 2 + self.flip(self.c, dc)

    def chip_rows(self, dx, dy, rows):
        first = (self.rank(dx, dy) - self.c) * rows
        return pl.ds(pl.multiple_of(first, 2 * rows), 2 * rows)

    def device(self, dx=0, dy=0, dc=0, z=None):
        x, y = self.xy(dx, dy)
        return ((self.z if z is None else z) * 2 + x, y * 2 + self.flip(self.c, dc))

    def slot(self, key):
        if key not in self.keys:
            self.keys[key] = self.used[0]
            self.used[0] += 1
        return self.keys[key]

    def remote(self, key, src, dst, device):
        at = self.slot(key)
        return pltpu.make_async_remote_copy(
            src_ref=src,
            dst_ref=dst,
            send_sem=self.send.at[at],
            recv_sem=self.recv.at[at],
            device_id=device,
            device_id_type=MESH,
        )

    def take_locals(self, count):
        first = self.used[1]
        self.used[1] += count
        return first

    def copy_at(self, at, src, dst):
        return pltpu.make_async_copy(src, dst, self.local.at[at])

    def copy(self, src, dst):
        return self.copy_at(self.take_locals(1), src, dst)


def add_rows(dst, terms):
    lead, height, width = dst.shape
    rows = min(max(16, 32768 // width), height)
    steps = height // rows

    def body(step, carry):
        at, off = lax.div(step, steps), pl.multiple_of(lax.rem(step, steps) * rows, rows)
        total = terms[0][at, pl.ds(off, rows), :].astype(F32)
        for term in terms[1:]:
            total = total + term[at, pl.ds(off, rows), :].astype(F32)
        dst[at, pl.ds(off, rows), :] = total.astype(dst.dtype)
        return carry

    lax.fori_loop(0, lead * steps, body, 0)


class FaceGather:
    moves = ("x", "y", "c")
    in_spec = IN_VMEM

    def __init__(self, own, nz, ny, hold_x=False, report=False):
        self.ins, self.hold_x, self.report = [own], hold_x, report
        m, t, d = own.shape
        self.outs = [(jax.ShapeDtypeStruct((m, 4 * ny * t, d), own.dtype), ANY)]
        self.scratch = []
        self.half = t // 2
        self.remotes, self.locals = 8 * ny, 1

    def run(self, net, ins, outs, scratch):
        (own,), (out,), half = ins, outs, self.half
        dys = range(1, net.ny)

        def piece(dx, dy, h):
            return out.at[:, pl.ds(pl.multiple_of(net.rank(dx, dy) * 2 * half + h * half, half), half), :]

        mine = [own.at[:, pl.ds(h * half, half), :] for h in (0, 1)]
        keep = net.copy(own, out.at[:, pl.ds(pl.multiple_of(net.rank() * 2 * half, half), 2 * half), :])
        keep.start()
        sent = {}

        def send(key, src, dst, device):
            sent[key] = net.remote((id(self), key), src, dst, device)
            sent[key].start()

        if not self.hold_x:
            send(("x", 0), mine[0], piece(0, 0, 0), net.device(1, 0))
        for dy in dys:
            send(("y", dy, 1), mine[1], piece(0, 0, 1), net.device(0, dy))
        if not self.hold_x:
            send(("x", 1), mine[1], piece(0, 0, 1), net.device(1, 0))
        for dy in dys:
            send(("y", dy, 0), mine[0], piece(0, 0, 0), net.device(0, dy))
        for h in (0, 1):
            send(("c", h), mine[h], piece(0, 0, h), net.device(0, 0, 1))
        if self.hold_x:
            yield
            for h in (0, 1):
                send(("x", h), mine[h], piece(0, 0, h), net.device(1, 0))

        def share(key, dx, dy, h):
            send(("c",) + key, piece(dx, dy, h), piece(dx, dy, h), net.device(0, 0, 1))

        def from_x(h):
            sent["x", h].wait_recv()
            if not h:
                for dy in dys:
                    send(("xy", dy), piece(1, 0, 0), piece(1, 0, 0), net.device(0, dy))
            share(("x", h), 1, 0, h)

        def from_y(dy, h):
            sent["y", dy, h].wait_recv()
            if h:
                send(("yx", dy), piece(0, -dy % net.ny, 1), piece(0, -dy % net.ny, 1), net.device(1, 0))
            share(("y", dy, h), 0, -dy % net.ny, h)

        arrivals = []
        for first in (True, False):
            on_x = [functools.partial(from_x, 0 if first else 1)]
            on_y = [functools.partial(from_y, dy, 1 if first else 0) for dy in dys]
            arrivals.append(on_x + on_y)
        if self.hold_x:
            arrivals = [arrivals[0][1:], arrivals[1][1:], arrivals[0][:1], arrivals[1][:1]]
        waited = set()

        def shared(*keys):
            for key in keys:
                sent[("c",) + key].wait_recv()
                waited.add(("c",) + key)

        if self.report:
            yield
            keep.wait()
            shared((0,), (1,))
            yield (0, 0)
        for group in arrivals:
            for arrive in group:
                yield
                arrive()
        if self.report:
            shared(("x", 0), ("x", 1))
            yield (1, 0)
            for dy in dys:
                shared(("y", dy, 1), ("y", dy, 0))
                yield (0, -dy % net.ny)
        for dy in dys:
            yield
            sent["xy", dy].wait_recv()
            share(("xy", dy), 1, -dy % net.ny, 0)
            yield
            sent["yx", dy].wait_recv()
            share(("yx", dy), 1, -dy % net.ny, 1)
        yield
        for key, copy in sent.items():
            if key[0] == "c" and key not in waited:
                copy.wait_recv()
        if self.report:
            for dy in dys:
                yield (1, -dy % net.ny)
        else:
            keep.wait()
        for copy in sent.values():
            copy.wait_send()


class FaceScatter:
    moves = ("x", "y", "c")

    def __init__(self, part, nz, ny, resident=False):
        self.ins, self.resident = [part], resident
        m, rows, d = part.shape
        t = rows // (4 * ny)
        self.outs = [(jax.ShapeDtypeStruct((m, t, d), F32), pl.BlockSpec(memory_space=pltpu.VMEM))]
        half = t // 2
        self.half = half
        self.scratch = [
            pltpu.VMEM((2 * ny, m, t, d), BF16),
            pltpu.VMEM((ny - 1, m, half, d), BF16),
            pltpu.VMEM((ny - 1, m, half, d), BF16),
            pltpu.VMEM((2, m, half, d), BF16),
            pltpu.VMEM((2, ny - 1, m, half, d), BF16),
        ]
        if not resident:
            self.scratch.append(pltpu.VMEM((2 * ny, m, t, d), BF16))
        self.remotes, self.locals = 6 * ny + 4, 2 * ny

    def run(self, net, ins, outs, scratch, produce=None):
        (part,), (out,), half = ins, outs, self.half
        from_core, x_diag, y_diag, x_in, y_in = scratch[:5]
        ny = net.ny
        dys = range(1, ny)
        order = [(1, dy) for dy in dys] + [(1, 0)] + [(0, dy) for dy in dys] + [(0, 0)]
        sent, loads = {}, {}

        def send(key, src, dst, device):
            sent[key] = net.remote((id(self), key), src, dst, device)
            sent[key].start()

        def rows(dx, dy, dc, first=0, size=2 * half):
            at = net.rank(dx, dy, dc) * 2 * half + first
            return part.at[:, pl.ds(pl.multiple_of(at, half), size), :]

        def work(dx, dy, first=0, size=2 * half):
            if self.resident:
                return rows(dx, dy, 0, first, size)
            return scratch[5].at[dx * ny + dy, :, pl.ds(first, size), :]

        def begin(dx, dy):
            at = dx * ny + dy
            if not self.resident:
                loads[at] = net.copy(rows(dx, dy, 0), work(dx, dy))
                loads[at].start()
            send(("c", at), rows(dx, dy, 1), from_core.at[at], net.device(0, 0, 1))

        def settle(dx, dy):
            at = dx * ny + dy
            if not self.resident:
                loads[at].wait()
            sent["c", at].wait_recv()
            add_rows(work(dx, dy), [work(dx, dy), from_core.at[at]])
            top, low = work(dx, dy, 0, half), work(dx, dy, half, half)
            if dx and dy:
                send(("xd", dy), top, x_diag.at[dy - 1], net.device(1, 0))
                send(("yd", dy), low, y_diag.at[dy - 1], net.device(0, dy))
            elif dx:
                send(("x", 0), top, x_in.at[0], net.device(1, 0))
            elif dy:
                send(("y", dy, 1), low, y_in.at[1, dy - 1], net.device(0, dy))

        for at, place in enumerate(order):
            if produce is not None:
                produce(*place)
            begin(*place)
            if produce is not None:
                yield
                if at:
                    settle(*order[at - 1])
        for place in order if produce is None else order[-1:]:
            yield
            settle(*place)
        for dy in dys:
            yield
            sent["xd", dy].wait_recv()
            top = work(0, dy, 0, half)
            add_rows(top, [top, x_diag.at[dy - 1]])
            send(("y", dy, 0), top, y_in.at[0, dy - 1], net.device(0, dy))
        low = work(1, 0, half, half)
        for dy in dys:
            yield
            sent["yd", dy].wait_recv()
            add_rows(low, [low, y_diag.at[dy - 1]])
        send(("x", 1), low, x_in.at[1], net.device(1, 0))
        for h in (0, 1):
            yield
            sent["x", h].wait_recv()
            for dy in dys:
                sent["y", dy, h].wait_recv()
            add_rows(
                out.at[:, pl.ds(h * half, half), :],
                [work(0, 0, h * half, half), x_in.at[h]] + [y_in.at[h, dy - 1] for dy in dys],
            )
        for copy in sent.values():
            copy.wait_send()


class LineGather:
    moves = ("x", "line", "c")
    in_spec = IN_VMEM

    def __init__(self, shards, kinds, nz, ny, share=(0, 1), given=()):
        self.ins, self.kinds, self.share = list(shards) + list(given), list(kinds), share
        self.outs, self.scratch = [], []
        for shard, kind in zip(shards, kinds):
            rows, columns = shard.shape
            if kind == "row":
                shape = (rows * 2 * nz, columns // 2 // share[1])
            elif kind == "col":
                shape = (rows // 2 // share[1], columns * 2 * nz)
            else:
                shape = (rows * 2 * nz, columns)
            self.outs.append((jax.ShapeDtypeStruct(shape, shard.dtype), ANY))
        count = len(self.kinds)
        self.remotes = count * (1 + 4 * (nz - 1)) + kinds.count("both") * (1 + 4 * (nz - 1))
        self.locals = 2 * count

    def run(self, net, ins, outs, scratch):
        nz, z = net.nz, net.z
        sent, locals_, shared = [], [], []
        weights = []
        given = ins[len(self.kinds) :]
        for at, (shard, out, kind) in enumerate(zip(ins, outs, self.kinds)):
            rows, columns = shard.shape

            if kind == "row":
                span = columns // 2 // self.share[1]

                def mine(dx, shard=shard, span=span):
                    first = (net.flip(net.x, dx) * self.share[1] + self.share[0]) * span
                    return shard.at[:, pl.ds(pl.multiple_of(first, span), span)]

                def block(line, dx, out=out, rows=rows):
                    first = (line * 2 + net.flip(net.x, dx)) * rows
                    return out.at[pl.ds(pl.multiple_of(first, rows), rows), :]

            elif kind == "col":
                span = rows // 2 // self.share[1]

                def mine(dx, shard=shard, span=span):
                    first = (net.flip(net.x, dx) * self.share[1] + self.share[0]) * span
                    return shard.at[pl.ds(pl.multiple_of(first, span), span), :]

                def block(line, dx, out=out, columns=columns):
                    first = (line * 2 + net.flip(net.x, dx)) * columns
                    return out.at[:, pl.ds(pl.multiple_of(first, columns), columns)]

            else:
                half = rows // 2

                def mine(dx, shard=shard, half=half):
                    return shard.at[pl.ds(pl.multiple_of(net.c * half, half), half), :]

                def block(line, dx, out=out, rows=rows, half=half):
                    first = (line * 2 + net.flip(net.x, dx)) * rows + net.c * half
                    return out.at[pl.ds(pl.multiple_of(first, half), half), :]

            weights.append((at, kind, mine, block))

        def hop(at, dx, step, up, block, src=None):
            origin = z - (step - 1) if up else z + (step - 1)
            there = z + 1 if up else z - 1
            copy = net.remote(
                (id(self), at, dx, step, up),
                block(origin, dx) if src is None else src,
                block(origin, dx),
                net.device(z=there),
            )
            fits = (origin >= 0) & (there < nz) if up else (origin < nz) & (there >= 0)
            return copy, fits

        def start(at, dx, step, up, block, src=None):
            copy, fits = hop(at, dx, step, up, block, src)
            pl.when(fits)(copy.start)
            sent.append((copy, fits))

        def arrived(at, dx, step, up, block, kind):
            copy, _ = hop(at, dx, step, up, block)
            origin = z - step if up else z + step
            fits = origin >= 0 if up else origin < nz
            pl.when(fits)(copy.wait_recv)
            if kind == "both":
                share = net.remote(
                    (id(self), "c", at, dx, step, up), block(origin, dx), block(origin, dx), net.device(0, 0, 1)
                )
                pl.when(fits)(share.start)
                shared.append((share, fits))

        swaps = {}
        for at, kind, mine, block in weights:
            if not given:
                swaps[at] = net.remote((id(self), at, "x"), mine(1), block(z, 0), net.device(1, 0))
                swaps[at].start()
            for up in (True, False):
                start(at, 0, 1, up, block, mine(0))
        for at, kind, mine, block in weights:
            if kind == "both":
                whole = ins[at].shape[0]
                into = outs[at].at[pl.ds(pl.multiple_of((z * 2 + net.x) * whole, whole), whole), :]
                locals_.append(net.copy(ins[at], into))
            else:
                locals_.append(net.copy(mine(0), block(z, 0)))
            locals_[-1].start()
        for (at, kind, mine, block), other in zip(weights, given):
            span = pl.ds(self.share[0] * other.shape[kind == "row"] // self.share[1], other.shape[kind == "row"] // self.share[1])
            other = other.at[:, span] if kind == "row" else other.at[span, :]
            locals_.append(net.copy(other, block(z, 1)))
            locals_[-1].start()
            for up in (True, False):
                start(at, 1, 1, up, block, other)
        yield
        for copy in locals_:
            copy.wait()
        for at, kind, mine, block in weights:
            if given:
                continue
            swaps[at].wait_recv()
            for up in (True, False):
                start(at, 1, 1, up, block)
            if kind == "both":
                share = net.remote((id(self), "c", at), block(z, 1), block(z, 1), net.device(0, 0, 1))
                share.start()
                shared.append((share, None))
        for step in range(1, nz):
            for at, kind, mine, block in weights:
                for dx in (0, 1):
                    yield
                    for up in (True, False):
                        arrived(at, dx, step, up, block, kind)
                        if step < nz - 1:
                            start(at, dx, step + 1, up, block)
        yield
        for copy, fits in shared:
            if fits is None:
                copy.wait_recv()
            else:
                pl.when(fits)(copy.wait_recv)
        yield READY
        for copy, fits in shared:
            if fits is None:
                copy.wait_send()
            else:
                pl.when(fits)(copy.wait_send)
        for copy, fits in sent:
            pl.when(fits)(copy.wait_send)
        for copy in swaps.values():
            copy.wait_send()


class HalfSwap:
    moves = ("x",)

    def __init__(self, shards, kinds, nz, ny):
        self.ins, self.kinds = list(shards), list(kinds)
        self.outs, self.scratch = [], []
        for shard, kind in zip(shards, kinds):
            rows, columns = shard.shape
            shape = (rows, columns // 2) if kind == "row" else (rows // 2, columns)
            self.outs.append((jax.ShapeDtypeStruct(shape, shard.dtype), ANY))
        self.remotes, self.locals = len(self.ins), 0

    def run(self, net, ins, outs, scratch):
        copies = []
        for at, (shard, out, kind) in enumerate(zip(ins, outs, self.kinds)):
            span = out.shape[kind == "row"]
            there = pl.ds(pl.multiple_of((1 - net.x) * span, span), span)
            src = shard.at[:, there] if kind == "row" else shard.at[there, :]
            copies.append(net.remote((id(self), at), src, out, net.device(1, 0)))
            copies[-1].start()
        yield
        for copy in copies:
            copy.wait_recv()
        yield READY
        for copy in copies:
            copy.wait_send()


class LineScatter:
    moves = ("x", "line")

    def __init__(self, parts, kinds, nz, ny, resident=False, joined=False):
        self.ins, self.kinds, self.resident, self.joined = list(parts), list(kinds), resident, joined
        self.outs, self.scratch = [], []
        for part, kind in zip(parts, kinds):
            rows, columns = part.shape
            shape = (rows // (2 * nz), columns) if kind == "row" else (rows, columns // (2 * nz))
            times = 2 * (len(parts) if joined else 1)
            whole = (shape[0], shape[1] * times) if kind == "row" else (shape[0] * times, shape[1])
            if not (joined and self.outs):
                self.outs.append((jax.ShapeDtypeStruct(whole, BF16), ANY))
            for lead in (nz - 1, nz - 1, 1) + (() if resident else (nz,)):
                self.scratch.append(pltpu.VMEM((lead, 2) + shape, BF16))
        count = len(self.ins)
        self.remotes = count * (1 + 4 * nz)
        self.locals = count * (2 * nz + 1)

    def run(self, net, ins, outs, scratch):
        nz, z = net.nz, net.z
        loads, grads = {}, []
        each = 3 if self.resident else 4
        outs = list(outs) * len(ins) if self.joined else outs

        def spot(at, out):
            rows, columns = scratch[each * at + 2].shape[2:]
            kind = self.kinds[at]
            size = columns if kind == "row" else rows
            first = (net.x * len(ins) + at) * size if self.joined else net.x * size
            span = pl.ds(pl.multiple_of(first, size), size)
            return out.at[:, span] if kind == "row" else out.at[span, :]

        for at, (part, out, kind) in enumerate(zip(ins, outs, self.kinds)):
            down, up, mine = scratch[each * at : each * at + 3]
            _, _, rows, columns = mine.shape

            def block(line, dx, part=part, kind=kind, rows=rows, columns=columns):
                size = rows if kind == "row" else columns
                first = pl.ds(pl.multiple_of((line * 2 + net.flip(net.x, dx)) * size, size), size)
                return part.at[first, :] if kind == "row" else part.at[:, first]

            if self.resident:
                work = block
            else:

                def work(line, dx, at=at):
                    return scratch[each * at + 3].at[line, dx]

                order = []
                for k in range(nz):
                    order += [k, nz - 1 - k]
                for line in dict.fromkeys(order):
                    for dx in (1, 0):
                        loads[at, line, dx] = net.copy(block(line, dx), work(line, dx))
                        loads[at, line, dx].start()
            grads.append((at, out, work, down, up, mine))

        def inbox(slots, line, dx, toward):
            return slots.at[line if toward < 0 else line - 1, dx]

        pieces = (1, 0)
        each_line = len(pieces)

        for at, *_ in grads:
            net.slot((id(self), at, "x"))
            for dx in (0, 1):
                for line in range(nz):
                    for toward in (-1, 1):
                        net.slot((id(self), at, line, dx, toward))

        def chain(grad, dx, line, toward):
            at, out, work, down, up, mine = grad
            slot = inbox(down if toward < 0 else up, line, dx, toward)
            copy = net.remote((id(self), at, line, dx, toward), work(line, dx), slot, net.device(z=z + toward))
            return copy, slot

        def forward(place, grad, dx, line, toward):
            at, out, work, down, up, mine = grad
            copy, slot = chain(grad, dx, line, toward)
            if not self.resident:
                loads[at, line, dx].wait()
            if place != (nz - 1 if toward < 0 else 0):
                copy.wait_recv()
                add_rows(_lead(work(line, dx)), [_lead(work(line, dx)), _lead(slot)])
            copy.start()

        def finish(place, grad, dx):
            at, out, work, down, up, mine = grad
            if not self.resident:
                loads[at, place, dx].wait()
            terms = [_lead(work(place, dx))]
            for toward in (-1, 1):
                if (place < nz - 1) if toward < 0 else (place > 0):
                    copy, slot = chain(grad, dx, place, toward)
                    copy.wait_recv()
                    terms.append(_lead(slot))
            total = mine.at[0, dx]
            add_rows(_lead(total), terms)
            if dx:
                net.remote((id(self), at, "x"), total, spot(at, out), net.device(1, 0)).start()
            else:
                net.copy_at(self.first_local + at, total, spot(at, out)).start()

        plan = {}
        for place in range(nz):
            waits_up, waits_down = place, nz - 1 - place
            todo = []
            for toward, waits, lines in (
                (1, waits_up, range(nz - 1, place, -1)),
                (-1, waits_down, range(place)),
            ):
                order = [(line, dx) for line in lines for dx in pieces]
                for j, (line, dx) in enumerate(order):
                    for grad in grads:
                        todo.append((waits + j if waits else 0, waits, (forward, grad, dx, line, toward)))
            for q, dx in enumerate(pieces):
                times = []
                if waits_up:
                    times.append(waits_up + each_line * (nz - 1 - place) + q)
                if waits_down:
                    times.append(waits_down + each_line * place + q)
                for grad in grads:
                    todo.append((max(times), nz, (finish, grad, dx)))
            for time, waits, item in sorted(todo, key=lambda entry: entry[:2]):
                plan.setdefault(time, {}).setdefault(place, []).append(item)
        self.first_local = net.take_locals(len(grads))
        for time in range(max(plan) + 1):
            if time:
                yield
            for place, items in sorted(plan.get(time, {}).items()):

                def act(place=place, items=items):
                    for item in items:
                        item[0](place, *item[1:])

                pl.when(z == place)(act)
        sent = [
            (chain(grad, dx, line, toward)[0], (z > line) if toward < 0 else (z < line))
            for grad in grads
            for dx in pieces
            for toward, lines in ((-1, range(nz - 1)), (1, range(1, nz)))
            for line in lines
        ]
        swaps, stores = [], []
        for at, out, _, _, _, mine in grads:
            swaps.append(net.remote((id(self), at, "x"), mine.at[0, 1], spot(at, out), net.device(1, 0)))
            stores.append(net.copy_at(self.first_local + at, mine.at[0, 0], spot(at, out)))
        yield
        for copy, sends in sent:
            pl.when(sends)(copy.wait_send)
        for copy in swaps:
            copy.wait()
        for copy in stores:
            copy.wait()


def _lead(ref):
    return Lead(ref)


class Lead:
    def __init__(self, ref):
        self.ref, self.shape, self.dtype = ref, (1,) + tuple(ref.shape), ref.dtype

    def __getitem__(self, index):
        return self.ref[index[1], index[2]]

    def __setitem__(self, index, value):
        self.ref[index[1], index[2]] = value


class KeysGather:
    moves = ("x", "line", "c")
    in_spec = IN_VMEM

    def __init__(self, face, nz, ny):
        m, rows, width = face.shape
        self.ins = [face]
        self.outs = [(jax.ShapeDtypeStruct((m, nz * rows, width), face.dtype), ANY)]
        self.scratch = []
        self.remotes, self.locals = 4 * (nz - 1), 1

    def run(self, net, ins, outs, scratch):
        (face,), (out,) = ins, outs
        nz, z = net.nz, net.z
        _, rows, width = face.shape
        part, side = rows // 2, width // 2

        def block(line, dx, dc):
            first = pl.multiple_of(line * rows + net.flip(net.x, dx) * part, part)
            column = pl.multiple_of(net.flip(net.c, dc) * side, side)
            return out.at[:, pl.ds(first, part), pl.ds(column, side)]

        own = face.at[
            :,
            pl.ds(pl.multiple_of(net.x * part, part), part),
            pl.ds(pl.multiple_of(net.c * side, side), side),
        ]
        sent, shared = [], []

        def line_copy(step):
            origin = z - (step - 1)
            src = own if step == 1 else block(origin, 0, 0)
            return net.remote((id(self), step), src, block(origin, 0, 0), net.device(z=z + 1))

        def start(step):
            copy, fits = line_copy(step), (z - (step - 1) >= 0) & (z + 1 < nz)
            pl.when(fits)(copy.start)
            sent.append((copy, fits))

        start(1)
        keep = net.copy(face, out.at[:, pl.ds(pl.multiple_of(z * rows, rows), rows), :])
        keep.start()
        later = []
        for step in range(1, nz):
            yield
            fits = z - step >= 0
            pl.when(fits)(line_copy(step).wait_recv)
            if step < nz - 1:
                start(step + 1)
            here = block(z - step, 0, 0)
            across = net.remote((id(self), "x", step), here, here, net.device(1, 0))
            beside = net.remote((id(self), "c", step), here, here, net.device(0, 0, 1))
            for copy in (across, beside):
                pl.when(fits)(copy.start)
                sent.append((copy, fits))
            later.append((step, fits, across))
            shared.append((beside, fits))
        for step, fits, across in later:
            yield
            pl.when(fits)(across.wait_recv)
            there = block(z - step, 1, 0)
            beside = net.remote((id(self), "xc", step), there, there, net.device(0, 0, 1))
            pl.when(fits)(beside.start)
            sent.append((beside, fits))
            shared.append((beside, fits))
        yield
        for copy, fits in shared:
            pl.when(fits)(copy.wait_recv)
        keep.wait()
        yield READY
        for copy, fits in sent:
            pl.when(fits)(copy.wait_send)


class WholeScatter(FaceScatter):
    moves = ("x", "y", "c", "z")

    def __init__(self, part, nz, ny, resident=False):
        m, _, rows, d = part.shape
        merged = jax.ShapeDtypeStruct((m * nz, rows, d), part.dtype) if resident else part.reshape(m * nz, rows, d)
        super().__init__(merged, nz, ny, resident)
        t = rows // (4 * ny)
        self.m, self.nz = m, nz
        self.outs = [(jax.ShapeDtypeStruct((m, t, d), F32), pl.BlockSpec(memory_space=pltpu.VMEM))]
        self.scratch = self.scratch + [pltpu.VMEM((m * nz, t, d), BF16), pltpu.VMEM((nz, m, t, d), BF16)]
        self.remotes = self.remotes + nz * m
        self.locals = self.locals + m

    def run(self, net, ins, outs, scratch):
        face, inbox = scratch[-2:]
        yield from super().run(net, ins, [face], scratch[:-2])
        nz, m = self.nz, self.m
        copies = []
        for far in range(1, nz):
            line = lax.rem(net.z + far, nz)
            for at in range(m):
                copies.append(
                    pltpu.make_async_remote_copy(
                        src_ref=face.at[at * nz + line],
                        dst_ref=inbox.at[far, at],
                        send_sem=net.send.at[net.slot((id(self), "z", far, at))],
                        recv_sem=net.recv.at[net.slot((id(self), "z", far, at))],
                        device_id=net.device(z=line),
                        device_id_type=MESH,
                    )
                )
                copies[-1].start()
        own = []
        for at in range(m):
            own.append(net.copy(face.at[at * nz + net.z], inbox.at[0, at]))
            own[-1].start()
        yield
        for copy in own:
            copy.wait()
        for copy in copies:
            copy.wait()
        add_rows(outs[0], [inbox.at[far] for far in range(nz)])


class QuickScatter:
    moves = ("c", "same", "z")

    def __init__(self, part, nz, ny):
        _, rows, d = part.shape
        t = rows // (4 * ny)
        self.ins, self.t = [part], t
        self.outs = [(jax.ShapeDtypeStruct((t, d), F32), pl.BlockSpec(memory_space=pltpu.VMEM))]
        self.scratch = [
            pltpu.VMEM((2 * ny, nz, t, d), BF16),
            pltpu.VMEM((2 * ny, nz, t, d), BF16),
            pltpu.VMEM((2 * ny, nz, t, d), BF16),
            pltpu.VMEM((nz, t, d), BF16),
            pltpu.VMEM((nz, 1, t, d), BF16),
        ]
        self.remotes, self.locals = 4 * ny + nz, 2 * ny + 1

    def run(self, net, ins, outs, scratch):
        (part,), (out,), t = ins, outs, self.t
        work, from_core, inbox, face, line_in = scratch
        ny, nz = net.ny, net.nz
        order = [(dx, dy) for dx in (1, 0) for dy in reversed(range(ny))]
        cores, loads, copies = {}, {}, {}

        def rows(dx, dy, dc):
            return part.at[:, pl.ds(pl.multiple_of(net.rank(dx, dy, dc) * t, t), t), :]

        for dx, dy in order:
            at = dx * ny + dy
            loads[at] = net.copy(rows(dx, dy, 0), work.at[at])
            loads[at].start()
            cores[at] = net.remote((id(self), "c", at), rows(dx, dy, 1), from_core.at[at], net.device(0, 0, 1))
            cores[at].start()
        for dx, dy in order:
            at = dx * ny + dy
            yield
            loads[at].wait()
            cores[at].wait_recv()
            add_rows(work.at[at], [work.at[at], from_core.at[at]])
            if at:
                copies[at] = net.remote((id(self), at), work.at[at], inbox.at[at], net.device(dx, dy))
                copies[at].start()
        yield
        for copy in copies.values():
            copy.wait_recv()
        add_rows(face, [work.at[0]] + [inbox.at[at] for at in copies])
        lines = []
        for far in range(1, nz):
            line = lax.rem(net.z + far, nz)
            lines.append(
                net.remote((id(self), "z", far), face.at[pl.ds(line, 1)], line_in.at[far], net.device(z=line))
            )
            lines[-1].start()
        own = net.copy(face.at[pl.ds(net.z, 1)], line_in.at[0])
        own.start()
        yield
        own.wait()
        for copy in lines:
            copy.wait_recv()
        add_rows(_lead(out), [line_in.at[far] for far in range(nz)])
        for copy in list(cores.values()) + list(copies.values()) + lines:
            copy.wait_send()


class PlaneGather:
    moves = ("plane",)
    in_spec = IN_VMEM

    def __init__(self, own, nz, ny):
        self.ins = [own]
        self.outs = [(jax.ShapeDtypeStruct((2 * nz,) + own.shape, own.dtype), ANY)]
        self.scratch = []
        self.remotes, self.locals = 2 * nz, 1

    def run(self, net, ins, outs, scratch):
        (own,), (out,) = ins, outs
        here = out.at[net.z * 2 + net.x]
        copies = []
        for far in range(net.nz):
            for dx in (0, 1):
                if far or dx:
                    line = lax.rem(net.z + far, net.nz)
                    copies.append(net.remote((id(self), far, dx), own, here, net.device(dx, z=line)))
                    copies[-1].start()
        keep = net.copy(own, here)
        keep.start()
        yield
        for copy in copies:
            copy.wait()
        keep.wait()


class SmallScatter:
    moves = ("face", "z")

    def __init__(self, part, nz, ny):
        ranks, _, rows, width = part.shape
        self.ins = [part]
        vmem = pl.BlockSpec(memory_space=pltpu.VMEM)
        self.outs = [(jax.ShapeDtypeStruct((rows, width), F32), vmem)]
        self.scratch = [
            pltpu.VMEM((ranks, nz, rows, width), F32),
            pltpu.VMEM((nz, rows, width), F32),
            pltpu.VMEM((nz, rows, width), F32),
        ]
        self.remotes, self.locals = ranks + nz, 2

    def run(self, net, ins, outs, scratch):
        (part,), (out,) = ins, outs
        inbox, total, line_in = scratch
        ny, nz = net.ny, net.nz
        copies = []
        for dx in (0, 1):
            for dy in range(ny):
                for dc in (0, 1):
                    if dx or dy or dc:
                        at = (dx * ny + dy) * 2 + dc
                        copies.append(
                            net.remote(
                                (id(self), at), part.at[net.rank(dx, dy, dc)], inbox.at[at], net.device(dx, dy, dc)
                            )
                        )
                        copies[-1].start()
        keep = net.copy(part.at[net.rank()], inbox.at[0])
        keep.start()
        yield
        keep.wait()
        for copy in copies:
            copy.wait()
        total[...] = jnp.sum(inbox[...], axis=0)
        lines = []
        for far in range(1, nz):
            line = lax.rem(net.z + far, nz)
            lines.append(net.remote((id(self), "z", far), total.at[line], line_in.at[far], net.device(z=line)))
            lines[-1].start()
        own = net.copy(total.at[net.z], line_in.at[0])
        own.start()
        yield
        own.wait()
        for copy in lines:
            copy.wait()
        out[...] = jnp.sum(line_in[...], axis=0)


def launch(body, ins, in_specs, outs, scratch, plans, nz, ny, collective_id, name, extra_locals=0, vmem=56):
    moves = set()
    for plan in plans:
        moves |= set(plan.moves)
    remotes = sum(plan.remotes for plan in plans)
    locals_ = max(1, extra_locals + sum(plan.locals for plan in plans))

    def kernel(*refs):
        in_refs, refs = refs[: len(ins)], refs[len(ins) :]
        out_refs, refs = refs[: len(outs)], refs[len(outs) :]
        scratch_refs, (send, recv, local) = refs[: len(scratch)], refs[len(scratch) :]
        net = Net(nz, ny, send, recv, local)
        peers = {}
        for far in range(nz):
            for dx in (0, 1):
                for dy in range(ny):
                    for dc in (0, 1):
                        kinds = set()
                        if not far:
                            kinds.add("face")
                            if dx and not dy and not dc:
                                kinds.add("x")
                            if dy and not dx and not dc:
                                kinds.add("y")
                            if dc and not dx and not dy:
                                kinds.add("c")
                            if not dc:
                                kinds.add("same")
                        if far and not dx and not dy and not dc:
                            kinds.add("z")
                            if far in (1, nz - 1):
                                kinds.add("line")
                        if not dy and not dc:
                            kinds.add("plane")
                        if (far or dx or dy or dc) and kinds & moves:
                            line = lax.rem(net.z + far, nz) if far else None
                            peers[far, dx, dy, dc] = net.device(dx, dy, dc, line)
        barrier = pltpu.get_barrier_semaphore()
        for device in peers.values():
            pl.semaphore_signal(barrier, inc=1, device_id=device, device_id_type=MESH)
        pl.semaphore_wait(barrier, len(peers))
        body(net, in_refs, out_refs, scratch_refs)

    return list(
        pl.pallas_call(
            kernel,
            out_shape=[shape for shape, _ in outs],
            in_specs=in_specs,
            out_specs=[spec for _, spec in outs],
            scratch_shapes=list(scratch)
            + [
                pltpu.SemaphoreType.DMA((remotes,)),
                pltpu.SemaphoreType.DMA((remotes,)),
                pltpu.SemaphoreType.DMA((locals_,)),
            ],
            compiler_params=pltpu.CompilerParams(
                collective_id=collective_id, has_side_effects=True, vmem_limit_bytes=vmem << 20
            ),
            name=name,
        )(*ins)
    )


def exchange(plans, nz, ny, collective_id, name, order=()):
    ins = [array for plan in plans for array in plan.ins]
    outs = [out for plan in plans for out in plan.outs]
    scratch = [entry for plan in plans for entry in plan.scratch]

    def body(net, in_refs, out_refs, scratch_refs):
        running = []
        for plan in plans:
            mine = []
            for refs_of, count in ((in_refs, plan.ins), (out_refs, plan.outs), (scratch_refs, plan.scratch)):
                mine.append(list(refs_of[: len(count)]))
            in_refs = in_refs[len(plan.ins) :]
            out_refs = out_refs[len(plan.outs) :]
            scratch_refs = scratch_refs[len(plan.scratch) :]
            running.append(plan.run(net, *mine))
        for at in order:
            next(running[at], None)
        while running:
            for steps in list(running):
                try:
                    next(steps)
                except StopIteration:
                    running.remove(steps)

    specs = [getattr(plan, "in_spec", ANY) for plan in plans for _ in plan.ins]
    results = launch(body, ins, specs, outs, scratch, plans, nz, ny, collective_id, name)
    grouped = []
    for plan in plans:
        grouped.append(results[: len(plan.outs)])
        results = results[len(plan.outs) :]
    return grouped


class Weave:
    def __init__(self):
        self.plans, self.ready = {}, set()

    def add(self, name, steps):
        self.plans[name] = steps

    def step(self, name):
        steps = self.plans.get(name)
        if steps is not None:
            state = next(steps, self)
            if state is self:
                del self.plans[name]
            elif state == READY:
                self.ready.add(name)

    def need(self, name):
        while name in self.plans and name not in self.ready:
            self.step(name)

    def finish(self, name):
        while name in self.plans:
            self.step(name)


def first_block(block, seq_len):
    longest = seq_len // 2 + BLOCK
    return jnp.maximum(block - (longest - 1 + BLOCK - 1) // BLOCK, 0)


def loop(count, body):
    def step(at, carry):
        body(at)
        return carry

    lax.fori_loop(0, count, step, 0)


def mlp_block(mixed, wo, inputs, cotangent, cot_face, norms, wexp_first, w_expand, w_reduce, nz, ny, collective_id):
    micro_count, own_rows, width = inputs.shape
    face_rows = cot_face.shape[1]
    tokens = micro_count * face_rows
    attn = mixed.shape[2]
    units = w_expand[0].shape[1] // 2
    half = units // 2
    tile = min(512, half)
    wide = 512
    part = jax.ShapeDtypeStruct((micro_count, face_rows, width), BF16)
    part_red = jax.ShapeDtypeStruct((units, width), BF16)
    own = (micro_count, own_rows, width)
    scatter_a, scatter_b = (FaceScatter(part, nz, ny, resident=True) for _ in range(2))
    gather = FaceGather(jax.ShapeDtypeStruct(own, BF16), nz, ny, report=True)
    line_e = LineGather(w_expand[:1], ["row"], nz, ny, share=(1, 2), given=w_expand[1:])
    line_r = LineGather(w_reduce[:1], ["col"], nz, ny, given=w_reduce[1:])
    line_s = LineScatter([part_red], ["col"], nz, ny, resident=True)
    plans = [scatter_a, scatter_b, gather, line_e, line_r, line_s]
    vmem = pl.BlockSpec(memory_space=pltpu.VMEM)
    outs = [
        (jax.ShapeDtypeStruct(own, F32), ANY),
        (jax.ShapeDtypeStruct(own, F32), ANY),
        (jax.ShapeDtypeStruct(own, BF16), ANY),
        (jax.ShapeDtypeStruct((2, 16, width), F32), vmem),
        (jax.ShapeDtypeStruct((width, half), BF16), ANY),
        (jax.ShapeDtypeStruct((width, half), BF16), ANY),
        (part, ANY),
    ] + line_s.outs
    scratch = [
        pltpu.VMEM((micro_count, face_rows, width), BF16),
        pltpu.VMEM(own, F32),
        pltpu.VMEM(own, F32),
        pltpu.VMEM(own, BF16),
        pltpu.VMEM(own, BF16),
        pltpu.VMEM(own, BF16),
        pltpu.VMEM((micro_count, face_rows, width), BF16),
        pltpu.VMEM((micro_count, face_rows, width), BF16),
        pltpu.VMEM((width, half), BF16),
        pltpu.VMEM((width, half), BF16),
        pltpu.VMEM((units, width), BF16),
        pltpu.VMEM((micro_count, face_rows, units), BF16),
        pltpu.VMEM((micro_count, face_rows, units), BF16),
        pltpu.VMEM((units, width), BF16),
        pltpu.VMEM((micro_count, face_rows, attn), BF16),
        pltpu.VMEM((attn, width), BF16),
    ]
    shared = len(scratch)
    scratch += scatter_a.scratch + line_s.scratch

    def body(net, ins, outs, scratch):
        mixed_in, wo_in, own_in, cot_in, face_in, norms, first_in, *weights_in = ins
        middle_out, grad_out, low_out, norm_out, expand_a, expand_b, reduced_out, reduce_out = outs
        p, branch, middle, own, cot_own, n_own, n_face, cot, we0, we1, wr, active, slope, pr, mixed, wo = scratch[:shared]
        we = (we0, we1)
        slots = list(scratch[shared : shared + len(scatter_a.scratch)])
        line_slots = list(scratch[shared + len(scatter_a.scratch) :])

        loads = [
            net.copy(*pair)
            for pair in (
                (mixed_in, mixed),
                (wo_in, wo),
                (own_in, own),
                (cot_in, cot_own),
                (first_in, we0),
                (face_in, cot),
            )
        ]
        weave = Weave()
        stores = []
        weave.add("e", line_e.run(net, weights_in[:2], [we1], []))
        weave.step("e")
        weave.add("r", line_r.run(net, weights_in[2:], [wr], []))
        weave.step("r")
        for load in loads:
            load.start()

        chip_tokens = micro_count * 2 * own_rows

        def branch_chip(dx, dy):
            rows = net.chip_rows(dx, dy, own_rows)

            def tile_at(n):
                columns = pl.ds(pl.multiple_of(n * wide, wide), wide)
                p[:, rows, columns] = (
                    jnp.dot(
                        mixed[:, rows, :].reshape(chip_tokens, attn), wo[:, columns], preferred_element_type=F32
                    )
                    .astype(BF16)
                    .reshape(micro_count, 2 * own_rows, wide)
                )

            loop(width // wide, tile_at)

        row_steps = own_rows // 16

        def own_rows_at(at):
            return lax.div(at, row_steps), pl.ds(pl.multiple_of(lax.rem(at, row_steps) * 16, 16), 16)

        def norm_rows(at):
            m, rows = own_rows_at(at)
            values = own[m, rows, :].astype(F32) + branch[m, rows, :]
            middle[m, rows, :] = values
            centered = values - jnp.mean(values, axis=-1, keepdims=True)
            spread = lax.rsqrt(jnp.mean(centered * centered, axis=-1, keepdims=True) + EPSILON)
            n_own[m, rows, :] = (centered * spread * norms[2:3, :] + norms[3:4, :]).astype(BF16)

        def hidden_chip(dx, dy, h):
            rows = net.chip_rows(dx, dy, own_rows)
            block = (micro_count, 2 * own_rows, tile)

            def tile_at(n):
                columns = pl.ds(pl.multiple_of(n * tile, tile), tile)
                into = pl.ds(pl.multiple_of(h * half + n * tile, tile), tile)
                hidden = jnp.dot(
                    n_face[:, rows, :].reshape(chip_tokens, width), we[h][:, columns], preferred_element_type=F32
                )
                square = hidden * hidden
                bend = jnp.tanh(GELU_A * hidden * (1.0 + GELU_B * square))
                active[:, rows, into] = (0.5 * hidden * (1.0 + bend)).astype(BF16).reshape(block)
                slope[:, rows, into] = (
                    (
                        0.5 * (1.0 + bend)
                        + (0.5 * GELU_A) * hidden * (1.0 - bend * bend) * (1.0 + (3.0 * GELU_B) * square)
                    )
                    .astype(BF16)
                    .reshape(block)
                )

            loop(half // tile, tile_at)

        across = (((0,), (0,)), ((), ()))
        along = (((1,), (1,)), ((), ()))
        def reduce_tile(first):
            def tile_at(at):
                f, n = lax.div(at, width // wide), lax.rem(at, width // wide)
                columns = pl.ds(pl.multiple_of(n * wide, wide), wide)
                rows = pl.ds(pl.multiple_of(first + f * tile, tile), tile)
                pr[rows, columns] = lax.dot_general(
                    active[:, :, rows].reshape(tokens, tile),
                    cot[:, :, columns].reshape(tokens, wide),
                    across,
                    preferred_element_type=F32,
                ).astype(BF16)

            return tile_at

        def slope_tile(at):
            m, n = lax.div(at, units // tile), lax.rem(at, units // tile)
            columns = pl.ds(pl.multiple_of(n * tile, tile), tile)
            grad = lax.dot_general(cot[m], wr[columns, :], along, preferred_element_type=F32)
            slope[m, :, columns] = (grad * slope[m, :, columns].astype(F32)).astype(BF16)

        made = []

        def normed_chip(dx, dy):
            made.append((dx, dy))
            rows = net.chip_rows(dx, dy, own_rows)

            def tile_at(n):
                columns = pl.ds(pl.multiple_of(n * wide, wide), wide)
                grad = lax.dot_general(
                    slope[:, rows, :half].reshape(chip_tokens, half), we0[columns, :], along, preferred_element_type=F32
                )
                grad = grad + lax.dot_general(
                    slope[:, rows, half:].reshape(chip_tokens, half), we1[columns, :], along, preferred_element_type=F32
                )
                p[:, rows, columns] = grad.astype(BF16).reshape(micro_count, 2 * own_rows, wide)

            loop(width // wide, tile_at)

        def reduced_tiles(m):
            def tile_at(n):
                columns = pl.ds(pl.multiple_of(n * wide, wide), wide)
                cot[m, :, columns] = jnp.dot(active[m], wr[:, columns], preferred_element_type=F32).astype(BF16)

            def act():
                loop(width // wide, tile_at)
                stores.append(net.copy(cot.at[m], reduced_out.at[m]))
                stores[-1].start()

            return act

        def expand_tiles(h):
            def tile_at(at):
                k, n = lax.div(at, half // tile), lax.rem(at, half // tile)
                rows = pl.ds(pl.multiple_of(k * wide, wide), wide)
                columns = pl.ds(pl.multiple_of(n * tile, tile), tile)
                grads = pl.ds(pl.multiple_of(h * half + n * tile, tile), tile)
                we[h][rows, columns] = lax.dot_general(
                    n_face[:, :, rows].reshape(tokens, wide),
                    slope[:, :, grads].reshape(tokens, tile),
                    across,
                    preferred_element_type=F32,
                ).astype(BF16)

            def act():
                loop((width // wide) * (half // tile), tile_at)
                stores.append(net.copy(we[h], (expand_a, expand_b)[h]))
                stores[-1].start()

            return act

        def back_rows(at):
            m, rows = own_rows_at(at)
            values = middle[m, rows, :]
            centered = values - jnp.mean(values, axis=-1, keepdims=True)
            spread = lax.rsqrt(jnp.mean(centered * centered, axis=-1, keepdims=True) + EPSILON)
            unit = centered * spread
            grad = branch[m, rows, :]
            norm_out[0] += grad * unit
            norm_out[1] += grad
            turned = grad * norms[2:3, :]
            inner = jnp.mean(turned * unit, axis=-1, keepdims=True)
            total = cot_own[m, rows, :].astype(F32) + spread * (
                turned - jnp.mean(turned, axis=-1, keepdims=True) - unit * inner
            )
            middle[m, rows, :] = total
            n_own[m, rows, :] = total.astype(BF16)

        def later():
            while len(made) < 2 * ny:
                weave.step("m")
            weave.finish("e")
            for h in (0, 1):
                expand_tiles(h)()
                yield
            for m in range(micro_count):
                reduced_tiles(m)()
                yield

        def main():
            loads[0].wait()
            loads[1].wait()
            yield from scatter_a.run(net, [p], [branch], slots, branch_chip)
            loads[2].wait()
            loop(micro_count * row_steps, norm_rows)
            keep_middle = net.copy(middle, middle_out)
            keep_middle.start()
            loads[4].wait()
            chips, halved = 0, []
            for place in gather.run(net, [n_own], [n_face], []):
                if place is not None:
                    hidden_chip(*place, 0)
                    halved.append(place)
                    chips += 1
                    if chips > ny:
                        yield
                        weave.need("e")
                        for place in halved:
                            hidden_chip(*place, 1)
                        halved = []
                yield
            loads[5].wait()
            loop((half // tile) * (width // wide), reduce_tile(0))
            yield
            loop((half // tile) * (width // wide), reduce_tile(half))
            weave.add("s", line_s.run(net, [pr], [reduce_out], line_slots))
            weave.step("s")
            yield
            weave.need("r")
            loop(micro_count * (units // tile), slope_tile)
            yield
            weave.add("x", later())
            yield from scatter_b.run(net, [p], [branch], slots, normed_chip)
            loads[3].wait()
            keep_middle.wait()
            norm_out[...] = jnp.zeros_like(norm_out)
            loop(micro_count * row_steps, back_rows)
            for pair in ((middle, grad_out), (n_own, low_out)):
                stores.append(net.copy(*pair))
                stores[-1].start()

        weave.add("m", main())
        for name in "".join(MLP_ORDER):
            weave.step(name)
        for name in "mxsre":
            weave.finish(name)
        for store in stores:
            store.wait()

    ins = [mixed, wo, inputs, cotangent, cot_face, norms, wexp_first, *w_expand, *w_reduce]
    specs = [ANY] * 5 + [vmem] + [ANY] * (len(ins) - 6)
    return launch(
        body, ins, specs, outs, scratch, plans, nz, ny, collective_id, "mlp_block", extra_locals=12, vmem=62
    )


def front_block(inputs, cotangent, w_query, w_attn_out, w_keyval, w_expand, norms, doc_ids, nz, ny, collective_id, head_dim):
    micro_count, own_rows, width = inputs.shape
    face_rows = own_rows * 4 * ny
    attn = w_query.shape[1] // 2
    seq_len = nz * face_rows
    blocks = face_rows // BLOCK
    heads = attn // head_dim
    tall = heads * BLOCK
    own = jax.ShapeDtypeStruct(inputs.shape, BF16)
    keys_face = jax.ShapeDtypeStruct((micro_count, face_rows, 2 * head_dim), BF16)
    shard = norms.shape[1] // 4
    norms_own = jax.ShapeDtypeStruct((8, shard), F32)
    plane = PlaneGather(norms_own, nz, ny)
    gather = FaceGather(own, nz, ny)
    gather_c = FaceGather(cotangent, nz, ny, hold_x=True)
    swap_e = HalfSwap([w_expand], ["row"], nz, ny)
    line_a = LineGather([w_keyval, w_query], ["both", "row"], nz, ny)
    line_o = LineGather([w_attn_out], ["col"], nz, ny)
    given = jax.ShapeDtypeStruct((w_expand.shape[0], w_expand.shape[1] // 2), BF16)
    line_e = LineGather([w_expand], ["row"], nz, ny, share=(0, 2), given=[given])
    keys = KeysGather(keys_face, nz, ny)
    plans = [plane, gather, gather_c, swap_e, line_a, line_o, line_e, keys]
    kept = [
        jax.ShapeDtypeStruct((micro_count, face_rows, width), BF16),
        line_a.outs[0][0],
        line_a.outs[1][0],
        given,
        jax.ShapeDtypeStruct((micro_count, face_rows, attn), BF16),
        keys.outs[0][0],
        jax.ShapeDtypeStruct((micro_count, face_rows, attn), BF16),
        jax.ShapeDtypeStruct((micro_count, blocks, 1, tall), F32),
        jax.ShapeDtypeStruct((micro_count, blocks, 2, BLOCK), jnp.int32),
        own,
    ]
    outs = [(shape, ANY) for shape in kept] + [
        (jax.ShapeDtypeStruct((8, width), F32), IN_VMEM),
        gather_c.outs[0],
        line_o.outs[0],
        line_e.outs[0],
    ]
    scratch = [pltpu.VMEM(shape.shape, shape.dtype) for shape in kept] + [
        pltpu.VMEM(keys_face.shape, BF16),
        pltpu.VMEM((8, shard), F32),
        pltpu.VMEM((2 * nz, 8, shard), F32),
    ]

    def body(net, ins, outs, scratch):
        inputs, cotangent, w_query, w_attn_out, w_keyval, w_expand, doc_ids, norms_in = ins
        norm_rows, cot_out, wo_out, first_out = outs[len(kept) :]
        normed, wkv, wq, given, queries, keys_vals, mixed, logs, limits, n_own, keys_face, norms, norms_out = scratch
        norms[...] = jnp.zeros_like(norms)
        for k in range(4):
            norms[k : k + 1, :] = norms_in[:, k * shard : (k + 1) * shard].astype(F32)
        stores = [net.copy(*pair) for pair in zip(scratch, outs[: len(kept)])]
        weave = Weave()
        weave.add("p", plane.run(net, [norms], [norms_out], []))
        weave.step("p")
        weave.add("a", line_a.run(net, [w_keyval, w_query], [wkv, wq], []))
        weave.step("a")
        weave.add("h", swap_e.run(net, [w_expand], [given], []))
        weave.add("o", line_o.run(net, [w_attn_out], [wo_out], []))
        weave.add("c", gather_c.run(net, [cotangent], [cot_out], []))

        def line_first():
            weave.need("h")
            yield from line_e.run(net, [w_expand, given], [first_out], [])

        weave.add("e", line_first())
        along = (((1,), (1,)), ((), ()))
        across = (((0,), (0,)), ((), ()))
        step = min(32, own_rows)

        def own_norm(at):
            m = lax.div(at, own_rows // step)
            rows = pl.ds(pl.multiple_of(lax.rem(at, own_rows // step) * step, step), step)
            gain, shift = norm_rows[0:1, :], norm_rows[1:2, :]
            values = inputs[m, rows, :].astype(F32)
            centered = values - jnp.mean(values, axis=-1, keepdims=True)
            spread = lax.rsqrt(jnp.mean(centered * centered, axis=-1, keepdims=True) + EPSILON)
            n_own[m, rows, :] = (centered * spread * gain + shift).astype(BF16)

        def keys_tile(m):
            keys_face[m] = jnp.dot(normed[m], wkv[...], preferred_element_type=F32).astype(BF16)

        def queries_tile(m):
            queries[m] = jnp.dot(normed[m], wq[...], preferred_element_type=F32).astype(BF16)

        def mixed_tile(m):
            def tile_at(b):
                rows = pl.ds(pl.multiple_of(b * BLOCK, BLOCK), BLOCK)
                query = jnp.concatenate(
                    [queries[m, rows, h * head_dim : (h + 1) * head_dim] for h in range(heads)], axis=0
                )
                starts = jnp.concatenate([limits[m, b, 0:1, :]] * heads, axis=1)
                ends = jnp.concatenate([limits[m, b, 1:2, :]] * heads, axis=1)
                place = lax.broadcasted_iota(jnp.int32, (BLOCK, tall), 0)

                def body(block, carry):
                    top, total, out = carry
                    first = pl.multiple_of(block * BLOCK, BLOCK)
                    keys = keys_vals[m, pl.ds(first, BLOCK), :head_dim]
                    values = keys_vals[m, pl.ds(first, BLOCK), head_dim:]
                    raw = lax.dot_general(keys, query, along, preferred_element_type=F32)
                    allowed = (place >= starts - first) & (place < ends - first)
                    scores = jnp.where(allowed, raw * (LOG2_E / math.sqrt(head_dim)), NEG_FILL)
                    new_top = jnp.maximum(top, jnp.max(scores, axis=0, keepdims=True))
                    weights = jnp.exp2(scores - new_top)
                    fade = jnp.exp2(top - new_top)
                    total = total * fade + jnp.sum(weights, axis=0, keepdims=True)
                    out = out * fade + lax.dot_general(
                        values, weights.astype(BF16), across, preferred_element_type=F32
                    )
                    return new_top, total, out

                top, total, out = lax.fori_loop(
                    first_block(net.z * blocks + b, seq_len),
                    net.z * blocks + b + 1,
                    body,
                    (
                        jnp.full((1, tall), NEG_FILL, F32),
                        jnp.zeros((1, tall), F32),
                        jnp.zeros((head_dim, tall), F32),
                    ),
                )
                out = jnp.transpose(out / total).astype(BF16)
                for h in range(heads):
                    mixed[m, rows, h * head_dim : (h + 1) * head_dim] = out[h * BLOCK : (h + 1) * BLOCK]
                logs[m, b] = top + jnp.log2(total)

            return tile_at

        def limits_tile(m):
            kinds = lax.broadcasted_iota(jnp.int32, (32, 1), 0)
            counts = jnp.sum((doc_ids[m : m + 1, :] == kinds).astype(F32), axis=1, keepdims=True)
            for b in range(blocks):
                first = pl.multiple_of(net.z * face_rows + b * BLOCK, BLOCK)
                docs = doc_ids[m : m + 1, pl.ds(first, BLOCK)]
                starts = jnp.sum(jnp.where(kinds < docs, counts, 0.0), axis=0, keepdims=True)
                ends = jnp.sum(jnp.where(kinds <= docs, counts, 0.0), axis=0, keepdims=True)
                limits[m, b, 0:1, :] = starts.astype(jnp.int32)
                limits[m, b, 1:2, :] = ends.astype(jnp.int32)

        def main():
            weave.finish("p")
            norm_rows[...] = jnp.concatenate([norms_out[d] for d in range(2 * nz)], axis=1)
            loop(micro_count * (own_rows // step), own_norm)
            stores[9].start()
            yield from gather.run(net, [n_own], [normed], [])
            stores[0].start()
            for m in range(micro_count):
                limits_tile(m)
            stores[8].start()
            yield
            weave.need("a")
            loop(micro_count, keys_tile)
            weave.add("k", keys.run(net, [keys_face], [keys_vals], []))
            weave.step("k")
            yield
            for at in (1, 2):
                stores[at].start()
            loop(micro_count, queries_tile)
            stores[4].start()
            yield
            weave.need("k")
            stores[5].start()
            for m in range(micro_count):
                loop(blocks, mixed_tile(m))
                yield
            for at in (6, 7):
                stores[at].start()

        weave.add("m", main())
        for name in "".join(FRONT_ORDER):
            weave.step(name)
        for name in "mhcoeak":
            weave.finish(name)
        stores[3].start()
        for store in stores:
            store.wait()

    ins = [inputs, cotangent, w_query, w_attn_out, w_keyval, w_expand, doc_ids, norms]
    results = launch(
        body, ins, [IN_VMEM] * len(ins), outs, scratch, plans, nz, ny, collective_id, "front_block", extra_locals=len(kept)
    )
    return results[: len(kept)], results[len(kept) :]


def back_block(low, reduced, parts, mixed, wo, wq, normed, queries, keys_vals, logs, limits, nz, ny, collective_id, head_dim):
    micro_count, own_rows, width = low.shape
    face_rows, attn = queries.shape[1:]
    seq_len = keys_vals.shape[1]
    tokens = micro_count * face_rows
    blocks = face_rows // BLOCK
    heads = attn // head_dim
    tall = heads * BLOCK
    scale = 1.0 / math.sqrt(head_dim)
    wide = 512
    half = parts[0].shape[1]
    part = jax.ShapeDtypeStruct((micro_count, face_rows, width), BF16)
    gather = FaceGather(low, nz, ny)
    scatter_r = FaceScatter(reduced, nz, ny)
    scatter_q = FaceScatter(part, nz, ny, resident=True)
    whole = WholeScatter(jax.ShapeDtypeStruct((micro_count, nz, face_rows, 2 * head_dim), BF16), nz, ny, resident=True)
    line_e = LineScatter(parts, ["row", "row"], nz, ny, resident=True, joined=True)
    attn_parts = [jax.ShapeDtypeStruct((attn, width), BF16), jax.ShapeDtypeStruct((width, attn), BF16)]
    line_a = LineScatter(attn_parts, ["col", "row"], nz, ny, resident=True)
    plans = [gather, scatter_r, scatter_q, whole, line_e, line_a]
    groups = [scatter_r, scatter_q, whole, line_e, line_a]
    outs = scatter_r.outs + scatter_q.outs + whole.outs + line_e.outs + line_a.outs
    normed = normed.reshape(micro_count, face_rows, width)
    given = [mixed, wo, wq, queries, keys_vals, logs, limits, *parts]
    scratch = [pltpu.VMEM(entry.shape, entry.dtype) for entry in given] + [
        pltpu.VMEM(part.shape, BF16),
        pltpu.VMEM(queries.shape, BF16),
        pltpu.VMEM(queries.shape, BF16),
        pltpu.VMEM((seq_len, 2 * head_dim), F32),
        pltpu.VMEM((micro_count * nz, face_rows, 2 * head_dim), BF16),
        pltpu.VMEM((attn, width), BF16),
        pltpu.VMEM((width, attn), BF16),
        pltpu.VMEM((2, micro_count, face_rows, wide), BF16),
    ]
    shared = len(scratch)
    for plan in groups:
        scratch = scratch + plan.scratch

    def body(net, ins, outs, scratch):
        low, reduced_in, normed_in, *given_in = ins
        reduced_out, from_out, keys_out, *line_outs = outs
        mixed, wo, wq, queries, keys_vals, logs, limits, *expand = scratch[: len(given)]
        face, grad_mixed, grad_queries, acc, grad_keys, part_out, part_query, normed = scratch[len(given) : shared]
        slots, first = {}, shared
        for name, plan in zip("rqwea", groups):
            slots[name] = list(scratch[first : first + len(plan.scratch)])
            first += len(plan.scratch)
        loads = [net.copy(*pair) for pair in zip(given_in, scratch)]
        order = [len(given) - 2, len(given) - 1] + list(range(len(given) - 2))
        weave = Weave()
        along = (((1,), (1,)), ((), ()))
        across = (((0,), (0,)), ((), ()))

        def mix_tile(m):
            grad_mixed[m] = lax.dot_general(face[m], wo[...], along, preferred_element_type=F32).astype(BF16)

        def attn_out_tile(n):
            columns = pl.ds(pl.multiple_of(n * wide, wide), wide)
            part_out[:, columns] = lax.dot_general(
                mixed[...].reshape(tokens, attn),
                face[:, :, columns].reshape(tokens, wide),
                across,
                preferred_element_type=F32,
            ).astype(BF16)

        def attn_tile(m):
            def tile_at(b):
                rows = pl.ds(pl.multiple_of(b * BLOCK, BLOCK), BLOCK)

                def stack(ref):
                    return jnp.concatenate(
                        [ref[m, rows, h * head_dim : (h + 1) * head_dim] for h in range(heads)], axis=0
                    )

                query, grad = stack(queries), stack(grad_mixed)
                products = grad.astype(F32) * stack(mixed).astype(F32)
                delta = jnp.sum(jnp.transpose(products), axis=0, keepdims=True)
                starts = jnp.concatenate([limits[m, b, 0:1, :]] * heads, axis=1)
                ends = jnp.concatenate([limits[m, b, 1:2, :]] * heads, axis=1)
                log_total = logs[m, b]
                place = lax.broadcasted_iota(jnp.int32, (BLOCK, tall), 0)

                def body(block, grad_query):
                    first = pl.multiple_of(block * BLOCK, BLOCK)
                    keys = keys_vals[m, pl.ds(first, BLOCK), :head_dim]
                    values = keys_vals[m, pl.ds(first, BLOCK), head_dim:]
                    raw = lax.dot_general(keys, query, along, preferred_element_type=F32)
                    allowed = (place >= starts - first) & (place < ends - first)
                    probs = jnp.where(allowed, jnp.exp2(raw * (LOG2_E * scale) - log_total), 0.0)
                    grad_probs = lax.dot_general(values, grad, along, preferred_element_type=F32)
                    grad_scores = (probs * (grad_probs - delta)).astype(BF16)
                    acc[pl.ds(first, BLOCK), :head_dim] += (
                        jnp.dot(grad_scores, query, preferred_element_type=F32) * scale
                    )
                    acc[pl.ds(first, BLOCK), head_dim:] += jnp.dot(
                        probs.astype(BF16), grad, preferred_element_type=F32
                    )
                    return grad_query + lax.dot_general(keys, grad_scores, across, preferred_element_type=F32)

                grad_query = lax.fori_loop(
                    first_block(net.z * blocks + b, seq_len),
                    net.z * blocks + b + 1,
                    body,
                    jnp.zeros((head_dim, tall), F32),
                )
                grad_query = jnp.transpose(grad_query * scale).astype(BF16)
                for h in range(heads):
                    grad_queries[m, rows, h * head_dim : (h + 1) * head_dim] = grad_query[h * BLOCK : (h + 1) * BLOCK]

            return tile_at

        def from_chip(dx, dy):
            rows = net.chip_rows(dx, dy, own_rows)

            def tile_at(n):
                columns = pl.ds(pl.multiple_of(n * wide, wide), wide)
                face[:, rows, columns] = (
                    lax.dot_general(
                        grad_queries[:, rows, :].reshape(micro_count * 2 * own_rows, attn),
                        wq[columns, :],
                        along,
                        preferred_element_type=F32,
                    )
                    .astype(BF16)
                    .reshape(micro_count, 2 * own_rows, wide)
                )

            loop(width // wide, tile_at)

        columns_in = [
            net.copy(normed_in.at[:, :, pl.ds(n * wide, wide)], normed.at[n % 2]) for n in range(width // wide)
        ]

        def query_tile(n):
            columns_in[n].wait()

            def tile_at(_):
                part_query[n * wide : (n + 1) * wide, :] = lax.dot_general(
                    normed[n % 2].reshape(tokens, wide),
                    grad_queries[...].reshape(tokens, attn),
                    across,
                    preferred_element_type=F32,
                ).astype(BF16)

            loop(1, tile_at)
            if n + 2 < width // wide:
                columns_in[n + 2].start()

        def main():
            yield from gather.run(net, [low], [face], [])
            for at in order[2:]:
                loads[at].wait()
            loop(micro_count, mix_tile)
            yield
            for m in range(micro_count):
                acc[...] = jnp.zeros_like(acc)
                loop(blocks, attn_tile(m))
                for k in range(nz):
                    grad_keys[m * nz + k] = acc[k * face_rows : (k + 1) * face_rows, :].astype(BF16)
                yield
            loop(width // wide, attn_out_tile)
            weave.add("w", whole.run(net, [grad_keys], [keys_out], slots["w"]))
            weave.step("w")
            weave.add("q", scatter_q.run(net, [face], [from_out], slots["q"], from_chip))
            weave.step("q")
            for n in range(width // wide):
                query_tile(n)
            weave.add("a", line_a.run(net, [part_out, part_query], line_outs[1:], slots["a"]))
            weave.step("a")

        weave.add("m", main())
        weave.step("m")
        for at in order:
            loads[at].start()
        for copy in columns_in[:2]:
            copy.start()
        for at in order[:2]:
            loads[at].wait()
        weave.add("e", line_e.run(net, expand, line_outs[:1], slots["e"]))
        weave.step("e")
        weave.add("r", scatter_r.run(net, [reduced_in], [reduced_out], slots["r"]))
        for name in "".join(BACK_ORDER):
            weave.step(name)
        for name in "mwqrea":
            weave.finish(name)

    ins = [low, reduced, normed, *given]
    specs = [IN_VMEM] + [ANY] * (len(ins) - 1)
    return launch(
        body, ins, specs, outs, scratch, plans, nz, ny, collective_id, "back_block", extra_locals=len(given) + width // wide, vmem=62
    )


def end_block(inputs, normed_own, grad_middle, from_query, grad_keys, wkv, norms, grad_norm_two, nz, ny, collective_id):
    micro_count, own_rows, width = inputs.shape
    rows_all = micro_count * own_rows
    side = grad_keys.shape[-1]
    ranks = 4 * ny
    own_width = width // (nz * ranks)
    step = min(32, own_rows)
    part = jax.ShapeDtypeStruct((nz, width // nz, side), BF16)
    small = jax.ShapeDtypeStruct((ranks, nz, 8, 128), F32)
    quick, tiny = QuickScatter(part, nz, ny), SmallScatter(small, nz, ny)
    plans = [quick, tiny]
    outs = [(jax.ShapeDtypeStruct(inputs.shape, F32), IN_VMEM)] + quick.outs + tiny.outs
    scratch = [
        pltpu.VMEM((rows_all, side), BF16),
        pltpu.VMEM(part.shape, BF16),
        pltpu.VMEM(small.shape, F32),
        pltpu.VMEM((2, step, width), F32),
    ] + quick.scratch + tiny.scratch

    def body(net, ins, outs, scratch):
        inputs, n_own, grad_middle, from_query, grad_keys, wkv, norms, grad_norm_two = ins
        grad_out, keyval_out, small_out = outs
        low_keys, part, small, sums, *slots = scratch
        weave = Weave()

        def place(at):
            m, first = lax.div(at, own_rows // step), lax.rem(at, own_rows // step) * step
            rows = pl.ds(pl.multiple_of(first, step), step)
            return m, rows, pl.ds(pl.multiple_of(at * step, step), step)

        def unit_rows(m, rows):
            values = inputs[m, rows, :].astype(F32)
            centered = values - jnp.mean(values, axis=-1, keepdims=True)
            spread = lax.rsqrt(jnp.mean(centered * centered, axis=-1, keepdims=True) + EPSILON)
            return centered * spread, spread

        def first_rows(at):
            m, rows, flat = place(at)
            low_keys[flat, :] = grad_keys[m, rows, :].astype(BF16)

        def keyval_tile(k):
            columns = pl.ds(pl.multiple_of(k * (width // nz), width // nz), width // nz)
            part[k] = lax.dot_general(
                n_own[:, :, columns].reshape(rows_all, width // nz),
                low_keys[...],
                (((0,), (0,)), ((), ())),
                preferred_element_type=F32,
            ).astype(BF16)

        def last_rows(at):
            m, rows, flat = place(at)
            unit, spread = unit_rows(m, rows)
            grad = from_query[m, rows, :] + lax.dot_general(
                low_keys[flat, :], wkv[...], (((1,), (1,)), ((), ())), preferred_element_type=F32
            )
            sums[0] += grad * unit
            sums[1] += grad
            turned = grad * norms[0:1, :]
            inner = jnp.mean(turned * unit, axis=-1, keepdims=True)
            grad_out[m, rows, :] = grad_middle[m, rows, :] + spread * (
                turned - jnp.mean(turned, axis=-1, keepdims=True) - unit * inner
            )

        count = rows_all // step
        loop(count, first_rows)
        loop(nz, keyval_tile)
        weave.add("q", quick.run(net, [part], [keyval_out], slots[: len(quick.scratch)]))
        for _ in range(2 * ny + 1):
            weave.step("q")
        sums[...] = jnp.zeros_like(sums)
        loop(count, last_rows)
        rows = [jnp.sum(sums[k], axis=0, keepdims=True) for k in (0, 1)]
        rows += [jnp.sum(grad_norm_two[k], axis=0, keepdims=True) for k in (0, 1)]
        rows = jnp.concatenate(rows + [jnp.zeros((4, width), F32)], axis=0)
        for line in range(nz):
            for rank in range(ranks):
                first = (line * ranks + rank) * own_width // 128 * 128
                small[rank, line] = rows[:, first : first + 128]
        weave.add("s", tiny.run(net, [small], [small_out], slots[len(quick.scratch) :]))
        for name in "sqsqs":
            weave.step(name)
        for name in "qs":
            weave.finish(name)

    ins = [inputs, normed_own, grad_middle, from_query, grad_keys, wkv, norms, grad_norm_two]
    return launch(body, ins, [IN_VMEM] * len(ins), outs, scratch, plans, nz, ny, collective_id, "end_block")


def widen(arrays):
    steps = 4

    def kernel(*refs):
        for source, target in zip(refs[: len(arrays)], refs[len(arrays) :]):
            target[...] = source[...].astype(F32)

    specs = [pl.BlockSpec((array.shape[0] // steps, array.shape[1]), lambda step: (step, 0)) for array in arrays]
    return pl.pallas_call(
        kernel,
        out_shape=[jax.ShapeDtypeStruct(array.shape, F32) for array in arrays],
        grid=(steps,),
        in_specs=specs,
        out_specs=specs,
        compiler_params=pltpu.CompilerParams(vmem_limit_bytes=60 << 20),
        name="widen",
    )(*arrays)


def local(
    inputs,
    cotangent,
    doc_ids,
    attn_gain,
    attn_shift,
    w_query,
    w_keyval,
    w_attn_out,
    mlp_gain,
    mlp_shift,
    w_expand,
    w_reduce,
):
    nz = lax.axis_size("dp") // 2
    tensor_count = lax.axis_size("tensor")
    ny = tensor_count // 2
    ranks = 2 * tensor_count
    micro_count, own_rows, width = inputs.shape
    face_rows = own_rows * ranks
    tokens = micro_count * face_rows
    seq_len = doc_ids.shape[1]
    head_dim = w_keyval.shape[1] // 2
    heads = w_query.shape[1] // (2 * head_dim)
    on = (nz, ny)

    gains = jnp.concatenate([attn_gain, attn_shift, mlp_gain, mlp_shift])[None, :]
    kept, rest = front_block(
        inputs,
        cotangent,
        w_query,
        w_attn_out,
        w_keyval,
        w_expand,
        gains,
        doc_ids,
        *on,
        collective_id=1,
        head_dim=head_dim,
    )
    normed, wkv, wq, expand_given, queries, keys_vals, mixed, log_total, limits, normed_own = kept
    norms, cot_face, wo, wexp_first = rest
    middle, grad_middle, low_middle, grad_norm_two, part_expand_a, part_expand_b, reduced, grad_reduce = mlp_block(
        mixed, wo, inputs, cotangent, cot_face, norms, wexp_first, (w_expand, expand_given), (w_reduce,), *on, collective_id=3
    )
    reduced, from_query, grad_keys, grad_expand, grad_attn_out, grad_query = back_block(
        low_middle,
        reduced,
        [part_expand_a, part_expand_b],
        mixed,
        wo,
        wq,
        normed,
        queries,
        keys_vals,
        log_total,
        limits,
        *on,
        collective_id=6,
        head_dim=head_dim,
    )
    outputs = (middle + reduced).astype(BF16)
    grad_inputs, grad_keyval, small = end_block(
        inputs, normed_own, grad_middle, from_query, grad_keys, wkv, norms, grad_norm_two, *on, collective_id=8
    )
    own_width = width // (nz * ranks)
    device = lax.axis_index("dp") * tensor_count + lax.axis_index("tensor")
    small = lax.dynamic_slice_in_dim(small[:4], device * own_width % 128, own_width, axis=1)

    grad_query, grad_attn_out, grad_expand, grad_reduce = widen([grad_query, grad_attn_out, grad_expand, grad_reduce])
    return (
        outputs,
        grad_inputs,
        small[0],
        small[1],
        grad_query,
        grad_keyval,
        grad_attn_out,
        small[2],
        small[3],
        grad_expand,
        grad_reduce,
    )


def solution(mesh):
    placed = (
        P(None, ("dp", "tensor"), None),
        P(None, ("dp", "tensor"), None),
        P(),
        P("dp"),
        P("dp"),
        P("dp", "tensor"),
        P("dp", None),
        P("tensor", "dp"),
        P("dp"),
        P("dp"),
        P("dp", "tensor"),
        P("tensor", "dp"),
    )
    return jax.shard_map(
        local,
        mesh=mesh,
        in_specs=placed,
        out_specs=(
            P(None, ("dp", "tensor"), None),
            P(None, ("dp", "tensor"), None),
            P(("dp", "tensor")),
            P(("dp", "tensor")),
            P("dp", "tensor"),
            P(("dp", "tensor"), None),
            P("tensor", "dp"),
            P(("dp", "tensor")),
            P(("dp", "tensor")),
            P("dp", "tensor"),
            P("tensor", "dp"),
        ),
        check_vma=False,
    )
```

```python
import functools
import math

import jax
import jax.numpy as jnp
from jax import lax
from jax.experimental import pallas as pl
from jax.experimental.pallas import tpu as pltpu
from jax.sharding import PartitionSpec as P

BLOCK = 256
EPSILON = 1e-05
NEG_FILL = -1e30
GELU_A = math.sqrt(2.0 / math.pi)
GELU_B = 0.044715
LOG2_E = 1.0 / math.log(2.0)
MLP_ORDER = ("memmmmeemmrmememmmrmmmmrmmrmmmmmmemmmsxs", "mmmmxxsxxrmm",)
BACK_ORDER = ("mremmmrrrrmemmmerrmmeemwqqwaawwwqqaqqwaa", "qwearwaerw",)
FRONT_ORDER = ("omaoaaamaaamcoaammhaaommommokkmekecaceme", "ckceme",)
MESH = pl.DeviceIdType.MESH
ANY = pl.BlockSpec(memory_space=pl.ANY)
READY = "ready"
IN_VMEM = pl.BlockSpec(memory_space=pltpu.VMEM)
BF16 = jnp.bfloat16
F32 = jnp.float32


def layer_norm(values, gain, shift):
    center = jnp.mean(values, axis=-1, keepdims=True)
    centered = values - center
    variance = jnp.mean(centered * centered, axis=-1, keepdims=True)
    return centered * lax.rsqrt(variance + EPSILON) * gain + shift


def gelu_tanh(values):
    return jax.nn.gelu(values, approximate=True)


class Net:
    def __init__(self, nz, ny, send, recv, local):
        dp, tensor = lax.axis_index("dp"), lax.axis_index("tensor")
        self.nz, self.ny = nz, ny
        self.z, self.x = lax.div(dp, 2), lax.rem(dp, 2)
        self.y, self.c = lax.div(tensor, 2), lax.rem(tensor, 2)
        self.tensor = tensor
        self.send, self.recv, self.local = send, recv, local
        self.used = [0, 0]
        self.keys = {}

    def flip(self, value, by):
        return value + by - 2 * by * value if by else value

    def xy(self, dx, dy):
        return self.flip(self.x, dx), lax.rem(self.y + dy, self.ny) if dy else self.y

    def rank(self, dx=0, dy=0, dc=0):
        x, y = self.xy(dx, dy)
        return x * (2 * self.ny) + y * 2 + self.flip(self.c, dc)

    def chip_rows(self, dx, dy, rows):
        first = (self.rank(dx, dy) - self.c) * rows
        return pl.ds(pl.multiple_of(first, 2 * rows), 2 * rows)

    def device(self, dx=0, dy=0, dc=0, z=None):
        x, y = self.xy(dx, dy)
        return ((self.z if z is None else z) * 2 + x, y * 2 + self.flip(self.c, dc))

    def slot(self, key):
        if key not in self.keys:
            self.keys[key] = self.used[0]
            self.used[0] += 1
        return self.keys[key]

    def remote(self, key, src, dst, device):
        at = self.slot(key)
        return pltpu.make_async_remote_copy(
            src_ref=src,
            dst_ref=dst,
            send_sem=self.send.at[at],
            recv_sem=self.recv.at[at],
            device_id=device,
            device_id_type=MESH,
        )

    def take_locals(self, count):
        first = self.used[1]
        self.used[1] += count
        return first

    def copy_at(self, at, src, dst):
        return pltpu.make_async_copy(src, dst, self.local.at[at])

    def copy(self, src, dst):
        return self.copy_at(self.take_locals(1), src, dst)


def add_rows(dst, terms):
    lead, height, width = dst.shape
    rows = min(max(16, 32768 // width), height)
    steps = height // rows

    def body(step, carry):
        at, off = lax.div(step, steps), pl.multiple_of(lax.rem(step, steps) * rows, rows)
        total = terms[0][at, pl.ds(off, rows), :].astype(F32)
        for term in terms[1:]:
            total = total + term[at, pl.ds(off, rows), :].astype(F32)
        dst[at, pl.ds(off, rows), :] = total.astype(dst.dtype)
        return carry

    lax.fori_loop(0, lead * steps, body, 0)


class FaceGather:
    moves = ("x", "y", "c")
    in_spec = IN_VMEM

    def __init__(self, own, nz, ny, hold_x=False, report=False):
        self.ins, self.hold_x, self.report = [own], hold_x, report
        m, t, d = own.shape
        self.outs = [(jax.ShapeDtypeStruct((m, 4 * ny * t, d), own.dtype), ANY)]
        self.scratch = []
        self.half = t // 2
        self.remotes, self.locals = 8 * ny, 1

    def run(self, net, ins, outs, scratch):
        (own,), (out,), half = ins, outs, self.half
        dys = range(1, net.ny)

        def piece(dx, dy, h):
            return out.at[:, pl.ds(pl.multiple_of(net.rank(dx, dy) * 2 * half + h * half, half), half), :]

        mine = [own.at[:, pl.ds(h * half, half), :] for h in (0, 1)]
        keep = net.copy(own, out.at[:, pl.ds(pl.multiple_of(net.rank() * 2 * half, half), 2 * half), :])
        keep.start()
        sent = {}

        def send(key, src, dst, device):
            sent[key] = net.remote((id(self), key), src, dst, device)
            sent[key].start()

        if not self.hold_x:
            send(("x", 0), mine[0], piece(0, 0, 0), net.device(1, 0))
        for dy in dys:
            send(("y", dy, 1), mine[1], piece(0, 0, 1), net.device(0, dy))
        if not self.hold_x:
            send(("x", 1), mine[1], piece(0, 0, 1), net.device(1, 0))
        for dy in dys:
            send(("y", dy, 0), mine[0], piece(0, 0, 0), net.device(0, dy))
        for h in (0, 1):
            send(("c", h), mine[h], piece(0, 0, h), net.device(0, 0, 1))
        if self.hold_x:
            yield
            for h in (0, 1):
                send(("x", h), mine[h], piece(0, 0, h), net.device(1, 0))

        def share(key, dx, dy, h):
            send(("c",) + key, piece(dx, dy, h), piece(dx, dy, h), net.device(0, 0, 1))

        def from_x(h):
            sent["x", h].wait_recv()
            if not h:
                for dy in dys:
                    send(("xy", dy), piece(1, 0, 0), piece(1, 0, 0), net.device(0, dy))
            share(("x", h), 1, 0, h)

        def from_y(dy, h):
            sent["y", dy, h].wait_recv()
            if h:
                send(("yx", dy), piece(0, -dy % net.ny, 1), piece(0, -dy % net.ny, 1), net.device(1, 0))
            share(("y", dy, h), 0, -dy % net.ny, h)

        arrivals = []
        for first in (True, False):
            on_x = [functools.partial(from_x, 0 if first else 1)]
            on_y = [functools.partial(from_y, dy, 1 if first else 0) for dy in dys]
            arrivals.append(on_x + on_y)
        if self.hold_x:
            arrivals = [arrivals[0][1:], arrivals[1][1:], arrivals[0][:1], arrivals[1][:1]]
        waited = set()

        def shared(*keys):
            for key in keys:
                sent[("c",) + key].wait_recv()
                waited.add(("c",) + key)

        if self.report:
            yield
            keep.wait()
            shared((0,), (1,))
            yield (0, 0)
        for group in arrivals:
            for arrive in group:
                yield
                arrive()
        if self.report:
            shared(("x", 0), ("x", 1))
            yield (1, 0)
            for dy in dys:
                shared(("y", dy, 1), ("y", dy, 0))
                yield (0, -dy % net.ny)
        for dy in dys:
            yield
            sent["xy", dy].wait_recv()
            share(("xy", dy), 1, -dy % net.ny, 0)
            yield
            sent["yx", dy].wait_recv()
            share(("yx", dy), 1, -dy % net.ny, 1)
        yield
        for key, copy in sent.items():
            if key[0] == "c" and key not in waited:
                copy.wait_recv()
        if self.report:
            for dy in dys:
                yield (1, -dy % net.ny)
        else:
            keep.wait()
        for copy in sent.values():
            copy.wait_send()


class FaceScatter:
    moves = ("x", "y", "c")

    def __init__(self, part, nz, ny, resident=False):
        self.ins, self.resident = [part], resident
        m, rows, d = part.shape
        t = rows // (4 * ny)
        self.outs = [(jax.ShapeDtypeStruct((m, t, d), F32), pl.BlockSpec(memory_space=pltpu.VMEM))]
        half = t // 2
        self.half = half
        self.scratch = [
            pltpu.VMEM((2 * ny, m, t, d), BF16),
            pltpu.VMEM((ny - 1, m, half, d), BF16),
            pltpu.VMEM((ny - 1, m, half, d), BF16),
            pltpu.VMEM((2, m, half, d), BF16),
            pltpu.VMEM((2, ny - 1, m, half, d), BF16),
        ]
        if not resident:
            self.scratch.append(pltpu.VMEM((2 * ny, m, t, d), BF16))
        self.remotes, self.locals = 6 * ny + 4, 2 * ny

    def run(self, net, ins, outs, scratch, produce=None):
        (part,), (out,), half = ins, outs, self.half
        from_core, x_diag, y_diag, x_in, y_in = scratch[:5]
        ny = net.ny
        dys = range(1, ny)
        order = [(1, dy) for dy in dys] + [(1, 0)] + [(0, dy) for dy in dys] + [(0, 0)]
        sent, loads = {}, {}

        def send(key, src, dst, device):
            sent[key] = net.remote((id(self), key), src, dst, device)
            sent[key].start()

        def rows(dx, dy, dc, first=0, size=2 * half):
            at = net.rank(dx, dy, dc) * 2 * half + first
            return part.at[:, pl.ds(pl.multiple_of(at, half), size), :]

        def work(dx, dy, first=0, size=2 * half):
            if self.resident:
                return rows(dx, dy, 0, first, size)
            return scratch[5].at[dx * ny + dy, :, pl.ds(first, size), :]

        def begin(dx, dy):
            at = dx * ny + dy
            if not self.resident:
                loads[at] = net.copy(rows(dx, dy, 0), work(dx, dy))
                loads[at].start()
            send(("c", at), rows(dx, dy, 1), from_core.at[at], net.device(0, 0, 1))

        def settle(dx, dy):
            at = dx * ny + dy
            if not self.resident:
                loads[at].wait()
            sent["c", at].wait_recv()
            add_rows(work(dx, dy), [work(dx, dy), from_core.at[at]])
            top, low = work(dx, dy, 0, half), work(dx, dy, half, half)
            if dx and dy:
                send(("xd", dy), top, x_diag.at[dy - 1], net.device(1, 0))
                send(("yd", dy), low, y_diag.at[dy - 1], net.device(0, dy))
            elif dx:
                send(("x", 0), top, x_in.at[0], net.device(1, 0))
            elif dy:
                send(("y", dy, 1), low, y_in.at[1, dy - 1], net.device(0, dy))

        for at, place in enumerate(order):
            if produce is not None:
                produce(*place)
            begin(*place)
            if produce is not None:
                yield
                if at:
                    settle(*order[at - 1])
        for place in order if produce is None else order[-1:]:
            yield
            settle(*place)
        for dy in dys:
            yield
            sent["xd", dy].wait_recv()
            top = work(0, dy, 0, half)
            add_rows(top, [top, x_diag.at[dy - 1]])
            send(("y", dy, 0), top, y_in.at[0, dy - 1], net.device(0, dy))
        low = work(1, 0, half, half)
        for dy in dys:
            yield
            sent["yd", dy].wait_recv()
            add_rows(low, [low, y_diag.at[dy - 1]])
        send(("x", 1), low, x_in.at[1], net.device(1, 0))
        for h in (0, 1):
            yield
            sent["x", h].wait_recv()
            for dy in dys:
                sent["y", dy, h].wait_recv()
            add_rows(
                out.at[:, pl.ds(h * half, half), :],
                [work(0, 0, h * half, half), x_in.at[h]] + [y_in.at[h, dy - 1] for dy in dys],
            )
        for copy in sent.values():
            copy.wait_send()


class LineGather:
    moves = ("x", "line", "c")
    in_spec = IN_VMEM

    def __init__(self, shards, kinds, nz, ny, share=(0, 1), given=()):
        self.ins, self.kinds, self.share = list(shards) + list(given), list(kinds), share
        self.outs, self.scratch = [], []
        for shard, kind in zip(shards, kinds):
            rows, columns = shard.shape
            if kind == "row":
                shape = (rows * 2 * nz, columns // 2 // share[1])
            elif kind == "col":
                shape = (rows // 2 // share[1], columns * 2 * nz)
            else:
                shape = (rows * 2 * nz, columns)
            self.outs.append((jax.ShapeDtypeStruct(shape, shard.dtype), ANY))
        count = len(self.kinds)
        self.remotes = count * (1 + 4 * (nz - 1)) + kinds.count("both") * (1 + 4 * (nz - 1))
        self.locals = 2 * count

    def run(self, net, ins, outs, scratch):
        nz, z = net.nz, net.z
        sent, locals_, shared = [], [], []
        weights = []
        given = ins[len(self.kinds) :]
        for at, (shard, out, kind) in enumerate(zip(ins, outs, self.kinds)):
            rows, columns = shard.shape

            if kind == "row":
                span = columns // 2 // self.share[1]

                def mine(dx, shard=shard, span=span):
                    first = (net.flip(net.x, dx) * self.share[1] + self.share[0]) * span
                    return shard.at[:, pl.ds(pl.multiple_of(first, span), span)]

                def block(line, dx, out=out, rows=rows):
                    first = (line * 2 + net.flip(net.x, dx)) * rows
                    return out.at[pl.ds(pl.multiple_of(first, rows), rows), :]

            elif kind == "col":
                span = rows // 2 // self.share[1]

                def mine(dx, shard=shard, span=span):
                    first = (net.flip(net.x, dx) * self.share[1] + self.share[0]) * span
                    return shard.at[pl.ds(pl.multiple_of(first, span), span), :]

                def block(line, dx, out=out, columns=columns):
                    first = (line * 2 + net.flip(net.x, dx)) * columns
                    return out.at[:, pl.ds(pl.multiple_of(first, columns), columns)]

            else:
                half = rows // 2

                def mine(dx, shard=shard, half=half):
                    return shard.at[pl.ds(pl.multiple_of(net.c * half, half), half), :]

                def block(line, dx, out=out, rows=rows, half=half):
                    first = (line * 2 + net.flip(net.x, dx)) * rows + net.c * half
                    return out.at[pl.ds(pl.multiple_of(first, half), half), :]

            weights.append((at, kind, mine, block))

        def hop(at, dx, step, up, block, src=None):
            origin = z - (step - 1) if up else z + (step - 1)
            there = z + 1 if up else z - 1
            copy = net.remote(
                (id(self), at, dx, step, up),
                block(origin, dx) if src is None else src,
                block(origin, dx),
                net.device(z=there),
            )
            fits = (origin >= 0) & (there < nz) if up else (origin < nz) & (there >= 0)
            return copy, fits

        def start(at, dx, step, up, block, src=None):
            copy, fits = hop(at, dx, step, up, block, src)
            pl.when(fits)(copy.start)
            sent.append((copy, fits))

        def arrived(at, dx, step, up, block, kind):
            copy, _ = hop(at, dx, step, up, block)
            origin = z - step if up else z + step
            fits = origin >= 0 if up else origin < nz
            pl.when(fits)(copy.wait_recv)
            if kind == "both":
                share = net.remote(
                    (id(self), "c", at, dx, step, up), block(origin, dx), block(origin, dx), net.device(0, 0, 1)
                )
                pl.when(fits)(share.start)
                shared.append((share, fits))

        swaps = {}
        for at, kind, mine, block in weights:
            if not given:
                swaps[at] = net.remote((id(self), at, "x"), mine(1), block(z, 0), net.device(1, 0))
                swaps[at].start()
            for up in (True, False):
                start(at, 0, 1, up, block, mine(0))
        for at, kind, mine, block in weights:
            if kind == "both":
                whole = ins[at].shape[0]
                into = outs[at].at[pl.ds(pl.multiple_of((z * 2 + net.x) * whole, whole), whole), :]
                locals_.append(net.copy(ins[at], into))
            else:
                locals_.append(net.copy(mine(0), block(z, 0)))
            locals_[-1].start()
        for (at, kind, mine, block), other in zip(weights, given):
            span = pl.ds(self.share[0] * other.shape[kind == "row"] // self.share[1], other.shape[kind == "row"] // self.share[1])
            other = other.at[:, span] if kind == "row" else other.at[span, :]
            locals_.append(net.copy(other, block(z, 1)))
            locals_[-1].start()
            for up in (True, False):
                start(at, 1, 1, up, block, other)
        yield
        for copy in locals_:
            copy.wait()
        for at, kind, mine, block in weights:
            if given:
                continue
            swaps[at].wait_recv()
            for up in (True, False):
                start(at, 1, 1, up, block)
            if kind == "both":
                share = net.remote((id(self), "c", at), block(z, 1), block(z, 1), net.device(0, 0, 1))
                share.start()
                shared.append((share, None))
        for step in range(1, nz):
            for at, kind, mine, block in weights:
                for dx in (0, 1):
                    yield
                    for up in (True, False):
                        arrived(at, dx, step, up, block, kind)
                        if step < nz - 1:
                            start(at, dx, step + 1, up, block)
        yield
        for copy, fits in shared:
            if fits is None:
                copy.wait_recv()
            else:
                pl.when(fits)(copy.wait_recv)
        yield READY
        for copy, fits in shared:
            if fits is None:
                copy.wait_send()
            else:
                pl.when(fits)(copy.wait_send)
        for copy, fits in sent:
            pl.when(fits)(copy.wait_send)
        for copy in swaps.values():
            copy.wait_send()


class HalfSwap:
    moves = ("x",)

    def __init__(self, shards, kinds, nz, ny):
        self.ins, self.kinds = list(shards), list(kinds)
        self.outs, self.scratch = [], []
        for shard, kind in zip(shards, kinds):
            rows, columns = shard.shape
            shape = (rows, columns // 2) if kind == "row" else (rows // 2, columns)
            self.outs.append((jax.ShapeDtypeStruct(shape, shard.dtype), ANY))
        self.remotes, self.locals = len(self.ins), 0

    def run(self, net, ins, outs, scratch):
        copies = []
        for at, (shard, out, kind) in enumerate(zip(ins, outs, self.kinds)):
            span = out.shape[kind == "row"]
            there = pl.ds(pl.multiple_of((1 - net.x) * span, span), span)
            src = shard.at[:, there] if kind == "row" else shard.at[there, :]
            copies.append(net.remote((id(self), at), src, out, net.device(1, 0)))
            copies[-1].start()
        yield
        for copy in copies:
            copy.wait_recv()
        yield READY
        for copy in copies:
            copy.wait_send()


class LineScatter:
    moves = ("x", "line")

    def __init__(self, parts, kinds, nz, ny, resident=False, joined=False):
        self.ins, self.kinds, self.resident, self.joined = list(parts), list(kinds), resident, joined
        self.outs, self.scratch = [], []
        for part, kind in zip(parts, kinds):
            rows, columns = part.shape
            shape = (rows // (2 * nz), columns) if kind == "row" else (rows, columns // (2 * nz))
            times = 2 * (len(parts) if joined else 1)
            whole = (shape[0], shape[1] * times) if kind == "row" else (shape[0] * times, shape[1])
            if not (joined and self.outs):
                self.outs.append((jax.ShapeDtypeStruct(whole, BF16), ANY))
            for lead in (nz - 1, nz - 1, 1) + (() if resident else (nz,)):
                self.scratch.append(pltpu.VMEM((lead, 2) + shape, BF16))
        count = len(self.ins)
        self.remotes = count * (1 + 4 * nz)
        self.locals = count * (2 * nz + 1)

    def run(self, net, ins, outs, scratch):
        nz, z = net.nz, net.z
        loads, grads = {}, []
        each = 3 if self.resident else 4
        outs = list(outs) * len(ins) if self.joined else outs

        def spot(at, out):
            rows, columns = scratch[each * at + 2].shape[2:]
            kind = self.kinds[at]
            size = columns if kind == "row" else rows
            first = (net.x * len(ins) + at) * size if self.joined else net.x * size
            span = pl.ds(pl.multiple_of(first, size), size)
            return out.at[:, span] if kind == "row" else out.at[span, :]

        for at, (part, out, kind) in enumerate(zip(ins, outs, self.kinds)):
            down, up, mine = scratch[each * at : each * at + 3]
            _, _, rows, columns = mine.shape

            def block(line, dx, part=part, kind=kind, rows=rows, columns=columns):
                size = rows if kind == "row" else columns
                first = pl.ds(pl.multiple_of((line * 2 + net.flip(net.x, dx)) * size, size), size)
                return part.at[first, :] if kind == "row" else part.at[:, first]

            if self.resident:
                work = block
            else:

                def work(line, dx, at=at):
                    return scratch[each * at + 3].at[line, dx]

                order = []
                for k in range(nz):
                    order += [k, nz - 1 - k]
                for line in dict.fromkeys(order):
                    for dx in (1, 0):
                        loads[at, line, dx] = net.copy(block(line, dx), work(line, dx))
                        loads[at, line, dx].start()
            grads.append((at, out, work, down, up, mine))

        def inbox(slots, line, dx, toward):
            return slots.at[line if toward < 0 else line - 1, dx]

        pieces = (1, 0)
        each_line = len(pieces)

        for at, *_ in grads:
            net.slot((id(self), at, "x"))
            for dx in (0, 1):
                for line in range(nz):
                    for toward in (-1, 1):
                        net.slot((id(self), at, line, dx, toward))

        def chain(grad, dx, line, toward):
            at, out, work, down, up, mine = grad
            slot = inbox(down if toward < 0 else up, line, dx, toward)
            copy = net.remote((id(self), at, line, dx, toward), work(line, dx), slot, net.device(z=z + toward))
            return copy, slot

        def forward(place, grad, dx, line, toward):
            at, out, work, down, up, mine = grad
            copy, slot = chain(grad, dx, line, toward)
            if not self.resident:
                loads[at, line, dx].wait()
            if place != (nz - 1 if toward < 0 else 0):
                copy.wait_recv()
                add_rows(_lead(work(line, dx)), [_lead(work(line, dx)), _lead(slot)])
            copy.start()

        def finish(place, grad, dx):
            at, out, work, down, up, mine = grad
            if not self.resident:
                loads[at, place, dx].wait()
            terms = [_lead(work(place, dx))]
            for toward in (-1, 1):
                if (place < nz - 1) if toward < 0 else (place > 0):
                    copy, slot = chain(grad, dx, place, toward)
                    copy.wait_recv()
                    terms.append(_lead(slot))
            total = mine.at[0, dx]
            add_rows(_lead(total), terms)
            if dx:
                net.remote((id(self), at, "x"), total, spot(at, out), net.device(1, 0)).start()
            else:
                net.copy_at(self.first_local + at, total, spot(at, out)).start()

        plan = {}
        for place in range(nz):
            waits_up, waits_down = place, nz - 1 - place
            todo = []
            for toward, waits, lines in (
                (1, waits_up, range(nz - 1, place, -1)),
                (-1, waits_down, range(place)),
            ):
                order = [(line, dx) for line in lines for dx in pieces]
                for j, (line, dx) in enumerate(order):
                    for grad in grads:
                        todo.append((waits + j if waits else 0, waits, (forward, grad, dx, line, toward)))
            for q, dx in enumerate(pieces):
                times = []
                if waits_up:
                    times.append(waits_up + each_line * (nz - 1 - place) + q)
                if waits_down:
                    times.append(waits_down + each_line * place + q)
                for grad in grads:
                    todo.append((max(times), nz, (finish, grad, dx)))
            for time, waits, item in sorted(todo, key=lambda entry: entry[:2]):
                plan.setdefault(time, {}).setdefault(place, []).append(item)
        self.first_local = net.take_locals(len(grads))
        for time in range(max(plan) + 1):
            if time:
                yield
            for place, items in sorted(plan.get(time, {}).items()):

                def act(place=place, items=items):
                    for item in items:
                        item[0](place, *item[1:])

                pl.when(z == place)(act)
        sent = [
            (chain(grad, dx, line, toward)[0], (z > line) if toward < 0 else (z < line))
            for grad in grads
            for dx in pieces
            for toward, lines in ((-1, range(nz - 1)), (1, range(1, nz)))
            for line in lines
        ]
        swaps, stores = [], []
        for at, out, _, _, _, mine in grads:
            swaps.append(net.remote((id(self), at, "x"), mine.at[0, 1], spot(at, out), net.device(1, 0)))
            stores.append(net.copy_at(self.first_local + at, mine.at[0, 0], spot(at, out)))
        yield
        for copy, sends in sent:
            pl.when(sends)(copy.wait_send)
        for copy in swaps:
            copy.wait()
        for copy in stores:
            copy.wait()


def _lead(ref):
    return Lead(ref)


class Lead:
    def __init__(self, ref):
        self.ref, self.shape, self.dtype = ref, (1,) + tuple(ref.shape), ref.dtype

    def __getitem__(self, index):
        return self.ref[index[1], index[2]]

    def __setitem__(self, index, value):
        self.ref[index[1], index[2]] = value


class KeysGather:
    moves = ("x", "line", "c")
    in_spec = IN_VMEM

    def __init__(self, face, nz, ny):
        m, rows, width = face.shape
        self.ins = [face]
        self.outs = [(jax.ShapeDtypeStruct((m, nz * rows, width), face.dtype), ANY)]
        self.scratch = []
        self.remotes, self.locals = 4 * (nz - 1), 1

    def run(self, net, ins, outs, scratch):
        (face,), (out,) = ins, outs
        nz, z = net.nz, net.z
        _, rows, width = face.shape
        part, side = rows // 2, width // 2

        def block(line, dx, dc):
            first = pl.multiple_of(line * rows + net.flip(net.x, dx) * part, part)
            column = pl.multiple_of(net.flip(net.c, dc) * side, side)
            return out.at[:, pl.ds(first, part), pl.ds(column, side)]

        own = face.at[
            :,
            pl.ds(pl.multiple_of(net.x * part, part), part),
            pl.ds(pl.multiple_of(net.c * side, side), side),
        ]
        sent, shared = [], []

        def line_copy(step):
            origin = z - (step - 1)
            src = own if step == 1 else block(origin, 0, 0)
            return net.remote((id(self), step), src, block(origin, 0, 0), net.device(z=z + 1))

        def start(step):
            copy, fits = line_copy(step), (z - (step - 1) >= 0) & (z + 1 < nz)
            pl.when(fits)(copy.start)
            sent.append((copy, fits))

        start(1)
        keep = net.copy(face, out.at[:, pl.ds(pl.multiple_of(z * rows, rows), rows), :])
        keep.start()
        later = []
        for step in range(1, nz):
            yield
            fits = z - step >= 0
            pl.when(fits)(line_copy(step).wait_recv)
            if step < nz - 1:
                start(step + 1)
            here = block(z - step, 0, 0)
            across = net.remote((id(self), "x", step), here, here, net.device(1, 0))
            beside = net.remote((id(self), "c", step), here, here, net.device(0, 0, 1))
            for copy in (across, beside):
                pl.when(fits)(copy.start)
                sent.append((copy, fits))
            later.append((step, fits, across))
            shared.append((beside, fits))
        for step, fits, across in later:
            yield
            pl.when(fits)(across.wait_recv)
            there = block(z - step, 1, 0)
            beside = net.remote((id(self), "xc", step), there, there, net.device(0, 0, 1))
            pl.when(fits)(beside.start)
            sent.append((beside, fits))
            shared.append((beside, fits))
        yield
        for copy, fits in shared:
            pl.when(fits)(copy.wait_recv)
        keep.wait()
        yield READY
        for copy, fits in sent:
            pl.when(fits)(copy.wait_send)


class WholeScatter(FaceScatter):
    moves = ("x", "y", "c", "z")

    def __init__(self, part, nz, ny, resident=False):
        m, _, rows, d = part.shape
        merged = jax.ShapeDtypeStruct((m * nz, rows, d), part.dtype) if resident else part.reshape(m * nz, rows, d)
        super().__init__(merged, nz, ny, resident)
        t = rows // (4 * ny)
        self.m, self.nz = m, nz
        self.outs = [(jax.ShapeDtypeStruct((m, t, d), F32), pl.BlockSpec(memory_space=pltpu.VMEM))]
        self.scratch = self.scratch + [pltpu.VMEM((m * nz, t, d), BF16), pltpu.VMEM((nz, m, t, d), BF16)]
        self.remotes = self.remotes + nz * m
        self.locals = self.locals + m

    def run(self, net, ins, outs, scratch):
        face, inbox = scratch[-2:]
        yield from super().run(net, ins, [face], scratch[:-2])
        nz, m = self.nz, self.m
        copies = []
        for far in range(1, nz):
            line = lax.rem(net.z + far, nz)
            for at in range(m):
                copies.append(
                    pltpu.make_async_remote_copy(
                        src_ref=face.at[at * nz + line],
                        dst_ref=inbox.at[far, at],
                        send_sem=net.send.at[net.slot((id(self), "z", far, at))],
                        recv_sem=net.recv.at[net.slot((id(self), "z", far, at))],
                        device_id=net.device(z=line),
                        device_id_type=MESH,
                    )
                )
                copies[-1].start()
        own = []
        for at in range(m):
            own.append(net.copy(face.at[at * nz + net.z], inbox.at[0, at]))
            own[-1].start()
        yield
        for copy in own:
            copy.wait()
        for copy in copies:
            copy.wait()
        add_rows(outs[0], [inbox.at[far] for far in range(nz)])


class QuickScatter:
    moves = ("c", "same", "z")

    def __init__(self, part, nz, ny):
        _, rows, d = part.shape
        t = rows // (4 * ny)
        self.ins, self.t = [part], t
        self.outs = [(jax.ShapeDtypeStruct((t, d), F32), pl.BlockSpec(memory_space=pltpu.VMEM))]
        self.scratch = [
            pltpu.VMEM((2 * ny, nz, t, d), BF16),
            pltpu.VMEM((2 * ny, nz, t, d), BF16),
            pltpu.VMEM((2 * ny, nz, t, d), BF16),
            pltpu.VMEM((nz, t, d), BF16),
            pltpu.VMEM((nz, 1, t, d), BF16),
        ]
        self.remotes, self.locals = 4 * ny + nz, 2 * ny + 1

    def run(self, net, ins, outs, scratch):
        (part,), (out,), t = ins, outs, self.t
        work, from_core, inbox, face, line_in = scratch
        ny, nz = net.ny, net.nz
        order = [(dx, dy) for dx in (1, 0) for dy in reversed(range(ny))]
        cores, loads, copies = {}, {}, {}

        def rows(dx, dy, dc):
            return part.at[:, pl.ds(pl.multiple_of(net.rank(dx, dy, dc) * t, t), t), :]

        for dx, dy in order:
            at = dx * ny + dy
            loads[at] = net.copy(rows(dx, dy, 0), work.at[at])
            loads[at].start()
            cores[at] = net.remote((id(self), "c", at), rows(dx, dy, 1), from_core.at[at], net.device(0, 0, 1))
            cores[at].start()
        for dx, dy in order:
            at = dx * ny + dy
            yield
            loads[at].wait()
            cores[at].wait_recv()
            add_rows(work.at[at], [work.at[at], from_core.at[at]])
            if at:
                copies[at] = net.remote((id(self), at), work.at[at], inbox.at[at], net.device(dx, dy))
                copies[at].start()
        yield
        for copy in copies.values():
            copy.wait_recv()
        add_rows(face, [work.at[0]] + [inbox.at[at] for at in copies])
        lines = []
        for far in range(1, nz):
            line = lax.rem(net.z + far, nz)
            lines.append(
                net.remote((id(self), "z", far), face.at[pl.ds(line, 1)], line_in.at[far], net.device(z=line))
            )
            lines[-1].start()
        own = net.copy(face.at[pl.ds(net.z, 1)], line_in.at[0])
        own.start()
        yield
        own.wait()
        for copy in lines:
            copy.wait_recv()
        add_rows(_lead(out), [line_in.at[far] for far in range(nz)])
        for copy in list(cores.values()) + list(copies.values()) + lines:
            copy.wait_send()


class PlaneGather:
    moves = ("plane",)
    in_spec = IN_VMEM

    def __init__(self, own, nz, ny):
        self.ins = [own]
        self.outs = [(jax.ShapeDtypeStruct((2 * nz,) + own.shape, own.dtype), ANY)]
        self.scratch = []
        self.remotes, self.locals = 2 * nz, 1

    def run(self, net, ins, outs, scratch):
        (own,), (out,) = ins, outs
        here = out.at[net.z * 2 + net.x]
        copies = []
        for far in range(net.nz):
            for dx in (0, 1):
                if far or dx:
                    line = lax.rem(net.z + far, net.nz)
                    copies.append(net.remote((id(self), far, dx), own, here, net.device(dx, z=line)))
                    copies[-1].start()
        keep = net.copy(own, here)
        keep.start()
        yield
        for copy in copies:
            copy.wait()
        keep.wait()


class SmallScatter:
    moves = ("face", "z")

    def __init__(self, part, nz, ny):
        ranks, _, rows, width = part.shape
        self.ins = [part]
        vmem = pl.BlockSpec(memory_space=pltpu.VMEM)
        self.outs = [(jax.ShapeDtypeStruct((rows, width), F32), vmem)]
        self.scratch = [
            pltpu.VMEM((ranks, nz, rows, width), F32),
            pltpu.VMEM((nz, rows, width), F32),
            pltpu.VMEM((nz, rows, width), F32),
        ]
        self.remotes, self.locals = ranks + nz, 2

    def run(self, net, ins, outs, scratch):
        (part,), (out,) = ins, outs
        inbox, total, line_in = scratch
        ny, nz = net.ny, net.nz
        copies = []
        for dx in (0, 1):
            for dy in range(ny):
                for dc in (0, 1):
                    if dx or dy or dc:
                        at = (dx * ny + dy) * 2 + dc
                        copies.append(
                            net.remote(
                                (id(self), at), part.at[net.rank(dx, dy, dc)], inbox.at[at], net.device(dx, dy, dc)
                            )
                        )
                        copies[-1].start()
        keep = net.copy(part.at[net.rank()], inbox.at[0])
        keep.start()
        yield
        keep.wait()
        for copy in copies:
            copy.wait()
        total[...] = jnp.sum(inbox[...], axis=0)
        lines = []
        for far in range(1, nz):
            line = lax.rem(net.z + far, nz)
            lines.append(net.remote((id(self), "z", far), total.at[line], line_in.at[far], net.device(z=line)))
            lines[-1].start()
        own = net.copy(total.at[net.z], line_in.at[0])
        own.start()
        yield
        own.wait()
        for copy in lines:
            copy.wait()
        out[...] = jnp.sum(line_in[...], axis=0)


def launch(body, ins, in_specs, outs, scratch, plans, nz, ny, collective_id, name, extra_locals=0, vmem=56):
    moves = set()
    for plan in plans:
        moves |= set(plan.moves)
    remotes = sum(plan.remotes for plan in plans)
    locals_ = max(1, extra_locals + sum(plan.locals for plan in plans))

    def kernel(*refs):
        in_refs, refs = refs[: len(ins)], refs[len(ins) :]
        out_refs, refs = refs[: len(outs)], refs[len(outs) :]
        scratch_refs, (send, recv, local) = refs[: len(scratch)], refs[len(scratch) :]
        net = Net(nz, ny, send, recv, local)
        peers = {}
        for far in range(nz):
            for dx in (0, 1):
                for dy in range(ny):
                    for dc in (0, 1):
                        kinds = set()
                        if not far:
                            kinds.add("face")
                            if dx and not dy and not dc:
                                kinds.add("x")
                            if dy and not dx and not dc:
                                kinds.add("y")
                            if dc and not dx and not dy:
                                kinds.add("c")
                            if not dc:
                                kinds.add("same")
                        if far and not dx and not dy and not dc:
                            kinds.add("z")
                            if far in (1, nz - 1):
                                kinds.add("line")
                        if not dy and not dc:
                            kinds.add("plane")
                        if (far or dx or dy or dc) and kinds & moves:
                            line = lax.rem(net.z + far, nz) if far else None
                            peers[far, dx, dy, dc] = net.device(dx, dy, dc, line)
        barrier = pltpu.get_barrier_semaphore()
        for device in peers.values():
            pl.semaphore_signal(barrier, inc=1, device_id=device, device_id_type=MESH)
        pl.semaphore_wait(barrier, len(peers))
        body(net, in_refs, out_refs, scratch_refs)

    return list(
        pl.pallas_call(
            kernel,
            out_shape=[shape for shape, _ in outs],
            in_specs=in_specs,
            out_specs=[spec for _, spec in outs],
            scratch_shapes=list(scratch)
            + [
                pltpu.SemaphoreType.DMA((remotes,)),
                pltpu.SemaphoreType.DMA((remotes,)),
                pltpu.SemaphoreType.DMA((locals_,)),
            ],
            compiler_params=pltpu.CompilerParams(
                collective_id=collective_id, has_side_effects=True, vmem_limit_bytes=vmem << 20
            ),
            name=name,
        )(*ins)
    )


def exchange(plans, nz, ny, collective_id, name, order=()):
    ins = [array for plan in plans for array in plan.ins]
    outs = [out for plan in plans for out in plan.outs]
    scratch = [entry for plan in plans for entry in plan.scratch]

    def body(net, in_refs, out_refs, scratch_refs):
        running = []
        for plan in plans:
            mine = []
            for refs_of, count in ((in_refs, plan.ins), (out_refs, plan.outs), (scratch_refs, plan.scratch)):
                mine.append(list(refs_of[: len(count)]))
            in_refs = in_refs[len(plan.ins) :]
            out_refs = out_refs[len(plan.outs) :]
            scratch_refs = scratch_refs[len(plan.scratch) :]
            running.append(plan.run(net, *mine))
        for at in order:
            next(running[at], None)
        while running:
            for steps in list(running):
                try:
                    next(steps)
                except StopIteration:
                    running.remove(steps)

    specs = [getattr(plan, "in_spec", ANY) for plan in plans for _ in plan.ins]
    results = launch(body, ins, specs, outs, scratch, plans, nz, ny, collective_id, name)
    grouped = []
    for plan in plans:
        grouped.append(results[: len(plan.outs)])
        results = results[len(plan.outs) :]
    return grouped


class Weave:
    def __init__(self):
        self.plans, self.ready = {}, set()

    def add(self, name, steps):
        self.plans[name] = steps

    def step(self, name):
        steps = self.plans.get(name)
        if steps is not None:
            state = next(steps, self)
            if state is self:
                del self.plans[name]
            elif state == READY:
                self.ready.add(name)

    def need(self, name):
        while name in self.plans and name not in self.ready:
            self.step(name)

    def finish(self, name):
        while name in self.plans:
            self.step(name)


def first_block(block, seq_len):
    longest = seq_len // 2 + BLOCK
    return jnp.maximum(block - (longest - 1 + BLOCK - 1) // BLOCK, 0)


def loop(count, body):
    def step(at, carry):
        body(at)
        return carry

    lax.fori_loop(0, count, step, 0)


def mlp_block(mixed, wo, inputs, cotangent, cot_face, norms, wexp_first, w_expand, w_reduce, nz, ny, collective_id):
    micro_count, own_rows, width = inputs.shape
    face_rows = cot_face.shape[1]
    tokens = micro_count * face_rows
    attn = mixed.shape[2]
    units = w_expand[0].shape[1] // 2
    half = units // 2
    tile = min(512, half)
    wide = 512
    part = jax.ShapeDtypeStruct((micro_count, face_rows, width), BF16)
    part_red = jax.ShapeDtypeStruct((units, width), BF16)
    own = (micro_count, own_rows, width)
    scatter_a, scatter_b = (FaceScatter(part, nz, ny, resident=True) for _ in range(2))
    gather = FaceGather(jax.ShapeDtypeStruct(own, BF16), nz, ny, report=True)
    line_e = LineGather(w_expand[:1], ["row"], nz, ny, share=(1, 2), given=w_expand[1:])
    line_r = LineGather(w_reduce[:1], ["col"], nz, ny, given=w_reduce[1:])
    line_s = LineScatter([part_red], ["col"], nz, ny, resident=True)
    plans = [scatter_a, scatter_b, gather, line_e, line_r, line_s]
    vmem = pl.BlockSpec(memory_space=pltpu.VMEM)
    outs = [
        (jax.ShapeDtypeStruct(own, F32), ANY),
        (jax.ShapeDtypeStruct(own, F32), ANY),
        (jax.ShapeDtypeStruct(own, BF16), ANY),
        (jax.ShapeDtypeStruct((2, 16, width), F32), vmem),
        (jax.ShapeDtypeStruct((width, half), BF16), ANY),
        (jax.ShapeDtypeStruct((width, half), BF16), ANY),
        (part, ANY),
    ] + line_s.outs
    scratch = [
        pltpu.VMEM((micro_count, face_rows, width), BF16),
        pltpu.VMEM(own, F32),
        pltpu.VMEM(own, F32),
        pltpu.VMEM(own, BF16),
        pltpu.VMEM(own, BF16),
        pltpu.VMEM(own, BF16),
        pltpu.VMEM((micro_count, face_rows, width), BF16),
        pltpu.VMEM((micro_count, face_rows, width), BF16),
        pltpu.VMEM((width, half), BF16),
        pltpu.VMEM((width, half), BF16),
        pltpu.VMEM((units, width), BF16),
        pltpu.VMEM((micro_count, face_rows, units), BF16),
        pltpu.VMEM((micro_count, face_rows, units), BF16),
        pltpu.VMEM((units, width), BF16),
        pltpu.VMEM((micro_count, face_rows, attn), BF16),
        pltpu.VMEM((attn, width), BF16),
    ]
    shared = len(scratch)
    scratch += scatter_a.scratch + line_s.scratch

    def body(net, ins, outs, scratch):
        mixed_in, wo_in, own_in, cot_in, face_in, norms, first_in, *weights_in = ins
        middle_out, grad_out, low_out, norm_out, expand_a, expand_b, reduced_out, reduce_out = outs
        p, branch, middle, own, cot_own, n_own, n_face, cot, we0, we1, wr, active, slope, pr, mixed, wo = scratch[:shared]
        we = (we0, we1)
        slots = list(scratch[shared : shared + len(scatter_a.scratch)])
        line_slots = list(scratch[shared + len(scatter_a.scratch) :])

        loads = [
            net.copy(*pair)
            for pair in (
                (mixed_in, mixed),
                (wo_in, wo),
                (own_in, own),
                (cot_in, cot_own),
                (first_in, we0),
                (face_in, cot),
            )
        ]
        weave = Weave()
        stores = []
        weave.add("e", line_e.run(net, weights_in[:2], [we1], []))
        weave.step("e")
        weave.add("r", line_r.run(net, weights_in[2:], [wr], []))
        weave.step("r")
        for load in loads:
            load.start()

        chip_tokens = micro_count * 2 * own_rows

        def branch_chip(dx, dy):
            rows = net.chip_rows(dx, dy, own_rows)

            def tile_at(n):
                columns = pl.ds(pl.multiple_of(n * wide, wide), wide)
                p[:, rows, columns] = (
                    jnp.dot(
                        mixed[:, rows, :].reshape(chip_tokens, attn), wo[:, columns], preferred_element_type=F32
                    )
                    .astype(BF16)
                    .reshape(micro_count, 2 * own_rows, wide)
                )

            loop(width // wide, tile_at)

        row_steps = own_rows // 16

        def own_rows_at(at):
            return lax.div(at, row_steps), pl.ds(pl.multiple_of(lax.rem(at, row_steps) * 16, 16), 16)

        def norm_rows(at):
            m, rows = own_rows_at(at)
            values = own[m, rows, :].astype(F32) + branch[m, rows, :]
            middle[m, rows, :] = values
            centered = values - jnp.mean(values, axis=-1, keepdims=True)
            spread = lax.rsqrt(jnp.mean(centered * centered, axis=-1, keepdims=True) + EPSILON)
            n_own[m, rows, :] = (centered * spread * norms[2:3, :] + norms[3:4, :]).astype(BF16)

        def hidden_chip(dx, dy, h):
            rows = net.chip_rows(dx, dy, own_rows)
            block = (micro_count, 2 * own_rows, tile)

            def tile_at(n):
                columns = pl.ds(pl.multiple_of(n * tile, tile), tile)
                into = pl.ds(pl.multiple_of(h * half + n * tile, tile), tile)
                hidden = jnp.dot(
                    n_face[:, rows, :].reshape(chip_tokens, width), we[h][:, columns], preferred_element_type=F32
                )
                square = hidden * hidden
                bend = jnp.tanh(GELU_A * hidden * (1.0 + GELU_B * square))
                active[:, rows, into] = (0.5 * hidden * (1.0 + bend)).astype(BF16).reshape(block)
                slope[:, rows, into] = (
                    (
                        0.5 * (1.0 + bend)
                        + (0.5 * GELU_A) * hidden * (1.0 - bend * bend) * (1.0 + (3.0 * GELU_B) * square)
                    )
                    .astype(BF16)
                    .reshape(block)
                )

            loop(half // tile, tile_at)

        across = (((0,), (0,)), ((), ()))
        along = (((1,), (1,)), ((), ()))
        def reduce_tile(first):
            def tile_at(at):
                f, n = lax.div(at, width // wide), lax.rem(at, width // wide)
                columns = pl.ds(pl.multiple_of(n * wide, wide), wide)
                rows = pl.ds(pl.multiple_of(first + f * tile, tile), tile)
                pr[rows, columns] = lax.dot_general(
                    active[:, :, rows].reshape(tokens, tile),
                    cot[:, :, columns].reshape(tokens, wide),
                    across,
                    preferred_element_type=F32,
                ).astype(BF16)

            return tile_at

        def slope_tile(at):
            m, n = lax.div(at, units // tile), lax.rem(at, units // tile)
            columns = pl.ds(pl.multiple_of(n * tile, tile), tile)
            grad = lax.dot_general(cot[m], wr[columns, :], along, preferred_element_type=F32)
            slope[m, :, columns] = (grad * slope[m, :, columns].astype(F32)).astype(BF16)

        made = []

        def normed_chip(dx, dy):
            made.append((dx, dy))
            rows = net.chip_rows(dx, dy, own_rows)

            def tile_at(n):
                columns = pl.ds(pl.multiple_of(n * wide, wide), wide)
                grad = lax.dot_general(
                    slope[:, rows, :half].reshape(chip_tokens, half), we0[columns, :], along, preferred_element_type=F32
                )
                grad = grad + lax.dot_general(
                    slope[:, rows, half:].reshape(chip_tokens, half), we1[columns, :], along, preferred_element_type=F32
                )
                p[:, rows, columns] = grad.astype(BF16).reshape(micro_count, 2 * own_rows, wide)

            loop(width // wide, tile_at)

        def reduced_tiles(m):
            def tile_at(n):
                columns = pl.ds(pl.multiple_of(n * wide, wide), wide)
                cot[m, :, columns] = jnp.dot(active[m], wr[:, columns], preferred_element_type=F32).astype(BF16)

            def act():
                loop(width // wide, tile_at)
                stores.append(net.copy(cot.at[m], reduced_out.at[m]))
                stores[-1].start()

            return act

        def expand_tiles(h):
            def tile_at(at):
                k, n = lax.div(at, half // tile), lax.rem(at, half // tile)
                rows = pl.ds(pl.multiple_of(k * wide, wide), wide)
                columns = pl.ds(pl.multiple_of(n * tile, tile), tile)
                grads = pl.ds(pl.multiple_of(h * half + n * tile, tile), tile)
                we[h][rows, columns] = lax.dot_general(
                    n_face[:, :, rows].reshape(tokens, wide),
                    slope[:, :, grads].reshape(tokens, tile),
                    across,
                    preferred_element_type=F32,
                ).astype(BF16)

            def act():
                loop((width // wide) * (half // tile), tile_at)
                stores.append(net.copy(we[h], (expand_a, expand_b)[h]))
                stores[-1].start()

            return act

        def back_rows(at):
            m, rows = own_rows_at(at)
            values = middle[m, rows, :]
            centered = values - jnp.mean(values, axis=-1, keepdims=True)
            spread = lax.rsqrt(jnp.mean(centered * centered, axis=-1, keepdims=True) + EPSILON)
            unit = centered * spread
            grad = branch[m, rows, :]
            norm_out[0] += grad * unit
            norm_out[1] += grad
            turned = grad * norms[2:3, :]
            inner = jnp.mean(turned * unit, axis=-1, keepdims=True)
            total = cot_own[m, rows, :].astype(F32) + spread * (
                turned - jnp.mean(turned, axis=-1, keepdims=True) - unit * inner
            )
            middle[m, rows, :] = total
            n_own[m, rows, :] = total.astype(BF16)

        def later():
            while len(made) < 2 * ny:
                weave.step("m")
            weave.finish("e")
            for h in (0, 1):
                expand_tiles(h)()
                yield
            for m in range(micro_count):
                reduced_tiles(m)()
                yield

        def main():
            loads[0].wait()
            loads[1].wait()
            yield from scatter_a.run(net, [p], [branch], slots, branch_chip)
            loads[2].wait()
            loop(micro_count * row_steps, norm_rows)
            keep_middle = net.copy(middle, middle_out)
            keep_middle.start()
            loads[4].wait()
            chips, halved = 0, []
            for place in gather.run(net, [n_own], [n_face], []):
                if place is not None:
                    hidden_chip(*place, 0)
                    halved.append(place)
                    chips += 1
                    if chips > ny:
                        yield
                        weave.need("e")
                        for place in halved:
                            hidden_chip(*place, 1)
                        halved = []
                yield
            loads[5].wait()
            loop((half // tile) * (width // wide), reduce_tile(0))
            yield
            loop((half // tile) * (width // wide), reduce_tile(half))
            weave.add("s", line_s.run(net, [pr], [reduce_out], line_slots))
            weave.step("s")
            yield
            weave.need("r")
            loop(micro_count * (units // tile), slope_tile)
            yield
            weave.add("x", later())
            yield from scatter_b.run(net, [p], [branch], slots, normed_chip)
            loads[3].wait()
            keep_middle.wait()
            norm_out[...] = jnp.zeros_like(norm_out)
            loop(micro_count * row_steps, back_rows)
            for pair in ((middle, grad_out), (n_own, low_out)):
                stores.append(net.copy(*pair))
                stores[-1].start()

        weave.add("m", main())
        for name in "".join(MLP_ORDER):
            weave.step(name)
        for name in "mxsre":
            weave.finish(name)
        for store in stores:
            store.wait()

    ins = [mixed, wo, inputs, cotangent, cot_face, norms, wexp_first, *w_expand, *w_reduce]
    specs = [ANY] * 5 + [vmem] + [ANY] * (len(ins) - 6)
    return launch(
        body, ins, specs, outs, scratch, plans, nz, ny, collective_id, "mlp_block", extra_locals=12, vmem=62
    )


def front_block(inputs, cotangent, w_query, w_attn_out, w_keyval, w_expand, norms, doc_ids, nz, ny, collective_id, head_dim):
    micro_count, own_rows, width = inputs.shape
    face_rows = own_rows * 4 * ny
    attn = w_query.shape[1] // 2
    seq_len = nz * face_rows
    blocks = face_rows // BLOCK
    heads = attn // head_dim
    tall = heads * BLOCK
    own = jax.ShapeDtypeStruct(inputs.shape, BF16)
    keys_face = jax.ShapeDtypeStruct((micro_count, face_rows, 2 * head_dim), BF16)
    shard = norms.shape[1] // 4
    norms_own = jax.ShapeDtypeStruct((8, shard), F32)
    plane = PlaneGather(norms_own, nz, ny)
    gather = FaceGather(own, nz, ny)
    gather_c = FaceGather(cotangent, nz, ny, hold_x=True)
    swap_e = HalfSwap([w_expand], ["row"], nz, ny)
    line_a = LineGather([w_keyval, w_query], ["both", "row"], nz, ny)
    line_o = LineGather([w_attn_out], ["col"], nz, ny)
    given = jax.ShapeDtypeStruct((w_expand.shape[0], w_expand.shape[1] // 2), BF16)
    line_e = LineGather([w_expand], ["row"], nz, ny, share=(0, 2), given=[given])
    keys = KeysGather(keys_face, nz, ny)
    plans = [plane, gather, gather_c, swap_e, line_a, line_o, line_e, keys]
    kept = [
        jax.ShapeDtypeStruct((micro_count, face_rows, width), BF16),
        line_a.outs[0][0],
        line_a.outs[1][0],
        given,
        jax.ShapeDtypeStruct((micro_count, face_rows, attn), BF16),
        keys.outs[0][0],
        jax.ShapeDtypeStruct((micro_count, face_rows, attn), BF16),
        jax.ShapeDtypeStruct((micro_count, blocks, 1, tall), F32),
        jax.ShapeDtypeStruct((micro_count, blocks, 2, BLOCK), jnp.int32),
        own,
    ]
    outs = [(shape, ANY) for shape in kept] + [
        (jax.ShapeDtypeStruct((8, width), F32), IN_VMEM),
        gather_c.outs[0],
        line_o.outs[0],
        line_e.outs[0],
    ]
    scratch = [pltpu.VMEM(shape.shape, shape.dtype) for shape in kept] + [
        pltpu.VMEM(keys_face.shape, BF16),
        pltpu.VMEM((8, shard), F32),
        pltpu.VMEM((2 * nz, 8, shard), F32),
    ]

    def body(net, ins, outs, scratch):
        inputs, cotangent, w_query, w_attn_out, w_keyval, w_expand, doc_ids, norms_in = ins
        norm_rows, cot_out, wo_out, first_out = outs[len(kept) :]
        normed, wkv, wq, given, queries, keys_vals, mixed, logs, limits, n_own, keys_face, norms, norms_out = scratch
        norms[...] = jnp.zeros_like(norms)
        for k in range(4):
            norms[k : k + 1, :] = norms_in[:, k * shard : (k + 1) * shard].astype(F32)
        stores = [net.copy(*pair) for pair in zip(scratch, outs[: len(kept)])]
        weave = Weave()
        weave.add("p", plane.run(net, [norms], [norms_out], []))
        weave.step("p")
        weave.add("a", line_a.run(net, [w_keyval, w_query], [wkv, wq], []))
        weave.step("a")
        weave.add("h", swap_e.run(net, [w_expand], [given], []))
        weave.add("o", line_o.run(net, [w_attn_out], [wo_out], []))
        weave.add("c", gather_c.run(net, [cotangent], [cot_out], []))

        def line_first():
            weave.need("h")
            yield from line_e.run(net, [w_expand, given], [first_out], [])

        weave.add("e", line_first())
        along = (((1,), (1,)), ((), ()))
        across = (((0,), (0,)), ((), ()))
        step = min(32, own_rows)

        def own_norm(at):
            m = lax.div(at, own_rows // step)
            rows = pl.ds(pl.multiple_of(lax.rem(at, own_rows // step) * step, step), step)
            gain, shift = norm_rows[0:1, :], norm_rows[1:2, :]
            values = inputs[m, rows, :].astype(F32)
            centered = values - jnp.mean(values, axis=-1, keepdims=True)
            spread = lax.rsqrt(jnp.mean(centered * centered, axis=-1, keepdims=True) + EPSILON)
            n_own[m, rows, :] = (centered * spread * gain + shift).astype(BF16)

        def keys_tile(m):
            keys_face[m] = jnp.dot(normed[m], wkv[...], preferred_element_type=F32).astype(BF16)

        def queries_tile(m):
            queries[m] = jnp.dot(normed[m], wq[...], preferred_element_type=F32).astype(BF16)

        def mixed_tile(m):
            def tile_at(b):
                rows = pl.ds(pl.multiple_of(b * BLOCK, BLOCK), BLOCK)
                query = jnp.concatenate(
                    [queries[m, rows, h * head_dim : (h + 1) * head_dim] for h in range(heads)], axis=0
                )
                starts = jnp.concatenate([limits[m, b, 0:1, :]] * heads, axis=1)
                ends = jnp.concatenate([limits[m, b, 1:2, :]] * heads, axis=1)
                place = lax.broadcasted_iota(jnp.int32, (BLOCK, tall), 0)

                def body(block, carry):
                    top, total, out = carry
                    first = pl.multiple_of(block * BLOCK, BLOCK)
                    keys = keys_vals[m, pl.ds(first, BLOCK), :head_dim]
                    values = keys_vals[m, pl.ds(first, BLOCK), head_dim:]
                    raw = lax.dot_general(keys, query, along, preferred_element_type=F32)
                    allowed = (place >= starts - first) & (place < ends - first)
                    scores = jnp.where(allowed, raw * (LOG2_E / math.sqrt(head_dim)), NEG_FILL)
                    new_top = jnp.maximum(top, jnp.max(scores, axis=0, keepdims=True))
                    weights = jnp.exp2(scores - new_top)
                    fade = jnp.exp2(top - new_top)
                    total = total * fade + jnp.sum(weights, axis=0, keepdims=True)
                    out = out * fade + lax.dot_general(
                        values, weights.astype(BF16), across, preferred_element_type=F32
                    )
                    return new_top, total, out

                top, total, out = lax.fori_loop(
                    first_block(net.z * blocks + b, seq_len),
                    net.z * blocks + b + 1,
                    body,
                    (
                        jnp.full((1, tall), NEG_FILL, F32),
                        jnp.zeros((1, tall), F32),
                        jnp.zeros((head_dim, tall), F32),
                    ),
                )
                out = jnp.transpose(out / total).astype(BF16)
                for h in range(heads):
                    mixed[m, rows, h * head_dim : (h + 1) * head_dim] = out[h * BLOCK : (h + 1) * BLOCK]
                logs[m, b] = top + jnp.log2(total)

            return tile_at

        def limits_tile(m):
            kinds = lax.broadcasted_iota(jnp.int32, (32, 1), 0)
            counts = jnp.sum((doc_ids[m : m + 1, :] == kinds).astype(F32), axis=1, keepdims=True)
            for b in range(blocks):
                first = pl.multiple_of(net.z * face_rows + b * BLOCK, BLOCK)
                docs = doc_ids[m : m + 1, pl.ds(first, BLOCK)]
                starts = jnp.sum(jnp.where(kinds < docs, counts, 0.0), axis=0, keepdims=True)
                ends = jnp.sum(jnp.where(kinds <= docs, counts, 0.0), axis=0, keepdims=True)
                limits[m, b, 0:1, :] = starts.astype(jnp.int32)
                limits[m, b, 1:2, :] = ends.astype(jnp.int32)

        def main():
            weave.finish("p")
            norm_rows[...] = jnp.concatenate([norms_out[d] for d in range(2 * nz)], axis=1)
            loop(micro_count * (own_rows // step), own_norm)
            stores[9].start()
            yield from gather.run(net, [n_own], [normed], [])
            stores[0].start()
            yield
            weave.need("a")
            loop(micro_count, keys_tile)
            weave.add("k", keys.run(net, [keys_face], [keys_vals], []))
            weave.step("k")
            yield
            for at in (1, 2):
                stores[at].start()
            for m in range(micro_count):
                limits_tile(m)
            stores[8].start()
            loop(micro_count, queries_tile)
            stores[4].start()
            yield
            weave.need("k")
            stores[5].start()
            for m in range(micro_count):
                loop(blocks, mixed_tile(m))
                yield
            for at in (6, 7):
                stores[at].start()

        weave.add("m", main())
        for name in "".join(FRONT_ORDER):
            weave.step(name)
        for name in "mhcoeak":
            weave.finish(name)
        stores[3].start()
        for store in stores:
            store.wait()

    ins = [inputs, cotangent, w_query, w_attn_out, w_keyval, w_expand, doc_ids, norms]
    results = launch(
        body, ins, [IN_VMEM] * len(ins), outs, scratch, plans, nz, ny, collective_id, "front_block", extra_locals=len(kept)
    )
    return results[: len(kept)], results[len(kept) :]


def back_block(low, reduced, parts, mixed, wo, wq, normed, queries, keys_vals, logs, limits, nz, ny, collective_id, head_dim):
    micro_count, own_rows, width = low.shape
    face_rows, attn = queries.shape[1:]
    seq_len = keys_vals.shape[1]
    tokens = micro_count * face_rows
    blocks = face_rows // BLOCK
    heads = attn // head_dim
    tall = heads * BLOCK
    scale = 1.0 / math.sqrt(head_dim)
    wide = 512
    half = parts[0].shape[1]
    part = jax.ShapeDtypeStruct((micro_count, face_rows, width), BF16)
    gather = FaceGather(low, nz, ny)
    scatter_r = FaceScatter(reduced, nz, ny)
    scatter_q = FaceScatter(part, nz, ny, resident=True)
    whole = WholeScatter(jax.ShapeDtypeStruct((micro_count, nz, face_rows, 2 * head_dim), BF16), nz, ny, resident=True)
    line_e = LineScatter(parts, ["row", "row"], nz, ny, resident=True, joined=True)
    attn_parts = [jax.ShapeDtypeStruct((attn, width), BF16), jax.ShapeDtypeStruct((width, attn), BF16)]
    line_a = LineScatter(attn_parts, ["col", "row"], nz, ny, resident=True)
    plans = [gather, scatter_r, scatter_q, whole, line_e, line_a]
    groups = [scatter_r, scatter_q, whole, line_e, line_a]
    outs = scatter_r.outs + scatter_q.outs + whole.outs + line_e.outs + line_a.outs
    normed = normed.reshape(micro_count, face_rows, width)
    given = [mixed, wo, wq, queries, keys_vals, logs, limits, *parts]
    scratch = [pltpu.VMEM(entry.shape, entry.dtype) for entry in given] + [
        pltpu.VMEM(part.shape, BF16),
        pltpu.VMEM(queries.shape, BF16),
        pltpu.VMEM(queries.shape, BF16),
        pltpu.VMEM((seq_len, 2 * head_dim), F32),
        pltpu.VMEM((micro_count * nz, face_rows, 2 * head_dim), BF16),
        pltpu.VMEM((attn, width), BF16),
        pltpu.VMEM((width, attn), BF16),
        pltpu.VMEM((2, micro_count, face_rows, wide), BF16),
    ]
    shared = len(scratch)
    for plan in groups:
        scratch = scratch + plan.scratch

    def body(net, ins, outs, scratch):
        low, reduced_in, normed_in, *given_in = ins
        reduced_out, from_out, keys_out, *line_outs = outs
        mixed, wo, wq, queries, keys_vals, logs, limits, *expand = scratch[: len(given)]
        face, grad_mixed, grad_queries, acc, grad_keys, part_out, part_query, normed = scratch[len(given) : shared]
        slots, first = {}, shared
        for name, plan in zip("rqwea", groups):
            slots[name] = list(scratch[first : first + len(plan.scratch)])
            first += len(plan.scratch)
        loads = [net.copy(*pair) for pair in zip(given_in, scratch)]
        order = [len(given) - 2, len(given) - 1] + list(range(len(given) - 2))
        weave = Weave()
        along = (((1,), (1,)), ((), ()))
        across = (((0,), (0,)), ((), ()))

        def mix_tile(m):
            grad_mixed[m] = lax.dot_general(face[m], wo[...], along, preferred_element_type=F32).astype(BF16)

        def attn_out_tile(n):
            columns = pl.ds(pl.multiple_of(n * wide, wide), wide)
            part_out[:, columns] = lax.dot_general(
                mixed[...].reshape(tokens, attn),
                face[:, :, columns].reshape(tokens, wide),
                across,
                preferred_element_type=F32,
            ).astype(BF16)

        def attn_tile(m):
            def tile_at(b):
                rows = pl.ds(pl.multiple_of(b * BLOCK, BLOCK), BLOCK)

                def stack(ref):
                    return jnp.concatenate(
                        [ref[m, rows, h * head_dim : (h + 1) * head_dim] for h in range(heads)], axis=0
                    )

                query, grad = stack(queries), stack(grad_mixed)
                products = grad.astype(F32) * stack(mixed).astype(F32)
                delta = jnp.sum(jnp.transpose(products), axis=0, keepdims=True)
                starts = jnp.concatenate([limits[m, b, 0:1, :]] * heads, axis=1)
                ends = jnp.concatenate([limits[m, b, 1:2, :]] * heads, axis=1)
                log_total = logs[m, b]
                place = lax.broadcasted_iota(jnp.int32, (BLOCK, tall), 0)

                def body(block, grad_query):
                    first = pl.multiple_of(block * BLOCK, BLOCK)
                    keys = keys_vals[m, pl.ds(first, BLOCK), :head_dim]
                    values = keys_vals[m, pl.ds(first, BLOCK), head_dim:]
                    raw = lax.dot_general(keys, query, along, preferred_element_type=F32)
                    allowed = (place >= starts - first) & (place < ends - first)
                    probs = jnp.where(allowed, jnp.exp2(raw * (LOG2_E * scale) - log_total), 0.0)
                    grad_probs = lax.dot_general(values, grad, along, preferred_element_type=F32)
                    grad_scores = (probs * (grad_probs - delta)).astype(BF16)
                    acc[pl.ds(first, BLOCK), :head_dim] += (
                        jnp.dot(grad_scores, query, preferred_element_type=F32) * scale
                    )
                    acc[pl.ds(first, BLOCK), head_dim:] += jnp.dot(
                        probs.astype(BF16), grad, preferred_element_type=F32
                    )
                    return grad_query + lax.dot_general(keys, grad_scores, across, preferred_element_type=F32)

                grad_query = lax.fori_loop(
                    first_block(net.z * blocks + b, seq_len),
                    net.z * blocks + b + 1,
                    body,
                    jnp.zeros((head_dim, tall), F32),
                )
                grad_query = jnp.transpose(grad_query * scale).astype(BF16)
                for h in range(heads):
                    grad_queries[m, rows, h * head_dim : (h + 1) * head_dim] = grad_query[h * BLOCK : (h + 1) * BLOCK]

            return tile_at

        def from_chip(dx, dy):
            rows = net.chip_rows(dx, dy, own_rows)

            def tile_at(n):
                columns = pl.ds(pl.multiple_of(n * wide, wide), wide)
                face[:, rows, columns] = (
                    lax.dot_general(
                        grad_queries[:, rows, :].reshape(micro_count * 2 * own_rows, attn),
                        wq[columns, :],
                        along,
                        preferred_element_type=F32,
                    )
                    .astype(BF16)
                    .reshape(micro_count, 2 * own_rows, wide)
                )

            loop(width // wide, tile_at)

        columns_in = [
            net.copy(normed_in.at[:, :, pl.ds(n * wide, wide)], normed.at[n % 2]) for n in range(width // wide)
        ]

        def query_tile(n):
            columns_in[n].wait()

            def tile_at(_):
                part_query[n * wide : (n + 1) * wide, :] = lax.dot_general(
                    normed[n % 2].reshape(tokens, wide),
                    grad_queries[...].reshape(tokens, attn),
                    across,
                    preferred_element_type=F32,
                ).astype(BF16)

            loop(1, tile_at)
            if n + 2 < width // wide:
                columns_in[n + 2].start()

        def main():
            yield from gather.run(net, [low], [face], [])
            for at in order[2:]:
                loads[at].wait()
            loop(micro_count, mix_tile)
            yield
            for m in range(micro_count):
                acc[...] = jnp.zeros_like(acc)
                loop(blocks, attn_tile(m))
                for k in range(nz):
                    grad_keys[m * nz + k] = acc[k * face_rows : (k + 1) * face_rows, :].astype(BF16)
                yield
            loop(width // wide, attn_out_tile)
            weave.add("w", whole.run(net, [grad_keys], [keys_out], slots["w"]))
            weave.step("w")
            weave.add("q", scatter_q.run(net, [face], [from_out], slots["q"], from_chip))
            weave.step("q")
            for n in range(width // wide):
                query_tile(n)
            weave.add("a", line_a.run(net, [part_out, part_query], line_outs[1:], slots["a"]))
            weave.step("a")

        weave.add("m", main())
        weave.step("m")
        for at in order:
            loads[at].start()
        for copy in columns_in[:2]:
            copy.start()
        for at in order[:2]:
            loads[at].wait()
        weave.add("e", line_e.run(net, expand, line_outs[:1], slots["e"]))
        weave.step("e")
        weave.add("r", scatter_r.run(net, [reduced_in], [reduced_out], slots["r"]))
        for name in "".join(BACK_ORDER):
            weave.step(name)
        for name in "mwqrea":
            weave.finish(name)

    ins = [low, reduced, normed, *given]
    specs = [IN_VMEM] + [ANY] * (len(ins) - 1)
    return launch(
        body, ins, specs, outs, scratch, plans, nz, ny, collective_id, "back_block", extra_locals=len(given) + width // wide, vmem=62
    )


def end_block(inputs, normed_own, grad_middle, from_query, grad_keys, wkv, norms, grad_norm_two, nz, ny, collective_id):
    micro_count, own_rows, width = inputs.shape
    rows_all = micro_count * own_rows
    side = grad_keys.shape[-1]
    ranks = 4 * ny
    own_width = width // (nz * ranks)
    step = min(32, own_rows)
    part = jax.ShapeDtypeStruct((nz, width // nz, side), BF16)
    small = jax.ShapeDtypeStruct((ranks, nz, 8, 128), F32)
    quick, tiny = QuickScatter(part, nz, ny), SmallScatter(small, nz, ny)
    plans = [quick, tiny]
    outs = [(jax.ShapeDtypeStruct(inputs.shape, F32), IN_VMEM)] + quick.outs + tiny.outs
    scratch = [
        pltpu.VMEM((rows_all, side), BF16),
        pltpu.VMEM(part.shape, BF16),
        pltpu.VMEM(small.shape, F32),
        pltpu.VMEM((2, step, width), F32),
    ] + quick.scratch + tiny.scratch

    def body(net, ins, outs, scratch):
        inputs, n_own, grad_middle, from_query, grad_keys, wkv, norms, grad_norm_two = ins
        grad_out, keyval_out, small_out = outs
        low_keys, part, small, sums, *slots = scratch
        weave = Weave()

        def place(at):
            m, first = lax.div(at, own_rows // step), lax.rem(at, own_rows // step) * step
            rows = pl.ds(pl.multiple_of(first, step), step)
            return m, rows, pl.ds(pl.multiple_of(at * step, step), step)

        def unit_rows(m, rows):
            values = inputs[m, rows, :].astype(F32)
            centered = values - jnp.mean(values, axis=-1, keepdims=True)
            spread = lax.rsqrt(jnp.mean(centered * centered, axis=-1, keepdims=True) + EPSILON)
            return centered * spread, spread

        def first_rows(at):
            m, rows, flat = place(at)
            low_keys[flat, :] = grad_keys[m, rows, :].astype(BF16)

        def keyval_tile(k):
            columns = pl.ds(pl.multiple_of(k * (width // nz), width // nz), width // nz)
            part[k] = lax.dot_general(
                n_own[:, :, columns].reshape(rows_all, width // nz),
                low_keys[...],
                (((0,), (0,)), ((), ())),
                preferred_element_type=F32,
            ).astype(BF16)

        def last_rows(at):
            m, rows, flat = place(at)
            unit, spread = unit_rows(m, rows)
            grad = from_query[m, rows, :] + lax.dot_general(
                low_keys[flat, :], wkv[...], (((1,), (1,)), ((), ())), preferred_element_type=F32
            )
            sums[0] += grad * unit
            sums[1] += grad
            turned = grad * norms[0:1, :]
            inner = jnp.mean(turned * unit, axis=-1, keepdims=True)
            grad_out[m, rows, :] = grad_middle[m, rows, :] + spread * (
                turned - jnp.mean(turned, axis=-1, keepdims=True) - unit * inner
            )

        count = rows_all // step
        loop(count, first_rows)
        loop(nz, keyval_tile)
        weave.add("q", quick.run(net, [part], [keyval_out], slots[: len(quick.scratch)]))
        for _ in range(2 * ny + 1):
            weave.step("q")
        sums[...] = jnp.zeros_like(sums)
        loop(count, last_rows)
        rows = [jnp.sum(sums[k], axis=0, keepdims=True) for k in (0, 1)]
        rows += [jnp.sum(grad_norm_two[k], axis=0, keepdims=True) for k in (0, 1)]
        rows = jnp.concatenate(rows + [jnp.zeros((4, width), F32)], axis=0)
        for line in range(nz):
            for rank in range(ranks):
                first = (line * ranks + rank) * own_width // 128 * 128
                small[rank, line] = rows[:, first : first + 128]
        weave.add("s", tiny.run(net, [small], [small_out], slots[len(quick.scratch) :]))
        for name in "sqsqs":
            weave.step(name)
        for name in "qs":
            weave.finish(name)

    ins = [inputs, normed_own, grad_middle, from_query, grad_keys, wkv, norms, grad_norm_two]
    return launch(body, ins, [IN_VMEM] * len(ins), outs, scratch, plans, nz, ny, collective_id, "end_block")


def widen(arrays, first, second):
    steps = 4
    lead, rows, width = first.shape

    def kernel(*refs):
        sources, (one, two), targets = refs[: len(arrays)], refs[len(arrays) : len(arrays) + 2], refs[len(arrays) + 2 :]
        for source, target in zip(sources, targets):
            target[...] = source[...].astype(F32)
        targets[-1][...] = (one[...] + two[...]).astype(BF16)

    specs = [pl.BlockSpec((array.shape[0] // steps, array.shape[1]), lambda step: (step, 0)) for array in arrays]
    wide = pl.BlockSpec((lead, rows // steps, width), lambda step: (0, step, 0))
    return pl.pallas_call(
        kernel,
        out_shape=[jax.ShapeDtypeStruct(array.shape, F32) for array in arrays]
        + [jax.ShapeDtypeStruct(first.shape, BF16)],
        grid=(steps,),
        in_specs=specs + [wide, wide],
        out_specs=specs + [wide],
        compiler_params=pltpu.CompilerParams(vmem_limit_bytes=60 << 20),
        name="widen",
    )(*arrays, first, second)


def local(
    inputs,
    cotangent,
    doc_ids,
    attn_gain,
    attn_shift,
    w_query,
    w_keyval,
    w_attn_out,
    mlp_gain,
    mlp_shift,
    w_expand,
    w_reduce,
):
    nz = lax.axis_size("dp") // 2
    tensor_count = lax.axis_size("tensor")
    ny = tensor_count // 2
    ranks = 2 * tensor_count
    micro_count, own_rows, width = inputs.shape
    face_rows = own_rows * ranks
    tokens = micro_count * face_rows
    seq_len = doc_ids.shape[1]
    head_dim = w_keyval.shape[1] // 2
    heads = w_query.shape[1] // (2 * head_dim)
    on = (nz, ny)

    gains = jnp.concatenate([attn_gain, attn_shift, mlp_gain, mlp_shift])[None, :]
    kept, rest = front_block(
        inputs,
        cotangent,
        w_query,
        w_attn_out,
        w_keyval,
        w_expand,
        gains,
        doc_ids,
        *on,
        collective_id=1,
        head_dim=head_dim,
    )
    normed, wkv, wq, expand_given, queries, keys_vals, mixed, log_total, limits, normed_own = kept
    norms, cot_face, wo, wexp_first = rest
    middle, grad_middle, low_middle, grad_norm_two, part_expand_a, part_expand_b, reduced, grad_reduce = mlp_block(
        mixed, wo, inputs, cotangent, cot_face, norms, wexp_first, (w_expand, expand_given), (w_reduce,), *on, collective_id=3
    )
    reduced, from_query, grad_keys, grad_expand, grad_attn_out, grad_query = back_block(
        low_middle,
        reduced,
        [part_expand_a, part_expand_b],
        mixed,
        wo,
        wq,
        normed,
        queries,
        keys_vals,
        log_total,
        limits,
        *on,
        collective_id=6,
        head_dim=head_dim,
    )
    grad_inputs, grad_keyval, small = end_block(
        inputs, normed_own, grad_middle, from_query, grad_keys, wkv, norms, grad_norm_two, *on, collective_id=8
    )
    own_width = width // (nz * ranks)
    device = lax.axis_index("dp") * tensor_count + lax.axis_index("tensor")
    small = lax.dynamic_slice_in_dim(small[:4], device * own_width % 128, own_width, axis=1)

    grad_query, grad_attn_out, grad_expand, grad_reduce, outputs = widen(
        [grad_query, grad_attn_out, grad_expand, grad_reduce], middle, reduced
    )
    return (
        outputs,
        grad_inputs,
        small[0],
        small[1],
        grad_query,
        grad_keyval,
        grad_attn_out,
        small[2],
        small[3],
        grad_expand,
        grad_reduce,
    )


def solution(mesh):
    placed = (
        P(None, ("dp", "tensor"), None),
        P(None, ("dp", "tensor"), None),
        P(),
        P("dp"),
        P("dp"),
        P("dp", "tensor"),
        P("dp", None),
        P("tensor", "dp"),
        P("dp"),
        P("dp"),
        P("dp", "tensor"),
        P("tensor", "dp"),
    )
    return jax.shard_map(
        local,
        mesh=mesh,
        in_specs=placed,
        out_specs=(
            P(None, ("dp", "tensor"), None),
            P(None, ("dp", "tensor"), None),
            P(("dp", "tensor")),
            P(("dp", "tensor")),
            P("dp", "tensor"),
            P(("dp", "tensor"), None),
            P("tensor", "dp"),
            P(("dp", "tensor")),
            P(("dp", "tensor")),
            P("dp", "tensor"),
            P("tensor", "dp"),
        ),
        check_vma=False,
    )
```

```python
import functools
import math

import jax
import jax.numpy as jnp
from jax import lax
from jax.experimental import pallas as pl
from jax.experimental.pallas import tpu as pltpu
from jax.sharding import PartitionSpec as P

BLOCK = 256
EPSILON = 1e-05
NEG_FILL = -1e30
GELU_A = math.sqrt(2.0 / math.pi)
GELU_B = 0.044715
LOG2_E = 1.0 / math.log(2.0)
MLP_ORDER = ("memmmmeemmrmememmmrmmmmrmmrmmmmmmemmmsxs", "mmmmxxsxxrmm",)
BACK_ORDER = ("amwwaamewqmarwraqawmwwrqwemwaqqmarwrmmer", "rmmeemmwmwemqqwmqeqmwewwrrarrqaqaqaawewq", "rerrqawrm",)
FRONT_ORDER = ("omaoaaamaaamcoaammhaaommommokkmekecaceme", "ckceme",)
MESH = pl.DeviceIdType.MESH
ANY = pl.BlockSpec(memory_space=pl.ANY)
READY = "ready"
IN_VMEM = pl.BlockSpec(memory_space=pltpu.VMEM)
BF16 = jnp.bfloat16
F32 = jnp.float32


def layer_norm(values, gain, shift):
    center = jnp.mean(values, axis=-1, keepdims=True)
    centered = values - center
    variance = jnp.mean(centered * centered, axis=-1, keepdims=True)
    return centered * lax.rsqrt(variance + EPSILON) * gain + shift


def gelu_tanh(values):
    return jax.nn.gelu(values, approximate=True)


class Net:
    def __init__(self, nz, ny, send, recv, local):
        dp, tensor = lax.axis_index("dp"), lax.axis_index("tensor")
        self.nz, self.ny = nz, ny
        self.z, self.x = lax.div(dp, 2), lax.rem(dp, 2)
        self.y, self.c = lax.div(tensor, 2), lax.rem(tensor, 2)
        self.tensor = tensor
        self.send, self.recv, self.local = send, recv, local
        self.used = [0, 0]
        self.keys = {}

    def flip(self, value, by):
        return value + by - 2 * by * value if by else value

    def xy(self, dx, dy):
        return self.flip(self.x, dx), lax.rem(self.y + dy, self.ny) if dy else self.y

    def rank(self, dx=0, dy=0, dc=0):
        x, y = self.xy(dx, dy)
        return x * (2 * self.ny) + y * 2 + self.flip(self.c, dc)

    def chip_rows(self, dx, dy, rows):
        first = (self.rank(dx, dy) - self.c) * rows
        return pl.ds(pl.multiple_of(first, 2 * rows), 2 * rows)

    def device(self, dx=0, dy=0, dc=0, z=None):
        x, y = self.xy(dx, dy)
        return ((self.z if z is None else z) * 2 + x, y * 2 + self.flip(self.c, dc))

    def slot(self, key):
        if key not in self.keys:
            self.keys[key] = self.used[0]
            self.used[0] += 1
        return self.keys[key]

    def remote(self, key, src, dst, device):
        at = self.slot(key)
        return pltpu.make_async_remote_copy(
            src_ref=src,
            dst_ref=dst,
            send_sem=self.send.at[at],
            recv_sem=self.recv.at[at],
            device_id=device,
            device_id_type=MESH,
        )

    def take_locals(self, count):
        first = self.used[1]
        self.used[1] += count
        return first

    def copy_at(self, at, src, dst):
        return pltpu.make_async_copy(src, dst, self.local.at[at])

    def copy(self, src, dst):
        return self.copy_at(self.take_locals(1), src, dst)


def add_rows(dst, terms):
    lead, height, width = dst.shape
    rows = min(max(16, 32768 // width), height)
    steps = height // rows

    def body(step, carry):
        at, off = lax.div(step, steps), pl.multiple_of(lax.rem(step, steps) * rows, rows)
        total = terms[0][at, pl.ds(off, rows), :].astype(F32)
        for term in terms[1:]:
            total = total + term[at, pl.ds(off, rows), :].astype(F32)
        dst[at, pl.ds(off, rows), :] = total.astype(dst.dtype)
        return carry

    lax.fori_loop(0, lead * steps, body, 0)


class FaceGather:
    moves = ("x", "y", "c")
    in_spec = IN_VMEM

    def __init__(self, own, nz, ny, hold_x=False, report=False):
        self.ins, self.hold_x, self.report = [own], hold_x, report
        m, t, d = own.shape
        self.outs = [(jax.ShapeDtypeStruct((m, 4 * ny * t, d), own.dtype), ANY)]
        self.scratch = []
        self.half = t // 2
        self.remotes, self.locals = 8 * ny, 1

    def run(self, net, ins, outs, scratch):
        (own,), (out,), half = ins, outs, self.half
        dys = range(1, net.ny)

        def piece(dx, dy, h):
            return out.at[:, pl.ds(pl.multiple_of(net.rank(dx, dy) * 2 * half + h * half, half), half), :]

        mine = [own.at[:, pl.ds(h * half, half), :] for h in (0, 1)]
        keep = net.copy(own, out.at[:, pl.ds(pl.multiple_of(net.rank() * 2 * half, half), 2 * half), :])
        keep.start()
        sent = {}

        def send(key, src, dst, device):
            sent[key] = net.remote((id(self), key), src, dst, device)
            sent[key].start()

        if not self.hold_x:
            send(("x", 0), mine[0], piece(0, 0, 0), net.device(1, 0))
        for dy in dys:
            send(("y", dy, 1), mine[1], piece(0, 0, 1), net.device(0, dy))
        if not self.hold_x:
            send(("x", 1), mine[1], piece(0, 0, 1), net.device(1, 0))
        for dy in dys:
            send(("y", dy, 0), mine[0], piece(0, 0, 0), net.device(0, dy))
        for h in (0, 1):
            send(("c", h), mine[h], piece(0, 0, h), net.device(0, 0, 1))
        if self.hold_x:
            yield
            for h in (0, 1):
                send(("x", h), mine[h], piece(0, 0, h), net.device(1, 0))

        def share(key, dx, dy, h):
            send(("c",) + key, piece(dx, dy, h), piece(dx, dy, h), net.device(0, 0, 1))

        def from_x(h):
            sent["x", h].wait_recv()
            if not h:
                for dy in dys:
                    send(("xy", dy), piece(1, 0, 0), piece(1, 0, 0), net.device(0, dy))
            share(("x", h), 1, 0, h)

        def from_y(dy, h):
            sent["y", dy, h].wait_recv()
            if h:
                send(("yx", dy), piece(0, -dy % net.ny, 1), piece(0, -dy % net.ny, 1), net.device(1, 0))
            share(("y", dy, h), 0, -dy % net.ny, h)

        arrivals = []
        for first in (True, False):
            on_x = [functools.partial(from_x, 0 if first else 1)]
            on_y = [functools.partial(from_y, dy, 1 if first else 0) for dy in dys]
            arrivals.append(on_x + on_y)
        if self.hold_x:
            arrivals = [arrivals[0][1:], arrivals[1][1:], arrivals[0][:1], arrivals[1][:1]]
        waited = set()

        def shared(*keys):
            for key in keys:
                sent[("c",) + key].wait_recv()
                waited.add(("c",) + key)

        if self.report:
            yield
            keep.wait()
            shared((0,), (1,))
            yield (0, 0)
        for group in arrivals:
            for arrive in group:
                yield
                arrive()
        if self.report:
            shared(("x", 0), ("x", 1))
            yield (1, 0)
            for dy in dys:
                shared(("y", dy, 1), ("y", dy, 0))
                yield (0, -dy % net.ny)
        for dy in dys:
            yield
            sent["xy", dy].wait_recv()
            share(("xy", dy), 1, -dy % net.ny, 0)
            yield
            sent["yx", dy].wait_recv()
            share(("yx", dy), 1, -dy % net.ny, 1)
        yield
        for key, copy in sent.items():
            if key[0] == "c" and key not in waited:
                copy.wait_recv()
        if self.report:
            for dy in dys:
                yield (1, -dy % net.ny)
        else:
            keep.wait()
        for copy in sent.values():
            copy.wait_send()


class FaceScatter:
    moves = ("x", "y", "c")

    def __init__(self, part, nz, ny, resident=False):
        self.ins, self.resident = [part], resident
        m, rows, d = part.shape
        t = rows // (4 * ny)
        self.outs = [(jax.ShapeDtypeStruct((m, t, d), F32), pl.BlockSpec(memory_space=pltpu.VMEM))]
        half = t // 2
        self.half = half
        self.scratch = [
            pltpu.VMEM((2 * ny, m, t, d), BF16),
            pltpu.VMEM((ny - 1, m, half, d), BF16),
            pltpu.VMEM((ny - 1, m, half, d), BF16),
            pltpu.VMEM((2, m, half, d), BF16),
            pltpu.VMEM((2, ny - 1, m, half, d), BF16),
        ]
        if not resident:
            self.scratch.append(pltpu.VMEM((2 * ny, m, t, d), BF16))
        self.remotes, self.locals = 6 * ny + 4, 2 * ny

    def run(self, net, ins, outs, scratch, produce=None):
        (part,), (out,), half = ins, outs, self.half
        from_core, x_diag, y_diag, x_in, y_in = scratch[:5]
        ny = net.ny
        dys = range(1, ny)
        order = [(1, dy) for dy in dys] + [(1, 0)] + [(0, dy) for dy in dys] + [(0, 0)]
        sent, loads = {}, {}

        def send(key, src, dst, device):
            sent[key] = net.remote((id(self), key), src, dst, device)
            sent[key].start()

        def rows(dx, dy, dc, first=0, size=2 * half):
            at = net.rank(dx, dy, dc) * 2 * half + first
            return part.at[:, pl.ds(pl.multiple_of(at, half), size), :]

        def work(dx, dy, first=0, size=2 * half):
            if self.resident:
                return rows(dx, dy, 0, first, size)
            return scratch[5].at[dx * ny + dy, :, pl.ds(first, size), :]

        def begin(dx, dy):
            at = dx * ny + dy
            if not self.resident:
                loads[at] = net.copy(rows(dx, dy, 0), work(dx, dy))
                loads[at].start()
            send(("c", at), rows(dx, dy, 1), from_core.at[at], net.device(0, 0, 1))

        def settle(dx, dy):
            at = dx * ny + dy
            if not self.resident:
                loads[at].wait()
            sent["c", at].wait_recv()
            add_rows(work(dx, dy), [work(dx, dy), from_core.at[at]])
            top, low = work(dx, dy, 0, half), work(dx, dy, half, half)
            if dx and dy:
                send(("xd", dy), top, x_diag.at[dy - 1], net.device(1, 0))
                send(("yd", dy), low, y_diag.at[dy - 1], net.device(0, dy))
            elif dx:
                send(("x", 0), top, x_in.at[0], net.device(1, 0))
            elif dy:
                send(("y", dy, 1), low, y_in.at[1, dy - 1], net.device(0, dy))

        for at, place in enumerate(order):
            if produce is not None:
                produce(*place)
            begin(*place)
            if produce is not None:
                yield
                if at:
                    settle(*order[at - 1])
        for place in order if produce is None else order[-1:]:
            yield
            settle(*place)
        for dy in dys:
            yield
            sent["xd", dy].wait_recv()
            top = work(0, dy, 0, half)
            add_rows(top, [top, x_diag.at[dy - 1]])
            send(("y", dy, 0), top, y_in.at[0, dy - 1], net.device(0, dy))
        low = work(1, 0, half, half)
        for dy in dys:
            yield
            sent["yd", dy].wait_recv()
            add_rows(low, [low, y_diag.at[dy - 1]])
        send(("x", 1), low, x_in.at[1], net.device(1, 0))
        for h in (0, 1):
            yield
            sent["x", h].wait_recv()
            for dy in dys:
                sent["y", dy, h].wait_recv()
            add_rows(
                out.at[:, pl.ds(h * half, half), :],
                [work(0, 0, h * half, half), x_in.at[h]] + [y_in.at[h, dy - 1] for dy in dys],
            )
        for copy in sent.values():
            copy.wait_send()


class LineGather:
    moves = ("x", "line", "c")
    in_spec = IN_VMEM

    def __init__(self, shards, kinds, nz, ny, share=(0, 1), given=()):
        self.ins, self.kinds, self.share = list(shards) + list(given), list(kinds), share
        self.outs, self.scratch = [], []
        for shard, kind in zip(shards, kinds):
            rows, columns = shard.shape
            if kind == "row":
                shape = (rows * 2 * nz, columns // 2 // share[1])
            elif kind == "col":
                shape = (rows // 2 // share[1], columns * 2 * nz)
            else:
                shape = (rows * 2 * nz, columns)
            self.outs.append((jax.ShapeDtypeStruct(shape, shard.dtype), ANY))
        count = len(self.kinds)
        self.remotes = count * (1 + 4 * (nz - 1)) + kinds.count("both") * (1 + 4 * (nz - 1))
        self.locals = 2 * count

    def run(self, net, ins, outs, scratch):
        nz, z = net.nz, net.z
        sent, locals_, shared = [], [], []
        weights = []
        given = ins[len(self.kinds) :]
        for at, (shard, out, kind) in enumerate(zip(ins, outs, self.kinds)):
            rows, columns = shard.shape

            if kind == "row":
                span = columns // 2 // self.share[1]

                def mine(dx, shard=shard, span=span):
                    first = (net.flip(net.x, dx) * self.share[1] + self.share[0]) * span
                    return shard.at[:, pl.ds(pl.multiple_of(first, span), span)]

                def block(line, dx, out=out, rows=rows):
                    first = (line * 2 + net.flip(net.x, dx)) * rows
                    return out.at[pl.ds(pl.multiple_of(first, rows), rows), :]

            elif kind == "col":
                span = rows // 2 // self.share[1]

                def mine(dx, shard=shard, span=span):
                    first = (net.flip(net.x, dx) * self.share[1] + self.share[0]) * span
                    return shard.at[pl.ds(pl.multiple_of(first, span), span), :]

                def block(line, dx, out=out, columns=columns):
                    first = (line * 2 + net.flip(net.x, dx)) * columns
                    return out.at[:, pl.ds(pl.multiple_of(first, columns), columns)]

            else:
                half = rows // 2

                def mine(dx, shard=shard, half=half):
                    return shard.at[pl.ds(pl.multiple_of(net.c * half, half), half), :]

                def block(line, dx, out=out, rows=rows, half=half):
                    first = (line * 2 + net.flip(net.x, dx)) * rows + net.c * half
                    return out.at[pl.ds(pl.multiple_of(first, half), half), :]

            weights.append((at, kind, mine, block))

        def hop(at, dx, step, up, block, src=None):
            origin = z - (step - 1) if up else z + (step - 1)
            there = z + 1 if up else z - 1
            copy = net.remote(
                (id(self), at, dx, step, up),
                block(origin, dx) if src is None else src,
                block(origin, dx),
                net.device(z=there),
            )
            fits = (origin >= 0) & (there < nz) if up else (origin < nz) & (there >= 0)
            return copy, fits

        def start(at, dx, step, up, block, src=None):
            copy, fits = hop(at, dx, step, up, block, src)
            pl.when(fits)(copy.start)
            sent.append((copy, fits))

        def arrived(at, dx, step, up, block, kind):
            copy, _ = hop(at, dx, step, up, block)
            origin = z - step if up else z + step
            fits = origin >= 0 if up else origin < nz
            pl.when(fits)(copy.wait_recv)
            if kind == "both":
                share = net.remote(
                    (id(self), "c", at, dx, step, up), block(origin, dx), block(origin, dx), net.device(0, 0, 1)
                )
                pl.when(fits)(share.start)
                shared.append((share, fits))

        swaps = {}
        for at, kind, mine, block in weights:
            if not given:
                swaps[at] = net.remote((id(self), at, "x"), mine(1), block(z, 0), net.device(1, 0))
                swaps[at].start()
            for up in (True, False):
                start(at, 0, 1, up, block, mine(0))
        for at, kind, mine, block in weights:
            if kind == "both":
                whole = ins[at].shape[0]
                into = outs[at].at[pl.ds(pl.multiple_of((z * 2 + net.x) * whole, whole), whole), :]
                locals_.append(net.copy(ins[at], into))
            else:
                locals_.append(net.copy(mine(0), block(z, 0)))
            locals_[-1].start()
        for (at, kind, mine, block), other in zip(weights, given):
            span = pl.ds(self.share[0] * other.shape[kind == "row"] // self.share[1], other.shape[kind == "row"] // self.share[1])
            other = other.at[:, span] if kind == "row" else other.at[span, :]
            locals_.append(net.copy(other, block(z, 1)))
            locals_[-1].start()
            for up in (True, False):
                start(at, 1, 1, up, block, other)
        yield
        for copy in locals_:
            copy.wait()
        for at, kind, mine, block in weights:
            if given:
                continue
            swaps[at].wait_recv()
            for up in (True, False):
                start(at, 1, 1, up, block)
            if kind == "both":
                share = net.remote((id(self), "c", at), block(z, 1), block(z, 1), net.device(0, 0, 1))
                share.start()
                shared.append((share, None))
        for step in range(1, nz):
            for at, kind, mine, block in weights:
                for dx in (0, 1):
                    yield
                    for up in (True, False):
                        arrived(at, dx, step, up, block, kind)
                        if step < nz - 1:
                            start(at, dx, step + 1, up, block)
        yield
        for copy, fits in shared:
            if fits is None:
                copy.wait_recv()
            else:
                pl.when(fits)(copy.wait_recv)
        yield READY
        for copy, fits in shared:
            if fits is None:
                copy.wait_send()
            else:
                pl.when(fits)(copy.wait_send)
        for copy, fits in sent:
            pl.when(fits)(copy.wait_send)
        for copy in swaps.values():
            copy.wait_send()


class HalfSwap:
    moves = ("x",)

    def __init__(self, shards, kinds, nz, ny):
        self.ins, self.kinds = list(shards), list(kinds)
        self.outs, self.scratch = [], []
        for shard, kind in zip(shards, kinds):
            rows, columns = shard.shape
            shape = (rows, columns // 2) if kind == "row" else (rows // 2, columns)
            self.outs.append((jax.ShapeDtypeStruct(shape, shard.dtype), ANY))
        self.remotes, self.locals = len(self.ins), 0

    def run(self, net, ins, outs, scratch):
        copies = []
        for at, (shard, out, kind) in enumerate(zip(ins, outs, self.kinds)):
            span = out.shape[kind == "row"]
            there = pl.ds(pl.multiple_of((1 - net.x) * span, span), span)
            src = shard.at[:, there] if kind == "row" else shard.at[there, :]
            copies.append(net.remote((id(self), at), src, out, net.device(1, 0)))
            copies[-1].start()
        yield
        for copy in copies:
            copy.wait_recv()
        yield READY
        for copy in copies:
            copy.wait_send()


class LineScatter:
    moves = ("x", "line")

    def __init__(self, parts, kinds, nz, ny, resident=False, joined=False):
        self.ins, self.kinds, self.resident, self.joined = list(parts), list(kinds), resident, joined
        self.outs, self.scratch = [], []
        for part, kind in zip(parts, kinds):
            rows, columns = part.shape
            shape = (rows // (2 * nz), columns) if kind == "row" else (rows, columns // (2 * nz))
            times = 2 * (len(parts) if joined else 1)
            whole = (shape[0], shape[1] * times) if kind == "row" else (shape[0] * times, shape[1])
            if not (joined and self.outs):
                self.outs.append((jax.ShapeDtypeStruct(whole, BF16), ANY))
            for lead in (nz - 1, nz - 1, 1) + (() if resident else (nz,)):
                self.scratch.append(pltpu.VMEM((lead, 2) + shape, BF16))
        count = len(self.ins)
        self.remotes = count * (1 + 4 * nz)
        self.locals = count * (2 * nz + 1)

    def run(self, net, ins, outs, scratch):
        nz, z = net.nz, net.z
        loads, grads = {}, []
        each = 3 if self.resident else 4
        outs = list(outs) * len(ins) if self.joined else outs

        def spot(at, out):
            rows, columns = scratch[each * at + 2].shape[2:]
            kind = self.kinds[at]
            size = columns if kind == "row" else rows
            first = (net.x * len(ins) + at) * size if self.joined else net.x * size
            span = pl.ds(pl.multiple_of(first, size), size)
            return out.at[:, span] if kind == "row" else out.at[span, :]

        for at, (part, out, kind) in enumerate(zip(ins, outs, self.kinds)):
            down, up, mine = scratch[each * at : each * at + 3]
            _, _, rows, columns = mine.shape

            def block(line, dx, part=part, kind=kind, rows=rows, columns=columns):
                size = rows if kind == "row" else columns
                first = pl.ds(pl.multiple_of((line * 2 + net.flip(net.x, dx)) * size, size), size)
                return part.at[first, :] if kind == "row" else part.at[:, first]

            if self.resident:
                work = block
            else:

                def work(line, dx, at=at):
                    return scratch[each * at + 3].at[line, dx]

                order = []
                for k in range(nz):
                    order += [k, nz - 1 - k]
                for line in dict.fromkeys(order):
                    for dx in (1, 0):
                        loads[at, line, dx] = net.copy(block(line, dx), work(line, dx))
                        loads[at, line, dx].start()
            grads.append((at, out, work, down, up, mine))

        def inbox(slots, line, dx, toward):
            return slots.at[line if toward < 0 else line - 1, dx]

        pieces = (1, 0)
        each_line = len(pieces)

        for at, *_ in grads:
            net.slot((id(self), at, "x"))
            for dx in (0, 1):
                for line in range(nz):
                    for toward in (-1, 1):
                        net.slot((id(self), at, line, dx, toward))

        def chain(grad, dx, line, toward):
            at, out, work, down, up, mine = grad
            slot = inbox(down if toward < 0 else up, line, dx, toward)
            copy = net.remote((id(self), at, line, dx, toward), work(line, dx), slot, net.device(z=z + toward))
            return copy, slot

        def forward(place, grad, dx, line, toward):
            at, out, work, down, up, mine = grad
            copy, slot = chain(grad, dx, line, toward)
            if not self.resident:
                loads[at, line, dx].wait()
            if place != (nz - 1 if toward < 0 else 0):
                copy.wait_recv()
                add_rows(_lead(work(line, dx)), [_lead(work(line, dx)), _lead(slot)])
            copy.start()

        def finish(place, grad, dx):
            at, out, work, down, up, mine = grad
            if not self.resident:
                loads[at, place, dx].wait()
            terms = [_lead(work(place, dx))]
            for toward in (-1, 1):
                if (place < nz - 1) if toward < 0 else (place > 0):
                    copy, slot = chain(grad, dx, place, toward)
                    copy.wait_recv()
                    terms.append(_lead(slot))
            total = mine.at[0, dx]
            add_rows(_lead(total), terms)
            if dx:
                net.remote((id(self), at, "x"), total, spot(at, out), net.device(1, 0)).start()
            else:
                net.copy_at(self.first_local + at, total, spot(at, out)).start()

        plan = {}
        for place in range(nz):
            waits_up, waits_down = place, nz - 1 - place
            todo = []
            for toward, waits, lines in (
                (1, waits_up, range(nz - 1, place, -1)),
                (-1, waits_down, range(place)),
            ):
                order = [(line, dx) for line in lines for dx in pieces]
                for j, (line, dx) in enumerate(order):
                    for grad in grads:
                        todo.append((waits + j if waits else 0, waits, (forward, grad, dx, line, toward)))
            for q, dx in enumerate(pieces):
                times = []
                if waits_up:
                    times.append(waits_up + each_line * (nz - 1 - place) + q)
                if waits_down:
                    times.append(waits_down + each_line * place + q)
                for grad in grads:
                    todo.append((max(times), nz, (finish, grad, dx)))
            for time, waits, item in sorted(todo, key=lambda entry: entry[:2]):
                plan.setdefault(time, {}).setdefault(place, []).append(item)
        self.first_local = net.take_locals(len(grads))
        for time in range(max(plan) + 1):
            if time:
                yield
            for place, items in sorted(plan.get(time, {}).items()):

                def act(place=place, items=items):
                    for item in items:
                        item[0](place, *item[1:])

                pl.when(z == place)(act)
        sent = [
            (chain(grad, dx, line, toward)[0], (z > line) if toward < 0 else (z < line))
            for grad in grads
            for dx in pieces
            for toward, lines in ((-1, range(nz - 1)), (1, range(1, nz)))
            for line in lines
        ]
        swaps, stores = [], []
        for at, out, _, _, _, mine in grads:
            swaps.append(net.remote((id(self), at, "x"), mine.at[0, 1], spot(at, out), net.device(1, 0)))
            stores.append(net.copy_at(self.first_local + at, mine.at[0, 0], spot(at, out)))
        yield
        for copy, sends in sent:
            pl.when(sends)(copy.wait_send)
        for copy in swaps:
            copy.wait()
        for copy in stores:
            copy.wait()


def _lead(ref):
    return Lead(ref)


class Lead:
    def __init__(self, ref):
        self.ref, self.shape, self.dtype = ref, (1,) + tuple(ref.shape), ref.dtype

    def __getitem__(self, index):
        return self.ref[index[1], index[2]]

    def __setitem__(self, index, value):
        self.ref[index[1], index[2]] = value


class KeysGather:
    moves = ("x", "line", "c")
    in_spec = IN_VMEM

    def __init__(self, face, nz, ny):
        m, rows, width = face.shape
        self.ins = [face]
        self.outs = [(jax.ShapeDtypeStruct((m, nz * rows, width), face.dtype), ANY)]
        self.scratch = []
        self.remotes, self.locals = 4 * (nz - 1), 1

    def run(self, net, ins, outs, scratch):
        (face,), (out,) = ins, outs
        nz, z = net.nz, net.z
        _, rows, width = face.shape
        part, side = rows // 2, width // 2

        def block(line, dx, dc):
            first = pl.multiple_of(line * rows + net.flip(net.x, dx) * part, part)
            column = pl.multiple_of(net.flip(net.c, dc) * side, side)
            return out.at[:, pl.ds(first, part), pl.ds(column, side)]

        own = face.at[
            :,
            pl.ds(pl.multiple_of(net.x * part, part), part),
            pl.ds(pl.multiple_of(net.c * side, side), side),
        ]
        sent, shared = [], []

        def line_copy(step):
            origin = z - (step - 1)
            src = own if step == 1 else block(origin, 0, 0)
            return net.remote((id(self), step), src, block(origin, 0, 0), net.device(z=z + 1))

        def start(step):
            copy, fits = line_copy(step), (z - (step - 1) >= 0) & (z + 1 < nz)
            pl.when(fits)(copy.start)
            sent.append((copy, fits))

        start(1)
        keep = net.copy(face, out.at[:, pl.ds(pl.multiple_of(z * rows, rows), rows), :])
        keep.start()
        later = []
        for step in range(1, nz):
            yield
            fits = z - step >= 0
            pl.when(fits)(line_copy(step).wait_recv)
            if step < nz - 1:
                start(step + 1)
            here = block(z - step, 0, 0)
            across = net.remote((id(self), "x", step), here, here, net.device(1, 0))
            beside = net.remote((id(self), "c", step), here, here, net.device(0, 0, 1))
            for copy in (across, beside):
                pl.when(fits)(copy.start)
                sent.append((copy, fits))
            later.append((step, fits, across))
            shared.append((beside, fits))
        for step, fits, across in later:
            yield
            pl.when(fits)(across.wait_recv)
            there = block(z - step, 1, 0)
            beside = net.remote((id(self), "xc", step), there, there, net.device(0, 0, 1))
            pl.when(fits)(beside.start)
            sent.append((beside, fits))
            shared.append((beside, fits))
        yield
        for copy, fits in shared:
            pl.when(fits)(copy.wait_recv)
        keep.wait()
        yield READY
        for copy, fits in sent:
            pl.when(fits)(copy.wait_send)


class WholeScatter(FaceScatter):
    moves = ("x", "y", "c", "z")

    def __init__(self, part, nz, ny, resident=False):
        m, _, rows, d = part.shape
        merged = jax.ShapeDtypeStruct((m * nz, rows, d), part.dtype) if resident else part.reshape(m * nz, rows, d)
        super().__init__(merged, nz, ny, resident)
        t = rows // (4 * ny)
        self.m, self.nz = m, nz
        self.outs = [(jax.ShapeDtypeStruct((m, t, d), F32), pl.BlockSpec(memory_space=pltpu.VMEM))]
        self.scratch = self.scratch + [pltpu.VMEM((m * nz, t, d), BF16), pltpu.VMEM((nz, m, t, d), BF16)]
        self.remotes = self.remotes + nz * m
        self.locals = self.locals + m

    def run(self, net, ins, outs, scratch):
        face, inbox = scratch[-2:]
        yield from super().run(net, ins, [face], scratch[:-2])
        nz, m = self.nz, self.m
        copies = []
        for far in range(1, nz):
            line = lax.rem(net.z + far, nz)
            for at in range(m):
                copies.append(
                    pltpu.make_async_remote_copy(
                        src_ref=face.at[at * nz + line],
                        dst_ref=inbox.at[far, at],
                        send_sem=net.send.at[net.slot((id(self), "z", far, at))],
                        recv_sem=net.recv.at[net.slot((id(self), "z", far, at))],
                        device_id=net.device(z=line),
                        device_id_type=MESH,
                    )
                )
                copies[-1].start()
        own = []
        for at in range(m):
            own.append(net.copy(face.at[at * nz + net.z], inbox.at[0, at]))
            own[-1].start()
        yield
        for copy in own:
            copy.wait()
        for copy in copies:
            copy.wait()
        add_rows(outs[0], [inbox.at[far] for far in range(nz)])


class QuickScatter:
    moves = ("c", "same", "z")

    def __init__(self, part, nz, ny):
        _, rows, d = part.shape
        t = rows // (4 * ny)
        self.ins, self.t = [part], t
        self.outs = [(jax.ShapeDtypeStruct((t, d), F32), pl.BlockSpec(memory_space=pltpu.VMEM))]
        self.scratch = [
            pltpu.VMEM((2 * ny, nz, t, d), BF16),
            pltpu.VMEM((2 * ny, nz, t, d), BF16),
            pltpu.VMEM((2 * ny, nz, t, d), BF16),
            pltpu.VMEM((nz, t, d), BF16),
            pltpu.VMEM((nz, 1, t, d), BF16),
        ]
        self.remotes, self.locals = 4 * ny + nz, 2 * ny + 1

    def run(self, net, ins, outs, scratch):
        (part,), (out,), t = ins, outs, self.t
        work, from_core, inbox, face, line_in = scratch
        ny, nz = net.ny, net.nz
        order = [(dx, dy) for dx in (1, 0) for dy in reversed(range(ny))]
        cores, loads, copies = {}, {}, {}

        def rows(dx, dy, dc):
            return part.at[:, pl.ds(pl.multiple_of(net.rank(dx, dy, dc) * t, t), t), :]

        for dx, dy in order:
            at = dx * ny + dy
            loads[at] = net.copy(rows(dx, dy, 0), work.at[at])
            loads[at].start()
            cores[at] = net.remote((id(self), "c", at), rows(dx, dy, 1), from_core.at[at], net.device(0, 0, 1))
            cores[at].start()
        for dx, dy in order:
            at = dx * ny + dy
            yield
            loads[at].wait()
            cores[at].wait_recv()
            add_rows(work.at[at], [work.at[at], from_core.at[at]])
            if at:
                copies[at] = net.remote((id(self), at), work.at[at], inbox.at[at], net.device(dx, dy))
                copies[at].start()
        yield
        for copy in copies.values():
            copy.wait_recv()
        add_rows(face, [work.at[0]] + [inbox.at[at] for at in copies])
        lines = []
        for far in range(1, nz):
            line = lax.rem(net.z + far, nz)
            lines.append(
                net.remote((id(self), "z", far), face.at[pl.ds(line, 1)], line_in.at[far], net.device(z=line))
            )
            lines[-1].start()
        own = net.copy(face.at[pl.ds(net.z, 1)], line_in.at[0])
        own.start()
        yield
        own.wait()
        for copy in lines:
            copy.wait_recv()
        add_rows(_lead(out), [line_in.at[far] for far in range(nz)])
        for copy in list(cores.values()) + list(copies.values()) + lines:
            copy.wait_send()


class PlaneGather:
    moves = ("plane",)
    in_spec = IN_VMEM

    def __init__(self, own, nz, ny):
        self.ins = [own]
        self.outs = [(jax.ShapeDtypeStruct((2 * nz,) + own.shape, own.dtype), ANY)]
        self.scratch = []
        self.remotes, self.locals = 2 * nz, 1

    def run(self, net, ins, outs, scratch):
        (own,), (out,) = ins, outs
        here = out.at[net.z * 2 + net.x]
        copies = []
        for far in range(net.nz):
            for dx in (0, 1):
                if far or dx:
                    line = lax.rem(net.z + far, net.nz)
                    copies.append(net.remote((id(self), far, dx), own, here, net.device(dx, z=line)))
                    copies[-1].start()
        keep = net.copy(own, here)
        keep.start()
        yield
        for copy in copies:
            copy.wait()
        keep.wait()


class SmallScatter:
    moves = ("face", "z")

    def __init__(self, part, nz, ny):
        ranks, _, rows, width = part.shape
        self.ins = [part]
        vmem = pl.BlockSpec(memory_space=pltpu.VMEM)
        self.outs = [(jax.ShapeDtypeStruct((rows, width), F32), vmem)]
        self.scratch = [
            pltpu.VMEM((ranks, nz, rows, width), F32),
            pltpu.VMEM((nz, rows, width), F32),
            pltpu.VMEM((nz, rows, width), F32),
        ]
        self.remotes, self.locals = ranks + nz, 2

    def run(self, net, ins, outs, scratch):
        (part,), (out,) = ins, outs
        inbox, total, line_in = scratch
        ny, nz = net.ny, net.nz
        copies = []
        for dx in (0, 1):
            for dy in range(ny):
                for dc in (0, 1):
                    if dx or dy or dc:
                        at = (dx * ny + dy) * 2 + dc
                        copies.append(
                            net.remote(
                                (id(self), at), part.at[net.rank(dx, dy, dc)], inbox.at[at], net.device(dx, dy, dc)
                            )
                        )
                        copies[-1].start()
        keep = net.copy(part.at[net.rank()], inbox.at[0])
        keep.start()
        yield
        keep.wait()
        for copy in copies:
            copy.wait()
        total[...] = jnp.sum(inbox[...], axis=0)
        lines = []
        for far in range(1, nz):
            line = lax.rem(net.z + far, nz)
            lines.append(net.remote((id(self), "z", far), total.at[line], line_in.at[far], net.device(z=line)))
            lines[-1].start()
        own = net.copy(total.at[net.z], line_in.at[0])
        own.start()
        yield
        own.wait()
        for copy in lines:
            copy.wait()
        out[...] = jnp.sum(line_in[...], axis=0)


def launch(body, ins, in_specs, outs, scratch, plans, nz, ny, collective_id, name, extra_locals=0, vmem=56):
    moves = set()
    for plan in plans:
        moves |= set(plan.moves)
    remotes = sum(plan.remotes for plan in plans)
    locals_ = max(1, extra_locals + sum(plan.locals for plan in plans))

    def kernel(*refs):
        in_refs, refs = refs[: len(ins)], refs[len(ins) :]
        out_refs, refs = refs[: len(outs)], refs[len(outs) :]
        scratch_refs, (send, recv, local) = refs[: len(scratch)], refs[len(scratch) :]
        net = Net(nz, ny, send, recv, local)
        peers = {}
        for far in range(nz):
            for dx in (0, 1):
                for dy in range(ny):
                    for dc in (0, 1):
                        kinds = set()
                        if not far:
                            kinds.add("face")
                            if dx and not dy and not dc:
                                kinds.add("x")
                            if dy and not dx and not dc:
                                kinds.add("y")
                            if dc and not dx and not dy:
                                kinds.add("c")
                            if not dc:
                                kinds.add("same")
                        if far and not dx and not dy and not dc:
                            kinds.add("z")
                            if far in (1, nz - 1):
                                kinds.add("line")
                        if not dy and not dc:
                            kinds.add("plane")
                        if (far or dx or dy or dc) and kinds & moves:
                            line = lax.rem(net.z + far, nz) if far else None
                            peers[far, dx, dy, dc] = net.device(dx, dy, dc, line)
        barrier = pltpu.get_barrier_semaphore()
        for device in peers.values():
            pl.semaphore_signal(barrier, inc=1, device_id=device, device_id_type=MESH)
        pl.semaphore_wait(barrier, len(peers))
        body(net, in_refs, out_refs, scratch_refs)

    return list(
        pl.pallas_call(
            kernel,
            out_shape=[shape for shape, _ in outs],
            in_specs=in_specs,
            out_specs=[spec for _, spec in outs],
            scratch_shapes=list(scratch)
            + [
                pltpu.SemaphoreType.DMA((remotes,)),
                pltpu.SemaphoreType.DMA((remotes,)),
                pltpu.SemaphoreType.DMA((locals_,)),
            ],
            compiler_params=pltpu.CompilerParams(
                collective_id=collective_id, has_side_effects=True, vmem_limit_bytes=vmem << 20
            ),
            name=name,
        )(*ins)
    )


def exchange(plans, nz, ny, collective_id, name, order=()):
    ins = [array for plan in plans for array in plan.ins]
    outs = [out for plan in plans for out in plan.outs]
    scratch = [entry for plan in plans for entry in plan.scratch]

    def body(net, in_refs, out_refs, scratch_refs):
        running = []
        for plan in plans:
            mine = []
            for refs_of, count in ((in_refs, plan.ins), (out_refs, plan.outs), (scratch_refs, plan.scratch)):
                mine.append(list(refs_of[: len(count)]))
            in_refs = in_refs[len(plan.ins) :]
            out_refs = out_refs[len(plan.outs) :]
            scratch_refs = scratch_refs[len(plan.scratch) :]
            running.append(plan.run(net, *mine))
        for at in order:
            next(running[at], None)
        while running:
            for steps in list(running):
                try:
                    next(steps)
                except StopIteration:
                    running.remove(steps)

    specs = [getattr(plan, "in_spec", ANY) for plan in plans for _ in plan.ins]
    results = launch(body, ins, specs, outs, scratch, plans, nz, ny, collective_id, name)
    grouped = []
    for plan in plans:
        grouped.append(results[: len(plan.outs)])
        results = results[len(plan.outs) :]
    return grouped


class Weave:
    def __init__(self):
        self.plans, self.ready = {}, set()

    def add(self, name, steps):
        self.plans[name] = steps

    def step(self, name):
        steps = self.plans.get(name)
        if steps is not None:
            state = next(steps, self)
            if state is self:
                del self.plans[name]
            elif state == READY:
                self.ready.add(name)

    def need(self, name):
        while name in self.plans and name not in self.ready:
            self.step(name)

    def finish(self, name):
        while name in self.plans:
            self.step(name)


def first_block(block, seq_len):
    longest = seq_len // 2 + BLOCK
    return jnp.maximum(block - (longest - 1 + BLOCK - 1) // BLOCK, 0)


def loop(count, body):
    def step(at, carry):
        body(at)
        return carry

    lax.fori_loop(0, count, step, 0)


def mlp_block(mixed, wo, inputs, cotangent, cot_face, norms, wexp_first, w_expand, w_reduce, nz, ny, collective_id):
    micro_count, own_rows, width = inputs.shape
    face_rows = cot_face.shape[1]
    tokens = micro_count * face_rows
    attn = mixed.shape[2]
    units = w_expand[0].shape[1] // 2
    half = units // 2
    tile = min(512, half)
    wide = 512
    part = jax.ShapeDtypeStruct((micro_count, face_rows, width), BF16)
    part_red = jax.ShapeDtypeStruct((units, width), BF16)
    own = (micro_count, own_rows, width)
    scatter_a, scatter_b = (FaceScatter(part, nz, ny, resident=True) for _ in range(2))
    gather = FaceGather(jax.ShapeDtypeStruct(own, BF16), nz, ny, report=True)
    line_e = LineGather(w_expand[:1], ["row"], nz, ny, share=(1, 2), given=w_expand[1:])
    line_r = LineGather(w_reduce[:1], ["col"], nz, ny, given=w_reduce[1:])
    line_s = LineScatter([part_red], ["col"], nz, ny, resident=True)
    plans = [scatter_a, scatter_b, gather, line_e, line_r, line_s]
    vmem = pl.BlockSpec(memory_space=pltpu.VMEM)
    outs = [
        (jax.ShapeDtypeStruct(own, F32), ANY),
        (jax.ShapeDtypeStruct(own, F32), ANY),
        (jax.ShapeDtypeStruct(own, BF16), ANY),
        (jax.ShapeDtypeStruct((2, 16, width), F32), vmem),
        (jax.ShapeDtypeStruct((width, half), BF16), ANY),
        (jax.ShapeDtypeStruct((width, half), BF16), ANY),
        (part, ANY),
    ] + line_s.outs
    scratch = [
        pltpu.VMEM((micro_count, face_rows, width), BF16),
        pltpu.VMEM(own, F32),
        pltpu.VMEM(own, F32),
        pltpu.VMEM(own, BF16),
        pltpu.VMEM(own, BF16),
        pltpu.VMEM(own, BF16),
        pltpu.VMEM((micro_count, face_rows, width), BF16),
        pltpu.VMEM((micro_count, face_rows, width), BF16),
        pltpu.VMEM((width, half), BF16),
        pltpu.VMEM((width, half), BF16),
        pltpu.VMEM((units, width), BF16),
        pltpu.VMEM((micro_count, face_rows, units), BF16),
        pltpu.VMEM((micro_count, face_rows, units), BF16),
        pltpu.VMEM((units, width), BF16),
        pltpu.VMEM((micro_count, face_rows, attn), BF16),
        pltpu.VMEM((attn, width), BF16),
    ]
    shared = len(scratch)
    scratch += scatter_a.scratch + line_s.scratch

    def body(net, ins, outs, scratch):
        mixed_in, wo_in, own_in, cot_in, face_in, norms, first_in, *weights_in = ins
        middle_out, grad_out, low_out, norm_out, expand_a, expand_b, reduced_out, reduce_out = outs
        p, branch, middle, own, cot_own, n_own, n_face, cot, we0, we1, wr, active, slope, pr, mixed, wo = scratch[:shared]
        we = (we0, we1)
        slots = list(scratch[shared : shared + len(scatter_a.scratch)])
        line_slots = list(scratch[shared + len(scatter_a.scratch) :])

        loads = [
            net.copy(*pair)
            for pair in (
                (mixed_in, mixed),
                (wo_in, wo),
                (own_in, own),
                (cot_in, cot_own),
                (first_in, we0),
                (face_in, cot),
            )
        ]
        weave = Weave()
        stores = []
        weave.add("e", line_e.run(net, weights_in[:2], [we1], []))
        weave.step("e")
        weave.add("r", line_r.run(net, weights_in[2:], [wr], []))
        weave.step("r")
        for load in loads:
            load.start()

        chip_tokens = micro_count * 2 * own_rows

        def branch_chip(dx, dy):
            rows = net.chip_rows(dx, dy, own_rows)

            def tile_at(n):
                columns = pl.ds(pl.multiple_of(n * wide, wide), wide)
                p[:, rows, columns] = (
                    jnp.dot(
                        mixed[:, rows, :].reshape(chip_tokens, attn), wo[:, columns], preferred_element_type=F32
                    )
                    .astype(BF16)
                    .reshape(micro_count, 2 * own_rows, wide)
                )

            loop(width // wide, tile_at)

        row_steps = own_rows // 16

        def own_rows_at(at):
            return lax.div(at, row_steps), pl.ds(pl.multiple_of(lax.rem(at, row_steps) * 16, 16), 16)

        def norm_rows(at):
            m, rows = own_rows_at(at)
            values = own[m, rows, :].astype(F32) + branch[m, rows, :]
            middle[m, rows, :] = values
            centered = values - jnp.mean(values, axis=-1, keepdims=True)
            spread = lax.rsqrt(jnp.mean(centered * centered, axis=-1, keepdims=True) + EPSILON)
            n_own[m, rows, :] = (centered * spread * norms[2:3, :] + norms[3:4, :]).astype(BF16)

        def hidden_chip(dx, dy, h):
            rows = net.chip_rows(dx, dy, own_rows)
            block = (micro_count, 2 * own_rows, tile)

            def tile_at(n):
                columns = pl.ds(pl.multiple_of(n * tile, tile), tile)
                into = pl.ds(pl.multiple_of(h * half + n * tile, tile), tile)
                hidden = jnp.dot(
                    n_face[:, rows, :].reshape(chip_tokens, width), we[h][:, columns], preferred_element_type=F32
                )
                square = hidden * hidden
                bend = jnp.tanh(GELU_A * hidden * (1.0 + GELU_B * square))
                active[:, rows, into] = (0.5 * hidden * (1.0 + bend)).astype(BF16).reshape(block)
                slope[:, rows, into] = (
                    (
                        0.5 * (1.0 + bend)
                        + (0.5 * GELU_A) * hidden * (1.0 - bend * bend) * (1.0 + (3.0 * GELU_B) * square)
                    )
                    .astype(BF16)
                    .reshape(block)
                )

            loop(half // tile, tile_at)

        across = (((0,), (0,)), ((), ()))
        along = (((1,), (1,)), ((), ()))
        def reduce_tile(first):
            def tile_at(at):
                f, n = lax.div(at, width // wide), lax.rem(at, width // wide)
                columns = pl.ds(pl.multiple_of(n * wide, wide), wide)
                rows = pl.ds(pl.multiple_of(first + f * tile, tile), tile)
                pr[rows, columns] = lax.dot_general(
                    active[:, :, rows].reshape(tokens, tile),
                    cot[:, :, columns].reshape(tokens, wide),
                    across,
                    preferred_element_type=F32,
                ).astype(BF16)

            return tile_at

        def slope_tile(at):
            m, n = lax.div(at, units // tile), lax.rem(at, units // tile)
            columns = pl.ds(pl.multiple_of(n * tile, tile), tile)
            grad = lax.dot_general(cot[m], wr[columns, :], along, preferred_element_type=F32)
            slope[m, :, columns] = (grad * slope[m, :, columns].astype(F32)).astype(BF16)

        made = []

        def normed_chip(dx, dy):
            made.append((dx, dy))
            rows = net.chip_rows(dx, dy, own_rows)

            def tile_at(n):
                columns = pl.ds(pl.multiple_of(n * wide, wide), wide)
                grad = lax.dot_general(
                    slope[:, rows, :half].reshape(chip_tokens, half), we0[columns, :], along, preferred_element_type=F32
                )
                grad = grad + lax.dot_general(
                    slope[:, rows, half:].reshape(chip_tokens, half), we1[columns, :], along, preferred_element_type=F32
                )
                p[:, rows, columns] = grad.astype(BF16).reshape(micro_count, 2 * own_rows, wide)

            loop(width // wide, tile_at)

        def reduced_tiles(m):
            def tile_at(n):
                columns = pl.ds(pl.multiple_of(n * wide, wide), wide)
                cot[m, :, columns] = jnp.dot(active[m], wr[:, columns], preferred_element_type=F32).astype(BF16)

            def act():
                loop(width // wide, tile_at)
                stores.append(net.copy(cot.at[m], reduced_out.at[m]))
                stores[-1].start()

            return act

        def expand_tiles(h):
            def tile_at(at):
                k, n = lax.div(at, half // tile), lax.rem(at, half // tile)
                rows = pl.ds(pl.multiple_of(k * wide, wide), wide)
                columns = pl.ds(pl.multiple_of(n * tile, tile), tile)
                grads = pl.ds(pl.multiple_of(h * half + n * tile, tile), tile)
                we[h][rows, columns] = lax.dot_general(
                    n_face[:, :, rows].reshape(tokens, wide),
                    slope[:, :, grads].reshape(tokens, tile),
                    across,
                    preferred_element_type=F32,
                ).astype(BF16)

            def act():
                loop((width // wide) * (half // tile), tile_at)
                stores.append(net.copy(we[h], (expand_a, expand_b)[h]))
                stores[-1].start()

            return act

        def back_rows(at):
            m, rows = own_rows_at(at)
            values = middle[m, rows, :]
            centered = values - jnp.mean(values, axis=-1, keepdims=True)
            spread = lax.rsqrt(jnp.mean(centered * centered, axis=-1, keepdims=True) + EPSILON)
            unit = centered * spread
            grad = branch[m, rows, :]
            norm_out[0] += grad * unit
            norm_out[1] += grad
            turned = grad * norms[2:3, :]
            inner = jnp.mean(turned * unit, axis=-1, keepdims=True)
            total = cot_own[m, rows, :].astype(F32) + spread * (
                turned - jnp.mean(turned, axis=-1, keepdims=True) - unit * inner
            )
            middle[m, rows, :] = total
            n_own[m, rows, :] = total.astype(BF16)

        def later():
            while len(made) < 2 * ny:
                weave.step("m")
            weave.finish("e")
            for h in (0, 1):
                expand_tiles(h)()
                yield
            for m in range(micro_count):
                reduced_tiles(m)()
                yield

        def main():
            loads[0].wait()
            loads[1].wait()
            yield from scatter_a.run(net, [p], [branch], slots, branch_chip)
            loads[2].wait()
            loop(micro_count * row_steps, norm_rows)
            keep_middle = net.copy(middle, middle_out)
            keep_middle.start()
            loads[4].wait()
            chips, halved = 0, []
            for place in gather.run(net, [n_own], [n_face], []):
                if place is not None:
                    hidden_chip(*place, 0)
                    halved.append(place)
                    chips += 1
                    if chips > ny:
                        yield
                        weave.need("e")
                        for place in halved:
                            hidden_chip(*place, 1)
                        halved = []
                yield
            loads[5].wait()
            loop((half // tile) * (width // wide), reduce_tile(0))
            yield
            loop((half // tile) * (width // wide), reduce_tile(half))
            weave.add("s", line_s.run(net, [pr], [reduce_out], line_slots))
            weave.step("s")
            yield
            weave.need("r")
            loop(micro_count * (units // tile), slope_tile)
            yield
            weave.add("x", later())
            yield from scatter_b.run(net, [p], [branch], slots, normed_chip)
            loads[3].wait()
            keep_middle.wait()
            norm_out[...] = jnp.zeros_like(norm_out)
            loop(micro_count * row_steps, back_rows)
            for pair in ((middle, grad_out), (n_own, low_out)):
                stores.append(net.copy(*pair))
                stores[-1].start()

        weave.add("m", main())
        for name in "".join(MLP_ORDER):
            weave.step(name)
        for name in "mxsre":
            weave.finish(name)
        for store in stores:
            store.wait()

    ins = [mixed, wo, inputs, cotangent, cot_face, norms, wexp_first, *w_expand, *w_reduce]
    specs = [ANY] * 5 + [vmem] + [ANY] * (len(ins) - 6)
    return launch(
        body, ins, specs, outs, scratch, plans, nz, ny, collective_id, "mlp_block", extra_locals=12, vmem=62
    )


def front_block(inputs, cotangent, w_query, w_attn_out, w_keyval, w_expand, norms, doc_ids, nz, ny, collective_id, head_dim):
    micro_count, own_rows, width = inputs.shape
    face_rows = own_rows * 4 * ny
    attn = w_query.shape[1] // 2
    seq_len = nz * face_rows
    blocks = face_rows // BLOCK
    heads = attn // head_dim
    tall = heads * BLOCK
    own = jax.ShapeDtypeStruct(inputs.shape, BF16)
    keys_face = jax.ShapeDtypeStruct((micro_count, face_rows, 2 * head_dim), BF16)
    shard = norms.shape[1] // 4
    norms_own = jax.ShapeDtypeStruct((8, shard), F32)
    plane = PlaneGather(norms_own, nz, ny)
    gather = FaceGather(own, nz, ny)
    gather_c = FaceGather(cotangent, nz, ny, hold_x=True)
    swap_e = HalfSwap([w_expand], ["row"], nz, ny)
    line_a = LineGather([w_keyval, w_query], ["both", "row"], nz, ny)
    line_o = LineGather([w_attn_out], ["col"], nz, ny)
    given = jax.ShapeDtypeStruct((w_expand.shape[0], w_expand.shape[1] // 2), BF16)
    line_e = LineGather([w_expand], ["row"], nz, ny, share=(0, 2), given=[given])
    keys = KeysGather(keys_face, nz, ny)
    plans = [plane, gather, gather_c, swap_e, line_a, line_o, line_e, keys]
    kept = [
        jax.ShapeDtypeStruct((micro_count, face_rows, width), BF16),
        line_a.outs[0][0],
        line_a.outs[1][0],
        given,
        jax.ShapeDtypeStruct((micro_count, face_rows, attn), BF16),
        keys.outs[0][0],
        jax.ShapeDtypeStruct((micro_count, face_rows, attn), BF16),
        jax.ShapeDtypeStruct((micro_count, blocks, 1, tall), F32),
        jax.ShapeDtypeStruct((micro_count, blocks, 2, BLOCK), jnp.int32),
        own,
    ]
    outs = [(shape, ANY) for shape in kept] + [
        (jax.ShapeDtypeStruct((8, width), F32), IN_VMEM),
        gather_c.outs[0],
        line_o.outs[0],
        line_e.outs[0],
    ]
    scratch = [pltpu.VMEM(shape.shape, shape.dtype) for shape in kept] + [
        pltpu.VMEM(keys_face.shape, BF16),
        pltpu.VMEM((8, shard), F32),
        pltpu.VMEM((2 * nz, 8, shard), F32),
    ]

    def body(net, ins, outs, scratch):
        inputs, cotangent, w_query, w_attn_out, w_keyval, w_expand, doc_ids, norms_in = ins
        norm_rows, cot_out, wo_out, first_out = outs[len(kept) :]
        normed, wkv, wq, given, queries, keys_vals, mixed, logs, limits, n_own, keys_face, norms, norms_out = scratch
        norms[...] = jnp.zeros_like(norms)
        for k in range(4):
            norms[k : k + 1, :] = norms_in[:, k * shard : (k + 1) * shard].astype(F32)
        stores = [net.copy(*pair) for pair in zip(scratch, outs[: len(kept)])]
        weave = Weave()
        weave.add("p", plane.run(net, [norms], [norms_out], []))
        weave.step("p")
        weave.add("a", line_a.run(net, [w_keyval, w_query], [wkv, wq], []))
        weave.step("a")
        weave.add("h", swap_e.run(net, [w_expand], [given], []))
        weave.add("o", line_o.run(net, [w_attn_out], [wo_out], []))
        weave.add("c", gather_c.run(net, [cotangent], [cot_out], []))

        def line_first():
            weave.need("h")
            yield from line_e.run(net, [w_expand, given], [first_out], [])

        weave.add("e", line_first())
        along = (((1,), (1,)), ((), ()))
        across = (((0,), (0,)), ((), ()))
        step = min(32, own_rows)

        def own_norm(at):
            m = lax.div(at, own_rows // step)
            rows = pl.ds(pl.multiple_of(lax.rem(at, own_rows // step) * step, step), step)
            gain, shift = norm_rows[0:1, :], norm_rows[1:2, :]
            values = inputs[m, rows, :].astype(F32)
            centered = values - jnp.mean(values, axis=-1, keepdims=True)
            spread = lax.rsqrt(jnp.mean(centered * centered, axis=-1, keepdims=True) + EPSILON)
            n_own[m, rows, :] = (centered * spread * gain + shift).astype(BF16)

        def keys_tile(m):
            keys_face[m] = jnp.dot(normed[m], wkv[...], preferred_element_type=F32).astype(BF16)

        def queries_tile(m):
            queries[m] = jnp.dot(normed[m], wq[...], preferred_element_type=F32).astype(BF16)

        def mixed_tile(m):
            def tile_at(b):
                rows = pl.ds(pl.multiple_of(b * BLOCK, BLOCK), BLOCK)
                query = jnp.concatenate(
                    [queries[m, rows, h * head_dim : (h + 1) * head_dim] for h in range(heads)], axis=0
                )
                starts = jnp.concatenate([limits[m, b, 0:1, :]] * heads, axis=1)
                ends = jnp.concatenate([limits[m, b, 1:2, :]] * heads, axis=1)
                place = lax.broadcasted_iota(jnp.int32, (BLOCK, tall), 0)

                def body(block, carry):
                    top, total, out = carry
                    first = pl.multiple_of(block * BLOCK, BLOCK)
                    keys = keys_vals[m, pl.ds(first, BLOCK), :head_dim]
                    values = keys_vals[m, pl.ds(first, BLOCK), head_dim:]
                    raw = lax.dot_general(keys, query, along, preferred_element_type=F32)
                    allowed = (place >= starts - first) & (place < ends - first)
                    scores = jnp.where(allowed, raw * (LOG2_E / math.sqrt(head_dim)), NEG_FILL)
                    new_top = jnp.maximum(top, jnp.max(scores, axis=0, keepdims=True))
                    weights = jnp.exp2(scores - new_top)
                    fade = jnp.exp2(top - new_top)
                    total = total * fade + jnp.sum(weights, axis=0, keepdims=True)
                    out = out * fade + lax.dot_general(
                        values, weights.astype(BF16), across, preferred_element_type=F32
                    )
                    return new_top, total, out

                top, total, out = lax.fori_loop(
                    first_block(net.z * blocks + b, seq_len),
                    net.z * blocks + b + 1,
                    body,
                    (
                        jnp.full((1, tall), NEG_FILL, F32),
                        jnp.zeros((1, tall), F32),
                        jnp.zeros((head_dim, tall), F32),
                    ),
                )
                out = jnp.transpose(out / total).astype(BF16)
                for h in range(heads):
                    mixed[m, rows, h * head_dim : (h + 1) * head_dim] = out[h * BLOCK : (h + 1) * BLOCK]
                logs[m, b] = top + jnp.log2(total)

            return tile_at

        def limits_tile(m):
            kinds = lax.broadcasted_iota(jnp.int32, (32, 1), 0)
            counts = jnp.sum((doc_ids[m : m + 1, :] == kinds).astype(F32), axis=1, keepdims=True)
            for b in range(blocks):
                first = pl.multiple_of(net.z * face_rows + b * BLOCK, BLOCK)
                docs = doc_ids[m : m + 1, pl.ds(first, BLOCK)]
                starts = jnp.sum(jnp.where(kinds < docs, counts, 0.0), axis=0, keepdims=True)
                ends = jnp.sum(jnp.where(kinds <= docs, counts, 0.0), axis=0, keepdims=True)
                limits[m, b, 0:1, :] = starts.astype(jnp.int32)
                limits[m, b, 1:2, :] = ends.astype(jnp.int32)

        def main():
            weave.finish("p")
            norm_rows[...] = jnp.concatenate([norms_out[d] for d in range(2 * nz)], axis=1)
            loop(micro_count * (own_rows // step), own_norm)
            stores[9].start()
            yield from gather.run(net, [n_own], [normed], [])
            stores[0].start()
            yield
            weave.need("a")
            loop(micro_count, keys_tile)
            weave.add("k", keys.run(net, [keys_face], [keys_vals], []))
            weave.step("k")
            yield
            for at in (1, 2):
                stores[at].start()
            for m in range(micro_count):
                limits_tile(m)
            stores[8].start()
            loop(micro_count, queries_tile)
            stores[4].start()
            yield
            weave.need("k")
            stores[5].start()
            for m in range(micro_count):
                loop(blocks, mixed_tile(m))
                yield
            for at in (6, 7):
                stores[at].start()

        weave.add("m", main())
        for name in "".join(FRONT_ORDER):
            weave.step(name)
        for name in "mhcoeak":
            weave.finish(name)
        stores[3].start()
        for store in stores:
            store.wait()

    ins = [inputs, cotangent, w_query, w_attn_out, w_keyval, w_expand, doc_ids, norms]
    results = launch(
        body, ins, [IN_VMEM] * len(ins), outs, scratch, plans, nz, ny, collective_id, "front_block", extra_locals=len(kept)
    )
    return results[: len(kept)], results[len(kept) :]


def back_block(low, reduced, parts, mixed, wo, wq, normed, queries, keys_vals, logs, limits, nz, ny, collective_id, head_dim):
    micro_count, own_rows, width = low.shape
    face_rows, attn = queries.shape[1:]
    seq_len = keys_vals.shape[1]
    tokens = micro_count * face_rows
    blocks = face_rows // BLOCK
    heads = attn // head_dim
    tall = heads * BLOCK
    scale = 1.0 / math.sqrt(head_dim)
    wide = 512
    half = parts[0].shape[1]
    part = jax.ShapeDtypeStruct((micro_count, face_rows, width), BF16)
    gather = FaceGather(low, nz, ny)
    scatter_r = FaceScatter(reduced, nz, ny)
    scatter_q = FaceScatter(part, nz, ny, resident=True)
    whole = WholeScatter(jax.ShapeDtypeStruct((micro_count, nz, face_rows, 2 * head_dim), BF16), nz, ny, resident=True)
    line_e = LineScatter(parts, ["row", "row"], nz, ny, resident=True, joined=True)
    attn_parts = [jax.ShapeDtypeStruct((attn, width), BF16), jax.ShapeDtypeStruct((width, attn), BF16)]
    line_a = LineScatter(attn_parts, ["col", "row"], nz, ny, resident=True)
    plans = [gather, scatter_r, scatter_q, whole, line_e, line_a]
    groups = [scatter_r, scatter_q, whole, line_e, line_a]
    outs = scatter_r.outs + scatter_q.outs + whole.outs + line_e.outs + line_a.outs
    normed = normed.reshape(micro_count, face_rows, width)
    given = [mixed, wo, wq, queries, keys_vals, logs, limits, *parts]
    scratch = [pltpu.VMEM(entry.shape, entry.dtype) for entry in given] + [
        pltpu.VMEM(part.shape, BF16),
        pltpu.VMEM(queries.shape, BF16),
        pltpu.VMEM(queries.shape, BF16),
        pltpu.VMEM((seq_len, 2 * head_dim), F32),
        pltpu.VMEM((micro_count * nz, face_rows, 2 * head_dim), BF16),
        pltpu.VMEM((attn, width), BF16),
        pltpu.VMEM((width, attn), BF16),
        pltpu.VMEM((2, micro_count, face_rows, wide), BF16),
    ]
    shared = len(scratch)
    for plan in groups:
        scratch = scratch + plan.scratch

    def body(net, ins, outs, scratch):
        low, reduced_in, normed_in, *given_in = ins
        reduced_out, from_out, keys_out, *line_outs = outs
        mixed, wo, wq, queries, keys_vals, logs, limits, *expand = scratch[: len(given)]
        face, grad_mixed, grad_queries, acc, grad_keys, part_out, part_query, normed = scratch[len(given) : shared]
        slots, first = {}, shared
        for name, plan in zip("rqwea", groups):
            slots[name] = list(scratch[first : first + len(plan.scratch)])
            first += len(plan.scratch)
        loads = [net.copy(*pair) for pair in zip(given_in, scratch)]
        order = [len(given) - 2, len(given) - 1] + list(range(len(given) - 2))
        weave = Weave()
        along = (((1,), (1,)), ((), ()))
        across = (((0,), (0,)), ((), ()))

        def mix_tile(m):
            grad_mixed[m] = lax.dot_general(face[m], wo[...], along, preferred_element_type=F32).astype(BF16)

        def attn_out_tile(n):
            columns = pl.ds(pl.multiple_of(n * wide, wide), wide)
            part_out[:, columns] = lax.dot_general(
                mixed[...].reshape(tokens, attn),
                face[:, :, columns].reshape(tokens, wide),
                across,
                preferred_element_type=F32,
            ).astype(BF16)

        def attn_tile(m):
            def tile_at(b):
                rows = pl.ds(pl.multiple_of(b * BLOCK, BLOCK), BLOCK)

                def stack(ref):
                    return jnp.concatenate(
                        [ref[m, rows, h * head_dim : (h + 1) * head_dim] for h in range(heads)], axis=0
                    )

                query, grad = stack(queries), stack(grad_mixed)
                products = grad.astype(F32) * stack(mixed).astype(F32)
                delta = jnp.sum(jnp.transpose(products), axis=0, keepdims=True)
                starts = jnp.concatenate([limits[m, b, 0:1, :]] * heads, axis=1)
                ends = jnp.concatenate([limits[m, b, 1:2, :]] * heads, axis=1)
                log_total = logs[m, b]
                place = lax.broadcasted_iota(jnp.int32, (BLOCK, tall), 0)

                def body(block, grad_query):
                    first = pl.multiple_of(block * BLOCK, BLOCK)
                    keys = keys_vals[m, pl.ds(first, BLOCK), :head_dim]
                    values = keys_vals[m, pl.ds(first, BLOCK), head_dim:]
                    raw = lax.dot_general(keys, query, along, preferred_element_type=F32)
                    allowed = (place >= starts - first) & (place < ends - first)
                    probs = jnp.where(allowed, jnp.exp2(raw * (LOG2_E * scale) - log_total), 0.0)
                    grad_probs = lax.dot_general(values, grad, along, preferred_element_type=F32)
                    grad_scores = (probs * (grad_probs - delta)).astype(BF16)
                    acc[pl.ds(first, BLOCK), :head_dim] += (
                        jnp.dot(grad_scores, query, preferred_element_type=F32) * scale
                    )
                    acc[pl.ds(first, BLOCK), head_dim:] += jnp.dot(
                        probs.astype(BF16), grad, preferred_element_type=F32
                    )
                    return grad_query + lax.dot_general(keys, grad_scores, across, preferred_element_type=F32)

                grad_query = lax.fori_loop(
                    first_block(net.z * blocks + b, seq_len),
                    net.z * blocks + b + 1,
                    body,
                    jnp.zeros((head_dim, tall), F32),
                )
                grad_query = jnp.transpose(grad_query * scale).astype(BF16)
                for h in range(heads):
                    grad_queries[m, rows, h * head_dim : (h + 1) * head_dim] = grad_query[h * BLOCK : (h + 1) * BLOCK]

            return tile_at

        def from_chip(dx, dy):
            rows = net.chip_rows(dx, dy, own_rows)

            def tile_at(n):
                columns = pl.ds(pl.multiple_of(n * wide, wide), wide)
                face[:, rows, columns] = (
                    lax.dot_general(
                        grad_queries[:, rows, :].reshape(micro_count * 2 * own_rows, attn),
                        wq[columns, :],
                        along,
                        preferred_element_type=F32,
                    )
                    .astype(BF16)
                    .reshape(micro_count, 2 * own_rows, wide)
                )

            loop(width // wide, tile_at)

        columns_in = [
            net.copy(normed_in.at[:, :, pl.ds(n * wide, wide)], normed.at[n % 2]) for n in range(width // wide)
        ]

        def query_tile(n):
            columns_in[n].wait()

            def tile_at(_):
                part_query[n * wide : (n + 1) * wide, :] = lax.dot_general(
                    normed[n % 2].reshape(tokens, wide),
                    grad_queries[...].reshape(tokens, attn),
                    across,
                    preferred_element_type=F32,
                ).astype(BF16)

            loop(1, tile_at)
            if n + 2 < width // wide:
                columns_in[n + 2].start()

        def main():
            yield from gather.run(net, [low], [face], [])
            for at in order[2:]:
                loads[at].wait()
            loop(micro_count, mix_tile)
            yield
            for m in range(micro_count):
                acc[...] = jnp.zeros_like(acc)
                loop(blocks, attn_tile(m))
                for k in range(nz):
                    grad_keys[m * nz + k] = acc[k * face_rows : (k + 1) * face_rows, :].astype(BF16)
                yield
            loop(width // wide, attn_out_tile)
            weave.add("w", whole.run(net, [grad_keys], [keys_out], slots["w"]))
            weave.step("w")
            weave.add("q", scatter_q.run(net, [face], [from_out], slots["q"], from_chip))
            weave.step("q")
            for n in range(width // wide):
                query_tile(n)
            weave.add("a", line_a.run(net, [part_out, part_query], line_outs[1:], slots["a"]))
            weave.step("a")

        weave.add("m", main())
        weave.step("m")
        for at in order:
            loads[at].start()
        for copy in columns_in[:2]:
            copy.start()
        for at in order[:2]:
            loads[at].wait()
        weave.add("e", line_e.run(net, expand, line_outs[:1], slots["e"]))
        weave.step("e")
        weave.add("r", scatter_r.run(net, [reduced_in], [reduced_out], slots["r"]))
        for name in "".join(BACK_ORDER):
            weave.step(name)
        for name in "mwqrea":
            weave.finish(name)

    ins = [low, reduced, normed, *given]
    specs = [IN_VMEM] + [ANY] * (len(ins) - 1)
    return launch(
        body, ins, specs, outs, scratch, plans, nz, ny, collective_id, "back_block", extra_locals=len(given) + width // wide, vmem=62
    )


def end_block(inputs, normed_own, grad_middle, from_query, grad_keys, wkv, norms, grad_norm_two, nz, ny, collective_id):
    micro_count, own_rows, width = inputs.shape
    rows_all = micro_count * own_rows
    side = grad_keys.shape[-1]
    ranks = 4 * ny
    own_width = width // (nz * ranks)
    step = min(32, own_rows)
    part = jax.ShapeDtypeStruct((nz, width // nz, side), BF16)
    small = jax.ShapeDtypeStruct((ranks, nz, 8, 128), F32)
    quick, tiny = QuickScatter(part, nz, ny), SmallScatter(small, nz, ny)
    plans = [quick, tiny]
    outs = [(jax.ShapeDtypeStruct(inputs.shape, F32), IN_VMEM)] + quick.outs + tiny.outs
    scratch = [
        pltpu.VMEM((rows_all, side), BF16),
        pltpu.VMEM(part.shape, BF16),
        pltpu.VMEM(small.shape, F32),
        pltpu.VMEM((2, step, width), F32),
    ] + quick.scratch + tiny.scratch

    def body(net, ins, outs, scratch):
        inputs, n_own, grad_middle, from_query, grad_keys, wkv, norms, grad_norm_two = ins
        grad_out, keyval_out, small_out = outs
        low_keys, part, small, sums, *slots = scratch
        weave = Weave()

        def place(at):
            m, first = lax.div(at, own_rows // step), lax.rem(at, own_rows // step) * step
            rows = pl.ds(pl.multiple_of(first, step), step)
            return m, rows, pl.ds(pl.multiple_of(at * step, step), step)

        def unit_rows(m, rows):
            values = inputs[m, rows, :].astype(F32)
            centered = values - jnp.mean(values, axis=-1, keepdims=True)
            spread = lax.rsqrt(jnp.mean(centered * centered, axis=-1, keepdims=True) + EPSILON)
            return centered * spread, spread

        def first_rows(at):
            m, rows, flat = place(at)
            low_keys[flat, :] = grad_keys[m, rows, :].astype(BF16)

        def keyval_tile(k):
            columns = pl.ds(pl.multiple_of(k * (width // nz), width // nz), width // nz)
            part[k] = lax.dot_general(
                n_own[:, :, columns].reshape(rows_all, width // nz),
                low_keys[...],
                (((0,), (0,)), ((), ())),
                preferred_element_type=F32,
            ).astype(BF16)

        def last_rows(at):
            m, rows, flat = place(at)
            unit, spread = unit_rows(m, rows)
            grad = from_query[m, rows, :] + lax.dot_general(
                low_keys[flat, :], wkv[...], (((1,), (1,)), ((), ())), preferred_element_type=F32
            )
            sums[0] += grad * unit
            sums[1] += grad
            turned = grad * norms[0:1, :]
            inner = jnp.mean(turned * unit, axis=-1, keepdims=True)
            grad_out[m, rows, :] = grad_middle[m, rows, :] + spread * (
                turned - jnp.mean(turned, axis=-1, keepdims=True) - unit * inner
            )

        count = rows_all // step
        loop(count, first_rows)
        loop(nz, keyval_tile)
        weave.add("q", quick.run(net, [part], [keyval_out], slots[: len(quick.scratch)]))
        for _ in range(2 * ny + 1):
            weave.step("q")
        sums[...] = jnp.zeros_like(sums)
        loop(count, last_rows)
        rows = [jnp.sum(sums[k], axis=0, keepdims=True) for k in (0, 1)]
        rows += [jnp.sum(grad_norm_two[k], axis=0, keepdims=True) for k in (0, 1)]
        rows = jnp.concatenate(rows + [jnp.zeros((4, width), F32)], axis=0)
        for line in range(nz):
            for rank in range(ranks):
                first = (line * ranks + rank) * own_width // 128 * 128
                small[rank, line] = rows[:, first : first + 128]
        weave.add("s", tiny.run(net, [small], [small_out], slots[len(quick.scratch) :]))
        for name in "sqsqs":
            weave.step(name)
        for name in "qs":
            weave.finish(name)

    ins = [inputs, normed_own, grad_middle, from_query, grad_keys, wkv, norms, grad_norm_two]
    return launch(body, ins, [IN_VMEM] * len(ins), outs, scratch, plans, nz, ny, collective_id, "end_block")


def widen(arrays, first, second):
    steps = 4
    lead, rows, width = first.shape

    def kernel(*refs):
        sources, (one, two), targets = refs[: len(arrays)], refs[len(arrays) : len(arrays) + 2], refs[len(arrays) + 2 :]
        for source, target in zip(sources, targets):
            target[...] = source[...].astype(F32)
        targets[-1][...] = (one[...] + two[...]).astype(BF16)

    specs = [pl.BlockSpec((array.shape[0] // steps, array.shape[1]), lambda step: (step, 0)) for array in arrays]
    wide = pl.BlockSpec((lead, rows // steps, width), lambda step: (0, step, 0))
    return pl.pallas_call(
        kernel,
        out_shape=[jax.ShapeDtypeStruct(array.shape, F32) for array in arrays]
        + [jax.ShapeDtypeStruct(first.shape, BF16)],
        grid=(steps,),
        in_specs=specs + [wide, wide],
        out_specs=specs + [wide],
        compiler_params=pltpu.CompilerParams(vmem_limit_bytes=60 << 20),
        name="widen",
    )(*arrays, first, second)


def local(
    inputs,
    cotangent,
    doc_ids,
    attn_gain,
    attn_shift,
    w_query,
    w_keyval,
    w_attn_out,
    mlp_gain,
    mlp_shift,
    w_expand,
    w_reduce,
):
    nz = lax.axis_size("dp") // 2
    tensor_count = lax.axis_size("tensor")
    ny = tensor_count // 2
    ranks = 2 * tensor_count
    micro_count, own_rows, width = inputs.shape
    face_rows = own_rows * ranks
    tokens = micro_count * face_rows
    seq_len = doc_ids.shape[1]
    head_dim = w_keyval.shape[1] // 2
    heads = w_query.shape[1] // (2 * head_dim)
    on = (nz, ny)

    gains = jnp.concatenate([attn_gain, attn_shift, mlp_gain, mlp_shift])[None, :]
    kept, rest = front_block(
        inputs,
        cotangent,
        w_query,
        w_attn_out,
        w_keyval,
        w_expand,
        gains,
        doc_ids,
        *on,
        collective_id=1,
        head_dim=head_dim,
    )
    normed, wkv, wq, expand_given, queries, keys_vals, mixed, log_total, limits, normed_own = kept
    norms, cot_face, wo, wexp_first = rest
    middle, grad_middle, low_middle, grad_norm_two, part_expand_a, part_expand_b, reduced, grad_reduce = mlp_block(
        mixed, wo, inputs, cotangent, cot_face, norms, wexp_first, (w_expand, expand_given), (w_reduce,), *on, collective_id=3
    )
    reduced, from_query, grad_keys, grad_expand, grad_attn_out, grad_query = back_block(
        low_middle,
        reduced,
        [part_expand_a, part_expand_b],
        mixed,
        wo,
        wq,
        normed,
        queries,
        keys_vals,
        log_total,
        limits,
        *on,
        collective_id=6,
        head_dim=head_dim,
    )
    grad_inputs, grad_keyval, small = end_block(
        inputs, normed_own, grad_middle, from_query, grad_keys, wkv, norms, grad_norm_two, *on, collective_id=8
    )
    own_width = width // (nz * ranks)
    device = lax.axis_index("dp") * tensor_count + lax.axis_index("tensor")
    small = lax.dynamic_slice_in_dim(small[:4], device * own_width % 128, own_width, axis=1)

    grad_query, grad_attn_out, grad_expand, grad_reduce, outputs = widen(
        [grad_query, grad_attn_out, grad_expand, grad_reduce], middle, reduced
    )
    return (
        outputs,
        grad_inputs,
        small[0],
        small[1],
        grad_query,
        grad_keyval,
        grad_attn_out,
        small[2],
        small[3],
        grad_expand,
        grad_reduce,
    )


def solution(mesh):
    placed = (
        P(None, ("dp", "tensor"), None),
        P(None, ("dp", "tensor"), None),
        P(),
        P("dp"),
        P("dp"),
        P("dp", "tensor"),
        P("dp", None),
        P("tensor", "dp"),
        P("dp"),
        P("dp"),
        P("dp", "tensor"),
        P("tensor", "dp"),
    )
    return jax.shard_map(
        local,
        mesh=mesh,
        in_specs=placed,
        out_specs=(
            P(None, ("dp", "tensor"), None),
            P(None, ("dp", "tensor"), None),
            P(("dp", "tensor")),
            P(("dp", "tensor")),
            P("dp", "tensor"),
            P(("dp", "tensor"), None),
            P("tensor", "dp"),
            P(("dp", "tensor")),
            P(("dp", "tensor")),
            P("dp", "tensor"),
            P("tensor", "dp"),
        ),
        check_vma=False,
    )
```
